32 devices in a mesh: depth: 2 (over core), dp: 16 (over z, y, x).
Axes of the slice: x: 2, y: 2, z: 4, core: 2. Of those that a mesh axis runs over, the one named last changes fastest.
Arguments:
- inputs: bfloat16 [64, 512, 768], P(('depth', 'dp')), may hold values from -6 to 6
- output_gradient: bfloat16 [64, 512, 768], P(('depth', 'dp')), may hold values from -6 to 6
- keep: int32 [64], P(('depth', 'dp')), may hold values 0 or 1
- lengths: int32 [64], P(('depth', 'dp')), may hold values from 64 to 512
- routes: int32 [64], P(('depth', 'dp')), may hold values from 0 to 1
- attn_weights: float32 [256, 96, 96], P(('depth', 'dp'))
- attn_stats: float32 [256, 2, 96, 96], P(('depth', 'dp'))
- attn_roots: float32 [256, 2, 96, 96], P(('depth', 'dp'))
- attn_momentum: float32 [256, 96, 96], P(('depth', 'dp')), may hold values from -0.005859375 to 0.005859375
- ffn_weights: float32 [512, 96, 96], P(('depth', 'dp'))
- ffn_stats: float32 [512, 2, 96, 96], P(('depth', 'dp'))
- ffn_roots: float32 [512, 2, 96, 96], P(('depth', 'dp'))
- ffn_momentum: float32 [512, 96, 96], P(('depth', 'dp')), may hold values from -0.005859375 to 0.005859375
- vec_weights: float32 [9216], P(('depth', 'dp'))
- vec_first: float32 [9216], P(('depth', 'dp')), may hold values from -0.0012207031 to 0.0012207031
- vec_second: float32 [9216], P(('depth', 'dp')), may hold values from 5.644054e-10 to 2.2576216e-09
Outputs:
- out: bfloat16 [64, 512, 768], P(('depth', 'dp'))
- in_grad: bfloat16 [64, 512, 768], P(('depth', 'dp'))
- grad_norm: float32 [], replicated
- attn_stats_new: float32 [256, 2, 96, 96], P(('depth', 'dp'))
- attn_momentum_new: float32 [256, 96, 96], P(('depth', 'dp'))
- attn_weights_new: float32 [256, 96, 96], P(('depth', 'dp'))
- ffn_stats_new: float32 [512, 2, 96, 96], P(('depth', 'dp'))
- ffn_momentum_new: float32 [512, 96, 96], P(('depth', 'dp'))
- ffn_weights_new: float32 [512, 96, 96], P(('depth', 'dp'))
- vec_first_new: float32 [9216], P(('depth', 'dp'))
- vec_second_new: float32 [9216], P(('depth', 'dp'))
- vec_weights_new: float32 [9216], P(('depth', 'dp'))
The draws below stay inside these ranges and needn't reach their ends.
All inputs are finite; a program needn't handle non-finite values. No bound on the sum of `keep` on one device may be relied on, other than what follows from the above.
Results may differ from the reference program's by a relative error of at most 0.012.
The reference program's roundings to bfloat16 on the way count: a program that leaves them out, or rounds other values in their place, can miss the bound.
Values may be sent and summed in bfloat16 or wider, within the bound.
A program may use at most 192 MiB of HBM per device.

```python
import math
import jax
import jax.numpy as jnp
from jax import lax

D = 768
HEADS = 12
HEAD = 64
FF = 3072
LEN = 512
MINLEN = 64
SEQ_DEV = 2
BLOCK = 96
STEP = 10
SEQS = 64
NBA = 256
NBF = 512
VECS = 9216
PARAMS = 7087104


def loguniform_draw(key, shape, lower, upper):
    return jnp.exp(jax.random.uniform(key, shape, jnp.float32, jnp.log(lower), jnp.log(upper)))


def square_blocks(key, count, level, lower, upper):
    first, second = jax.random.split(key)
    noise = jax.random.normal(first, (count, 2, BLOCK, BLOCK), jnp.float32)
    symmetric = (noise + jnp.swapaxes(noise, 2, 3)) * (0.4 / (2.0 * BLOCK) ** 0.5)
    diagonal = loguniform_draw(second, (count, 2, BLOCK, 1), lower, upper)
    return level * (diagonal * jnp.eye(BLOCK, dtype=jnp.float32) + symmetric)


def draw_lengths(key, part):
    drawn = jax.random.randint(key, (SEQS,), MINLEN, LEN + 1, dtype=jnp.int32)
    return drawn.at[0].set(LEN).at[1].set(MINLEN)


def draw_attn_weights(key, part):
    count = 4 * D * D // (BLOCK * BLOCK)
    noise = jax.random.normal(key, (count, BLOCK, BLOCK), jnp.float32) * D ** (-0.5)
    order = jnp.arange(count)[:, None, None]
    return noise * jnp.where(order >= 3 * count // 4, (LEN / 4.0) ** 0.5, 1.0)


def draw_ffn_weights(key, part):
    count = 2 * D * FF // (BLOCK * BLOCK)
    noise = jax.random.normal(key, (count, BLOCK, BLOCK), jnp.float32)
    order = jnp.arange(count)[:, None, None]
    return noise * jnp.where(order >= count // 2, FF ** (-0.5), D ** (-0.5))


def draw_attn_stats(key, part):
    count = 4 * D * D // (BLOCK * BLOCK)
    return square_blocks(key, count, 0.05 / 0.95 * BLOCK / PARAMS, 1.0, 4.0)


def draw_ffn_stats(key, part):
    count = 2 * D * FF // (BLOCK * BLOCK)
    return square_blocks(key, count, 0.05 / 0.95 * BLOCK / PARAMS, 1.0, 4.0)


def draw_attn_roots(key, part):
    count = 4 * D * D // (BLOCK * BLOCK)
    return square_blocks(key, count, (PARAMS / BLOCK) ** 0.25, 0.5, 2.0)


def draw_ffn_roots(key, part):
    count = 2 * D * FF // (BLOCK * BLOCK)
    return square_blocks(key, count, 0.55 * (PARAMS / BLOCK) ** 0.25, 0.5, 2.0)


def draw_vec_weights(key, part):
    first, second, third = jax.random.split(key, 3)
    biases = jax.random.normal(first, (4 * D + FF,), jnp.float32) * 0.3
    gains = jax.random.uniform(second, (2, D), jnp.float32, 0.6, 1.4)
    shifts = jax.random.normal(third, (2, D), jnp.float32) * 0.3
    return jnp.concatenate([biases, gains[0], shifts[0], gains[1], shifts[1]])


def touch_ends(array, stream_key, low, high):
    index_at = [jax.random.randint(jax.random.fold_in(stream_key, axis), (), 0, length) for axis, length in enumerate(array.shape)]
    main_axis = array.shape.index(max(array.shape))
    next_to = index_at[:main_axis] + [(index_at[main_axis] + 1) % array.shape[main_axis]] + index_at[main_axis + 1:]
    return array.at[tuple(index_at)].set(low).at[tuple(next_to)].set(high)


def block_levels(own_key, dims, shards, low, high):
    def one(axis_at, blocks):
        heights = jax.random.uniform(jax.random.fold_in(jax.random.fold_in(own_key, 6), axis_at), (blocks,), jnp.float32, low / len(shards), high / len(shards))
        return jnp.repeat(jnp.exp(heights), dims[axis_at] // blocks).reshape((-1,) + (1,) * (len(dims) - axis_at - 1))

    factor_of = one(*shards[0])
    for cut in shards[1:]:
        factor_of = factor_of * one(*cut)
    return factor_of


def centred(own_key, extent, spread, reach, cuts=(), kind=jnp.bfloat16):
    entries = spread * jax.random.normal(own_key, extent, jnp.float32)
    if cuts:
        entries = entries * block_levels(own_key, extent, cuts, -0.22, 0.18)
    return jnp.clip(entries, -reach, reach).astype(kind)


def setup_inputs(seed: int = 0) -> dict:
    key_list = jax.random.split(jax.random.key(seed), 17)
    inputs = centred(key_list[0], (SEQS, LEN, D), 1.0, 6.0, ((0, 32),))
    output_gradient = centred(key_list[1], (SEQS, LEN, D), 1.0, 6.0, ((0, 32),))
    keep = touch_ends((jax.random.randint(key_list[2], (SEQS,), 0, 5) < 4).astype(jnp.int32), jax.random.fold_in(key_list[2], 1), 0, 1)
    lengths = draw_lengths(jax.random.fold_in(key_list[16], 71), 0)
    routes = touch_ends(jax.random.randint(key_list[4], (SEQS,), 0, SEQ_DEV), jax.random.fold_in(key_list[4], 1), 0, SEQ_DEV - 1).astype(jnp.int32)
    attn_weights = draw_attn_weights(jax.random.fold_in(key_list[16], 71), 0)
    attn_stats = draw_attn_stats(jax.random.fold_in(key_list[16], 71), 0)
    attn_roots = draw_attn_roots(jax.random.fold_in(key_list[16], 71), 0)
    attn_momentum = centred(key_list[8], (NBA, BLOCK, BLOCK), (PARAMS ** -0.5), 0.005859375, ((0, 32),), jnp.float32)
    ffn_weights = draw_ffn_weights(jax.random.fold_in(key_list[16], 71), 0)
    ffn_stats = draw_ffn_stats(jax.random.fold_in(key_list[16], 71), 0)
    ffn_roots = draw_ffn_roots(jax.random.fold_in(key_list[16], 71), 0)
    ffn_momentum = centred(key_list[12], (NBF, BLOCK, BLOCK), (PARAMS ** -0.5), 0.005859375, ((0, 32),), jnp.float32)
    vec_weights = draw_vec_weights(jax.random.fold_in(key_list[16], 71), 0)
    vec_first = centred(key_list[14], (VECS,), (0.22 * PARAMS ** -0.5), 0.0012207031, ((0, 32),), jnp.float32)
    vec_second = jnp.clip(jnp.exp(math.log(2.2576216451852815e-09) - 1.3862944 * jax.random.uniform(key_list[15], (VECS,), jnp.float32) ** block_levels(key_list[15], (VECS,), ((0, 32),), -0.2, 0.2)), 5.644054112963204e-10, 2.2576216451852815e-09)
    return {"inputs": inputs, "output_gradient": output_gradient, "keep": keep, "lengths": lengths, "routes": routes, "attn_weights": attn_weights, "attn_stats": attn_stats, "attn_roots": attn_roots, "attn_momentum": attn_momentum, "ffn_weights": ffn_weights, "ffn_stats": ffn_stats, "ffn_roots": ffn_roots, "ffn_momentum": ffn_momentum, "vec_weights": vec_weights, "vec_first": vec_first, "vec_second": vec_second}


@jax.custom_vjp
def low(v):
    return lax.optimization_barrier(v.astype(jnp.bfloat16)).astype(jnp.float32)

@jax.custom_vjp
def low_back(v):
    return v

def low_keep(v):
    return (low(v), None)

def low_pass(kept, grad):
    return (grad,)

def back_keep(v):
    return (v, None)

def back_low(kept, grad):
    return (low(grad),)
low.defvjp(low_keep, low_pass)
low_back.defvjp(back_keep, back_low)
norm_floor = 1e-05
masked_fill = -1000000000.0
momentum_decay = 0.9
stat_decay = 0.95
matrix_rate = 1.0
matrix_decay = 0.01
clip_bound = 1.0
first_decay = 0.9
second_decay = 0.999
vector_rate = 0.5
adam_floor = 1e-08

def serve_flags(keep_rows, route_rows):
    count = keep_rows.shape[-1]
    order = jnp.arange(count, dtype=jnp.int32)
    earlier = (order[None, :] < order[:, None]).astype(jnp.int32)
    same = (route_rows[:, :, None] == route_rows[:, None, :]).astype(jnp.int32)
    clash = lax.optimization_barrier(jnp.sum(same * earlier[None, :, :] * keep_rows[:, None, :], axis=2))
    return keep_rows * (clash == 0).astype(jnp.int32)

def to_matrix(blocks, height, breadth):
    edge = blocks.shape[-1]
    shaped = blocks.reshape(height // edge, breadth // edge, edge, edge)
    return shaped.transpose(0, 2, 1, 3).reshape(height, breadth)

def to_blocks(matrix):
    height, breadth = matrix.shape
    shaped = matrix.reshape(height // BLOCK, BLOCK, breadth // BLOCK, BLOCK)
    return shaped.transpose(0, 2, 1, 3).reshape(-1, BLOCK, BLOCK)

def norm_rows(resid, gain, shift):
    center = resid - lax.optimization_barrier(jnp.mean(resid, axis=-1, keepdims=True))
    variance = lax.optimization_barrier(jnp.mean(center * center, axis=-1, keepdims=True))
    return center * lax.rsqrt(variance + norm_floor) * gain + shift

def layer(block_in, group_len, query_w, key_w, value_w, output_w, hidden_w, return_weight, vectors):
    count = block_in.shape[0]
    tokens = count * LEN
    scale = 1.0 / math.sqrt(HEAD)
    highest = lax.Precision.HIGHEST
    query_w = low(query_w)
    key_w = low(key_w)
    value_w = low(value_w)
    output_w = low(output_w)
    hidden_w = low(hidden_w)
    return_weight = low(return_weight)
    vectors = low(vectors)
    q_bias = vectors[0:D]
    v_bias = vectors[D:2 * D]
    out_bias = vectors[2 * D:3 * D]
    hidden_bias = vectors[3 * D:3 * D + FF]
    ffn_bias = vectors[3 * D + FF:4 * D + FF]
    gain_one = vectors[4 * D + FF:5 * D + FF]
    shift_one = vectors[5 * D + FF:6 * D + FF]
    gain_two = vectors[6 * D + FF:7 * D + FF]
    shift_two = vectors[7 * D + FF:8 * D + FF]
    flat = block_in.reshape(tokens, D)
    query = low(low_back(jnp.dot(flat, query_w, precision=highest) + q_bias))
    keys = low(low_back(jnp.dot(flat, key_w, precision=highest)))
    values = low(low_back(jnp.dot(flat, value_w, precision=highest) + v_bias))
    four = (count, LEN, HEADS, HEAD)
    scores = jnp.einsum('gqhe,gkhe->ghqk', query.reshape(four), keys.reshape(four), precision=highest)
    scores = low_back(scores * scale)
    visible = jnp.arange(LEN, dtype=jnp.int32)[None, :] < group_len[:, None]
    scores = jnp.where(visible[:, None, None, :], scores, masked_fill)
    probs = low(jax.nn.softmax(scores, axis=-1))
    context = jnp.einsum('ghqk,gkhe->gqhe', probs, values.reshape(four), precision=highest).reshape(tokens, D)
    context = low(low_back(context))
    attended = low_back(jnp.dot(context, output_w, precision=highest) + out_bias)
    hidden_in = norm_rows(flat + attended, gain_one, shift_one)
    before = low_back(jnp.dot(low(hidden_in), hidden_w, precision=highest) + hidden_bias)
    active = low(jax.nn.gelu(before, approximate=False))
    branch = low_back(jnp.dot(active, return_weight, precision=highest) + ffn_bias)
    result = norm_rows(hidden_in + branch, gain_two, shift_two)
    return result.reshape(count, LEN, D)

def shampoo(weights, stats, roots, momentum, grads, factor):
    highest = lax.Precision.HIGHEST
    clipped = grads * factor
    moment = momentum_decay * momentum + clipped
    left = jnp.einsum('nab,ncb->nac', clipped, clipped, precision=highest)
    right = jnp.einsum('nab,nac->nbc', clipped, clipped, precision=highest)
    fresh = stat_decay * stats + (1.0 - stat_decay) * jnp.stack([left, right], axis=1)
    turned = jnp.einsum('nab,nbc->nac', roots[:, 0], moment, precision=highest)
    turned = jnp.einsum('nab,nbc->nac', turned, roots[:, 1], precision=highest)
    updated = weights - matrix_rate * (turned + matrix_decay * weights)
    return (fresh, moment, updated)

def adam_step(weights, first, second, grads, factor):
    clipped = grads * factor
    first_new = first_decay * first + (1.0 - first_decay) * clipped
    second_new = second_decay * second + (1.0 - second_decay) * clipped * clipped
    first_hat = first_new / (1.0 - first_decay ** STEP)
    second_hat = second_new / (1.0 - second_decay ** STEP)
    updated = weights - vector_rate * first_hat / (jnp.sqrt(second_hat) + adam_floor)
    return (first_new, second_new, updated)

def reference(inputs, output_gradient, keep, lengths, routes, attn_weights, attn_stats, attn_roots, attn_momentum, ffn_weights, ffn_stats, ffn_roots, ffn_momentum, vec_weights, vec_first, vec_second):
    grid = (D // BLOCK) ** 2
    half_ffn = D * FF // (BLOCK * BLOCK)
    matrices = (to_matrix(attn_weights[0:grid], D, D), to_matrix(attn_weights[grid:2 * grid], D, D), to_matrix(attn_weights[2 * grid:3 * grid], D, D), to_matrix(attn_weights[3 * grid:4 * grid], D, D), to_matrix(ffn_weights[0:half_ffn], D, FF), to_matrix(ffn_weights[half_ffn:], FF, D), vec_weights)
    served = serve_flags(keep.reshape(-1, SEQ_DEV), routes.reshape(-1, SEQ_DEV)).reshape(SEQS)
    served_f = served.astype(jnp.float32)[:, None, None]
    group = math.gcd(SEQS, max(1, 4096 // LEN))
    turns = SEQS // group
    rows_all = inputs.astype(jnp.float32).reshape(turns, group, LEN, D)
    cot_all = (output_gradient.astype(jnp.float32) * served_f).reshape(turns, group, LEN, D)
    len_all = lengths.reshape(turns, group)

    def one_group(carry, pieces):
        rows_in, grad_in, group_len = pieces

        def forward(rows, *params):
            return layer(rows, group_len, *params)
        result, pullback = jax.vjp(forward, rows_in, *matrices)
        grads = pullback(grad_in)
        summed = tuple((total + piece for total, piece in zip(carry, grads[1:])))
        return (summed, (result, grads[0]))
    zeros = tuple((jnp.zeros_like(matrix) for matrix in matrices))
    totals, (results, input_grads) = lax.scan(one_group, zeros, (rows_all, cot_all, len_all))
    results = results.reshape(SEQS, LEN, D)
    input_grads = input_grads.reshape(SEQS, LEN, D)
    out = (served_f * results + (1.0 - served_f) * inputs.astype(jnp.float32)).astype(jnp.bfloat16)
    in_grad = (served_f * input_grads + (1.0 - served_f) * output_gradient.astype(jnp.float32)).astype(jnp.bfloat16)
    grad_query_w, grad_key_w, grad_value_w, grad_output_w, grad_hidden_w, gradient_return_weight, gradient_vector = totals
    attn_grad = jnp.concatenate([to_blocks(grad_query_w), to_blocks(grad_key_w), to_blocks(grad_value_w), to_blocks(grad_output_w)], axis=0)
    ffn_grad = jnp.concatenate([to_blocks(grad_hidden_w), to_blocks(gradient_return_weight)], axis=0)
    square = jnp.sum(attn_grad * attn_grad) + jnp.sum(ffn_grad * ffn_grad) + jnp.sum(gradient_vector * gradient_vector)
    grad_norm = jnp.sqrt(square)
    factor = clip_bound / jnp.maximum(grad_norm, clip_bound)
    attn_fresh, attn_moment, attn_updated = shampoo(attn_weights, attn_stats, attn_roots, attn_momentum, attn_grad, factor)
    ffn_fresh, ffn_moment, ffn_updated = shampoo(ffn_weights, ffn_stats, ffn_roots, ffn_momentum, ffn_grad, factor)
    first_new, second_new, vec_updated = adam_step(vec_weights, vec_first, vec_second, gradient_vector, factor)
    return (out, in_grad, grad_norm, attn_fresh, attn_moment, attn_updated, ffn_fresh, ffn_moment, ffn_updated, first_new, second_new, vec_updated)
```

```python
import functools
import math

import jax
import jax.numpy as jnp
from jax import lax
from jax.experimental import pallas as pl
from jax.experimental.pallas import tpu as pltpu
from jax.sharding import PartitionSpec as P

HEADS = 12
FF = 3072
BLOCK = 96
STEP = 10


norm_floor = 1e-05
masked_fill = -1000000000.0
momentum_decay = 0.9
stat_decay = 0.95
matrix_rate = 1.0
matrix_decay = 0.01
clip_bound = 1.0
first_decay = 0.9
second_decay = 0.999
vector_rate = 0.5
adam_floor = 1e-08


def serve_flags(keep_rows, route_rows):
    count = keep_rows.shape[-1]
    order = jnp.arange(count, dtype=jnp.int32)
    earlier = (order[None, :] < order[:, None]).astype(jnp.int32)
    same = (route_rows[:, :, None] == route_rows[:, None, :]).astype(jnp.int32)
    clash = jnp.sum(same * earlier[None, :, :] * keep_rows[:, None, :], axis=2)
    return keep_rows * (clash == 0).astype(jnp.int32)


def to_matrix(blocks, height, breadth):
    shaped = blocks.reshape(height // BLOCK, breadth // BLOCK, BLOCK, BLOCK)
    return shaped.transpose(0, 2, 1, 3).reshape(height, breadth)


def to_flat_blocks(matrix):
    height, breadth = matrix.shape
    shaped = matrix.reshape(height // BLOCK, BLOCK, breadth // BLOCK, BLOCK)
    return shaped.transpose(0, 2, 1, 3).reshape(-1, BLOCK * BLOCK)


def norm_parts(resid):
    center = resid - jnp.mean(resid, axis=-1, keepdims=True)
    factor = lax.rsqrt(jnp.mean(center * center, axis=-1, keepdims=True) + norm_floor)
    return (center * factor, factor)


def norm_back(grad_normed, normed, factor):
    middle = jnp.mean(grad_normed, axis=-1, keepdims=True)
    along = jnp.mean(grad_normed * normed, axis=-1, keepdims=True)
    return factor * (grad_normed - middle - normed * along)


def gelu_slope(value):
    cumulative = 0.5 * (1.0 + lax.erf(value * (1.0 / math.sqrt(2.0))))
    density = jnp.exp(-0.5 * value * value) * (1.0 / math.sqrt(2.0 * math.pi))
    return cumulative + value * density


def product(left, right):
    return jnp.dot(left, right, preferred_element_type=jnp.float32)


def contract_rows(left, right):
    return lax.dot_general(
        left, right, (((0,), (0,)), ((), ())), preferred_element_type=jnp.float32
    )


def times_transpose(left, right):
    return lax.dot_general(
        left, right, (((1,), (1,)), ((), ())), preferred_element_type=jnp.float32
    )


def masked_scores(query, keys, visible_len):
    scale = 1.0 / math.sqrt(query.shape[-1])
    scores = jnp.einsum("qhe,khe->hqk", query, keys, preferred_element_type=jnp.float32) * scale
    visible = jnp.arange(keys.shape[0], dtype=jnp.int32) < visible_len
    return jnp.where(visible[None, None, :], scores, masked_fill)


def attend_forward(pieces):
    query, keys, values, visible_len = pieces
    scores = masked_scores(query, keys, visible_len)
    peak = jnp.max(scores, axis=-1, keepdims=True)
    expo = jnp.exp(scores - peak)
    total = jnp.sum(expo, axis=-1, keepdims=True)
    probs_low = (expo / total).astype(jnp.bfloat16)
    context = jnp.einsum("hqk,khe->qhe", probs_low, values, preferred_element_type=jnp.float32)
    return (context, peak[..., 0] + jnp.log(total[..., 0]))


def attend_backward(pieces):
    query, keys, values, grad_ctx, log_total, visible_len = pieces
    scale = 1.0 / math.sqrt(query.shape[-1])
    scores = masked_scores(query, keys, visible_len)
    probs = jnp.exp(scores - log_total[..., None])
    probs_low = probs.astype(jnp.bfloat16)
    grad_probs = jnp.einsum("qhe,khe->hqk", grad_ctx, values, preferred_element_type=jnp.float32)
    grad_values = jnp.einsum(
        "hqk,qhe->khe", probs_low, grad_ctx, preferred_element_type=jnp.float32
    )
    along = jnp.sum(probs * grad_probs, axis=-1, keepdims=True)
    grad_scores = (probs * (grad_probs - along)).astype(jnp.bfloat16)
    grad_query = (
        jnp.einsum("hqk,khe->qhe", grad_scores, keys, preferred_element_type=jnp.float32) * scale
    )
    grad_keys = (
        jnp.einsum("hqk,qhe->khe", grad_scores, query, preferred_element_type=jnp.float32) * scale
    )
    return (grad_query, grad_keys, grad_values)


def shampoo(weights, stats, roots, momentum, grads, factor):
    highest = lax.Precision.HIGHEST
    clipped = grads * factor
    moment = momentum_decay * momentum + clipped
    left = jnp.einsum("nab,ncb->nac", clipped, clipped, precision=highest)
    right = jnp.einsum("nab,nac->nbc", clipped, clipped, precision=highest)
    fresh = stat_decay * stats + (1.0 - stat_decay) * jnp.stack([left, right], axis=1)
    turned = jnp.einsum("nab,nbc->nac", roots[:, 0], moment, precision=highest)
    turned = jnp.einsum("nab,nbc->nac", turned, roots[:, 1], precision=highest)
    updated = weights - matrix_rate * (turned + matrix_decay * weights)
    return (fresh, moment, updated)


def adam_step(weights, first, second, grads, factor):
    clipped = grads * factor
    first_new = first_decay * first + (1.0 - first_decay) * clipped
    second_new = second_decay * second + (1.0 - second_decay) * clipped * clipped
    first_hat = first_new / (1.0 - first_decay**STEP)
    second_hat = second_new / (1.0 - second_decay**STEP)
    updated = weights - vector_rate * first_hat / (jnp.sqrt(second_hat) + adam_floor)
    return (first_new, second_new, updated)


def per_device_general(
    inputs,
    output_gradient,
    keep,
    lengths,
    routes,
    attn_weights,
    attn_stats,
    attn_roots,
    attn_momentum,
    ffn_weights,
    ffn_stats,
    ffn_roots,
    ffn_momentum,
    vec_weights,
    vec_first,
    vec_second,
):
    slots, seq_len, width = inputs.shape
    tokens = slots * seq_len
    head_size = width // HEADS
    hidden_width = FF
    depth_count = lax.axis_size("depth")
    peer_slots = slots // depth_count
    grid = (width // BLOCK) ** 2
    half_ffn = width * hidden_width // (BLOCK * BLOCK)
    area = BLOCK * BLOCK
    low_type = jnp.bfloat16
    attn_flat = attn_weights.reshape(-1, area).astype(low_type)
    ffn_flat = ffn_weights.reshape(-1, area).astype(low_type)
    attn_all, ffn_all, vec_all = (
        lax.all_gather(attn_flat, ("depth", "dp"), axis=0, tiled=True),
        lax.all_gather(ffn_flat, ("depth", "dp"), axis=0, tiled=True),
        lax.all_gather(vec_weights.astype(low_type), ("depth", "dp"), axis=0, tiled=True),
    )
    table_keep, table_len, table_route = (
        lax.all_gather(keep, "depth", axis=0, tiled=True),
        lax.all_gather(lengths, "depth", axis=0, tiled=True),
        lax.all_gather(routes, "depth", axis=0, tiled=True),
    )
    mine = serve_flags(keep[None, :], routes[None, :])[0]
    slot_order = jnp.arange(slots, dtype=jnp.int32)
    selection = ((routes[None, :] == slot_order[:, None]).astype(jnp.int32) * mine[None, :]).astype(
        low_type
    )
    outgoing_rows = jnp.einsum(
        "gz,zrp->grp", selection, inputs, preferred_element_type=jnp.float32
    ).astype(low_type)
    send_grad = jnp.einsum(
        "gz,zrp->grp", selection, output_gradient, preferred_element_type=jnp.float32
    ).astype(low_type)
    come_rows, come_grad = (
        lax.all_to_all(outgoing_rows, "depth", split_axis=0, concat_axis=0, tiled=True),
        lax.all_to_all(send_grad, "depth", split_axis=0, concat_axis=0, tiled=True),
    )
    all_keep = table_keep.reshape(depth_count, slots)
    all_route = table_route.reshape(depth_count, slots)
    all_len = table_len.reshape(depth_count, slots)
    all_served = serve_flags(all_keep, all_route)
    here = lax.axis_index("depth")
    source = slot_order // peer_slots
    target = here * peer_slots + slot_order % peer_slots
    source_hot = (source[:, None] == jnp.arange(depth_count, dtype=jnp.int32)[None, :]).astype(
        jnp.int32
    )
    match = (all_route[None, :, :] == target[:, None, None]).astype(jnp.int32) * all_served[
        None, :, :
    ]
    slot_len = jnp.sum(source_hot[:, :, None] * match * all_len[None, :, :], axis=(1, 2))
    visible_len = jnp.maximum(slot_len, 1)
    query_w = to_matrix(attn_all[0:grid], width, width)
    key_w = to_matrix(attn_all[grid : 2 * grid], width, width)
    value_w = to_matrix(attn_all[2 * grid : 3 * grid], width, width)
    output_w = to_matrix(attn_all[3 * grid : 4 * grid], width, width)
    vectors = vec_all.astype(jnp.float32)
    q_bias = vectors[0:width]
    v_bias = vectors[width : 2 * width]
    out_bias = vectors[2 * width : 3 * width]
    hidden_bias = vectors[3 * width : 3 * width + hidden_width]
    ffn_bias = vectors[3 * width + hidden_width : 4 * width + hidden_width]
    gain_one = vectors[4 * width + hidden_width : 5 * width + hidden_width]
    shift_one = vectors[5 * width + hidden_width : 6 * width + hidden_width]
    gain_two = vectors[6 * width + hidden_width : 7 * width + hidden_width]
    shift_two = vectors[7 * width + hidden_width : 8 * width + hidden_width]
    flat = come_rows.reshape(tokens, width)
    four = (slots, seq_len, HEADS, head_size)
    query = (product(flat, query_w) + q_bias).astype(low_type).reshape(four)
    keys = product(flat, key_w).astype(low_type).reshape(four)
    values = (product(flat, value_w) + v_bias).astype(low_type).reshape(four)
    context, log_total = lax.map(attend_forward, (query, keys, values, visible_len))
    context_low = context.reshape(tokens, width).astype(low_type)
    attended = product(context_low, output_w) + out_bias
    normed_one, factor_one = norm_parts(flat.astype(jnp.float32) + attended)
    hidden_in = normed_one * gain_one + shift_one
    hidden_low = hidden_in.astype(low_type)
    hidden_w = to_matrix(ffn_all[0:half_ffn], width, hidden_width)
    return_weight = to_matrix(ffn_all[half_ffn:], hidden_width, width)
    before = product(hidden_low, hidden_w) + hidden_bias
    active_low = jax.nn.gelu(before, approximate=False).astype(low_type)
    branch = product(active_low, return_weight) + ffn_bias
    normed_two, factor_two = norm_parts(hidden_in + branch)
    result_low = (normed_two * gain_two + shift_two).astype(low_type)
    grad_rows = come_grad.reshape(tokens, width).astype(jnp.float32)
    grad_gain_two = jnp.sum(grad_rows * normed_two, axis=0)
    grad_shift_two = jnp.sum(grad_rows, axis=0)
    grad_resid_two = norm_back(grad_rows * gain_two, normed_two, factor_two)
    grad_branch = grad_resid_two.astype(low_type)
    grad_ffn_bias = jnp.sum(grad_branch.astype(jnp.float32), axis=0)
    gradient_return_weight = contract_rows(active_low, grad_branch)
    grad_active = times_transpose(grad_branch, return_weight)
    grad_before = (grad_active * gelu_slope(before)).astype(low_type)
    grad_hidden_bias = jnp.sum(grad_before.astype(jnp.float32), axis=0)
    grad_hidden_w = contract_rows(hidden_low, grad_before)
    grad_hidden = times_transpose(grad_before, hidden_w) + grad_resid_two
    grad_gain_one = jnp.sum(grad_hidden * normed_one, axis=0)
    grad_shift_one = jnp.sum(grad_hidden, axis=0)
    grad_resid_one = norm_back(grad_hidden * gain_one, normed_one, factor_one)
    ffn_grad = jnp.concatenate(
        [to_flat_blocks(grad_hidden_w), to_flat_blocks(gradient_return_weight)], axis=0
    )
    grad_attended = grad_resid_one.astype(low_type)
    grad_out_bias = jnp.sum(grad_attended.astype(jnp.float32), axis=0)
    grad_output_w = contract_rows(context_low, grad_attended)
    grad_context = times_transpose(grad_attended, output_w).astype(low_type).reshape(four)
    grad_query, grad_keys, grad_values = lax.map(
        attend_backward, (query, keys, values, grad_context, log_total, visible_len)
    )
    grad_query = grad_query.reshape(tokens, width).astype(low_type)
    grad_keys = grad_keys.reshape(tokens, width).astype(low_type)
    grad_values = grad_values.reshape(tokens, width).astype(low_type)
    grad_q_bias = jnp.sum(grad_query.astype(jnp.float32), axis=0)
    grad_v_bias = jnp.sum(grad_values.astype(jnp.float32), axis=0)
    grad_query_w = contract_rows(flat, grad_query)
    grad_key_w = contract_rows(flat, grad_keys)
    grad_value_w = contract_rows(flat, grad_values)
    in_rows = (
        grad_resid_one
        + times_transpose(grad_query, query_w)
        + times_transpose(grad_keys, key_w)
        + times_transpose(grad_values, value_w)
    )
    attn_grad = jnp.concatenate(
        [
            to_flat_blocks(grad_query_w),
            to_flat_blocks(grad_key_w),
            to_flat_blocks(grad_value_w),
            to_flat_blocks(grad_output_w),
        ],
        axis=0,
    )
    vec_grad = jnp.concatenate(
        [
            grad_q_bias,
            grad_v_bias,
            grad_out_bias,
            grad_hidden_bias,
            grad_ffn_bias,
            grad_gain_one,
            grad_shift_one,
            grad_gain_two,
            grad_shift_two,
        ]
    )
    attn_share, ffn_share, vec_share = (
        lax.psum_scatter(attn_grad, ("depth", "dp"), scatter_dimension=0, tiled=True),
        lax.psum_scatter(ffn_grad, ("depth", "dp"), scatter_dimension=0, tiled=True),
        lax.psum_scatter(vec_grad, ("depth", "dp"), scatter_dimension=0, tiled=True),
    )
    returned_rows, returned_gradient = (
        lax.all_to_all(
            result_low.reshape(slots, seq_len, width),
            "depth",
            split_axis=0,
            concat_axis=0,
            tiled=True,
        ),
        lax.all_to_all(
            in_rows.astype(low_type).reshape(slots, seq_len, width),
            "depth",
            split_axis=0,
            concat_axis=0,
            tiled=True,
        ),
    )
    stay = (1 - mine).astype(jnp.float32)[:, None, None]
    out = (
        jnp.einsum("rx,rmp->xmp", selection, returned_rows, preferred_element_type=jnp.float32)
        + stay * inputs.astype(jnp.float32)
    ).astype(low_type)
    in_grad = (
        jnp.einsum("rx,rmp->xmp", selection, returned_gradient, preferred_element_type=jnp.float32)
        + stay * output_gradient.astype(jnp.float32)
    ).astype(low_type)
    square = (
        jnp.sum(attn_share * attn_share)
        + jnp.sum(ffn_share * ffn_share)
        + jnp.sum(vec_share * vec_share)
    )
    total = lax.psum(square, ("depth", "dp"))
    grad_norm = jnp.sqrt(total)
    factor = clip_bound / jnp.maximum(grad_norm, clip_bound)
    attn_square = attn_share.reshape(-1, BLOCK, BLOCK)
    ffn_square = ffn_share.reshape(-1, BLOCK, BLOCK)
    attn_fresh, attn_moment, attn_updated = shampoo(
        attn_weights, attn_stats, attn_roots, attn_momentum, attn_square, factor
    )
    ffn_fresh, ffn_moment, ffn_updated = shampoo(
        ffn_weights, ffn_stats, ffn_roots, ffn_momentum, ffn_square, factor
    )
    first_new, second_new, vec_updated = adam_step(
        vec_weights, vec_first, vec_second, vec_share, factor
    )
    return (
        out,
        in_grad,
        grad_norm,
        attn_fresh,
        attn_moment,
        attn_updated,
        ffn_fresh,
        ffn_moment,
        ffn_updated,
        first_new,
        second_new,
        vec_updated,
    )


MESH = pl.DeviceIdType.MESH
BF = jnp.bfloat16
F32 = jnp.float32


def place():
    d = lax.axis_index("depth")
    i = lax.axis_index("dp")
    x = i % 2
    y = (i // 2) % 2
    z = i // 4
    c = i % 4
    nx = i + 1 - 2 * x
    ny = i + 2 - 4 * y
    na = ny + d * (nx - ny)
    nb = nx + d * (ny - nx)
    return dict(d=d, i=i, z=z, c=c, na=na, nb=nb, ca=na % 4, cb=nb % 4, cd=3 - c)


def greet(p):
    barrier = pltpu.get_barrier_semaphore()
    peers = [(p["d"], p["na"]), (p["d"], p["nb"]), (1 - p["d"], p["i"])]
    peers += [(p["d"], ((p["z"] + k) % 4) * 4 + p["c"]) for k in (1, 2, 3)]
    for peer in peers:
        pl.semaphore_signal(barrier, inc=1, device_id=peer, device_id_type=MESH)
    pl.semaphore_wait(barrier, len(peers))


def remote(src, dst, send, recv, k, dev):
    return pltpu.make_async_remote_copy(src_ref=src, dst_ref=dst, send_sem=send.at[k], recv_sem=recv.at[k],
                                        device_id=dev, device_id_type=MESH)


class Spread:
    def __init__(self, p, own, out, send, recv, local):
        self.p, self.own, self.out, self.send, self.recv, self.local = p, own, out, send, recv, local
        self.sent = []

    def go(self, src, dst, k, dev):
        copy = remote(src, dst, self.send, self.recv, k, dev)
        copy.start()
        self.sent.append(copy)

    def start(self):
        p = self.p
        here = self.out.at[p["d"], p["z"], p["c"]]
        self.keep = pltpu.make_async_copy(self.own, here, self.local)
        self.keep.start()
        for k in (2, 1, 3):
            self.go(self.own, here, k - 1, (p["d"], ((p["z"] + k) % 4) * 4 + p["c"]))

    def wait(self, dst, k):
        remote(dst, dst, self.send, self.recv, k, (self.p["d"], self.p["na"])).wait_recv()

    def column(self, half, col):
        return self.out.at[half, :, col]

    def second(self):
        p = self.p
        self.keep.wait()
        for k in (1, 2, 3):
            self.wait(self.out.at[p["d"], (p["z"] + 4 - k) % 4, p["c"]], k - 1)
        mine = self.column(p["d"], p["c"])
        self.go(mine, mine, 3, (p["d"], p["na"]))
        self.go(mine, mine, 4, (p["d"], p["nb"]))
        self.go(mine, mine, 6, (1 - p["d"], p["i"]))

    def third(self):
        p = self.p
        got = self.column(p["d"], p["ca"])
        self.wait(got, 3)
        self.go(got, got, 5, (p["d"], p["nb"]))
        self.go(got, got, 8 - p["d"], (1 - p["d"], p["i"]))

    def fourth(self):
        p = self.p
        got = self.column(p["d"], p["cb"])
        self.wait(got, 4)
        self.go(got, got, 7 + p["d"], (1 - p["d"], p["i"]))

    def fifth(self):
        p = self.p
        got = self.column(p["d"], p["cd"])
        self.wait(got, 5)
        self.go(got, got, 9, (1 - p["d"], p["i"]))

    def sixth(self):
        p = self.p
        for k, col in ((6, p["c"]), (8 - p["d"], p["ca"]), (7 + p["d"], p["cb"]), (9, p["cd"])):
            self.wait(self.column(1 - p["d"], col), k)

    def drain(self):
        for copy in self.sent:
            copy.wait_send()


def gather_kernel(a, v, f, ga, gv, gf, *sems):
    p = place()
    greet(p)
    parts = [Spread(p, own, out, sems[3 * n], sems[3 * n + 1], sems[3 * n + 2])
             for n, (own, out) in enumerate(((a, ga), (v, gv), (f, gf)))]
    for s in parts:
        s.start()
    for s in parts[:2]:
        s.second()
    for s in parts[:2]:
        s.third()
    for s in parts[:2]:
        s.fourth()
    parts[2].second()
    for s in parts[:2]:
        s.fifth()
    parts[2].third()
    parts[2].fourth()
    parts[2].fifth()
    for s in parts:
        s.sixth()
    for s in parts:
        s.drain()


def gather(a, v, f):
    sem = [pltpu.SemaphoreType.DMA((10,)), pltpu.SemaphoreType.DMA((10,)), pltpu.SemaphoreType.DMA]
    return pl.pallas_call(
        gather_kernel,
        out_shape=[jax.ShapeDtypeStruct((2, 4, 4) + t.shape, t.dtype) for t in (a, v, f)],
        in_specs=[pl.BlockSpec(memory_space=pltpu.VMEM)] * 3,
        out_specs=[pl.BlockSpec(memory_space=pl.ANY)] * 3,
        scratch_shapes=sem * 3,
        compiler_params=pltpu.CompilerParams(collective_id=0, has_side_effects=True),
        name="weight_gather",
    )(a, v, f)


class Fold:
    def __init__(self, p, mine, pair, diag, flat, late, line, send, recv):
        self.p, self.mine, self.pair, self.diag, self.flat, self.late, self.line = p, mine, pair, diag, flat, late, line
        self.send, self.recv, self.sent = send, recv, []

    def go(self, src, dst, k, dev):
        copy = remote(src, dst, self.send, self.recv, k, dev)
        copy.start()
        self.sent.append(copy)

    def wait(self, dst, k):
        remote(dst, dst, self.send, self.recv, k, (self.p["d"], self.p["na"])).wait_recv()

    def add(self, dst, *others):
        total = dst[...].astype(F32)
        for o in others:
            total += o[...].astype(F32)
        dst[...] = total.astype(dst.dtype)

    def start(self):
        p = self.p
        self.go(self.mine.at[1 - p["d"]], self.pair, 0, (1 - p["d"], p["i"]))

    def second(self):
        p = self.p
        self.wait(self.pair, 0)
        for col, dst, k in ((p["cd"], self.diag, 1), (p["cb"], self.flat, 2)):
            self.add(self.pair.at[:, col], self.mine.at[p["d"], :, col])
            self.go(self.pair.at[:, col], dst, k, (p["d"], p["nb"]))
        for col in (p["ca"], p["c"]):
            self.add(self.pair.at[:, col], self.mine.at[p["d"], :, col])

    def third(self):
        p = self.p
        self.wait(self.diag, 1)
        src = self.pair.at[:, p["ca"]]
        self.add(src, self.diag)
        self.go(src, self.late, 3, (p["d"], p["na"]))

    def fourth(self):
        p = self.p
        self.wait(self.flat, 2)
        self.wait(self.late, 3)
        for k in (2, 1, 3, 0):
            dst = (p["z"] + k) % 4
            self.add(self.pair.at[dst, p["c"]], self.flat.at[dst], self.late.at[dst])
            if k:
                self.go(self.pair.at[dst, p["c"]], self.line.at[k - 1], 3 + k, (p["d"], dst * 4 + p["c"]))

    def fifth(self, out):
        p = self.p
        total = self.pair[p["z"], p["c"]].astype(F32)
        for k in (1, 2, 3):
            self.wait(self.line.at[k - 1], 3 + k)
            total += self.line[k - 1].astype(F32)
        out[...] = total

    def drain(self):
        for copy in self.sent:
            copy.wait_send()


def fold_scratch(shape, dtype):
    return [pltpu.VMEM((4, 4) + shape, dtype), pltpu.VMEM((4,) + shape, dtype), pltpu.VMEM((4,) + shape, dtype),
            pltpu.VMEM((4,) + shape, dtype), pltpu.VMEM((3,) + shape, dtype),
            pltpu.SemaphoreType.DMA((7,)), pltpu.SemaphoreType.DMA((7,))]


def greet_all(p):
    barrier = pltpu.get_barrier_semaphore()
    me = p["d"] * 16 + p["i"]
    for k in range(1, 32):
        t = (me + k) % 32
        pl.semaphore_signal(barrier, inc=1, device_id=(t // 16, t % 16), device_id_type=MESH)
    pl.semaphore_wait(barrier, 31)


def norm_sum(p, square, slots, send, recv):
    me = p["d"] * 16 + p["i"]
    slots[0] = jnp.full((8, 128), square, F32)
    copies = []
    for k in range(1, 32):
        t = (me + k) % 32
        copy = remote(slots.at[0], slots.at[k], send, recv, k, (t // 16, t % 16))
        copy.start()
        copies.append(copy)
    for copy in copies:
        copy.wait_recv()
    total = jnp.sum(slots[...], axis=0)[0:1, 0:1]
    for copy in copies:
        copy.wait_send()
    return total


def scatter_kernel(f, a, v, bf, ba, sv, norm, sf, sa, slots, nsend, nrecv, *scratch):
    p = place()
    greet_all(p)
    parts = [Fold(p, mine, *scratch[7 * n:7 * n + 7]) for n, mine in enumerate((f, a, v))]
    for step in ("start", "second", "third", "fourth"):
        for s in parts:
            getattr(s, step)()
    for s, out in zip(parts, (sf, sa, sv)):
        s.fifth(out)
    square = jnp.sum(sa[...] * sa[...]) + jnp.sum(sf[...] * sf[...]) + jnp.sum(sv[...] * sv[...])
    total = norm_sum(p, square, slots, nsend, nrecv)
    norm[...] = jnp.sqrt(total)
    for b in range(8):
        ba[b] = sa[:, b * BLOCK:(b + 1) * BLOCK]
        for j in range(2):
            bf[8 * j + b] = sf[j, :, b * BLOCK:(b + 1) * BLOCK]
    for s in parts:
        s.drain()


def scatter(f, a, v):
    outs = [jax.ShapeDtypeStruct(s, F32) for s in ((16, BLOCK, BLOCK), (8, BLOCK, BLOCK), v.shape[3:], (1, 1))]
    return pl.pallas_call(
        scatter_kernel,
        out_shape=outs,
        in_specs=[pl.BlockSpec(memory_space=pltpu.VMEM)] * 3,
        out_specs=[pl.BlockSpec(memory_space=pltpu.VMEM)] * 4,
        scratch_shapes=[pltpu.VMEM(f.shape[3:], F32), pltpu.VMEM(a.shape[3:], F32), pltpu.VMEM((32, 8, 128), F32),
                        pltpu.SemaphoreType.DMA((32,)), pltpu.SemaphoreType.DMA((32,))]
        + sum((fold_scratch(t.shape[3:], t.dtype) for t in (f, a, v)), []),
        compiler_params=pltpu.CompilerParams(collective_id=1, has_side_effects=True, vmem_limit_bytes=60 << 20),
        name="grad_scatter",
    )(f, a, v)


TOP = lax.Precision.HIGHEST


def shampoo_block(grad, w, st, ro, mo, st_new, mo_new, w_new, b, factor):
    clipped = grad * factor
    moment = momentum_decay * mo[b] + clipped
    left = lax.dot_general(clipped, clipped, (((1,), (1,)), ((), ())), precision=TOP, preferred_element_type=F32)
    right = lax.dot_general(clipped, clipped, (((0,), (0,)), ((), ())), precision=TOP, preferred_element_type=F32)
    st_new[b, 0] = stat_decay * st[b, 0] + (1.0 - stat_decay) * left
    st_new[b, 1] = stat_decay * st[b, 1] + (1.0 - stat_decay) * right
    mo_new[b] = moment
    turned = jnp.dot(ro[b, 0], moment, precision=TOP, preferred_element_type=F32)
    turned = jnp.dot(turned, ro[b, 1], precision=TOP, preferred_element_type=F32)
    w_new[b] = w[b] - matrix_rate * (turned + matrix_decay * w[b])


def optimizer_kernel(norm, ga, gf, sv, aw, ast, ar, am, fw, fst, fr, fm, vw, v1, v2,
                     ast_n, am_n, aw_n, fst_n, fm_n, fw_n, v1_n, v2_n, vw_n):
    factor = clip_bound / jnp.maximum(norm[...], clip_bound)
    shampoo_block(ga[0], aw, ast, ar, am, ast_n, am_n, aw_n, 0, factor)
    shampoo_block(gf[0], fw, fst, fr, fm, fst_n, fm_n, fw_n, 0, factor)
    shampoo_block(gf[1], fw, fst, fr, fm, fst_n, fm_n, fw_n, 1, factor)

    @pl.when(pl.program_id(0) == 0)
    def _():
        size = vw.shape[0]
        clipped = (sv[0:1, 0:size] * factor)[0]
        first_new = first_decay * v1[...] + (1.0 - first_decay) * clipped
        second_new = second_decay * v2[...] + (1.0 - second_decay) * clipped * clipped
        first_hat = first_new / (1.0 - first_decay**STEP)
        second_hat = second_new / (1.0 - second_decay**STEP)
        v1_n[...] = first_new
        v2_n[...] = second_new
        vw_n[...] = vw[...] - vector_rate * first_hat / (jnp.sqrt(second_hat) + adam_floor)


def optimizer(norm, ga, gf, sv, aw, ast, ar, am, fw, fst, fr, fm, vw, v1, v2):
    def steps(t, n):
        shape = (n,) + t.shape[1:]
        return pl.BlockSpec(shape, lambda g: (g,) + (0,) * (len(shape) - 1))

    def whole(t):
        return pl.BlockSpec(t.shape, lambda g: (0,) * t.ndim)

    like = lambda t: jax.ShapeDtypeStruct(t.shape, F32)
    args = (norm, ga, gf, sv, aw, ast, ar, am, fw, fst, fr, fm, vw, v1, v2)
    specs = [whole(norm), steps(ga, 1), steps(gf, 2), whole(sv)]
    specs += [steps(t, 1) for t in (aw, ast, ar, am)] + [steps(t, 2) for t in (fw, fst, fr, fm)]
    specs += [whole(t) for t in (vw, v1, v2)]
    outs = (ast, am, aw, fst, fm, fw, v1, v2, vw)
    return pl.pallas_call(
        optimizer_kernel,
        out_shape=[like(t) for t in outs],
        grid=(8,),
        in_specs=specs,
        out_specs=[steps(t, 1) for t in outs[:3]] + [steps(t, 2) for t in outs[3:6]] + [whole(t) for t in outs[6:]],
        name="optimizer",
    )(*args)


def per_device(
    inputs,
    output_gradient,
    keep,
    lengths,
    routes,
    attn_weights,
    attn_stats,
    attn_roots,
    attn_momentum,
    ffn_weights,
    ffn_stats,
    ffn_roots,
    ffn_momentum,
    vec_weights,
    vec_first,
    vec_second,
):
    slots, seq_len, width = inputs.shape
    tokens = slots * seq_len
    head_size = width // HEADS
    per_row = width // BLOCK
    share = vec_weights.shape[0]
    strip = attn_weights.astype(BF).transpose(1, 0, 2).reshape(BLOCK, width)
    pair = ffn_weights.astype(BF).reshape(2, per_row, BLOCK, BLOCK).transpose(0, 2, 1, 3).reshape(2, BLOCK, width)
    vec = jnp.pad(vec_weights.astype(BF).astype(F32)[None], ((0, 7), (0, 96)))
    ga, gv, gf = gather(strip, vec, pair)
    attn = ga.reshape(4, width, width)
    query_w, key_w, value_w, output_w = attn[0], attn[1], attn[2], attn[3]
    up = gf[0].reshape(4, 2, 2, 2, BLOCK, width).transpose(0, 1, 4, 2, 3, 5).reshape(width, FF)
    down = gf[1].reshape(FF, width)
    vectors = gv[..., 0, :share].reshape(-1)
    q_bias, v_bias, out_bias = (vectors[n * width:(n + 1) * width] for n in range(3))
    hidden_bias = vectors[3 * width:3 * width + FF]
    ffn_bias, gain_one, shift_one, gain_two, shift_two = (
        vectors[n * width + FF:(n + 1) * width + FF] for n in range(3, 8)
    )
    served = serve_flags(keep[None, :], routes[None, :])[0]
    flat = inputs.reshape(tokens, width)
    four = (slots, seq_len, HEADS, head_size)
    query = (product(flat, query_w) + q_bias).astype(BF).reshape(four)
    keys = product(flat, key_w).astype(BF).reshape(four)
    values = (product(flat, value_w) + v_bias).astype(BF).reshape(four)
    context, log_total = lax.map(attend_forward, (query, keys, values, lengths))
    context_low = context.reshape(tokens, width).astype(BF)
    attended = product(context_low, output_w) + out_bias
    normed_one, factor_one = norm_parts(flat.astype(F32) + attended)
    hidden_in = normed_one * gain_one + shift_one
    hidden_low = hidden_in.astype(BF)
    before = product(hidden_low, up) + hidden_bias
    active_low = jax.nn.gelu(before, approximate=False).astype(BF)
    branch = product(active_low, down) + ffn_bias
    normed_two, factor_two = norm_parts(hidden_in + branch)
    result = normed_two * gain_two + shift_two
    flag = jnp.repeat(served, seq_len)[:, None] > 0
    grad_flat = output_gradient.reshape(tokens, width)
    grad_rows = jnp.where(flag, grad_flat.astype(F32), 0.0)
    grad_gain_two = jnp.sum(grad_rows * normed_two, axis=0)
    grad_shift_two = jnp.sum(grad_rows, axis=0)
    grad_resid_two = norm_back(grad_rows * gain_two, normed_two, factor_two)
    grad_branch = grad_resid_two.astype(BF)
    grad_ffn_bias = jnp.sum(grad_branch.astype(F32), axis=0)
    grad_down = contract_rows(active_low, grad_branch)
    grad_active = times_transpose(grad_branch, down)
    grad_before = (grad_active * gelu_slope(before)).astype(BF)
    grad_hidden_bias = jnp.sum(grad_before.astype(F32), axis=0)
    grad_up = contract_rows(hidden_low, grad_before)
    grad_hidden = times_transpose(grad_before, up) + grad_resid_two
    grad_gain_one = jnp.sum(grad_hidden * normed_one, axis=0)
    grad_shift_one = jnp.sum(grad_hidden, axis=0)
    grad_resid_one = norm_back(grad_hidden * gain_one, normed_one, factor_one)
    grad_attended = grad_resid_one.astype(BF)
    grad_out_bias = jnp.sum(grad_attended.astype(F32), axis=0)
    grad_output_w = contract_rows(context_low, grad_attended)
    grad_context = times_transpose(grad_attended, output_w).astype(BF).reshape(four)
    grad_query, grad_keys, grad_values = lax.map(
        attend_backward, (query, keys, values, grad_context, log_total, lengths)
    )
    grad_query = grad_query.reshape(tokens, width).astype(BF)
    grad_keys = grad_keys.reshape(tokens, width).astype(BF)
    grad_values = grad_values.reshape(tokens, width).astype(BF)
    grad_q_bias = jnp.sum(grad_query.astype(F32), axis=0)
    grad_v_bias = jnp.sum(grad_values.astype(F32), axis=0)
    in_rows = (
        grad_resid_one
        + times_transpose(grad_query, query_w)
        + times_transpose(grad_keys, key_w)
        + times_transpose(grad_values, value_w)
    )
    out = jnp.where(flag, result.astype(BF), flat).reshape(inputs.shape)
    in_grad = jnp.where(flag, in_rows.astype(BF), grad_flat).reshape(inputs.shape)
    ha = jnp.stack(
        [
            contract_rows(flat, grad_query).astype(BF),
            contract_rows(flat, grad_keys).astype(BF),
            contract_rows(flat, grad_values).astype(BF),
            grad_output_w.astype(BF),
        ]
    ).reshape(2, 4, 4, BLOCK, width)
    hf = jnp.stack(
        [
            grad_up.astype(BF).reshape(4, 2, BLOCK, 2, 2, width).transpose(0, 1, 3, 4, 2, 5).reshape(4, 4, 2, BLOCK, width),
            grad_down.astype(BF).reshape(4, 4, 2, BLOCK, width),
        ]
    )
    vec_grad = jnp.concatenate(
        [
            grad_q_bias,
            grad_v_bias,
            grad_out_bias,
            grad_hidden_bias,
            grad_ffn_bias,
            grad_gain_one,
            grad_shift_one,
            grad_gain_two,
            grad_shift_two,
        ]
    )
    hv = jnp.pad(vec_grad.reshape(2, 4, 4, 1, share), ((0, 0),) * 3 + ((0, 7), (0, 96)))
    bf, ba, sv, norm = scatter(hf, ha, hv)
    rest = optimizer(
        norm, ba, bf, sv,
        attn_weights, attn_stats, attn_roots, attn_momentum,
        ffn_weights, ffn_stats, ffn_roots, ffn_momentum,
        vec_weights, vec_first, vec_second,
    )
    return (out, in_grad, norm.reshape(()), *rest)


def solution(mesh):
    small = mesh.shape["depth"] == 2 and mesh.shape["dp"] == 16
    return jax.shard_map(
        per_device if small else per_device_general,
        mesh=mesh,
        in_specs=(
            P(("depth", "dp"), None, None),
            P(("depth", "dp"), None, None),
            P(("depth", "dp")),
            P(("depth", "dp")),
            P(("depth", "dp")),
            P(("depth", "dp"), None, None),
            P(("depth", "dp"), None, None, None),
            P(("depth", "dp"), None, None, None),
            P(("depth", "dp"), None, None),
            P(("depth", "dp"), None, None),
            P(("depth", "dp"), None, None, None),
            P(("depth", "dp"), None, None, None),
            P(("depth", "dp"), None, None),
            P(("depth", "dp")),
            P(("depth", "dp")),
            P(("depth", "dp")),
        ),
        out_specs=(
            P(("depth", "dp"), None, None),
            P(("depth", "dp"), None, None),
            P(),
            P(("depth", "dp"), None, None, None),
            P(("depth", "dp"), None, None),
            P(("depth", "dp"), None, None),
            P(("depth", "dp"), None, None, None),
            P(("depth", "dp"), None, None),
            P(("depth", "dp"), None, None),
            P(("depth", "dp")),
            P(("depth", "dp")),
            P(("depth", "dp")),
        ),
        check_vma=False,
    )
```

```python
import functools
import math

import jax
import jax.numpy as jnp
from jax import lax
from jax.experimental import pallas as pl
from jax.experimental.pallas import tpu as pltpu
from jax.sharding import PartitionSpec as P

HEADS = 12
FF = 3072
BLOCK = 96
STEP = 10


norm_floor = 1e-05
masked_fill = -1000000000.0
momentum_decay = 0.9
stat_decay = 0.95
matrix_rate = 1.0
matrix_decay = 0.01
clip_bound = 1.0
first_decay = 0.9
second_decay = 0.999
vector_rate = 0.5
adam_floor = 1e-08


def serve_flags(keep_rows, route_rows):
    count = keep_rows.shape[-1]
    order = jnp.arange(count, dtype=jnp.int32)
    earlier = (order[None, :] < order[:, None]).astype(jnp.int32)
    same = (route_rows[:, :, None] == route_rows[:, None, :]).astype(jnp.int32)
    clash = jnp.sum(same * earlier[None, :, :] * keep_rows[:, None, :], axis=2)
    return keep_rows * (clash == 0).astype(jnp.int32)


def to_matrix(blocks, height, breadth):
    shaped = blocks.reshape(height // BLOCK, breadth // BLOCK, BLOCK, BLOCK)
    return shaped.transpose(0, 2, 1, 3).reshape(height, breadth)


def to_flat_blocks(matrix):
    height, breadth = matrix.shape
    shaped = matrix.reshape(height // BLOCK, BLOCK, breadth // BLOCK, BLOCK)
    return shaped.transpose(0, 2, 1, 3).reshape(-1, BLOCK * BLOCK)


def norm_parts(resid):
    center = resid - jnp.mean(resid, axis=-1, keepdims=True)
    factor = lax.rsqrt(jnp.mean(center * center, axis=-1, keepdims=True) + norm_floor)
    return (center * factor, factor)


def norm_back(grad_normed, normed, factor):
    middle = jnp.mean(grad_normed, axis=-1, keepdims=True)
    along = jnp.mean(grad_normed * normed, axis=-1, keepdims=True)
    return factor * (grad_normed - middle - normed * along)


def gelu_slope(value):
    cumulative = 0.5 * (1.0 + lax.erf(value * (1.0 / math.sqrt(2.0))))
    density = jnp.exp(-0.5 * value * value) * (1.0 / math.sqrt(2.0 * math.pi))
    return cumulative + value * density


def product(left, right):
    return jnp.dot(left, right, preferred_element_type=jnp.float32)


def contract_rows(left, right):
    return lax.dot_general(
        left, right, (((0,), (0,)), ((), ())), preferred_element_type=jnp.float32
    )


def times_transpose(left, right):
    return lax.dot_general(
        left, right, (((1,), (1,)), ((), ())), preferred_element_type=jnp.float32
    )


def masked_scores(query, keys, visible_len):
    scale = 1.0 / math.sqrt(query.shape[-1])
    scores = jnp.einsum("qhe,khe->hqk", query, keys, preferred_element_type=jnp.float32) * scale
    visible = jnp.arange(keys.shape[0], dtype=jnp.int32) < visible_len
    return jnp.where(visible[None, None, :], scores, masked_fill)


def attend_forward(pieces):
    query, keys, values, visible_len = pieces
    scores = masked_scores(query, keys, visible_len)
    peak = jnp.max(scores, axis=-1, keepdims=True)
    expo = jnp.exp(scores - peak)
    total = jnp.sum(expo, axis=-1, keepdims=True)
    probs_low = (expo / total).astype(jnp.bfloat16)
    context = jnp.einsum("hqk,khe->qhe", probs_low, values, preferred_element_type=jnp.float32)
    return (context, peak[..., 0] + jnp.log(total[..., 0]))


def attend_backward(pieces):
    query, keys, values, grad_ctx, log_total, visible_len = pieces
    scale = 1.0 / math.sqrt(query.shape[-1])
    scores = masked_scores(query, keys, visible_len)
    probs = jnp.exp(scores - log_total[..., None])
    probs_low = probs.astype(jnp.bfloat16)
    grad_probs = jnp.einsum("qhe,khe->hqk", grad_ctx, values, preferred_element_type=jnp.float32)
    grad_values = jnp.einsum(
        "hqk,qhe->khe", probs_low, grad_ctx, preferred_element_type=jnp.float32
    )
    along = jnp.sum(probs * grad_probs, axis=-1, keepdims=True)
    grad_scores = (probs * (grad_probs - along)).astype(jnp.bfloat16)
    grad_query = (
        jnp.einsum("hqk,khe->qhe", grad_scores, keys, preferred_element_type=jnp.float32) * scale
    )
    grad_keys = (
        jnp.einsum("hqk,qhe->khe", grad_scores, query, preferred_element_type=jnp.float32) * scale
    )
    return (grad_query, grad_keys, grad_values)


def shampoo(weights, stats, roots, momentum, grads, factor):
    highest = lax.Precision.HIGHEST
    clipped = grads * factor
    moment = momentum_decay * momentum + clipped
    left = jnp.einsum("nab,ncb->nac", clipped, clipped, precision=highest)
    right = jnp.einsum("nab,nac->nbc", clipped, clipped, precision=highest)
    fresh = stat_decay * stats + (1.0 - stat_decay) * jnp.stack([left, right], axis=1)
    turned = jnp.einsum("nab,nbc->nac", roots[:, 0], moment, precision=highest)
    turned = jnp.einsum("nab,nbc->nac", turned, roots[:, 1], precision=highest)
    updated = weights - matrix_rate * (turned + matrix_decay * weights)
    return (fresh, moment, updated)


def adam_step(weights, first, second, grads, factor):
    clipped = grads * factor
    first_new = first_decay * first + (1.0 - first_decay) * clipped
    second_new = second_decay * second + (1.0 - second_decay) * clipped * clipped
    first_hat = first_new / (1.0 - first_decay**STEP)
    second_hat = second_new / (1.0 - second_decay**STEP)
    updated = weights - vector_rate * first_hat / (jnp.sqrt(second_hat) + adam_floor)
    return (first_new, second_new, updated)


def per_device_general(
    inputs,
    output_gradient,
    keep,
    lengths,
    routes,
    attn_weights,
    attn_stats,
    attn_roots,
    attn_momentum,
    ffn_weights,
    ffn_stats,
    ffn_roots,
    ffn_momentum,
    vec_weights,
    vec_first,
    vec_second,
):
    slots, seq_len, width = inputs.shape
    tokens = slots * seq_len
    head_size = width // HEADS
    hidden_width = FF
    depth_count = lax.axis_size("depth")
    peer_slots = slots // depth_count
    grid = (width // BLOCK) ** 2
    half_ffn = width * hidden_width // (BLOCK * BLOCK)
    area = BLOCK * BLOCK
    low_type = jnp.bfloat16
    attn_flat = attn_weights.reshape(-1, area).astype(low_type)
    ffn_flat = ffn_weights.reshape(-1, area).astype(low_type)
    attn_all, ffn_all, vec_all = (
        lax.all_gather(attn_flat, ("depth", "dp"), axis=0, tiled=True),
        lax.all_gather(ffn_flat, ("depth", "dp"), axis=0, tiled=True),
        lax.all_gather(vec_weights.astype(low_type), ("depth", "dp"), axis=0, tiled=True),
    )
    table_keep, table_len, table_route = (
        lax.all_gather(keep, "depth", axis=0, tiled=True),
        lax.all_gather(lengths, "depth", axis=0, tiled=True),
        lax.all_gather(routes, "depth", axis=0, tiled=True),
    )
    mine = serve_flags(keep[None, :], routes[None, :])[0]
    slot_order = jnp.arange(slots, dtype=jnp.int32)
    selection = ((routes[None, :] == slot_order[:, None]).astype(jnp.int32) * mine[None, :]).astype(
        low_type
    )
    outgoing_rows = jnp.einsum(
        "gz,zrp->grp", selection, inputs, preferred_element_type=jnp.float32
    ).astype(low_type)
    send_grad = jnp.einsum(
        "gz,zrp->grp", selection, output_gradient, preferred_element_type=jnp.float32
    ).astype(low_type)
    come_rows, come_grad = (
        lax.all_to_all(outgoing_rows, "depth", split_axis=0, concat_axis=0, tiled=True),
        lax.all_to_all(send_grad, "depth", split_axis=0, concat_axis=0, tiled=True),
    )
    all_keep = table_keep.reshape(depth_count, slots)
    all_route = table_route.reshape(depth_count, slots)
    all_len = table_len.reshape(depth_count, slots)
    all_served = serve_flags(all_keep, all_route)
    here = lax.axis_index("depth")
    source = slot_order // peer_slots
    target = here * peer_slots + slot_order % peer_slots
    source_hot = (source[:, None] == jnp.arange(depth_count, dtype=jnp.int32)[None, :]).astype(
        jnp.int32
    )
    match = (all_route[None, :, :] == target[:, None, None]).astype(jnp.int32) * all_served[
        None, :, :
    ]
    slot_len = jnp.sum(source_hot[:, :, None] * match * all_len[None, :, :], axis=(1, 2))
    visible_len = jnp.maximum(slot_len, 1)
    query_w = to_matrix(attn_all[0:grid], width, width)
    key_w = to_matrix(attn_all[grid : 2 * grid], width, width)
    value_w = to_matrix(attn_all[2 * grid : 3 * grid], width, width)
    output_w = to_matrix(attn_all[3 * grid : 4 * grid], width, width)
    vectors = vec_all.astype(jnp.float32)
    q_bias = vectors[0:width]
    v_bias = vectors[width : 2 * width]
    out_bias = vectors[2 * width : 3 * width]
    hidden_bias = vectors[3 * width : 3 * width + hidden_width]
    ffn_bias = vectors[3 * width + hidden_width : 4 * width + hidden_width]
    gain_one = vectors[4 * width + hidden_width : 5 * width + hidden_width]
    shift_one = vectors[5 * width + hidden_width : 6 * width + hidden_width]
    gain_two = vectors[6 * width + hidden_width : 7 * width + hidden_width]
    shift_two = vectors[7 * width + hidden_width : 8 * width + hidden_width]
    flat = come_rows.reshape(tokens, width)
    four = (slots, seq_len, HEADS, head_size)
    query = (product(flat, query_w) + q_bias).astype(low_type).reshape(four)
    keys = product(flat, key_w).astype(low_type).reshape(four)
    values = (product(flat, value_w) + v_bias).astype(low_type).reshape(four)
    context, log_total = lax.map(attend_forward, (query, keys, values, visible_len))
    context_low = context.reshape(tokens, width).astype(low_type)
    attended = product(context_low, output_w) + out_bias
    normed_one, factor_one = norm_parts(flat.astype(jnp.float32) + attended)
    hidden_in = normed_one * gain_one + shift_one
    hidden_low = hidden_in.astype(low_type)
    hidden_w = to_matrix(ffn_all[0:half_ffn], width, hidden_width)
    return_weight = to_matrix(ffn_all[half_ffn:], hidden_width, width)
    before = product(hidden_low, hidden_w) + hidden_bias
    active_low = jax.nn.gelu(before, approximate=False).astype(low_type)
    branch = product(active_low, return_weight) + ffn_bias
    normed_two, factor_two = norm_parts(hidden_in + branch)
    result_low = (normed_two * gain_two + shift_two).astype(low_type)
    grad_rows = come_grad.reshape(tokens, width).astype(jnp.float32)
    grad_gain_two = jnp.sum(grad_rows * normed_two, axis=0)
    grad_shift_two = jnp.sum(grad_rows, axis=0)
    grad_resid_two = norm_back(grad_rows * gain_two, normed_two, factor_two)
    grad_branch = grad_resid_two.astype(low_type)
    grad_ffn_bias = jnp.sum(grad_branch.astype(jnp.float32), axis=0)
    gradient_return_weight = contract_rows(active_low, grad_branch)
    grad_active = times_transpose(grad_branch, return_weight)
    grad_before = (grad_active * gelu_slope(before)).astype(low_type)
    grad_hidden_bias = jnp.sum(grad_before.astype(jnp.float32), axis=0)
    grad_hidden_w = contract_rows(hidden_low, grad_before)
    grad_hidden = times_transpose(grad_before, hidden_w) + grad_resid_two
    grad_gain_one = jnp.sum(grad_hidden * normed_one, axis=0)
    grad_shift_one = jnp.sum(grad_hidden, axis=0)
    grad_resid_one = norm_back(grad_hidden * gain_one, normed_one, factor_one)
    ffn_grad = jnp.concatenate(
        [to_flat_blocks(grad_hidden_w), to_flat_blocks(gradient_return_weight)], axis=0
    )
    grad_attended = grad_resid_one.astype(low_type)
    grad_out_bias = jnp.sum(grad_attended.astype(jnp.float32), axis=0)
    grad_output_w = contract_rows(context_low, grad_attended)
    grad_context = times_transpose(grad_attended, output_w).astype(low_type).reshape(four)
    grad_query, grad_keys, grad_values = lax.map(
        attend_backward, (query, keys, values, grad_context, log_total, visible_len)
    )
    grad_query = grad_query.reshape(tokens, width).astype(low_type)
    grad_keys = grad_keys.reshape(tokens, width).astype(low_type)
    grad_values = grad_values.reshape(tokens, width).astype(low_type)
    grad_q_bias = jnp.sum(grad_query.astype(jnp.float32), axis=0)
    grad_v_bias = jnp.sum(grad_values.astype(jnp.float32), axis=0)
    grad_query_w = contract_rows(flat, grad_query)
    grad_key_w = contract_rows(flat, grad_keys)
    grad_value_w = contract_rows(flat, grad_values)
    in_rows = (
        grad_resid_one
        + times_transpose(grad_query, query_w)
        + times_transpose(grad_keys, key_w)
        + times_transpose(grad_values, value_w)
    )
    attn_grad = jnp.concatenate(
        [
            to_flat_blocks(grad_query_w),
            to_flat_blocks(grad_key_w),
            to_flat_blocks(grad_value_w),
            to_flat_blocks(grad_output_w),
        ],
        axis=0,
    )
    vec_grad = jnp.concatenate(
        [
            grad_q_bias,
            grad_v_bias,
            grad_out_bias,
            grad_hidden_bias,
            grad_ffn_bias,
            grad_gain_one,
            grad_shift_one,
            grad_gain_two,
            grad_shift_two,
        ]
    )
    attn_share, ffn_share, vec_share = (
        lax.psum_scatter(attn_grad, ("depth", "dp"), scatter_dimension=0, tiled=True),
        lax.psum_scatter(ffn_grad, ("depth", "dp"), scatter_dimension=0, tiled=True),
        lax.psum_scatter(vec_grad, ("depth", "dp"), scatter_dimension=0, tiled=True),
    )
    returned_rows, returned_gradient = (
        lax.all_to_all(
            result_low.reshape(slots, seq_len, width),
            "depth",
            split_axis=0,
            concat_axis=0,
            tiled=True,
        ),
        lax.all_to_all(
            in_rows.astype(low_type).reshape(slots, seq_len, width),
            "depth",
            split_axis=0,
            concat_axis=0,
            tiled=True,
        ),
    )
    stay = (1 - mine).astype(jnp.float32)[:, None, None]
    out = (
        jnp.einsum("rx,rmp->xmp", selection, returned_rows, preferred_element_type=jnp.float32)
        + stay * inputs.astype(jnp.float32)
    ).astype(low_type)
    in_grad = (
        jnp.einsum("rx,rmp->xmp", selection, returned_gradient, preferred_element_type=jnp.float32)
        + stay * output_gradient.astype(jnp.float32)
    ).astype(low_type)
    square = (
        jnp.sum(attn_share * attn_share)
        + jnp.sum(ffn_share * ffn_share)
        + jnp.sum(vec_share * vec_share)
    )
    total = lax.psum(square, ("depth", "dp"))
    grad_norm = jnp.sqrt(total)
    factor = clip_bound / jnp.maximum(grad_norm, clip_bound)
    attn_square = attn_share.reshape(-1, BLOCK, BLOCK)
    ffn_square = ffn_share.reshape(-1, BLOCK, BLOCK)
    attn_fresh, attn_moment, attn_updated = shampoo(
        attn_weights, attn_stats, attn_roots, attn_momentum, attn_square, factor
    )
    ffn_fresh, ffn_moment, ffn_updated = shampoo(
        ffn_weights, ffn_stats, ffn_roots, ffn_momentum, ffn_square, factor
    )
    first_new, second_new, vec_updated = adam_step(
        vec_weights, vec_first, vec_second, vec_share, factor
    )
    return (
        out,
        in_grad,
        grad_norm,
        attn_fresh,
        attn_moment,
        attn_updated,
        ffn_fresh,
        ffn_moment,
        ffn_updated,
        first_new,
        second_new,
        vec_updated,
    )


MESH = pl.DeviceIdType.MESH
BF = jnp.bfloat16
F32 = jnp.float32


def place():
    d = lax.axis_index("depth")
    i = lax.axis_index("dp")
    x = i % 2
    y = (i // 2) % 2
    z = i // 4
    c = i % 4
    nx = i + 1 - 2 * x
    ny = i + 2 - 4 * y
    na = ny + d * (nx - ny)
    nb = nx + d * (ny - nx)
    return dict(d=d, i=i, z=z, c=c, na=na, nb=nb, ca=na % 4, cb=nb % 4, cd=3 - c)


def greet(p):
    barrier = pltpu.get_barrier_semaphore()
    peers = [(p["d"], p["na"]), (p["d"], p["nb"]), (1 - p["d"], p["i"])]
    peers += [(p["d"], ((p["z"] + k) % 4) * 4 + p["c"]) for k in (1, 2, 3)]
    for peer in peers:
        pl.semaphore_signal(barrier, inc=1, device_id=peer, device_id_type=MESH)
    pl.semaphore_wait(barrier, len(peers))


def remote(src, dst, send, recv, k, dev):
    return pltpu.make_async_remote_copy(src_ref=src, dst_ref=dst, send_sem=send.at[k], recv_sem=recv.at[k],
                                        device_id=dev, device_id_type=MESH)


class Spread:
    def __init__(self, p, own, out, send, recv, local):
        self.p, self.own, self.out, self.send, self.recv, self.local = p, own, out, send, recv, local
        self.sent = []

    def go(self, src, dst, k, dev):
        copy = remote(src, dst, self.send, self.recv, k, dev)
        copy.start()
        self.sent.append(copy)

    def start(self):
        p = self.p
        here = self.out.at[p["d"], p["z"], p["c"]]
        self.keep = pltpu.make_async_copy(self.own, here, self.local)
        self.keep.start()
        for k in (2, 1, 3):
            self.go(self.own, here, k - 1, (p["d"], ((p["z"] + k) % 4) * 4 + p["c"]))

    def wait(self, dst, k):
        remote(dst, dst, self.send, self.recv, k, (self.p["d"], self.p["na"])).wait_recv()

    def column(self, half, col):
        return self.out.at[half, :, col]

    def second(self):
        p = self.p
        self.keep.wait()
        for k in (1, 2, 3):
            self.wait(self.out.at[p["d"], (p["z"] + 4 - k) % 4, p["c"]], k - 1)
        mine = self.column(p["d"], p["c"])
        self.go(mine, mine, 3, (p["d"], p["na"]))
        self.go(mine, mine, 4, (p["d"], p["nb"]))
        self.go(mine, mine, 6, (1 - p["d"], p["i"]))

    def third(self):
        p = self.p
        got = self.column(p["d"], p["ca"])
        self.wait(got, 3)
        self.go(got, got, 5, (p["d"], p["nb"]))
        self.go(got, got, 8 - p["d"], (1 - p["d"], p["i"]))

    def fourth(self):
        p = self.p
        got = self.column(p["d"], p["cb"])
        self.wait(got, 4)
        self.go(got, got, 7 + p["d"], (1 - p["d"], p["i"]))

    def fifth(self):
        p = self.p
        got = self.column(p["d"], p["cd"])
        self.wait(got, 5)
        self.go(got, got, 9, (1 - p["d"], p["i"]))

    def sixth(self):
        p = self.p
        for k, col in ((6, p["c"]), (8 - p["d"], p["ca"]), (7 + p["d"], p["cb"]), (9, p["cd"])):
            self.wait(self.column(1 - p["d"], col), k)

    def drain(self):
        for copy in self.sent:
            copy.wait_send()


def gather_kernel(a, v, f, ga, gv, gf, *sems):
    p = place()
    greet(p)
    parts = [Spread(p, own, out, sems[3 * n], sems[3 * n + 1], sems[3 * n + 2])
             for n, (own, out) in enumerate(((a, ga), (v, gv), (f, gf)))]
    for s in parts:
        s.start()
    for s in parts[:2]:
        s.second()
    for s in parts[:2]:
        s.third()
    for s in parts[:2]:
        s.fourth()
    parts[2].second()
    for s in parts[:2]:
        s.fifth()
    parts[2].third()
    parts[2].fourth()
    parts[2].fifth()
    for s in parts:
        s.sixth()
    for s in parts:
        s.drain()


def gather(a, v, f):
    sem = [pltpu.SemaphoreType.DMA((10,)), pltpu.SemaphoreType.DMA((10,)), pltpu.SemaphoreType.DMA]
    return pl.pallas_call(
        gather_kernel,
        out_shape=[jax.ShapeDtypeStruct((2, 4, 4) + t.shape, t.dtype) for t in (a, v, f)],
        in_specs=[pl.BlockSpec(memory_space=pltpu.VMEM)] * 3,
        out_specs=[pl.BlockSpec(memory_space=pl.ANY)] * 3,
        scratch_shapes=sem * 3,
        compiler_params=pltpu.CompilerParams(collective_id=0, has_side_effects=True),
        name="weight_gather",
    )(a, v, f)


class Fold:
    def __init__(self, p, mine, pair, diag, flat, late, line, send, recv):
        self.p, self.mine, self.pair, self.diag, self.flat, self.late, self.line = p, mine, pair, diag, flat, late, line
        self.send, self.recv, self.sent = send, recv, []

    def go(self, src, dst, k, dev):
        copy = remote(src, dst, self.send, self.recv, k, dev)
        copy.start()
        self.sent.append(copy)

    def wait(self, dst, k):
        remote(dst, dst, self.send, self.recv, k, (self.p["d"], self.p["na"])).wait_recv()

    def add(self, dst, *others):
        total = dst[...].astype(F32)
        for o in others:
            total += o[...].astype(F32)
        dst[...] = total.astype(dst.dtype)

    def start(self):
        p = self.p
        self.go(self.mine.at[1 - p["d"]], self.pair, 0, (1 - p["d"], p["i"]))

    def second(self):
        p = self.p
        self.wait(self.pair, 0)
        for col, dst, k in ((p["cd"], self.diag, 1), (p["cb"], self.flat, 2)):
            self.add(self.pair.at[:, col], self.mine.at[p["d"], :, col])
            self.go(self.pair.at[:, col], dst, k, (p["d"], p["nb"]))
        for col in (p["ca"], p["c"]):
            self.add(self.pair.at[:, col], self.mine.at[p["d"], :, col])

    def third(self):
        p = self.p
        self.wait(self.diag, 1)
        src = self.pair.at[:, p["ca"]]
        self.add(src, self.diag)
        self.go(src, self.late, 3, (p["d"], p["na"]))

    def fourth(self):
        p = self.p
        self.wait(self.flat, 2)
        self.wait(self.late, 3)
        for k in (2, 1, 3, 0):
            dst = (p["z"] + k) % 4
            self.add(self.pair.at[dst, p["c"]], self.flat.at[dst], self.late.at[dst])
            if k:
                self.go(self.pair.at[dst, p["c"]], self.line.at[k - 1], 3 + k, (p["d"], dst * 4 + p["c"]))

    def fifth(self, out):
        p = self.p
        total = self.pair[p["z"], p["c"]].astype(F32)
        for k in (1, 2, 3):
            self.wait(self.line.at[k - 1], 3 + k)
            total += self.line[k - 1].astype(F32)
        out[...] = total

    def drain(self):
        for copy in self.sent:
            copy.wait_send()


def fold_scratch(shape, dtype):
    return [pltpu.VMEM((4, 4) + shape, dtype), pltpu.VMEM((4,) + shape, dtype), pltpu.VMEM((4,) + shape, dtype),
            pltpu.VMEM((4,) + shape, dtype), pltpu.VMEM((3,) + shape, dtype),
            pltpu.SemaphoreType.DMA((7,)), pltpu.SemaphoreType.DMA((7,))]


def greet_all(p):
    barrier = pltpu.get_barrier_semaphore()
    me = p["d"] * 16 + p["i"]
    for k in range(1, 32):
        t = (me + k) % 32
        pl.semaphore_signal(barrier, inc=1, device_id=(t // 16, t % 16), device_id_type=MESH)
    pl.semaphore_wait(barrier, 31)


def norm_sum(p, square, slots, send, recv):
    me = p["d"] * 16 + p["i"]
    slots[0] = jnp.full((8, 128), square, F32)
    copies = []
    for k in range(1, 32):
        t = (me + k) % 32
        copy = remote(slots.at[0], slots.at[k], send, recv, k, (t // 16, t % 16))
        copy.start()
        copies.append(copy)
    for copy in copies:
        copy.wait_recv()
    total = jnp.sum(slots[...], axis=0)[0:1, 0:1]
    for copy in copies:
        copy.wait_send()
    return total


def scatter_kernel(f, a, v, bf, ba, sv, norm, sf, sa, slots, nsend, nrecv, *scratch):
    p = place()
    greet_all(p)
    parts = [Fold(p, mine, *scratch[7 * n:7 * n + 7]) for n, mine in enumerate((f, a, v))]
    for step in ("start", "second", "third", "fourth"):
        for s in parts:
            getattr(s, step)()
    for s, out in zip(parts, (sf, sa, sv)):
        s.fifth(out)
    square = jnp.sum(sa[...] * sa[...]) + jnp.sum(sf[...] * sf[...]) + jnp.sum(sv[...] * sv[...])
    total = norm_sum(p, square, slots, nsend, nrecv)
    norm[...] = jnp.sqrt(total)
    for b in range(8):
        ba[b] = sa[:, b * BLOCK:(b + 1) * BLOCK]
        for j in range(2):
            bf[8 * j + b] = sf[j, :, b * BLOCK:(b + 1) * BLOCK]
    for s in parts:
        s.drain()


def scatter(f, a, v):
    outs = [jax.ShapeDtypeStruct(s, F32) for s in ((16, BLOCK, BLOCK), (8, BLOCK, BLOCK), v.shape[3:], (1, 1))]
    return pl.pallas_call(
        scatter_kernel,
        out_shape=outs,
        in_specs=[pl.BlockSpec(memory_space=pltpu.VMEM)] * 3,
        out_specs=[pl.BlockSpec(memory_space=pltpu.VMEM)] * 4,
        scratch_shapes=[pltpu.VMEM(f.shape[3:], F32), pltpu.VMEM(a.shape[3:], F32), pltpu.VMEM((32, 8, 128), F32),
                        pltpu.SemaphoreType.DMA((32,)), pltpu.SemaphoreType.DMA((32,))]
        + sum((fold_scratch(t.shape[3:], t.dtype) for t in (f, a, v)), []),
        compiler_params=pltpu.CompilerParams(collective_id=1, has_side_effects=True, vmem_limit_bytes=60 << 20),
        name="grad_scatter",
    )(f, a, v)


LEN = 512


def dot_nn(a, b):
    return lax.dot_general(a, b, (((1,), (0,)), ((), ())), preferred_element_type=F32)


def dot_nt(a, b):
    return lax.dot_general(a, b, (((1,), (1,)), ((), ())), preferred_element_type=F32)


def dot_tn(a, b):
    return lax.dot_general(a, b, (((0,), (0,)), ((), ())), preferred_element_type=F32)


def square_of(value):
    return value.reshape(value.shape[0] * value.shape[1] * value.shape[2], value.shape[3])


def seq_rows(s):
    return pl.ds(s * LEN, LEN) if isinstance(s, int) else pl.ds(pl.multiple_of(s * LEN, LEN), LEN)


def tile_rows(s, size):
    return pl.ds(pl.multiple_of(s * size, size), size)


def served_flag(keep, routes, s):
    other = keep[0] * (routes[0] == routes[1]).astype(jnp.int32)
    return jnp.where(s == 0, keep[0], keep[1] * (1 - other))


def projections(x, ga, vec, q, k, v):
    width = x.shape[1]

    def tile(s, carry):
        rows = seq_rows(s)
        xr = x[rows]
        q[rows] = (dot_nn(xr, square_of(ga[0, 0:2])) + vec[:, 0:width]).astype(BF)
        k[rows] = dot_nn(xr, square_of(ga[0, 2:4])).astype(BF)
        v[rows] = (dot_nn(xr, square_of(ga[1, 0:2])) + vec[:, width:2 * width]).astype(BF)
        return carry

    lax.fori_loop(0, x.shape[0] // LEN, tile, 0)


def head_pairs(n, lens):
    s, g = n // 6, n % 6
    first = lax.broadcasted_iota(jnp.int32, (1, 128), 1) < 64
    return s, seq_rows(s), pl.ds(pl.multiple_of(g * 128, 128), 128), (first, jnp.logical_not(first))


def attend(n, q, k, v, lens, context, log_total):
    s, rows, cols, halves = head_pairs(n, lens)
    qp, kp, vp = q[rows, cols], k[rows, cols], v[rows, cols]
    seen = lax.broadcasted_iota(jnp.int32, (1, LEN), 1) < lens[s]
    found = []
    for h in range(2):
        qm = jnp.where(halves[h], qp, jnp.zeros_like(qp))
        scores = jnp.where(seen, dot_nt(qm, kp) * 0.125, masked_fill)
        peak = jnp.max(scores, axis=1, keepdims=True)
        expo = jnp.exp(scores - peak)
        total = jnp.sum(expo, axis=1, keepdims=True)
        found.append(dot_nn((expo * (1.0 / total)).astype(BF), vp))
        log_total[n, h] = (peak + jnp.log(total))[:, 0]
    context[rows, cols] = jnp.where(halves[0], found[0], found[1]).astype(BF)


def attend_back(n, q, k, v, grad_context, log_total, lens, gq, gk, gv):
    s, rows, cols, halves = head_pairs(n, lens)
    qp, kp, vp, gp = q[rows, cols], k[rows, cols], v[rows, cols], grad_context[rows, cols]
    seen = lax.broadcasted_iota(jnp.int32, (LEN, 1), 0) < lens[s]
    zero = jnp.zeros_like(qp)
    aq = ak = av = jnp.zeros((LEN, 128), F32)
    for h in range(2):
        qm, km, gm = (jnp.where(halves[h], t, zero) for t in (qp, kp, gp))
        scores = jnp.where(seen, dot_nt(kp, qm) * 0.125, masked_fill)
        probs = jnp.exp(scores - log_total[n, h][None, :])
        grad_probs = dot_nt(vp, gm)
        along = jnp.sum(probs * grad_probs, axis=0, keepdims=True)
        grad_scores = (probs * (grad_probs - along)).astype(BF)
        av += dot_nn(probs.astype(BF), gm)
        ak += dot_nn(grad_scores, qm)
        aq += dot_tn(grad_scores, km)
    gq[rows, cols] = (aq * 0.125).astype(BF)
    gk[rows, cols] = (ak * 0.125).astype(BF)
    gv[rows, cols] = av.astype(BF)


def mean_of(t):
    return jnp.mean(t, axis=-1, keepdims=True)


def attention_end(x, context, ga, vec, normed, factor):
    width = x.shape[1]

    def tile(s, carry):
        rows = seq_rows(s)
        attended = dot_nn(context[rows], square_of(ga[1, 2:4])) + vec[:, 2 * width:3 * width]
        resid = x[rows].astype(F32) + attended
        center = resid - mean_of(resid)
        scale = lax.rsqrt(mean_of(center * center) + norm_floor)
        normed[rows] = center * scale
        factor[rows] = scale
        return carry

    lax.fori_loop(0, x.shape[0] // LEN, tile, 0)


def attention_kernel(x, ga, vec, lens, q, k, v, context, log_total, normed, factor):
    projections(x, ga, vec, q, k, v)

    def step(n, carry):
        attend(n, q, k, v, lens, context, log_total)
        return carry

    lax.fori_loop(0, 12, step, 0)
    attention_end(x, context, ga, vec, normed, factor)


def vmem_call(kernel, args, outs, scratch, name, smem=(), limit=62 << 20):
    space = lambda n: pltpu.SMEM if n in smem else pltpu.VMEM
    return pl.pallas_call(
        kernel,
        out_shape=outs,
        in_specs=[pl.BlockSpec(memory_space=space(n)) for n in range(len(args))],
        out_specs=[pl.BlockSpec(memory_space=pltpu.VMEM)] * len(outs),
        scratch_shapes=scratch,
        compiler_params=pltpu.CompilerParams(vmem_limit_bytes=limit),
        name=name,
    )(*args)


def attention(x, ga, vec, lens):
    low = jax.ShapeDtypeStruct(x.shape, BF)
    outs = [low] * 4 + [jax.ShapeDtypeStruct((12, 2, LEN), F32), jax.ShapeDtypeStruct(x.shape, F32),
                        jax.ShapeDtypeStruct((x.shape[0], 1), F32)]
    return vmem_call(attention_kernel, (x, ga, vec, lens), outs, [], "attention", smem=(3,))


def vec_part(vec, n, width):
    start = n * width if n < 3 else (3 * width + (0 if n == 3 else FF + (n - 4) * width))
    return vec[:, start:start + (FF if n == 3 else width)]


def feed_forward(x, normed, factor, gf, vec, cot, keep, routes, out, hf, grad_resid, gvec, active, slope, middle, low, grad_low):
    width = x.shape[1]
    seqs = x.shape[0] // LEN

    def up(q):
        c, j = q // 2, q % 2
        return jnp.concatenate([gf[0, z, 2 * y + c, j] for z in range(4) for y in range(2)], axis=0)

    def enter(s, carry):
        rows = seq_rows(s)
        low[rows] = (normed[rows] * vec_part(vec, 5, width) + vec_part(vec, 6, width)).astype(BF)
        for q in range(4):
            cols = slice(q * width, (q + 1) * width)
            before = dot_nn(low[rows], up(q)) + vec_part(vec, 3, width)[:, cols]
            cumulative = 0.5 * (1.0 + lax.erf(before * (1.0 / math.sqrt(2.0))))
            active[rows, cols] = (before * cumulative).astype(BF)
            slope[rows, cols] = cumulative + before * (jnp.exp(-0.5 * before * before) * (1.0 / math.sqrt(2.0 * math.pi)))
        return carry

    lax.fori_loop(0, seqs, enter, 0)
    gvec[...] = jnp.zeros_like(gvec)

    def add_vec(n, value):
        start = n * width if n < 3 else (3 * width + (0 if n == 3 else FF + (n - 4) * width))
        gvec[:, start:start + value.shape[1]] += value

    def leave(s, carry):
        rows = seq_rows(s)
        down = gf[1].reshape(FF, width)
        branch = dot_nn(active[rows], down) + vec_part(vec, 4, width)
        resid = normed[rows] * vec_part(vec, 5, width) + vec_part(vec, 6, width) + branch
        center = resid - mean_of(resid)
        scale = lax.rsqrt(mean_of(center * center) + norm_floor)
        second = center * scale
        served = served_flag(keep, routes, s) > 0
        result = second * vec_part(vec, 7, width) + vec_part(vec, 8, width)
        out[rows] = jnp.where(served, result.astype(BF), x[rows])
        grad = jnp.where(served, cot[rows].astype(F32), 0.0)
        add_vec(7, jnp.sum(grad * second, axis=0, keepdims=True))
        add_vec(8, jnp.sum(grad, axis=0, keepdims=True))
        grad = grad * vec_part(vec, 7, width)
        grad = scale * (grad - mean_of(grad) - second * mean_of(grad * second))
        middle[rows] = grad
        grad_low[rows] = grad.astype(BF)
        add_vec(4, jnp.sum(grad.astype(BF).astype(F32), axis=0, keepdims=True))
        return carry

    lax.fori_loop(0, seqs, leave, 0)
    for q in range(4):
        cols = slice(q * width, (q + 1) * width)
        hf[1, q] = dot_tn(active[:, cols], grad_low[...]).astype(BF).reshape(4, 2, BLOCK, width)

        def turn(s, carry):
            rows = seq_rows(s)
            back = dot_nt(grad_low[rows], gf[1, q].reshape(width, width)) * slope[rows, cols]
            active[rows, cols] = back.astype(BF)
            start = 3 * width + q * width
            gvec[:, start:start + width] += jnp.sum(back.astype(BF).astype(F32), axis=0, keepdims=True)
            return carry

        lax.fori_loop(0, seqs, turn, 0)
        c, j = q // 2, q % 2
        found = dot_tn(low[...], active[:, cols]).astype(BF).reshape(4, 2, BLOCK, width)
        for y in range(2):
            hf[0, :, 2 * y + c, j] = found[:, y]

    def close(s, carry):
        rows = seq_rows(s)
        grad = middle[rows]
        for q in range(4):
            grad += dot_nt(active[rows, q * width:(q + 1) * width], up(q))
        first = normed[rows]
        add_vec(5, jnp.sum(grad * first, axis=0, keepdims=True))
        add_vec(6, jnp.sum(grad, axis=0, keepdims=True))
        grad = grad * vec_part(vec, 5, width)
        grad_resid[rows] = factor[rows] * (grad - mean_of(grad) - first * mean_of(grad * first))
        return carry

    lax.fori_loop(0, seqs, close, 0)


def feed(x, normed, factor, gf, vec, cot, keep, routes):
    tokens, width = x.shape
    outs = [jax.ShapeDtypeStruct(x.shape, BF), jax.ShapeDtypeStruct(gf.shape, BF), jax.ShapeDtypeStruct(x.shape, F32),
            jax.ShapeDtypeStruct(vec.shape, F32)]
    scratch = [pltpu.VMEM((tokens, FF), BF), pltpu.VMEM((tokens, FF), F32), pltpu.VMEM(x.shape, F32),
               pltpu.VMEM(x.shape, BF), pltpu.VMEM(x.shape, BF)]
    return vmem_call(feed_forward, (x, normed, factor, gf, vec, cot, keep, routes), outs, scratch, "feed_forward", smem=(6, 7))


def attention_back_start(ga, context, grad_resid, grad_low, grad_context, ha, gvec):
    width = context.shape[1]

    def tile(s, carry):
        rows = seq_rows(s)
        grad_low[rows] = grad_resid[rows].astype(BF)
        grad_context[rows] = dot_nt(grad_low[rows], square_of(ga[1, 2:4])).astype(BF)
        return carry

    lax.fori_loop(0, context.shape[0] // LEN, tile, 0)
    gvec[:, 2 * width:] = jnp.sum(grad_low[...].astype(F32), axis=0, keepdims=True)
    ha[1, 2:4] = dot_tn(context[...], grad_low[...]).astype(BF).reshape(2, 4, BLOCK, width)


def attention_back_end(x, cot, ga, grad_resid, keep, routes, gq, gk, gv, in_grad, ha, gvec):
    width = x.shape[1]
    gvec[:, 0:width] = jnp.sum(gq[...].astype(F32), axis=0, keepdims=True)
    gvec[:, width:2 * width] = jnp.sum(gv[...].astype(F32), axis=0, keepdims=True)
    ha[0, 0:2] = dot_tn(x[...], gq[...]).astype(BF).reshape(2, 4, BLOCK, width)
    ha[0, 2:4] = dot_tn(x[...], gk[...]).astype(BF).reshape(2, 4, BLOCK, width)
    ha[1, 0:2] = dot_tn(x[...], gv[...]).astype(BF).reshape(2, 4, BLOCK, width)
    input_gradient(x, cot, ga, grad_resid, keep, routes, gq, gk, gv, in_grad)


def input_gradient(x, cot, ga, grad_resid, keep, routes, gq, gk, gv, in_grad):
    def tile(s, carry):
        rows = seq_rows(s)
        total = grad_resid[rows] + dot_nt(gq[rows], square_of(ga[0, 0:2]))
        total += dot_nt(gk[rows], square_of(ga[0, 2:4]))
        total += dot_nt(gv[rows], square_of(ga[1, 0:2]))
        in_grad[rows] = jnp.where(served_flag(keep, routes, s) > 0, total.astype(BF), cot[rows])
        return carry

    lax.fori_loop(0, x.shape[0] // LEN, tile, 0)


def attention_back_kernel(x, cot, ga, q, k, v, context, log_total, grad_resid, lens, keep, routes,
                          in_grad, ha, gvec, grad_low, grad_context, gq, gk, gv):
    attention_back_start(ga, context, grad_resid, grad_low, grad_context, ha, gvec)

    def step(n, carry):
        attend_back(n, q, k, v, grad_context, log_total, lens, gq, gk, gv)
        return carry

    lax.fori_loop(0, 12, step, 0)
    attention_back_end(x, cot, ga, grad_resid, keep, routes, gq, gk, gv, in_grad, ha, gvec)


def attention_back(x, cot, ga, q, k, v, context, log_total, grad_resid, lens, keep, routes):
    width = x.shape[1]
    outs = [jax.ShapeDtypeStruct(x.shape, BF), jax.ShapeDtypeStruct(ga.shape, BF), jax.ShapeDtypeStruct((1, 3 * width), F32)]
    scratch = [pltpu.VMEM(x.shape, BF)] * 5
    return vmem_call(attention_back_kernel, (x, cot, ga, q, k, v, context, log_total, grad_resid, lens, keep, routes),
                     outs, scratch, "attention_back", smem=(9, 10, 11))


TOP = lax.Precision.HIGHEST


def shampoo_block(grad, w, st, ro, mo, st_new, mo_new, w_new, b, factor):
    clipped = grad * factor
    moment = momentum_decay * mo[b] + clipped
    left = lax.dot_general(clipped, clipped, (((1,), (1,)), ((), ())), precision=TOP, preferred_element_type=F32)
    right = lax.dot_general(clipped, clipped, (((0,), (0,)), ((), ())), precision=TOP, preferred_element_type=F32)
    st_new[b, 0] = stat_decay * st[b, 0] + (1.0 - stat_decay) * left
    st_new[b, 1] = stat_decay * st[b, 1] + (1.0 - stat_decay) * right
    mo_new[b] = moment
    turned = jnp.dot(ro[b, 0], moment, precision=TOP, preferred_element_type=F32)
    turned = jnp.dot(turned, ro[b, 1], precision=TOP, preferred_element_type=F32)
    w_new[b] = w[b] - matrix_rate * (turned + matrix_decay * w[b])


def optimizer_kernel(norm, ga, gf, sv, aw, ast, ar, am, fw, fst, fr, fm, vw, v1, v2,
                     ast_n, am_n, aw_n, fst_n, fm_n, fw_n, v1_n, v2_n, vw_n):
    factor = clip_bound / jnp.maximum(norm[...], clip_bound)
    shampoo_block(ga[0], aw, ast, ar, am, ast_n, am_n, aw_n, 0, factor)
    shampoo_block(gf[0], fw, fst, fr, fm, fst_n, fm_n, fw_n, 0, factor)
    shampoo_block(gf[1], fw, fst, fr, fm, fst_n, fm_n, fw_n, 1, factor)

    @pl.when(pl.program_id(0) == 0)
    def _():
        size = vw.shape[0]
        clipped = (sv[0:1, 0:size] * factor)[0]
        first_new = first_decay * v1[...] + (1.0 - first_decay) * clipped
        second_new = second_decay * v2[...] + (1.0 - second_decay) * clipped * clipped
        first_hat = first_new / (1.0 - first_decay**STEP)
        second_hat = second_new / (1.0 - second_decay**STEP)
        v1_n[...] = first_new
        v2_n[...] = second_new
        vw_n[...] = vw[...] - vector_rate * first_hat / (jnp.sqrt(second_hat) + adam_floor)


def optimizer(norm, ga, gf, sv, aw, ast, ar, am, fw, fst, fr, fm, vw, v1, v2):
    def steps(t, n):
        shape = (n,) + t.shape[1:]
        return pl.BlockSpec(shape, lambda g: (g,) + (0,) * (len(shape) - 1))

    def whole(t):
        return pl.BlockSpec(t.shape, lambda g: (0,) * t.ndim)

    like = lambda t: jax.ShapeDtypeStruct(t.shape, F32)
    args = (norm, ga, gf, sv, aw, ast, ar, am, fw, fst, fr, fm, vw, v1, v2)
    specs = [whole(norm), steps(ga, 1), steps(gf, 2), whole(sv)]
    specs += [steps(t, 1) for t in (aw, ast, ar, am)] + [steps(t, 2) for t in (fw, fst, fr, fm)]
    specs += [whole(t) for t in (vw, v1, v2)]
    outs = (ast, am, aw, fst, fm, fw, v1, v2, vw)
    return pl.pallas_call(
        optimizer_kernel,
        out_shape=[like(t) for t in outs],
        grid=(8,),
        in_specs=specs,
        out_specs=[steps(t, 1) for t in outs[:3]] + [steps(t, 2) for t in outs[3:6]] + [whole(t) for t in outs[6:]],
        name="optimizer",
    )(*args)


def per_device(
    inputs,
    output_gradient,
    keep,
    lengths,
    routes,
    attn_weights,
    attn_stats,
    attn_roots,
    attn_momentum,
    ffn_weights,
    ffn_stats,
    ffn_roots,
    ffn_momentum,
    vec_weights,
    vec_first,
    vec_second,
):
    slots, seq_len, width = inputs.shape
    tokens = slots * seq_len
    per_row = width // BLOCK
    share = vec_weights.shape[0]
    strip = attn_weights.astype(BF).transpose(1, 0, 2).reshape(BLOCK, width)
    pair = ffn_weights.astype(BF).reshape(2, per_row, BLOCK, BLOCK).transpose(0, 2, 1, 3).reshape(2, BLOCK, width)
    own = jnp.pad(vec_weights.astype(BF).astype(F32)[None], ((0, 7), (0, 96)))
    ga, gv, gf = gather(strip, own, pair)
    vec = gv[..., 0, :share].reshape(1, -1)
    x = inputs.reshape(tokens, width)
    cot = output_gradient.reshape(tokens, width)
    q, k, v, context, log_total, normed, factor = attention(x, ga, vec, lengths)
    out, hf, grad_resid, ffn_vec = feed(x, normed, factor, gf, vec, cot, keep, routes)
    in_grad, ha, attn_vec = attention_back(x, cot, ga, q, k, v, context, log_total, grad_resid, lengths, keep, routes)
    vec_grad = jnp.concatenate([attn_vec, ffn_vec[:, 3 * width:]], axis=1)
    hv = jnp.pad(vec_grad.reshape(2, 4, 4, 1, share), ((0, 0),) * 3 + ((0, 7), (0, 96)))
    bf, ba, sv, norm = scatter(hf, ha, hv)
    rest = optimizer(
        norm, ba, bf, sv,
        attn_weights, attn_stats, attn_roots, attn_momentum,
        ffn_weights, ffn_stats, ffn_roots, ffn_momentum,
        vec_weights, vec_first, vec_second,
    )
    return (out.reshape(inputs.shape), in_grad.reshape(inputs.shape), norm.reshape(()), *rest)


def solution(mesh):
    small = mesh.shape["depth"] == 2 and mesh.shape["dp"] == 16
    return jax.shard_map(
        per_device if small else per_device_general,
        mesh=mesh,
        in_specs=(
            P(("depth", "dp"), None, None),
            P(("depth", "dp"), None, None),
            P(("depth", "dp")),
            P(("depth", "dp")),
            P(("depth", "dp")),
            P(("depth", "dp"), None, None),
            P(("depth", "dp"), None, None, None),
            P(("depth", "dp"), None, None, None),
            P(("depth", "dp"), None, None),
            P(("depth", "dp"), None, None),
            P(("depth", "dp"), None, None, None),
            P(("depth", "dp"), None, None, None),
            P(("depth", "dp"), None, None),
            P(("depth", "dp")),
            P(("depth", "dp")),
            P(("depth", "dp")),
        ),
        out_specs=(
            P(("depth", "dp"), None, None),
            P(("depth", "dp"), None, None),
            P(),
            P(("depth", "dp"), None, None, None),
            P(("depth", "dp"), None, None),
            P(("depth", "dp"), None, None),
            P(("depth", "dp"), None, None, None),
            P(("depth", "dp"), None, None),
            P(("depth", "dp"), None, None),
            P(("depth", "dp")),
            P(("depth", "dp")),
            P(("depth", "dp")),
        ),
        check_vma=False,
    )
```

```python
import functools
import math

import jax
import jax.numpy as jnp
from jax import lax
from jax.experimental import pallas as pl
from jax.experimental.pallas import tpu as pltpu
from jax.sharding import PartitionSpec as P

HEADS = 12
FF = 3072
BLOCK = 96
STEP = 10


norm_floor = 1e-05
masked_fill = -1000000000.0
momentum_decay = 0.9
stat_decay = 0.95
matrix_rate = 1.0
matrix_decay = 0.01
clip_bound = 1.0
first_decay = 0.9
second_decay = 0.999
vector_rate = 0.5
adam_floor = 1e-08


def serve_flags(keep_rows, route_rows):
    count = keep_rows.shape[-1]
    order = jnp.arange(count, dtype=jnp.int32)
    earlier = (order[None, :] < order[:, None]).astype(jnp.int32)
    same = (route_rows[:, :, None] == route_rows[:, None, :]).astype(jnp.int32)
    clash = jnp.sum(same * earlier[None, :, :] * keep_rows[:, None, :], axis=2)
    return keep_rows * (clash == 0).astype(jnp.int32)


def to_matrix(blocks, height, breadth):
    shaped = blocks.reshape(height // BLOCK, breadth // BLOCK, BLOCK, BLOCK)
    return shaped.transpose(0, 2, 1, 3).reshape(height, breadth)


def to_flat_blocks(matrix):
    height, breadth = matrix.shape
    shaped = matrix.reshape(height // BLOCK, BLOCK, breadth // BLOCK, BLOCK)
    return shaped.transpose(0, 2, 1, 3).reshape(-1, BLOCK * BLOCK)


def norm_parts(resid):
    center = resid - jnp.mean(resid, axis=-1, keepdims=True)
    factor = lax.rsqrt(jnp.mean(center * center, axis=-1, keepdims=True) + norm_floor)
    return (center * factor, factor)


def norm_back(grad_normed, normed, factor):
    middle = jnp.mean(grad_normed, axis=-1, keepdims=True)
    along = jnp.mean(grad_normed * normed, axis=-1, keepdims=True)
    return factor * (grad_normed - middle - normed * along)


def gelu_slope(value):
    cumulative = 0.5 * (1.0 + lax.erf(value * (1.0 / math.sqrt(2.0))))
    density = jnp.exp(-0.5 * value * value) * (1.0 / math.sqrt(2.0 * math.pi))
    return cumulative + value * density


def product(left, right):
    return jnp.dot(left, right, preferred_element_type=jnp.float32)


def contract_rows(left, right):
    return lax.dot_general(
        left, right, (((0,), (0,)), ((), ())), preferred_element_type=jnp.float32
    )


def times_transpose(left, right):
    return lax.dot_general(
        left, right, (((1,), (1,)), ((), ())), preferred_element_type=jnp.float32
    )


def masked_scores(query, keys, visible_len):
    scale = 1.0 / math.sqrt(query.shape[-1])
    scores = jnp.einsum("qhe,khe->hqk", query, keys, preferred_element_type=jnp.float32) * scale
    visible = jnp.arange(keys.shape[0], dtype=jnp.int32) < visible_len
    return jnp.where(visible[None, None, :], scores, masked_fill)


def attend_forward(pieces):
    query, keys, values, visible_len = pieces
    scores = masked_scores(query, keys, visible_len)
    peak = jnp.max(scores, axis=-1, keepdims=True)
    expo = jnp.exp(scores - peak)
    total = jnp.sum(expo, axis=-1, keepdims=True)
    probs_low = (expo / total).astype(jnp.bfloat16)
    context = jnp.einsum("hqk,khe->qhe", probs_low, values, preferred_element_type=jnp.float32)
    return (context, peak[..., 0] + jnp.log(total[..., 0]))


def attend_backward(pieces):
    query, keys, values, grad_ctx, log_total, visible_len = pieces
    scale = 1.0 / math.sqrt(query.shape[-1])
    scores = masked_scores(query, keys, visible_len)
    probs = jnp.exp(scores - log_total[..., None])
    probs_low = probs.astype(jnp.bfloat16)
    grad_probs = jnp.einsum("qhe,khe->hqk", grad_ctx, values, preferred_element_type=jnp.float32)
    grad_values = jnp.einsum(
        "hqk,qhe->khe", probs_low, grad_ctx, preferred_element_type=jnp.float32
    )
    along = jnp.sum(probs * grad_probs, axis=-1, keepdims=True)
    grad_scores = (probs * (grad_probs - along)).astype(jnp.bfloat16)
    grad_query = (
        jnp.einsum("hqk,khe->qhe", grad_scores, keys, preferred_element_type=jnp.float32) * scale
    )
    grad_keys = (
        jnp.einsum("hqk,qhe->khe", grad_scores, query, preferred_element_type=jnp.float32) * scale
    )
    return (grad_query, grad_keys, grad_values)


def shampoo(weights, stats, roots, momentum, grads, factor):
    highest = lax.Precision.HIGHEST
    clipped = grads * factor
    moment = momentum_decay * momentum + clipped
    left = jnp.einsum("nab,ncb->nac", clipped, clipped, precision=highest)
    right = jnp.einsum("nab,nac->nbc", clipped, clipped, precision=highest)
    fresh = stat_decay * stats + (1.0 - stat_decay) * jnp.stack([left, right], axis=1)
    turned = jnp.einsum("nab,nbc->nac", roots[:, 0], moment, precision=highest)
    turned = jnp.einsum("nab,nbc->nac", turned, roots[:, 1], precision=highest)
    updated = weights - matrix_rate * (turned + matrix_decay * weights)
    return (fresh, moment, updated)


def adam_step(weights, first, second, grads, factor):
    clipped = grads * factor
    first_new = first_decay * first + (1.0 - first_decay) * clipped
    second_new = second_decay * second + (1.0 - second_decay) * clipped * clipped
    first_hat = first_new / (1.0 - first_decay**STEP)
    second_hat = second_new / (1.0 - second_decay**STEP)
    updated = weights - vector_rate * first_hat / (jnp.sqrt(second_hat) + adam_floor)
    return (first_new, second_new, updated)


def per_device_general(
    inputs,
    output_gradient,
    keep,
    lengths,
    routes,
    attn_weights,
    attn_stats,
    attn_roots,
    attn_momentum,
    ffn_weights,
    ffn_stats,
    ffn_roots,
    ffn_momentum,
    vec_weights,
    vec_first,
    vec_second,
):
    slots, seq_len, width = inputs.shape
    tokens = slots * seq_len
    head_size = width // HEADS
    hidden_width = FF
    depth_count = lax.axis_size("depth")
    peer_slots = slots // depth_count
    grid = (width // BLOCK) ** 2
    half_ffn = width * hidden_width // (BLOCK * BLOCK)
    area = BLOCK * BLOCK
    low_type = jnp.bfloat16
    attn_flat = attn_weights.reshape(-1, area).astype(low_type)
    ffn_flat = ffn_weights.reshape(-1, area).astype(low_type)
    attn_all, ffn_all, vec_all = (
        lax.all_gather(attn_flat, ("depth", "dp"), axis=0, tiled=True),
        lax.all_gather(ffn_flat, ("depth", "dp"), axis=0, tiled=True),
        lax.all_gather(vec_weights.astype(low_type), ("depth", "dp"), axis=0, tiled=True),
    )
    table_keep, table_len, table_route = (
        lax.all_gather(keep, "depth", axis=0, tiled=True),
        lax.all_gather(lengths, "depth", axis=0, tiled=True),
        lax.all_gather(routes, "depth", axis=0, tiled=True),
    )
    mine = serve_flags(keep[None, :], routes[None, :])[0]
    slot_order = jnp.arange(slots, dtype=jnp.int32)
    selection = ((routes[None, :] == slot_order[:, None]).astype(jnp.int32) * mine[None, :]).astype(
        low_type
    )
    outgoing_rows = jnp.einsum(
        "gz,zrp->grp", selection, inputs, preferred_element_type=jnp.float32
    ).astype(low_type)
    send_grad = jnp.einsum(
        "gz,zrp->grp", selection, output_gradient, preferred_element_type=jnp.float32
    ).astype(low_type)
    come_rows, come_grad = (
        lax.all_to_all(outgoing_rows, "depth", split_axis=0, concat_axis=0, tiled=True),
        lax.all_to_all(send_grad, "depth", split_axis=0, concat_axis=0, tiled=True),
    )
    all_keep = table_keep.reshape(depth_count, slots)
    all_route = table_route.reshape(depth_count, slots)
    all_len = table_len.reshape(depth_count, slots)
    all_served = serve_flags(all_keep, all_route)
    here = lax.axis_index("depth")
    source = slot_order // peer_slots
    target = here * peer_slots + slot_order % peer_slots
    source_hot = (source[:, None] == jnp.arange(depth_count, dtype=jnp.int32)[None, :]).astype(
        jnp.int32
    )
    match = (all_route[None, :, :] == target[:, None, None]).astype(jnp.int32) * all_served[
        None, :, :
    ]
    slot_len = jnp.sum(source_hot[:, :, None] * match * all_len[None, :, :], axis=(1, 2))
    visible_len = jnp.maximum(slot_len, 1)
    query_w = to_matrix(attn_all[0:grid], width, width)
    key_w = to_matrix(attn_all[grid : 2 * grid], width, width)
    value_w = to_matrix(attn_all[2 * grid : 3 * grid], width, width)
    output_w = to_matrix(attn_all[3 * grid : 4 * grid], width, width)
    vectors = vec_all.astype(jnp.float32)
    q_bias = vectors[0:width]
    v_bias = vectors[width : 2 * width]
    out_bias = vectors[2 * width : 3 * width]
    hidden_bias = vectors[3 * width : 3 * width + hidden_width]
    ffn_bias = vectors[3 * width + hidden_width : 4 * width + hidden_width]
    gain_one = vectors[4 * width + hidden_width : 5 * width + hidden_width]
    shift_one = vectors[5 * width + hidden_width : 6 * width + hidden_width]
    gain_two = vectors[6 * width + hidden_width : 7 * width + hidden_width]
    shift_two = vectors[7 * width + hidden_width : 8 * width + hidden_width]
    flat = come_rows.reshape(tokens, width)
    four = (slots, seq_len, HEADS, head_size)
    query = (product(flat, query_w) + q_bias).astype(low_type).reshape(four)
    keys = product(flat, key_w).astype(low_type).reshape(four)
    values = (product(flat, value_w) + v_bias).astype(low_type).reshape(four)
    context, log_total = lax.map(attend_forward, (query, keys, values, visible_len))
    context_low = context.reshape(tokens, width).astype(low_type)
    attended = product(context_low, output_w) + out_bias
    normed_one, factor_one = norm_parts(flat.astype(jnp.float32) + attended)
    hidden_in = normed_one * gain_one + shift_one
    hidden_low = hidden_in.astype(low_type)
    hidden_w = to_matrix(ffn_all[0:half_ffn], width, hidden_width)
    return_weight = to_matrix(ffn_all[half_ffn:], hidden_width, width)
    before = product(hidden_low, hidden_w) + hidden_bias
    active_low = jax.nn.gelu(before, approximate=False).astype(low_type)
    branch = product(active_low, return_weight) + ffn_bias
    normed_two, factor_two = norm_parts(hidden_in + branch)
    result_low = (normed_two * gain_two + shift_two).astype(low_type)
    grad_rows = come_grad.reshape(tokens, width).astype(jnp.float32)
    grad_gain_two = jnp.sum(grad_rows * normed_two, axis=0)
    grad_shift_two = jnp.sum(grad_rows, axis=0)
    grad_resid_two = norm_back(grad_rows * gain_two, normed_two, factor_two)
    grad_branch = grad_resid_two.astype(low_type)
    grad_ffn_bias = jnp.sum(grad_branch.astype(jnp.float32), axis=0)
    gradient_return_weight = contract_rows(active_low, grad_branch)
    grad_active = times_transpose(grad_branch, return_weight)
    grad_before = (grad_active * gelu_slope(before)).astype(low_type)
    grad_hidden_bias = jnp.sum(grad_before.astype(jnp.float32), axis=0)
    grad_hidden_w = contract_rows(hidden_low, grad_before)
    grad_hidden = times_transpose(grad_before, hidden_w) + grad_resid_two
    grad_gain_one = jnp.sum(grad_hidden * normed_one, axis=0)
    grad_shift_one = jnp.sum(grad_hidden, axis=0)
    grad_resid_one = norm_back(grad_hidden * gain_one, normed_one, factor_one)
    ffn_grad = jnp.concatenate(
        [to_flat_blocks(grad_hidden_w), to_flat_blocks(gradient_return_weight)], axis=0
    )
    grad_attended = grad_resid_one.astype(low_type)
    grad_out_bias = jnp.sum(grad_attended.astype(jnp.float32), axis=0)
    grad_output_w = contract_rows(context_low, grad_attended)
    grad_context = times_transpose(grad_attended, output_w).astype(low_type).reshape(four)
    grad_query, grad_keys, grad_values = lax.map(
        attend_backward, (query, keys, values, grad_context, log_total, visible_len)
    )
    grad_query = grad_query.reshape(tokens, width).astype(low_type)
    grad_keys = grad_keys.reshape(tokens, width).astype(low_type)
    grad_values = grad_values.reshape(tokens, width).astype(low_type)
    grad_q_bias = jnp.sum(grad_query.astype(jnp.float32), axis=0)
    grad_v_bias = jnp.sum(grad_values.astype(jnp.float32), axis=0)
    grad_query_w = contract_rows(flat, grad_query)
    grad_key_w = contract_rows(flat, grad_keys)
    grad_value_w = contract_rows(flat, grad_values)
    in_rows = (
        grad_resid_one
        + times_transpose(grad_query, query_w)
        + times_transpose(grad_keys, key_w)
        + times_transpose(grad_values, value_w)
    )
    attn_grad = jnp.concatenate(
        [
            to_flat_blocks(grad_query_w),
            to_flat_blocks(grad_key_w),
            to_flat_blocks(grad_value_w),
            to_flat_blocks(grad_output_w),
        ],
        axis=0,
    )
    vec_grad = jnp.concatenate(
        [
            grad_q_bias,
            grad_v_bias,
            grad_out_bias,
            grad_hidden_bias,
            grad_ffn_bias,
            grad_gain_one,
            grad_shift_one,
            grad_gain_two,
            grad_shift_two,
        ]
    )
    attn_share, ffn_share, vec_share = (
        lax.psum_scatter(attn_grad, ("depth", "dp"), scatter_dimension=0, tiled=True),
        lax.psum_scatter(ffn_grad, ("depth", "dp"), scatter_dimension=0, tiled=True),
        lax.psum_scatter(vec_grad, ("depth", "dp"), scatter_dimension=0, tiled=True),
    )
    returned_rows, returned_gradient = (
        lax.all_to_all(
            result_low.reshape(slots, seq_len, width),
            "depth",
            split_axis=0,
            concat_axis=0,
            tiled=True,
        ),
        lax.all_to_all(
            in_rows.astype(low_type).reshape(slots, seq_len, width),
            "depth",
            split_axis=0,
            concat_axis=0,
            tiled=True,
        ),
    )
    stay = (1 - mine).astype(jnp.float32)[:, None, None]
    out = (
        jnp.einsum("rx,rmp->xmp", selection, returned_rows, preferred_element_type=jnp.float32)
        + stay * inputs.astype(jnp.float32)
    ).astype(low_type)
    in_grad = (
        jnp.einsum("rx,rmp->xmp", selection, returned_gradient, preferred_element_type=jnp.float32)
        + stay * output_gradient.astype(jnp.float32)
    ).astype(low_type)
    square = (
        jnp.sum(attn_share * attn_share)
        + jnp.sum(ffn_share * ffn_share)
        + jnp.sum(vec_share * vec_share)
    )
    total = lax.psum(square, ("depth", "dp"))
    grad_norm = jnp.sqrt(total)
    factor = clip_bound / jnp.maximum(grad_norm, clip_bound)
    attn_square = attn_share.reshape(-1, BLOCK, BLOCK)
    ffn_square = ffn_share.reshape(-1, BLOCK, BLOCK)
    attn_fresh, attn_moment, attn_updated = shampoo(
        attn_weights, attn_stats, attn_roots, attn_momentum, attn_square, factor
    )
    ffn_fresh, ffn_moment, ffn_updated = shampoo(
        ffn_weights, ffn_stats, ffn_roots, ffn_momentum, ffn_square, factor
    )
    first_new, second_new, vec_updated = adam_step(
        vec_weights, vec_first, vec_second, vec_share, factor
    )
    return (
        out,
        in_grad,
        grad_norm,
        attn_fresh,
        attn_moment,
        attn_updated,
        ffn_fresh,
        ffn_moment,
        ffn_updated,
        first_new,
        second_new,
        vec_updated,
    )


MESH = pl.DeviceIdType.MESH
BF = jnp.bfloat16
F32 = jnp.float32
LEN = 512
ROWS = 16


def place():
    d = lax.axis_index("depth")
    i = lax.axis_index("dp")
    x = i % 2
    y = (i // 2) % 2
    nx = i + 1 - 2 * x
    ny = i + 2 - 4 * y
    na = ny + d * (nx - ny)
    nb = nx + d * (ny - nx)
    return dict(d=d, i=i, z=i // 4, c=i % 4, na=na, nb=nb, ca=na % 4, cb=nb % 4, cd=3 - i % 4)


def near(p):
    peers = [(p["d"], p["na"]), (p["d"], p["nb"]), (1 - p["d"], p["i"])]
    return peers + [(p["d"], ((p["z"] + k) % 4) * 4 + p["c"]) for k in (1, 2, 3)]


def greet(peers):
    barrier = pltpu.get_barrier_semaphore()
    for peer in peers:
        pl.semaphore_signal(barrier, inc=1, device_id=peer, device_id_type=MESH)


def meet(peers):
    pl.semaphore_wait(pltpu.get_barrier_semaphore(), len(peers))


def remote(src, dst, send, recv, k, dev):
    return pltpu.make_async_remote_copy(src_ref=src, dst_ref=dst, send_sem=send.at[k], recv_sem=recv.at[k],
                                        device_id=dev, device_id_type=MESH)


class Mail:
    def __init__(self, p, send, recv):
        self.p, self.send, self.recv, self.sent = p, send, recv, []

    def go(self, src, dst, k, dev):
        copy = remote(src, dst, self.send, self.recv, k, dev)
        copy.start()
        self.sent.append(copy)

    def wait(self, dst, k):
        remote(dst, dst, self.send, self.recv, k, (self.p["d"], self.p["na"])).wait_recv()

    def drain(self):
        for copy in self.sent:
            copy.wait_send()


class Spread(Mail):
    def __init__(self, p, own, slot, column, send, recv, local):
        Mail.__init__(self, p, send, recv)
        self.own, self.slot, self.column, self.local = own, slot, column, local

    def start(self):
        p = self.p
        here = self.slot(p["d"], p["z"], p["c"])
        self.keep = pltpu.make_async_copy(self.own, here, self.local)
        self.keep.start()
        for k in (2, 1, 3):
            self.go(self.own, here, k - 1, (p["d"], ((p["z"] + k) % 4) * 4 + p["c"]))

    def second(self):
        p = self.p
        self.keep.wait()
        for k in (1, 2, 3):
            self.wait(self.slot(p["d"], (p["z"] + 4 - k) % 4, p["c"]), k - 1)
        mine = self.column(p["d"], p["c"])
        self.go(mine, mine, 3, (p["d"], p["na"]))
        self.go(mine, mine, 4, (p["d"], p["nb"]))
        self.go(mine, mine, 6, (1 - p["d"], p["i"]))

    def third(self):
        p = self.p
        got = self.column(p["d"], p["ca"])
        self.wait(got, 3)
        self.go(got, got, 5, (p["d"], p["nb"]))
        self.go(got, got, 8 - p["d"], (1 - p["d"], p["i"]))

    def fourth(self):
        p = self.p
        got = self.column(p["d"], p["cb"])
        self.wait(got, 4)
        self.go(got, got, 7 + p["d"], (1 - p["d"], p["i"]))

    def fifth(self):
        p = self.p
        got = self.column(p["d"], p["cd"])
        self.wait(got, 5)
        self.go(got, got, 9, (1 - p["d"], p["i"]))

    def sixth(self):
        p = self.p
        for k, col in ((6, p["c"]), (8 - p["d"], p["ca"]), (7 + p["d"], p["cb"]), (9, p["cd"])):
            self.wait(self.column(1 - p["d"], col), k)


def spread_sems():
    return [pltpu.SemaphoreType.DMA((10,)), pltpu.SemaphoreType.DMA((10,)), pltpu.SemaphoreType.DMA]


def one_hot(shape, row, col):
    r = lax.broadcasted_iota(jnp.int32, shape, 0)
    c = lax.broadcasted_iota(jnp.int32, shape, 1)
    return (row(r) == col(c)).astype(F32)


def unfold_vec(pieces, vec, share):
    per = share // BLOCK
    stack = pieces[...][:, :, :, 0, :].reshape(32, pieces.shape[-1])
    units = sum(
        jnp.dot(one_hot((32 * per, 32), lambda u: u, lambda k, a=a: per * k + a), stack[:, a * BLOCK:(a + 1) * BLOCK],
                preferred_element_type=F32)
        for a in range(per)
    )
    for b in range(8):
        vec[:, b * BLOCK:(b + 1) * BLOCK] = jnp.dot(
            one_hot((ROWS, 32 * per), lambda r, b=b: 8 * r + b, lambda u: u), units, preferred_element_type=F32)


def dot_nn(a, b):
    return lax.dot_general(a, b, (((1,), (0,)), ((), ())), preferred_element_type=F32)


def dot_nt(a, b):
    return lax.dot_general(a, b, (((1,), (1,)), ((), ())), preferred_element_type=F32)


def dot_tn(a, b):
    return lax.dot_general(a, b, (((0,), (0,)), ((), ())), preferred_element_type=F32)


def square_of(value):
    return value.reshape(value.shape[0] * value.shape[1] * value.shape[2], value.shape[3])


def seq_rows(s):
    return pl.ds(s * LEN, LEN) if isinstance(s, int) else pl.ds(pl.multiple_of(s * LEN, LEN), LEN)


def tile_rows(s, size):
    return pl.ds(pl.multiple_of(s * size, size), size)


def served_flag(keep, routes, s):
    other = keep[0] * (routes[0] == routes[1]).astype(jnp.int32)
    return jnp.where(s == 0, keep[0], keep[1] * (1 - other))


def projections(x, ga, vec, q, k, v):
    width = x.shape[1]

    def tile(s, carry):
        rows = seq_rows(s)
        xr = x[rows]
        q[rows] = (dot_nn(xr, square_of(ga[0, 0:2])) + vec[0:1]).astype(BF)
        k[rows] = dot_nn(xr, square_of(ga[0, 2:4])).astype(BF)
        v[rows] = (dot_nn(xr, square_of(ga[1, 0:2])) + vec[1:2]).astype(BF)
        return carry

    lax.fori_loop(0, x.shape[0] // LEN, tile, 0)


def head_pairs(n, lens):
    s, g = n // 6, n % 6
    first = lax.broadcasted_iota(jnp.int32, (1, 128), 1) < 64
    return s, seq_rows(s), pl.ds(pl.multiple_of(g * 128, 128), 128), (first, jnp.logical_not(first))


def attend(n, q, k, v, lens, context, log_total):
    s, rows, cols, halves = head_pairs(n, lens)
    qp, kp, vp = q[rows, cols], k[rows, cols], v[rows, cols]
    seen = lax.broadcasted_iota(jnp.int32, (1, LEN), 1) < lens[s]
    found = []
    for h in range(2):
        qm = jnp.where(halves[h], qp, jnp.zeros_like(qp))
        scores = jnp.where(seen, dot_nt(qm, kp) * 0.125, masked_fill)
        peak = jnp.max(scores, axis=1, keepdims=True)
        expo = jnp.exp(scores - peak)
        total = jnp.sum(expo, axis=1, keepdims=True)
        found.append(dot_nn((expo * (1.0 / total)).astype(BF), vp))
        log_total[n, h] = (peak + jnp.log(total))[:, 0]
    context[rows, cols] = jnp.where(halves[0], found[0], found[1]).astype(BF)


def attend_back(n, q, k, v, grad_context, log_total, lens, gq, gk, gv):
    s, rows, cols, halves = head_pairs(n, lens)
    qp, kp, vp, gp = q[rows, cols], k[rows, cols], v[rows, cols], grad_context[rows, cols]
    seen = lax.broadcasted_iota(jnp.int32, (LEN, 1), 0) < lens[s]
    zero = jnp.zeros_like(qp)
    aq = ak = av = jnp.zeros((LEN, 128), F32)
    for h in range(2):
        qm, km, gm = (jnp.where(halves[h], t, zero) for t in (qp, kp, gp))
        scores = jnp.where(seen, dot_nt(kp, qm) * 0.125, masked_fill)
        probs = jnp.exp(scores - log_total[n, h][None, :])
        grad_probs = dot_nt(vp, gm)
        along = jnp.sum(probs * grad_probs, axis=0, keepdims=True)
        grad_scores = (probs * (grad_probs - along)).astype(BF)
        av += dot_nn(probs.astype(BF), gm)
        ak += dot_nn(grad_scores, qm)
        aq += dot_tn(grad_scores, km)
    gq[rows, cols] = (aq * 0.125).astype(BF)
    gk[rows, cols] = (ak * 0.125).astype(BF)
    gv[rows, cols] = av.astype(BF)


def mean_of(t):
    return jnp.mean(t, axis=-1, keepdims=True)


def attention_end(x, context, ga, vec, normed, factor):
    width = x.shape[1]

    def tile(s, carry):
        rows = seq_rows(s)
        attended = dot_nn(context[rows], square_of(ga[1, 2:4])) + vec[2:3]
        resid = x[rows].astype(F32) + attended
        center = resid - mean_of(resid)
        scale = lax.rsqrt(mean_of(center * center) + norm_floor)
        normed[rows] = center * scale
        factor[rows] = scale
        return carry

    lax.fori_loop(0, x.shape[0] // LEN, tile, 0)


def attention_kernel(x, ga, vec, lens, q, k, v, context, log_total, normed, factor):
    projections(x, ga, vec, q, k, v)

    def step(n, carry):
        attend(n, q, k, v, lens, context, log_total)
        return carry

    lax.fori_loop(0, 12, step, 0)
    attention_end(x, context, ga, vec, normed, factor)


def vmem_call(kernel, args, outs, scratch, name, smem=(), limit=62 << 20):
    space = lambda n: pltpu.SMEM if n in smem else pltpu.VMEM
    return pl.pallas_call(
        kernel,
        out_shape=outs,
        in_specs=[pl.BlockSpec(memory_space=space(n)) for n in range(len(args))],
        out_specs=[pl.BlockSpec(memory_space=pltpu.VMEM)] * len(outs),
        scratch_shapes=scratch,
        compiler_params=pltpu.CompilerParams(vmem_limit_bytes=limit),
        name=name,
    )(*args)


def attention(x, ga, vec, lens):
    low = jax.ShapeDtypeStruct(x.shape, BF)
    outs = [low] * 4 + [jax.ShapeDtypeStruct((12, 2, LEN), F32), jax.ShapeDtypeStruct(x.shape, F32),
                        jax.ShapeDtypeStruct((x.shape[0], 1), F32)]
    return vmem_call(attention_kernel, (x, ga, vec, lens), outs, [], "attention", smem=(3,))


def vec_part(vec, n):
    return vec[n:n + 1]


def feed_forward(x, normed, factor, gf, vec, cot, keep, routes, out, hf, grad_resid, gvec, active, slope, middle, low, grad_low):
    width = x.shape[1]
    seqs = x.shape[0] // LEN

    def up(q):
        c, j = q // 2, q % 2
        return jnp.concatenate([gf[0, z, 2 * y + c, j] for z in range(4) for y in range(2)], axis=0)

    def enter(s, carry):
        rows = seq_rows(s)
        low[rows] = (normed[rows] * vec_part(vec, 8) + vec_part(vec, 9)).astype(BF)
        for q in range(4):
            cols = slice(q * width, (q + 1) * width)
            before = dot_nn(low[rows], up(q)) + vec_part(vec, 3 + q)
            cumulative = 0.5 * (1.0 + lax.erf(before * (1.0 / math.sqrt(2.0))))
            active[rows, cols] = (before * cumulative).astype(BF)
            slope[rows, cols] = cumulative + before * (jnp.exp(-0.5 * before * before) * (1.0 / math.sqrt(2.0 * math.pi)))
        return carry

    lax.fori_loop(0, seqs, enter, 0)
    gvec[...] = jnp.zeros_like(gvec)

    def add_vec(n, value):
        gvec[n:n + 1] += value

    def leave(s, carry):
        rows = seq_rows(s)
        down = gf[1].reshape(FF, width)
        branch = dot_nn(active[rows], down) + vec_part(vec, 7)
        resid = normed[rows] * vec_part(vec, 8) + vec_part(vec, 9) + branch
        center = resid - mean_of(resid)
        scale = lax.rsqrt(mean_of(center * center) + norm_floor)
        second = center * scale
        served = served_flag(keep, routes, s) > 0
        result = second * vec_part(vec, 10) + vec_part(vec, 11)
        out[rows] = jnp.where(served, result.astype(BF), x[rows])
        grad = jnp.where(served, cot[rows].astype(F32), 0.0)
        add_vec(10, jnp.sum(grad * second, axis=0, keepdims=True))
        add_vec(11, jnp.sum(grad, axis=0, keepdims=True))
        grad = grad * vec_part(vec, 10)
        grad = scale * (grad - mean_of(grad) - second * mean_of(grad * second))
        middle[rows] = grad
        grad_low[rows] = grad.astype(BF)
        add_vec(7, jnp.sum(grad.astype(BF).astype(F32), axis=0, keepdims=True))
        return carry

    lax.fori_loop(0, seqs, leave, 0)
    for q in range(4):
        cols = slice(q * width, (q + 1) * width)
        hf[1, q] = dot_tn(active[:, cols], grad_low[...]).astype(BF).reshape(4, 2, BLOCK, width)

        def turn(s, carry):
            rows = seq_rows(s)
            back = dot_nt(grad_low[rows], gf[1, q].reshape(width, width)) * slope[rows, cols]
            active[rows, cols] = back.astype(BF)
            add_vec(3 + q, jnp.sum(back.astype(BF).astype(F32), axis=0, keepdims=True))
            return carry

        lax.fori_loop(0, seqs, turn, 0)
        c, j = q // 2, q % 2
        found = dot_tn(low[...], active[:, cols]).astype(BF).reshape(4, 2, BLOCK, width)
        for y in range(2):
            hf[0, :, 2 * y + c, j] = found[:, y]

    def close(s, carry):
        rows = seq_rows(s)
        grad = middle[rows]
        for q in range(4):
            grad += dot_nt(active[rows, q * width:(q + 1) * width], up(q))
        first = normed[rows]
        add_vec(8, jnp.sum(grad * first, axis=0, keepdims=True))
        add_vec(9, jnp.sum(grad, axis=0, keepdims=True))
        grad = grad * vec_part(vec, 8)
        grad_resid[rows] = factor[rows] * (grad - mean_of(grad) - first * mean_of(grad * first))
        return carry

    lax.fori_loop(0, seqs, close, 0)


def feed(x, normed, factor, gf, vec, cot, keep, routes):
    tokens, width = x.shape
    outs = [jax.ShapeDtypeStruct(x.shape, BF), jax.ShapeDtypeStruct(gf.shape, BF), jax.ShapeDtypeStruct(x.shape, F32),
            jax.ShapeDtypeStruct(vec.shape, F32)]
    scratch = [pltpu.VMEM((tokens, FF), BF), pltpu.VMEM((tokens, FF), F32), pltpu.VMEM(x.shape, F32),
               pltpu.VMEM(x.shape, BF), pltpu.VMEM(x.shape, BF)]
    return vmem_call(feed_forward, (x, normed, factor, gf, vec, cot, keep, routes), outs, scratch, "feed_forward", smem=(6, 7))


def attention_back_start(ga, context, grad_resid, grad_low, grad_context, ha, gvec):
    width = context.shape[1]

    def tile(s, carry):
        rows = seq_rows(s)
        grad_low[rows] = grad_resid[rows].astype(BF)
        grad_context[rows] = dot_nt(grad_low[rows], square_of(ga[1, 2:4])).astype(BF)
        return carry

    lax.fori_loop(0, context.shape[0] // LEN, tile, 0)
    gvec[2:3] = jnp.sum(grad_low[...].astype(F32), axis=0, keepdims=True)
    ha[1, 2:4] = dot_tn(context[...], grad_low[...]).astype(BF).reshape(2, 4, BLOCK, width)


def attention_back_end(x, cot, ga, grad_resid, keep, routes, gq, gk, gv, in_grad, ha, gvec):
    width = x.shape[1]
    gvec[0:1] = jnp.sum(gq[...].astype(F32), axis=0, keepdims=True)
    gvec[1:2] = jnp.sum(gv[...].astype(F32), axis=0, keepdims=True)
    ha[0, 0:2] = dot_tn(x[...], gq[...]).astype(BF).reshape(2, 4, BLOCK, width)
    ha[0, 2:4] = dot_tn(x[...], gk[...]).astype(BF).reshape(2, 4, BLOCK, width)
    ha[1, 0:2] = dot_tn(x[...], gv[...]).astype(BF).reshape(2, 4, BLOCK, width)
    input_gradient(x, cot, ga, grad_resid, keep, routes, gq, gk, gv, in_grad)


def input_gradient(x, cot, ga, grad_resid, keep, routes, gq, gk, gv, in_grad):
    def tile(s, carry):
        rows = seq_rows(s)
        total = grad_resid[rows] + dot_nt(gq[rows], square_of(ga[0, 0:2]))
        total += dot_nt(gk[rows], square_of(ga[0, 2:4]))
        total += dot_nt(gv[rows], square_of(ga[1, 0:2]))
        in_grad[rows] = jnp.where(served_flag(keep, routes, s) > 0, total.astype(BF), cot[rows])
        return carry

    lax.fori_loop(0, x.shape[0] // LEN, tile, 0)


def attention_back_kernel(x, cot, ga, q, k, v, context, log_total, grad_resid, lens, keep, routes,
                          in_grad, ha, gvec, grad_low, grad_context, gq, gk, gv):
    attention_back_start(ga, context, grad_resid, grad_low, grad_context, ha, gvec)

    def step(n, carry):
        attend_back(n, q, k, v, grad_context, log_total, lens, gq, gk, gv)
        return carry

    lax.fori_loop(0, 12, step, 0)
    attention_back_end(x, cot, ga, grad_resid, keep, routes, gq, gk, gv, in_grad, ha, gvec)


def attention_back(x, cot, ga, q, k, v, context, log_total, grad_resid, lens, keep, routes):
    width = x.shape[1]
    outs = [jax.ShapeDtypeStruct(x.shape, BF), jax.ShapeDtypeStruct(ga.shape, BF), jax.ShapeDtypeStruct((8, width), F32)]
    scratch = [pltpu.VMEM(x.shape, BF)] * 5
    return vmem_call(attention_back_kernel, (x, cot, ga, q, k, v, context, log_total, grad_resid, lens, keep, routes),
                     outs, scratch, "attention_back", smem=(9, 10, 11))


def gather_attention_kernel(aw, fw, vw, x, lens, gf, ga, vec, q_out, k_out, v_out, context_out, log_total, normed_out, factor,
                            gv, strip, pair, own, q, k, v, context, normed, store, *sems):
    p = place()
    peers = near(p)
    greet(peers)
    share = vw.shape[0]
    own[...] = jnp.zeros_like(own)
    own[0:1, 0:share] = vw[...].astype(BF).astype(F32).reshape(1, share)
    for b in range(8):
        strip[:, b * BLOCK:(b + 1) * BLOCK] = aw[b].astype(BF)
    for j in range(2):
        for b in range(8):
            pair[j, :, b * BLOCK:(b + 1) * BLOCK] = fw[8 * j + b].astype(BF)
    half = BLOCK // 2

    def attn_part(h):
        rows = pl.ds(h * half, half)
        return strip.at[rows], lambda d, z, c: ga.at[d, z, c, rows], lambda d, c: ga.at[d, :, c, rows]

    def feed_part(j):
        return pair.at[j], lambda d, z, c: gf.at[d, z, c, j], lambda d, c: gf.at[d, :, c, j]

    vec_part = own, lambda d, z, c: gv.at[d, z, c], lambda d, c: gv.at[d, :, c]
    parts = [attn_part(0), vec_part, attn_part(1), feed_part(0), feed_part(1)]
    a0, w, a1, f0, f1 = every = [Spread(p, *part, *sems[3 * n:3 * n + 3]) for n, part in enumerate(parts)]
    meet(peers)
    for s in every:
        s.start()
    a0.second()
    w.second()
    a1.second()
    for s in (a0, w, a1):
        s.third()
        s.fourth()
    f0.second()
    for s in (a0, w, a1):
        s.fifth()
    w.sixth()
    unfold_vec(gv, vec, share)
    a0.sixth()
    a1.sixth()
    projections(x, ga, vec, q, k, v)
    stores = [pltpu.make_async_copy(src, dst, store.at[n])
              for n, (src, dst) in enumerate(((q, q_out), (k, k_out), (v, v_out), (context, context_out), (normed, normed_out)))]
    for copy in stores[:3]:
        copy.start()

    def step(n, carry):
        attend(n, q, k, v, lens, context, log_total)
        return carry

    lax.fori_loop(0, 3, step, 0)
    f0.third()
    f0.fourth()
    f1.second()
    lax.fori_loop(3, 9, step, 0)
    f0.fifth()
    lax.fori_loop(9, 12, step, 0)
    stores[3].start()
    attention_end(x, context, ga, vec, normed, factor)
    stores[4].start()
    f1.third()
    f1.fourth()
    f1.fifth()
    f0.sixth()
    f1.sixth()
    for s in every:
        s.drain()
    for copy in stores:
        copy.wait()


def gather_attention(aw, fw, vw, x, lens):
    width = x.shape[1]
    low = jax.ShapeDtypeStruct(x.shape, BF)
    outs = [jax.ShapeDtypeStruct((2, 4, 4, 2, BLOCK, width), BF), jax.ShapeDtypeStruct((2, 4, 4, BLOCK, width), BF),
            jax.ShapeDtypeStruct((ROWS, width), F32)] + [low] * 4
    outs += [jax.ShapeDtypeStruct((12, 2, LEN), F32), jax.ShapeDtypeStruct(x.shape, F32),
             jax.ShapeDtypeStruct((x.shape[0], 1), F32)]
    vmem = pl.BlockSpec(memory_space=pltpu.VMEM)
    hbm = pl.BlockSpec(memory_space=pl.ANY)
    return pl.pallas_call(
        gather_attention_kernel,
        out_shape=outs,
        in_specs=[vmem] * 4 + [pl.BlockSpec(memory_space=pltpu.SMEM)],
        out_specs=[hbm, vmem, vmem] + [hbm] * 4 + [vmem, hbm, vmem],
        scratch_shapes=[pltpu.VMEM((2, 4, 4, 8, 384), F32), pltpu.VMEM((BLOCK, width), BF),
                        pltpu.VMEM((2, BLOCK, width), BF), pltpu.VMEM((8, 384), F32)]
        + [pltpu.VMEM(x.shape, BF)] * 4 + [pltpu.VMEM(x.shape, F32), pltpu.SemaphoreType.DMA((5,))]
        + spread_sems() * 5,
        compiler_params=pltpu.CompilerParams(collective_id=0, has_side_effects=True, vmem_limit_bytes=62 << 20),
        name="gather_attention",
    )(aw, fw, vw, x, lens)


class Fold:
    def __init__(self, p, mine, pair, diag, flat, late, line, send, recv):
        self.p, self.mine, self.pair, self.diag, self.flat, self.late, self.line = p, mine, pair, diag, flat, late, line
        self.send, self.recv, self.sent = send, recv, []

    def go(self, src, dst, k, dev):
        copy = remote(src, dst, self.send, self.recv, k, dev)
        copy.start()
        self.sent.append(copy)

    def wait(self, dst, k):
        remote(dst, dst, self.send, self.recv, k, (self.p["d"], self.p["na"])).wait_recv()

    def add(self, dst, *others):
        total = dst[...].astype(F32)
        for o in others:
            total += o[...].astype(F32)
        dst[...] = total.astype(dst.dtype)

    def start(self):
        p = self.p
        self.go(self.mine.at[1 - p["d"]], self.pair, 0, (1 - p["d"], p["i"]))

    def second(self):
        p = self.p
        self.wait(self.pair, 0)
        for col, dst, k in ((p["cd"], self.diag, 1), (p["cb"], self.flat, 2)):
            self.add(self.pair.at[:, col], self.mine.at[p["d"], :, col])
            self.go(self.pair.at[:, col], dst, k, (p["d"], p["nb"]))
        for col in (p["ca"], p["c"]):
            self.add(self.pair.at[:, col], self.mine.at[p["d"], :, col])

    def third(self):
        p = self.p
        self.wait(self.diag, 1)
        src = self.pair.at[:, p["ca"]]
        self.add(src, self.diag)
        self.go(src, self.late, 3, (p["d"], p["na"]))

    def fourth(self):
        p = self.p
        self.wait(self.flat, 2)
        self.wait(self.late, 3)
        for k in (2, 1, 3, 0):
            dst = (p["z"] + k) % 4
            self.add(self.pair.at[dst, p["c"]], self.flat.at[dst], self.late.at[dst])
            if k:
                self.go(self.pair.at[dst, p["c"]], self.line.at[k - 1], 3 + k, (p["d"], dst * 4 + p["c"]))

    def fifth(self, out):
        p = self.p
        total = self.pair[p["z"], p["c"]].astype(F32)
        for k in (1, 2, 3):
            self.wait(self.line.at[k - 1], 3 + k)
            total += self.line[k - 1].astype(F32)
        out[...] = total

    def drain(self):
        for copy in self.sent:
            copy.wait_send()


def fold_scratch(shape, dtype):
    return [pltpu.VMEM((4, 4) + shape, dtype), pltpu.VMEM((4,) + shape, dtype), pltpu.VMEM((4,) + shape, dtype),
            pltpu.VMEM((4,) + shape, dtype), pltpu.VMEM((3,) + shape, dtype),
            pltpu.SemaphoreType.DMA((7,)), pltpu.SemaphoreType.DMA((7,))]


def greet_all(p):
    barrier = pltpu.get_barrier_semaphore()
    me = p["d"] * 16 + p["i"]
    for k in range(1, 32):
        t = (me + k) % 32
        pl.semaphore_signal(barrier, inc=1, device_id=(t // 16, t % 16), device_id_type=MESH)
    pl.semaphore_wait(barrier, 31)


def norm_sum(p, square, slots, send, recv):
    me = p["d"] * 16 + p["i"]
    slots[0] = jnp.full((8, 128), square, F32)
    copies = []
    for k in range(1, 32):
        t = (me + k) % 32
        copy = remote(slots.at[0], slots.at[k], send, recv, k, (t // 16, t % 16))
        copy.start()
        copies.append(copy)
    for copy in copies:
        copy.wait_recv()
    total = jnp.sum(slots[...], axis=0)[0:1, 0:1]
    for copy in copies:
        copy.wait_send()
    return total


def scatter_kernel(f, a, v, bf, ba, sv, norm, sf, sa, slots, nsend, nrecv, *scratch):
    p = place()
    greet_all(p)
    parts = [Fold(p, mine, *scratch[7 * n:7 * n + 7]) for n, mine in enumerate((f, a, v))]
    for step in ("start", "second", "third", "fourth"):
        for s in parts:
            getattr(s, step)()
    for s, out in zip(parts, (sf, sa, sv)):
        s.fifth(out)
    square = jnp.sum(sa[...] * sa[...]) + jnp.sum(sf[...] * sf[...]) + jnp.sum(sv[...] * sv[...])
    total = norm_sum(p, square, slots, nsend, nrecv)
    norm[...] = jnp.sqrt(total)
    for b in range(8):
        ba[b] = sa[:, b * BLOCK:(b + 1) * BLOCK]
        for j in range(2):
            bf[8 * j + b] = sf[j, :, b * BLOCK:(b + 1) * BLOCK]
    for s in parts:
        s.drain()


def scatter(f, a, v):
    outs = [jax.ShapeDtypeStruct(s, F32) for s in ((16, BLOCK, BLOCK), (8, BLOCK, BLOCK), v.shape[3:], (1, 1))]
    return pl.pallas_call(
        scatter_kernel,
        out_shape=outs,
        in_specs=[pl.BlockSpec(memory_space=pltpu.VMEM)] * 3,
        out_specs=[pl.BlockSpec(memory_space=pltpu.VMEM)] * 4,
        scratch_shapes=[pltpu.VMEM(f.shape[3:], F32), pltpu.VMEM(a.shape[3:], F32), pltpu.VMEM((32, 8, 128), F32),
                        pltpu.SemaphoreType.DMA((32,)), pltpu.SemaphoreType.DMA((32,))]
        + sum((fold_scratch(t.shape[3:], t.dtype) for t in (f, a, v)), []),
        compiler_params=pltpu.CompilerParams(collective_id=1, has_side_effects=True, vmem_limit_bytes=60 << 20),
        name="grad_scatter",
    )(f, a, v)


TOP = lax.Precision.HIGHEST


def shampoo_block(grad, w, st, ro, mo, st_new, mo_new, w_new, b, factor):
    clipped = grad * factor
    moment = momentum_decay * mo[b] + clipped
    left = lax.dot_general(clipped, clipped, (((1,), (1,)), ((), ())), precision=TOP, preferred_element_type=F32)
    right = lax.dot_general(clipped, clipped, (((0,), (0,)), ((), ())), precision=TOP, preferred_element_type=F32)
    st_new[b, 0] = stat_decay * st[b, 0] + (1.0 - stat_decay) * left
    st_new[b, 1] = stat_decay * st[b, 1] + (1.0 - stat_decay) * right
    mo_new[b] = moment
    turned = jnp.dot(ro[b, 0], moment, precision=TOP, preferred_element_type=F32)
    turned = jnp.dot(turned, ro[b, 1], precision=TOP, preferred_element_type=F32)
    w_new[b] = w[b] - matrix_rate * (turned + matrix_decay * w[b])


def optimizer_kernel(norm, ga, gf, sv, aw, ast, ar, am, fw, fst, fr, fm, vw, v1, v2,
                     ast_n, am_n, aw_n, fst_n, fm_n, fw_n, v1_n, v2_n, vw_n):
    factor = clip_bound / jnp.maximum(norm[...], clip_bound)
    shampoo_block(ga[0], aw, ast, ar, am, ast_n, am_n, aw_n, 0, factor)
    shampoo_block(gf[0], fw, fst, fr, fm, fst_n, fm_n, fw_n, 0, factor)
    shampoo_block(gf[1], fw, fst, fr, fm, fst_n, fm_n, fw_n, 1, factor)

    @pl.when(pl.program_id(0) == 0)
    def _():
        size = vw.shape[0]
        clipped = (sv[0:1, 0:size] * factor)[0]
        first_new = first_decay * v1[...] + (1.0 - first_decay) * clipped
        second_new = second_decay * v2[...] + (1.0 - second_decay) * clipped * clipped
        first_hat = first_new / (1.0 - first_decay**STEP)
        second_hat = second_new / (1.0 - second_decay**STEP)
        v1_n[...] = first_new
        v2_n[...] = second_new
        vw_n[...] = vw[...] - vector_rate * first_hat / (jnp.sqrt(second_hat) + adam_floor)


def optimizer(norm, ga, gf, sv, aw, ast, ar, am, fw, fst, fr, fm, vw, v1, v2):
    def steps(t, n):
        shape = (n,) + t.shape[1:]
        return pl.BlockSpec(shape, lambda g: (g,) + (0,) * (len(shape) - 1))

    def whole(t):
        return pl.BlockSpec(t.shape, lambda g: (0,) * t.ndim)

    like = lambda t: jax.ShapeDtypeStruct(t.shape, F32)
    args = (norm, ga, gf, sv, aw, ast, ar, am, fw, fst, fr, fm, vw, v1, v2)
    specs = [whole(norm), steps(ga, 1), steps(gf, 2), whole(sv)]
    specs += [steps(t, 1) for t in (aw, ast, ar, am)] + [steps(t, 2) for t in (fw, fst, fr, fm)]
    specs += [whole(t) for t in (vw, v1, v2)]
    outs = (ast, am, aw, fst, fm, fw, v1, v2, vw)
    return pl.pallas_call(
        optimizer_kernel,
        out_shape=[like(t) for t in outs],
        grid=(8,),
        in_specs=specs,
        out_specs=[steps(t, 1) for t in outs[:3]] + [steps(t, 2) for t in outs[3:6]] + [whole(t) for t in outs[6:]],
        name="optimizer",
    )(*args)


def per_device(
    inputs,
    output_gradient,
    keep,
    lengths,
    routes,
    attn_weights,
    attn_stats,
    attn_roots,
    attn_momentum,
    ffn_weights,
    ffn_stats,
    ffn_roots,
    ffn_momentum,
    vec_weights,
    vec_first,
    vec_second,
):
    slots, seq_len, width = inputs.shape
    tokens = slots * seq_len
    share = vec_weights.shape[0]
    x = inputs.reshape(tokens, width)
    cot = output_gradient.reshape(tokens, width)
    gf, ga, vec, q, k, v, context, log_total, normed, factor = gather_attention(attn_weights, ffn_weights, vec_weights, x, lengths)
    out, hf, grad_resid, ffn_vec = feed(x, normed, factor, gf, vec, cot, keep, routes)
    in_grad, ha, attn_vec = attention_back(x, cot, ga, q, k, v, context, log_total, grad_resid, lengths, keep, routes)
    vec_grad = jnp.concatenate([attn_vec[:3], ffn_vec[3:12]], axis=0)
    hv = jnp.pad(vec_grad.reshape(2, 4, 4, 1, share), ((0, 0),) * 3 + ((0, 7), (0, 96)))
    bf, ba, sv, norm = scatter(hf, ha, hv)
    rest = optimizer(
        norm, ba, bf, sv,
        attn_weights, attn_stats, attn_roots, attn_momentum,
        ffn_weights, ffn_stats, ffn_roots, ffn_momentum,
        vec_weights, vec_first, vec_second,
    )
    return (out.reshape(inputs.shape), in_grad.reshape(inputs.shape), norm.reshape(()), *rest)


def solution(mesh):
    small = mesh.shape["depth"] == 2 and mesh.shape["dp"] == 16
    return jax.shard_map(
        per_device if small else per_device_general,
        mesh=mesh,
        in_specs=(
            P(("depth", "dp"), None, None),
            P(("depth", "dp"), None, None),
            P(("depth", "dp")),
            P(("depth", "dp")),
            P(("depth", "dp")),
            P(("depth", "dp"), None, None),
            P(("depth", "dp"), None, None, None),
            P(("depth", "dp"), None, None, None),
            P(("depth", "dp"), None, None),
            P(("depth", "dp"), None, None),
            P(("depth", "dp"), None, None, None),
            P(("depth", "dp"), None, None, None),
            P(("depth", "dp"), None, None),
            P(("depth", "dp")),
            P(("depth", "dp")),
            P(("depth", "dp")),
        ),
        out_specs=(
            P(("depth", "dp"), None, None),
            P(("depth", "dp"), None, None),
            P(),
            P(("depth", "dp"), None, None, None),
            P(("depth", "dp"), None, None),
            P(("depth", "dp"), None, None),
            P(("depth", "dp"), None, None, None),
            P(("depth", "dp"), None, None),
            P(("depth", "dp"), None, None),
            P(("depth", "dp")),
            P(("depth", "dp")),
            P(("depth", "dp")),
        ),
        check_vma=False,
    )
```

```python
import functools
import math

import jax
import jax.numpy as jnp
from jax import lax
from jax.experimental import pallas as pl
from jax.experimental.pallas import tpu as pltpu
from jax.sharding import PartitionSpec as P

HEADS = 12
FF = 3072
BLOCK = 96
STEP = 10


norm_floor = 1e-05
masked_fill = -1000000000.0
momentum_decay = 0.9
stat_decay = 0.95
matrix_rate = 1.0
matrix_decay = 0.01
clip_bound = 1.0
first_decay = 0.9
second_decay = 0.999
vector_rate = 0.5
adam_floor = 1e-08


def serve_flags(keep_rows, route_rows):
    count = keep_rows.shape[-1]
    order = jnp.arange(count, dtype=jnp.int32)
    earlier = (order[None, :] < order[:, None]).astype(jnp.int32)
    same = (route_rows[:, :, None] == route_rows[:, None, :]).astype(jnp.int32)
    clash = jnp.sum(same * earlier[None, :, :] * keep_rows[:, None, :], axis=2)
    return keep_rows * (clash == 0).astype(jnp.int32)


def to_matrix(blocks, height, breadth):
    shaped = blocks.reshape(height // BLOCK, breadth // BLOCK, BLOCK, BLOCK)
    return shaped.transpose(0, 2, 1, 3).reshape(height, breadth)


def to_flat_blocks(matrix):
    height, breadth = matrix.shape
    shaped = matrix.reshape(height // BLOCK, BLOCK, breadth // BLOCK, BLOCK)
    return shaped.transpose(0, 2, 1, 3).reshape(-1, BLOCK * BLOCK)


def norm_parts(resid):
    center = resid - jnp.mean(resid, axis=-1, keepdims=True)
    factor = lax.rsqrt(jnp.mean(center * center, axis=-1, keepdims=True) + norm_floor)
    return (center * factor, factor)


def norm_back(grad_normed, normed, factor):
    middle = jnp.mean(grad_normed, axis=-1, keepdims=True)
    along = jnp.mean(grad_normed * normed, axis=-1, keepdims=True)
    return factor * (grad_normed - middle - normed * along)


def gelu_slope(value):
    cumulative = 0.5 * (1.0 + lax.erf(value * (1.0 / math.sqrt(2.0))))
    density = jnp.exp(-0.5 * value * value) * (1.0 / math.sqrt(2.0 * math.pi))
    return cumulative + value * density


def product(left, right):
    return jnp.dot(left, right, preferred_element_type=jnp.float32)


def contract_rows(left, right):
    return lax.dot_general(
        left, right, (((0,), (0,)), ((), ())), preferred_element_type=jnp.float32
    )


def times_transpose(left, right):
    return lax.dot_general(
        left, right, (((1,), (1,)), ((), ())), preferred_element_type=jnp.float32
    )


def masked_scores(query, keys, visible_len):
    scale = 1.0 / math.sqrt(query.shape[-1])
    scores = jnp.einsum("qhe,khe->hqk", query, keys, preferred_element_type=jnp.float32) * scale
    visible = jnp.arange(keys.shape[0], dtype=jnp.int32) < visible_len
    return jnp.where(visible[None, None, :], scores, masked_fill)


def attend_forward(pieces):
    query, keys, values, visible_len = pieces
    scores = masked_scores(query, keys, visible_len)
    peak = jnp.max(scores, axis=-1, keepdims=True)
    expo = jnp.exp(scores - peak)
    total = jnp.sum(expo, axis=-1, keepdims=True)
    probs_low = (expo / total).astype(jnp.bfloat16)
    context = jnp.einsum("hqk,khe->qhe", probs_low, values, preferred_element_type=jnp.float32)
    return (context, peak[..., 0] + jnp.log(total[..., 0]))


def attend_backward(pieces):
    query, keys, values, grad_ctx, log_total, visible_len = pieces
    scale = 1.0 / math.sqrt(query.shape[-1])
    scores = masked_scores(query, keys, visible_len)
    probs = jnp.exp(scores - log_total[..., None])
    probs_low = probs.astype(jnp.bfloat16)
    grad_probs = jnp.einsum("qhe,khe->hqk", grad_ctx, values, preferred_element_type=jnp.float32)
    grad_values = jnp.einsum(
        "hqk,qhe->khe", probs_low, grad_ctx, preferred_element_type=jnp.float32
    )
    along = jnp.sum(probs * grad_probs, axis=-1, keepdims=True)
    grad_scores = (probs * (grad_probs - along)).astype(jnp.bfloat16)
    grad_query = (
        jnp.einsum("hqk,khe->qhe", grad_scores, keys, preferred_element_type=jnp.float32) * scale
    )
    grad_keys = (
        jnp.einsum("hqk,qhe->khe", grad_scores, query, preferred_element_type=jnp.float32) * scale
    )
    return (grad_query, grad_keys, grad_values)


def shampoo(weights, stats, roots, momentum, grads, factor):
    highest = lax.Precision.HIGHEST
    clipped = grads * factor
    moment = momentum_decay * momentum + clipped
    left = jnp.einsum("nab,ncb->nac", clipped, clipped, precision=highest)
    right = jnp.einsum("nab,nac->nbc", clipped, clipped, precision=highest)
    fresh = stat_decay * stats + (1.0 - stat_decay) * jnp.stack([left, right], axis=1)
    turned = jnp.einsum("nab,nbc->nac", roots[:, 0], moment, precision=highest)
    turned = jnp.einsum("nab,nbc->nac", turned, roots[:, 1], precision=highest)
    updated = weights - matrix_rate * (turned + matrix_decay * weights)
    return (fresh, moment, updated)


def adam_step(weights, first, second, grads, factor):
    clipped = grads * factor
    first_new = first_decay * first + (1.0 - first_decay) * clipped
    second_new = second_decay * second + (1.0 - second_decay) * clipped * clipped
    first_hat = first_new / (1.0 - first_decay**STEP)
    second_hat = second_new / (1.0 - second_decay**STEP)
    updated = weights - vector_rate * first_hat / (jnp.sqrt(second_hat) + adam_floor)
    return (first_new, second_new, updated)


def per_device_general(
    inputs,
    output_gradient,
    keep,
    lengths,
    routes,
    attn_weights,
    attn_stats,
    attn_roots,
    attn_momentum,
    ffn_weights,
    ffn_stats,
    ffn_roots,
    ffn_momentum,
    vec_weights,
    vec_first,
    vec_second,
):
    slots, seq_len, width = inputs.shape
    tokens = slots * seq_len
    head_size = width // HEADS
    hidden_width = FF
    depth_count = lax.axis_size("depth")
    peer_slots = slots // depth_count
    grid = (width // BLOCK) ** 2
    half_ffn = width * hidden_width // (BLOCK * BLOCK)
    area = BLOCK * BLOCK
    low_type = jnp.bfloat16
    attn_flat = attn_weights.reshape(-1, area).astype(low_type)
    ffn_flat = ffn_weights.reshape(-1, area).astype(low_type)
    attn_all, ffn_all, vec_all = (
        lax.all_gather(attn_flat, ("depth", "dp"), axis=0, tiled=True),
        lax.all_gather(ffn_flat, ("depth", "dp"), axis=0, tiled=True),
        lax.all_gather(vec_weights.astype(low_type), ("depth", "dp"), axis=0, tiled=True),
    )
    table_keep, table_len, table_route = (
        lax.all_gather(keep, "depth", axis=0, tiled=True),
        lax.all_gather(lengths, "depth", axis=0, tiled=True),
        lax.all_gather(routes, "depth", axis=0, tiled=True),
    )
    mine = serve_flags(keep[None, :], routes[None, :])[0]
    slot_order = jnp.arange(slots, dtype=jnp.int32)
    selection = ((routes[None, :] == slot_order[:, None]).astype(jnp.int32) * mine[None, :]).astype(
        low_type
    )
    outgoing_rows = jnp.einsum(
        "gz,zrp->grp", selection, inputs, preferred_element_type=jnp.float32
    ).astype(low_type)
    send_grad = jnp.einsum(
        "gz,zrp->grp", selection, output_gradient, preferred_element_type=jnp.float32
    ).astype(low_type)
    come_rows, come_grad = (
        lax.all_to_all(outgoing_rows, "depth", split_axis=0, concat_axis=0, tiled=True),
        lax.all_to_all(send_grad, "depth", split_axis=0, concat_axis=0, tiled=True),
    )
    all_keep = table_keep.reshape(depth_count, slots)
    all_route = table_route.reshape(depth_count, slots)
    all_len = table_len.reshape(depth_count, slots)
    all_served = serve_flags(all_keep, all_route)
    here = lax.axis_index("depth")
    source = slot_order // peer_slots
    target = here * peer_slots + slot_order % peer_slots
    source_hot = (source[:, None] == jnp.arange(depth_count, dtype=jnp.int32)[None, :]).astype(
        jnp.int32
    )
    match = (all_route[None, :, :] == target[:, None, None]).astype(jnp.int32) * all_served[
        None, :, :
    ]
    slot_len = jnp.sum(source_hot[:, :, None] * match * all_len[None, :, :], axis=(1, 2))
    visible_len = jnp.maximum(slot_len, 1)
    query_w = to_matrix(attn_all[0:grid], width, width)
    key_w = to_matrix(attn_all[grid : 2 * grid], width, width)
    value_w = to_matrix(attn_all[2 * grid : 3 * grid], width, width)
    output_w = to_matrix(attn_all[3 * grid : 4 * grid], width, width)
    vectors = vec_all.astype(jnp.float32)
    q_bias = vectors[0:width]
    v_bias = vectors[width : 2 * width]
    out_bias = vectors[2 * width : 3 * width]
    hidden_bias = vectors[3 * width : 3 * width + hidden_width]
    ffn_bias = vectors[3 * width + hidden_width : 4 * width + hidden_width]
    gain_one = vectors[4 * width + hidden_width : 5 * width + hidden_width]
    shift_one = vectors[5 * width + hidden_width : 6 * width + hidden_width]
    gain_two = vectors[6 * width + hidden_width : 7 * width + hidden_width]
    shift_two = vectors[7 * width + hidden_width : 8 * width + hidden_width]
    flat = come_rows.reshape(tokens, width)
    four = (slots, seq_len, HEADS, head_size)
    query = (product(flat, query_w) + q_bias).astype(low_type).reshape(four)
    keys = product(flat, key_w).astype(low_type).reshape(four)
    values = (product(flat, value_w) + v_bias).astype(low_type).reshape(four)
    context, log_total = lax.map(attend_forward, (query, keys, values, visible_len))
    context_low = context.reshape(tokens, width).astype(low_type)
    attended = product(context_low, output_w) + out_bias
    normed_one, factor_one = norm_parts(flat.astype(jnp.float32) + attended)
    hidden_in = normed_one * gain_one + shift_one
    hidden_low = hidden_in.astype(low_type)
    hidden_w = to_matrix(ffn_all[0:half_ffn], width, hidden_width)
    return_weight = to_matrix(ffn_all[half_ffn:], hidden_width, width)
    before = product(hidden_low, hidden_w) + hidden_bias
    active_low = jax.nn.gelu(before, approximate=False).astype(low_type)
    branch = product(active_low, return_weight) + ffn_bias
    normed_two, factor_two = norm_parts(hidden_in + branch)
    result_low = (normed_two * gain_two + shift_two).astype(low_type)
    grad_rows = come_grad.reshape(tokens, width).astype(jnp.float32)
    grad_gain_two = jnp.sum(grad_rows * normed_two, axis=0)
    grad_shift_two = jnp.sum(grad_rows, axis=0)
    grad_resid_two = norm_back(grad_rows * gain_two, normed_two, factor_two)
    grad_branch = grad_resid_two.astype(low_type)
    grad_ffn_bias = jnp.sum(grad_branch.astype(jnp.float32), axis=0)
    gradient_return_weight = contract_rows(active_low, grad_branch)
    grad_active = times_transpose(grad_branch, return_weight)
    grad_before = (grad_active * gelu_slope(before)).astype(low_type)
    grad_hidden_bias = jnp.sum(grad_before.astype(jnp.float32), axis=0)
    grad_hidden_w = contract_rows(hidden_low, grad_before)
    grad_hidden = times_transpose(grad_before, hidden_w) + grad_resid_two
    grad_gain_one = jnp.sum(grad_hidden * normed_one, axis=0)
    grad_shift_one = jnp.sum(grad_hidden, axis=0)
    grad_resid_one = norm_back(grad_hidden * gain_one, normed_one, factor_one)
    ffn_grad = jnp.concatenate(
        [to_flat_blocks(grad_hidden_w), to_flat_blocks(gradient_return_weight)], axis=0
    )
    grad_attended = grad_resid_one.astype(low_type)
    grad_out_bias = jnp.sum(grad_attended.astype(jnp.float32), axis=0)
    grad_output_w = contract_rows(context_low, grad_attended)
    grad_context = times_transpose(grad_attended, output_w).astype(low_type).reshape(four)
    grad_query, grad_keys, grad_values = lax.map(
        attend_backward, (query, keys, values, grad_context, log_total, visible_len)
    )
    grad_query = grad_query.reshape(tokens, width).astype(low_type)
    grad_keys = grad_keys.reshape(tokens, width).astype(low_type)
    grad_values = grad_values.reshape(tokens, width).astype(low_type)
    grad_q_bias = jnp.sum(grad_query.astype(jnp.float32), axis=0)
    grad_v_bias = jnp.sum(grad_values.astype(jnp.float32), axis=0)
    grad_query_w = contract_rows(flat, grad_query)
    grad_key_w = contract_rows(flat, grad_keys)
    grad_value_w = contract_rows(flat, grad_values)
    in_rows = (
        grad_resid_one
        + times_transpose(grad_query, query_w)
        + times_transpose(grad_keys, key_w)
        + times_transpose(grad_values, value_w)
    )
    attn_grad = jnp.concatenate(
        [
            to_flat_blocks(grad_query_w),
            to_flat_blocks(grad_key_w),
            to_flat_blocks(grad_value_w),
            to_flat_blocks(grad_output_w),
        ],
        axis=0,
    )
    vec_grad = jnp.concatenate(
        [
            grad_q_bias,
            grad_v_bias,
            grad_out_bias,
            grad_hidden_bias,
            grad_ffn_bias,
            grad_gain_one,
            grad_shift_one,
            grad_gain_two,
            grad_shift_two,
        ]
    )
    attn_share, ffn_share, vec_share = (
        lax.psum_scatter(attn_grad, ("depth", "dp"), scatter_dimension=0, tiled=True),
        lax.psum_scatter(ffn_grad, ("depth", "dp"), scatter_dimension=0, tiled=True),
        lax.psum_scatter(vec_grad, ("depth", "dp"), scatter_dimension=0, tiled=True),
    )
    returned_rows, returned_gradient = (
        lax.all_to_all(
            result_low.reshape(slots, seq_len, width),
            "depth",
            split_axis=0,
            concat_axis=0,
            tiled=True,
        ),
        lax.all_to_all(
            in_rows.astype(low_type).reshape(slots, seq_len, width),
            "depth",
            split_axis=0,
            concat_axis=0,
            tiled=True,
        ),
    )
    stay = (1 - mine).astype(jnp.float32)[:, None, None]
    out = (
        jnp.einsum("rx,rmp->xmp", selection, returned_rows, preferred_element_type=jnp.float32)
        + stay * inputs.astype(jnp.float32)
    ).astype(low_type)
    in_grad = (
        jnp.einsum("rx,rmp->xmp", selection, returned_gradient, preferred_element_type=jnp.float32)
        + stay * output_gradient.astype(jnp.float32)
    ).astype(low_type)
    square = (
        jnp.sum(attn_share * attn_share)
        + jnp.sum(ffn_share * ffn_share)
        + jnp.sum(vec_share * vec_share)
    )
    total = lax.psum(square, ("depth", "dp"))
    grad_norm = jnp.sqrt(total)
    factor = clip_bound / jnp.maximum(grad_norm, clip_bound)
    attn_square = attn_share.reshape(-1, BLOCK, BLOCK)
    ffn_square = ffn_share.reshape(-1, BLOCK, BLOCK)
    attn_fresh, attn_moment, attn_updated = shampoo(
        attn_weights, attn_stats, attn_roots, attn_momentum, attn_square, factor
    )
    ffn_fresh, ffn_moment, ffn_updated = shampoo(
        ffn_weights, ffn_stats, ffn_roots, ffn_momentum, ffn_square, factor
    )
    first_new, second_new, vec_updated = adam_step(
        vec_weights, vec_first, vec_second, vec_share, factor
    )
    return (
        out,
        in_grad,
        grad_norm,
        attn_fresh,
        attn_moment,
        attn_updated,
        ffn_fresh,
        ffn_moment,
        ffn_updated,
        first_new,
        second_new,
        vec_updated,
    )


MESH = pl.DeviceIdType.MESH
BF = jnp.bfloat16
F32 = jnp.float32
LEN = 512
ROWS = 16


def place():
    d = lax.axis_index("depth")
    i = lax.axis_index("dp")
    x = i % 2
    y = (i // 2) % 2
    nx = i + 1 - 2 * x
    ny = i + 2 - 4 * y
    na = ny + d * (nx - ny)
    nb = nx + d * (ny - nx)
    return dict(d=d, i=i, z=i // 4, c=i % 4, na=na, nb=nb, ca=na % 4, cb=nb % 4, cd=3 - i % 4)


def near(p):
    peers = [(p["d"], p["na"]), (p["d"], p["nb"]), (1 - p["d"], p["i"])]
    return peers + [(p["d"], ((p["z"] + k) % 4) * 4 + p["c"]) for k in (1, 2, 3)]


def greet(peers):
    barrier = pltpu.get_barrier_semaphore()
    for peer in peers:
        pl.semaphore_signal(barrier, inc=1, device_id=peer, device_id_type=MESH)


def meet(peers):
    pl.semaphore_wait(pltpu.get_barrier_semaphore(), len(peers))


def remote(src, dst, send, recv, k, dev):
    return pltpu.make_async_remote_copy(src_ref=src, dst_ref=dst, send_sem=send.at[k], recv_sem=recv.at[k],
                                        device_id=dev, device_id_type=MESH)


class Mail:
    def __init__(self, p, send, recv):
        self.p, self.send, self.recv, self.sent = p, send, recv, []

    def go(self, src, dst, k, dev):
        copy = remote(src, dst, self.send, self.recv, k, dev)
        copy.start()
        self.sent.append(copy)

    def wait(self, dst, k):
        remote(dst, dst, self.send, self.recv, k, (self.p["d"], self.p["na"])).wait_recv()

    def drain(self):
        for copy in self.sent:
            copy.wait_send()


class Spread(Mail):
    def __init__(self, p, own, slot, column, send, recv, local):
        Mail.__init__(self, p, send, recv)
        self.own, self.slot, self.column, self.local = own, slot, column, local

    def start(self):
        p = self.p
        here = self.slot(p["d"], p["z"], p["c"])
        self.keep = pltpu.make_async_copy(self.own, here, self.local)
        self.keep.start()
        for k in (2, 1, 3):
            self.go(self.own, here, k - 1, (p["d"], ((p["z"] + k) % 4) * 4 + p["c"]))

    def second(self):
        p = self.p
        self.keep.wait()
        for k in (1, 2, 3):
            self.wait(self.slot(p["d"], (p["z"] + 4 - k) % 4, p["c"]), k - 1)
        mine = self.column(p["d"], p["c"])
        self.go(mine, mine, 3, (p["d"], p["na"]))
        self.go(mine, mine, 4, (p["d"], p["nb"]))
        self.go(mine, mine, 6, (1 - p["d"], p["i"]))

    def third(self):
        p = self.p
        got = self.column(p["d"], p["ca"])
        self.wait(got, 3)
        self.go(got, got, 5, (p["d"], p["nb"]))
        self.go(got, got, 8 - p["d"], (1 - p["d"], p["i"]))

    def fourth(self):
        p = self.p
        got = self.column(p["d"], p["cb"])
        self.wait(got, 4)
        self.go(got, got, 7 + p["d"], (1 - p["d"], p["i"]))

    def fifth(self):
        p = self.p
        got = self.column(p["d"], p["cd"])
        self.wait(got, 5)
        self.go(got, got, 9, (1 - p["d"], p["i"]))

    def sixth(self):
        p = self.p
        for k, col in ((6, p["c"]), (8 - p["d"], p["ca"]), (7 + p["d"], p["cb"]), (9, p["cd"])):
            self.wait(self.column(1 - p["d"], col), k)


def spread_sems():
    return [pltpu.SemaphoreType.DMA((10,)), pltpu.SemaphoreType.DMA((10,)), pltpu.SemaphoreType.DMA]


def one_hot(shape, row, col):
    r = lax.broadcasted_iota(jnp.int32, shape, 0)
    c = lax.broadcasted_iota(jnp.int32, shape, 1)
    return (row(r) == col(c)).astype(F32)


def unfold_vec(pieces, vec, share):
    per = share // BLOCK
    stack = pieces[...][:, :, :, 0, :].reshape(32, pieces.shape[-1])
    units = sum(
        jnp.dot(one_hot((32 * per, 32), lambda u: u, lambda k, a=a: per * k + a), stack[:, a * BLOCK:(a + 1) * BLOCK],
                preferred_element_type=F32)
        for a in range(per)
    )
    for b in range(8):
        vec[:, b * BLOCK:(b + 1) * BLOCK] = jnp.dot(
            one_hot((ROWS, 32 * per), lambda r, b=b: 8 * r + b, lambda u: u), units, preferred_element_type=F32)


def dot_nn(a, b):
    return lax.dot_general(a, b, (((1,), (0,)), ((), ())), preferred_element_type=F32)


def dot_nt(a, b):
    return lax.dot_general(a, b, (((1,), (1,)), ((), ())), preferred_element_type=F32)


def dot_tn(a, b):
    return lax.dot_general(a, b, (((0,), (0,)), ((), ())), preferred_element_type=F32)


def square_of(value):
    return value.reshape(value.shape[0] * value.shape[1] * value.shape[2], value.shape[3])


def seq_rows(s):
    return pl.ds(s * LEN, LEN) if isinstance(s, int) else pl.ds(pl.multiple_of(s * LEN, LEN), LEN)


def tile_rows(s, size):
    return pl.ds(pl.multiple_of(s * size, size), size)


def served_flag(keep, routes, s):
    other = keep[0] * (routes[0] == routes[1]).astype(jnp.int32)
    return jnp.where(s == 0, keep[0], keep[1] * (1 - other))


def projections(x, ga, vec, q, k, v):
    width = x.shape[1]

    def tile(s, carry):
        rows = seq_rows(s)
        xr = x[rows]
        q[rows] = (dot_nn(xr, square_of(ga[0, 0:2])) + vec[0:1]).astype(BF)
        k[rows] = dot_nn(xr, square_of(ga[0, 2:4])).astype(BF)
        v[rows] = (dot_nn(xr, square_of(ga[1, 0:2])) + vec[1:2]).astype(BF)
        return carry

    lax.fori_loop(0, x.shape[0] // LEN, tile, 0)


def head_pairs(n, lens):
    s, g = n // 6, n % 6
    first = lax.broadcasted_iota(jnp.int32, (1, 128), 1) < 64
    return s, seq_rows(s), pl.ds(pl.multiple_of(g * 128, 128), 128), (first, jnp.logical_not(first))


def attend(n, q, k, v, lens, context, log_total):
    s, rows, cols, halves = head_pairs(n, lens)
    qp, kp, vp = q[rows, cols], k[rows, cols], v[rows, cols]
    seen = lax.broadcasted_iota(jnp.int32, (1, LEN), 1) < lens[s]
    found = []
    for h in range(2):
        qm = jnp.where(halves[h], qp, jnp.zeros_like(qp))
        scores = jnp.where(seen, dot_nt(qm, kp) * 0.125, masked_fill)
        peak = jnp.max(scores, axis=1, keepdims=True)
        expo = jnp.exp(scores - peak)
        total = jnp.sum(expo, axis=1, keepdims=True)
        found.append(dot_nn((expo * (1.0 / total)).astype(BF), vp))
        log_total[n, h] = (peak + jnp.log(total))[:, 0]
    context[rows, cols] = jnp.where(halves[0], found[0], found[1]).astype(BF)


def attend_back(n, q, k, v, grad_context, log_total, lens, gq, gk, gv):
    s, rows, cols, halves = head_pairs(n, lens)
    qp, kp, vp, gp = q[rows, cols], k[rows, cols], v[rows, cols], grad_context[rows, cols]
    seen = lax.broadcasted_iota(jnp.int32, (LEN, 1), 0) < lens[s]
    zero = jnp.zeros_like(qp)
    aq = ak = av = jnp.zeros((LEN, 128), F32)
    for h in range(2):
        qm, km, gm = (jnp.where(halves[h], t, zero) for t in (qp, kp, gp))
        scores = jnp.where(seen, dot_nt(kp, qm) * 0.125, masked_fill)
        probs = jnp.exp(scores - log_total[n, h][None, :])
        grad_probs = dot_nt(vp, gm)
        along = jnp.sum(probs * grad_probs, axis=0, keepdims=True)
        grad_scores = (probs * (grad_probs - along)).astype(BF)
        av += dot_nn(probs.astype(BF), gm)
        ak += dot_nn(grad_scores, qm)
        aq += dot_tn(grad_scores, km)
    gq[rows, cols] = (aq * 0.125).astype(BF)
    gk[rows, cols] = (ak * 0.125).astype(BF)
    gv[rows, cols] = av.astype(BF)


def mean_of(t):
    return jnp.mean(t, axis=-1, keepdims=True)


def attention_end(x, context, ga, vec, normed, factor):
    width = x.shape[1]

    def tile(s, carry):
        rows = seq_rows(s)
        attended = dot_nn(context[rows], square_of(ga[1, 2:4])) + vec[2:3]
        resid = x[rows].astype(F32) + attended
        center = resid - mean_of(resid)
        scale = lax.rsqrt(mean_of(center * center) + norm_floor)
        normed[rows] = center * scale
        factor[rows] = scale
        return carry

    lax.fori_loop(0, x.shape[0] // LEN, tile, 0)


def vmem_call(kernel, args, outs, scratch, name, smem=(), limit=62 << 20):
    space = lambda n: pltpu.SMEM if n in smem else pltpu.VMEM
    return pl.pallas_call(
        kernel,
        out_shape=outs,
        in_specs=[pl.BlockSpec(memory_space=space(n)) for n in range(len(args))],
        out_specs=[pl.BlockSpec(memory_space=pltpu.VMEM)] * len(outs),
        scratch_shapes=scratch,
        compiler_params=pltpu.CompilerParams(vmem_limit_bytes=limit),
        name=name,
    )(*args)


def vec_part(vec, n):
    return vec[n:n + 1]


def feed_forward(x, normed, factor, gf, vec, cot, keep, routes, out, hf, grad_resid, gvec, active, slope, middle, low, grad_low):
    width = x.shape[1]
    seqs = x.shape[0] // LEN

    def up(q):
        c, j = q // 2, q % 2
        return jnp.concatenate([gf[0, z, 2 * y + c, j] for z in range(4) for y in range(2)], axis=0)

    def enter(s, carry):
        rows = seq_rows(s)
        low[rows] = (normed[rows] * vec_part(vec, 8) + vec_part(vec, 9)).astype(BF)
        for q in range(4):
            cols = slice(q * width, (q + 1) * width)
            before = dot_nn(low[rows], up(q)) + vec_part(vec, 3 + q)
            cumulative = 0.5 * (1.0 + lax.erf(before * (1.0 / math.sqrt(2.0))))
            active[rows, cols] = (before * cumulative).astype(BF)
            slope[rows, cols] = cumulative + before * (jnp.exp(-0.5 * before * before) * (1.0 / math.sqrt(2.0 * math.pi)))
        return carry

    lax.fori_loop(0, seqs, enter, 0)
    gvec[...] = jnp.zeros_like(gvec)

    def add_vec(n, value):
        gvec[n:n + 1] += value

    def leave(s, carry):
        rows = seq_rows(s)
        down = gf[1].reshape(FF, width)
        branch = dot_nn(active[rows], down) + vec_part(vec, 7)
        resid = normed[rows] * vec_part(vec, 8) + vec_part(vec, 9) + branch
        center = resid - mean_of(resid)
        scale = lax.rsqrt(mean_of(center * center) + norm_floor)
        second = center * scale
        served = served_flag(keep, routes, s) > 0
        result = second * vec_part(vec, 10) + vec_part(vec, 11)
        out[rows] = jnp.where(served, result.astype(BF), x[rows])
        grad = jnp.where(served, cot[rows].astype(F32), 0.0)
        add_vec(10, jnp.sum(grad * second, axis=0, keepdims=True))
        add_vec(11, jnp.sum(grad, axis=0, keepdims=True))
        grad = grad * vec_part(vec, 10)
        grad = scale * (grad - mean_of(grad) - second * mean_of(grad * second))
        middle[rows] = grad
        grad_low[rows] = grad.astype(BF)
        add_vec(7, jnp.sum(grad.astype(BF).astype(F32), axis=0, keepdims=True))
        return carry

    lax.fori_loop(0, seqs, leave, 0)
    for q in range(4):
        cols = slice(q * width, (q + 1) * width)
        hf[1, q] = dot_tn(active[:, cols], grad_low[...]).astype(BF).reshape(4, 2, BLOCK, width)

        def turn(s, carry):
            rows = seq_rows(s)
            back = dot_nt(grad_low[rows], gf[1, q].reshape(width, width)) * slope[rows, cols]
            active[rows, cols] = back.astype(BF)
            add_vec(3 + q, jnp.sum(back.astype(BF).astype(F32), axis=0, keepdims=True))
            return carry

        lax.fori_loop(0, seqs, turn, 0)
        c, j = q // 2, q % 2
        found = dot_tn(low[...], active[:, cols]).astype(BF).reshape(4, 2, BLOCK, width)
        for y in range(2):
            hf[0, :, 2 * y + c, j] = found[:, y]

    def close(s, carry):
        rows = seq_rows(s)
        grad = middle[rows]
        for q in range(4):
            grad += dot_nt(active[rows, q * width:(q + 1) * width], up(q))
        first = normed[rows]
        add_vec(8, jnp.sum(grad * first, axis=0, keepdims=True))
        add_vec(9, jnp.sum(grad, axis=0, keepdims=True))
        grad = grad * vec_part(vec, 8)
        grad_resid[rows] = factor[rows] * (grad - mean_of(grad) - first * mean_of(grad * first))
        return carry

    lax.fori_loop(0, seqs, close, 0)


def feed(x, normed, factor, gf, vec, cot, keep, routes):
    tokens, width = x.shape
    outs = [jax.ShapeDtypeStruct(x.shape, BF), jax.ShapeDtypeStruct(gf.shape, BF), jax.ShapeDtypeStruct(x.shape, F32),
            jax.ShapeDtypeStruct(vec.shape, F32)]
    scratch = [pltpu.VMEM((tokens, FF), BF), pltpu.VMEM((tokens, FF), F32), pltpu.VMEM(x.shape, F32),
               pltpu.VMEM(x.shape, BF), pltpu.VMEM(x.shape, BF)]
    return vmem_call(feed_forward, (x, normed, factor, gf, vec, cot, keep, routes), outs, scratch, "feed_forward", smem=(6, 7))


def input_gradient(x, cot, ga, grad_resid, keep, routes, gq, gk, gv, in_grad):
    def tile(s, carry):
        rows = seq_rows(s)
        total = grad_resid[rows] + dot_nt(gq[rows], square_of(ga[0, 0:2]))
        total += dot_nt(gk[rows], square_of(ga[0, 2:4]))
        total += dot_nt(gv[rows], square_of(ga[1, 0:2]))
        in_grad[rows] = jnp.where(served_flag(keep, routes, s) > 0, total.astype(BF), cot[rows])
        return carry

    lax.fori_loop(0, x.shape[0] // LEN, tile, 0)


def gather_attention_kernel(aw, fw, vw, x, lens, gf, ga, vec, q_out, k_out, v_out, context_out, log_total, normed_out, factor,
                            gv, strip, pair, own, q, k, v, context, normed, store, *sems):
    p = place()
    peers = near(p)
    greet(peers)
    share = vw.shape[0]
    own[...] = jnp.zeros_like(own)
    own[0:1, 0:share] = vw[...].astype(BF).astype(F32).reshape(1, share)
    for b in range(8):
        strip[:, b * BLOCK:(b + 1) * BLOCK] = aw[b].astype(BF)
    for j in range(2):
        for b in range(8):
            pair[j, :, b * BLOCK:(b + 1) * BLOCK] = fw[8 * j + b].astype(BF)
    half = BLOCK // 2

    def attn_part(h):
        rows = pl.ds(h * half, half)
        return strip.at[rows], lambda d, z, c: ga.at[d, z, c, rows], lambda d, c: ga.at[d, :, c, rows]

    def feed_part(j):
        return pair.at[j], lambda d, z, c: gf.at[d, z, c, j], lambda d, c: gf.at[d, :, c, j]

    vec_part = own, lambda d, z, c: gv.at[d, z, c], lambda d, c: gv.at[d, :, c]
    parts = [attn_part(0), vec_part, attn_part(1), feed_part(0), feed_part(1)]
    a0, w, a1, f0, f1 = every = [Spread(p, *part, *sems[3 * n:3 * n + 3]) for n, part in enumerate(parts)]
    meet(peers)
    for s in every:
        s.start()
    a0.second()
    w.second()
    a1.second()
    for s in (a0, w, a1):
        s.third()
        s.fourth()
    f0.second()
    for s in (a0, w, a1):
        s.fifth()
    w.sixth()
    unfold_vec(gv, vec, share)
    a0.sixth()
    a1.sixth()
    projections(x, ga, vec, q, k, v)
    stores = [pltpu.make_async_copy(src, dst, store.at[n])
              for n, (src, dst) in enumerate(((q, q_out), (k, k_out), (v, v_out), (context, context_out), (normed, normed_out)))]
    for copy in stores[:3]:
        copy.start()

    def step(n, carry):
        attend(n, q, k, v, lens, context, log_total)
        return carry

    lax.fori_loop(0, 3, step, 0)
    f0.third()
    f0.fourth()
    f1.second()
    lax.fori_loop(3, 9, step, 0)
    f0.fifth()
    lax.fori_loop(9, 12, step, 0)
    stores[3].start()
    attention_end(x, context, ga, vec, normed, factor)
    stores[4].start()
    f1.third()
    f1.fourth()
    f1.fifth()
    f0.sixth()
    f1.sixth()
    for s in every:
        s.drain()
    for copy in stores:
        copy.wait()


def gather_attention(aw, fw, vw, x, lens):
    width = x.shape[1]
    low = jax.ShapeDtypeStruct(x.shape, BF)
    outs = [jax.ShapeDtypeStruct((2, 4, 4, 2, BLOCK, width), BF), jax.ShapeDtypeStruct((2, 4, 4, BLOCK, width), BF),
            jax.ShapeDtypeStruct((ROWS, width), F32)] + [low] * 4
    outs += [jax.ShapeDtypeStruct((12, 2, LEN), F32), jax.ShapeDtypeStruct(x.shape, F32),
             jax.ShapeDtypeStruct((x.shape[0], 1), F32)]
    vmem = pl.BlockSpec(memory_space=pltpu.VMEM)
    hbm = pl.BlockSpec(memory_space=pl.ANY)
    return pl.pallas_call(
        gather_attention_kernel,
        out_shape=outs,
        in_specs=[vmem] * 4 + [pl.BlockSpec(memory_space=pltpu.SMEM)],
        out_specs=[hbm, vmem, vmem] + [hbm] * 4 + [vmem, hbm, vmem],
        scratch_shapes=[pltpu.VMEM((2, 4, 4, 8, 384), F32), pltpu.VMEM((BLOCK, width), BF),
                        pltpu.VMEM((2, BLOCK, width), BF), pltpu.VMEM((8, 384), F32)]
        + [pltpu.VMEM(x.shape, BF)] * 4 + [pltpu.VMEM(x.shape, F32), pltpu.SemaphoreType.DMA((5,))]
        + spread_sems() * 5,
        compiler_params=pltpu.CompilerParams(collective_id=0, has_side_effects=True, vmem_limit_bytes=62 << 20),
        name="gather_attention",
    )(aw, fw, vw, x, lens)


class Fold(Mail):
    def __init__(self, p, away, home, pair, diag, flat, late, line, send, recv):
        Mail.__init__(self, p, send, recv)
        self.away, self.home, self.pair, self.diag, self.flat, self.late, self.line = away, home, pair, diag, flat, late, line

    def add(self, dst, *others):
        total = dst[...].astype(F32)
        for o in others:
            total += o[...].astype(F32)
        dst[...] = total.astype(dst.dtype)

    def start(self):
        self.go(self.away, self.pair, 0, (1 - self.p["d"], self.p["i"]))

    def second(self):
        p = self.p
        self.wait(self.pair, 0)
        for col, dst, k in ((p["cd"], self.diag, 1), (p["cb"], self.flat, 2)):
            self.add(self.pair.at[:, col], self.home.at[:, col])
            self.go(self.pair.at[:, col], dst, k, (p["d"], p["nb"]))
        for col in (p["ca"], p["c"]):
            self.add(self.pair.at[:, col], self.home.at[:, col])

    def third(self):
        p = self.p
        self.wait(self.diag, 1)
        src = self.pair.at[:, p["ca"]]
        self.add(src, self.diag)
        self.go(src, self.late, 3, (p["d"], p["na"]))

    def fourth(self):
        p = self.p
        self.wait(self.flat, 2)
        self.wait(self.late, 3)
        for k in (2, 1, 3, 0):
            dst = (p["z"] + k) % 4
            self.add(self.pair.at[dst, p["c"]], self.flat.at[dst], self.late.at[dst])
            if k:
                self.go(self.pair.at[dst, p["c"]], self.line.at[k - 1], 3 + k, (p["d"], dst * 4 + p["c"]))

    def fifth(self, out):
        p = self.p
        total = self.pair[p["z"], p["c"]].astype(F32)
        for k in (1, 2, 3):
            self.wait(self.line.at[k - 1], 3 + k)
            total += self.line[k - 1].astype(F32)
        out[...] = total


def fold_scratch(width):
    shape = (BLOCK, width)
    return [pltpu.VMEM((4, 4) + shape, BF), pltpu.VMEM((4,) + shape, BF), pltpu.VMEM((4,) + shape, BF),
            pltpu.VMEM((4,) + shape, BF), pltpu.VMEM((3,) + shape, BF),
            pltpu.SemaphoreType.DMA((7,)), pltpu.SemaphoreType.DMA((7,))]


class Total(Mail):
    def __init__(self, p, held, came, send, recv):
        Mail.__init__(self, p, send, recv)
        self.held, self.came = held, came
        self.peers = ((1 - p["d"], p["i"]), (p["d"], p["na"]), (p["d"], p["nb"]))

    def start(self):
        self.go(self.held.at[0], self.came.at[0], 0, self.peers[0])

    def hop(self, n):
        p = self.p
        self.wait(self.came.at[n], n)
        self.held[n + 1] = self.held[n] + self.came[n]
        if n < 2:
            self.go(self.held.at[n + 1], self.came.at[n + 1], n + 1, self.peers[n + 1])
        else:
            for k in (1, 2, 3):
                self.go(self.held.at[3], self.came.at[2 + k], 2 + k, (p["d"], ((p["z"] + k) % 4) * 4 + p["c"]))

    def end(self):
        total = self.held[3]
        for k in (1, 2, 3):
            self.wait(self.came.at[2 + k], 2 + k)
            total += self.came[2 + k]
        return total


def own_share(p, rows, out, share):
    per = share // BLOCK
    me = p["d"] * 16 + p["i"]
    units = sum(
        jnp.dot(one_hot((8, ROWS), lambda a: per * me + jnp.where(a < per, a, -8 * 32 * per), lambda r, b=b: 8 * r + b),
                rows[:, b * BLOCK:(b + 1) * BLOCK], precision=lax.Precision.HIGHEST, preferred_element_type=F32)
        for b in range(8)
    )
    for a in range(per):
        out[0:1, a * BLOCK:(a + 1) * BLOCK] = units[a:a + 1]


def everyone(p):
    me = p["d"] * 16 + p["i"]

    def other(k):
        t = (me + k) % 32
        return (t // 16, t % 16)

    return me, other


def greet_all(p):
    me, other = everyone(p)
    barrier = pltpu.get_barrier_semaphore()

    def one(k, carry):
        pl.semaphore_signal(barrier, inc=1, device_id=other(k), device_id_type=MESH)
        return carry

    lax.fori_loop(1, 32, one, 0)


def meet_all():
    pl.semaphore_wait(pltpu.get_barrier_semaphore(), 31)


def norm_sum(p, square, slots, send, recv):
    me, other = everyone(p)
    slots[me] = jnp.full((8, 128), square, F32)
    to = lambda k, slot: remote(slots.at[slot], slots.at[slot], send, recv, slot, other(k))

    def push(k, carry):
        remote(slots.at[me], slots.at[me], send.at[pl.ds(k, 1)], recv.at[pl.ds(me, 1)], 0, other(k)).start()
        return carry

    def take(k, carry):
        slot = (me + k) % 32
        remote(slots.at[slot], slots.at[slot], send.at[pl.ds(k, 1)], recv.at[pl.ds(slot, 1)], 0, other(k)).wait_recv()
        return carry

    def done(k, carry):
        remote(slots.at[me], slots.at[me], send.at[pl.ds(k, 1)], recv.at[pl.ds(me, 1)], 0, other(k)).wait_send()
        return carry

    lax.fori_loop(1, 32, push, 0)
    lax.fori_loop(1, 32, take, 0)
    total = jnp.sum(slots[...], axis=0)[0:1, 0:1]
    lax.fori_loop(1, 32, done, 0)
    return total


def attention_back_kernel(x, cot, ga, q, k, v, context, log_total, grad_resid, gvec_in, lens, keep, routes, hf,
                          in_grad, bf, ba, sv, norm,
                          grad_low, grad_context, gq, gk, gv, ha, held, came, homes, sf, sa, slots,
                          load, nsend, nrecv, tsend, trecv, *scratch):
    p = place()
    greet_all(p)
    width = x.shape[1]
    half = width // 2
    lanes = (pl.ds(0, half), pl.ds(half, half))
    loads = [pltpu.make_async_copy(hf.at[p["d"], :, :, j], homes.at[j], load.at[j]) for j in range(2)]
    for copy in loads:
        copy.start()
    f0, f1 = [Fold(p, hf.at[1 - p["d"], :, :, j], homes.at[j], *scratch[7 * j:7 * j + 7]) for j in range(2)]
    a0, a1 = [Fold(p, ha.at[1 - p["d"], :, :, :, lanes[n]], ha.at[p["d"], :, :, :, lanes[n]], *scratch[14 + 7 * n:21 + 7 * n])
              for n in range(2)]
    total = Total(p, held, came, tsend, trecv)

    def enter(s, carry):
        rows = seq_rows(s)
        grad_low[rows] = grad_resid[rows].astype(BF)
        grad_context[rows] = dot_nt(grad_low[rows], square_of(ga[1, 2:4])).astype(BF)
        return carry

    lax.fori_loop(0, x.shape[0] // LEN, enter, 0)
    meet_all()
    f0.start()
    f1.start()
    held[0] = gvec_in[...]
    held[0, 2:3] = jnp.sum(grad_low[...].astype(F32), axis=0, keepdims=True)
    ha[1, 2:4] = dot_tn(context[...], grad_low[...]).astype(BF).reshape(2, 4, BLOCK, width)

    def step(m, carry):
        n = ((m % 6) // 3) * 6 + (m // 6) * 3 + m % 3
        attend_back(n, q, k, v, grad_context, log_total, lens, gq, gk, gv)
        return carry

    def weight_grads(n):
        cols = lanes[n]
        for dst, src in ((ha.at[0, 0:2], gq), (ha.at[0, 2:4], gk), (ha.at[1, 0:2], gv)):
            dst[:, :, :, cols] = dot_tn(x[...], src[:, cols]).astype(BF).reshape(2, 4, BLOCK, half)

    lax.fori_loop(0, 1, step, 0)
    loads[0].wait()
    f0.second()
    lax.fori_loop(1, 3, step, 0)
    loads[1].wait()
    f1.second()
    lax.fori_loop(3, 6, step, 0)
    f0.third()
    weight_grads(0)
    a0.start()
    lax.fori_loop(6, 8, step, 0)
    a0.second()
    lax.fori_loop(8, 10, step, 0)
    f1.third()
    lax.fori_loop(10, 12, step, 0)
    f0.fourth()
    weight_grads(1)
    a1.start()
    held[0, 0:1] = jnp.sum(gq[...].astype(F32), axis=0, keepdims=True)
    held[0, 1:2] = jnp.sum(gv[...].astype(F32), axis=0, keepdims=True)
    total.start()
    a0.third()
    a1.second()
    total.hop(0)
    f1.fourth()
    input_gradient(x, cot, ga, grad_resid, keep, routes, gq, gk, gv, in_grad)
    total.hop(1)
    a1.third()
    a0.fourth()
    total.hop(2)
    f0.fifth(sf.at[0])
    f1.fifth(sf.at[1])
    a1.fourth()
    square = jnp.sum(sf[...] * sf[...])
    for b in range(8):
        for j in range(2):
            bf[8 * j + b] = sf[j, :, b * BLOCK:(b + 1) * BLOCK]
    held[4] = total.end()
    sv[...] = jnp.zeros_like(sv)
    own_share(p, held[4], sv, 12 * width // 32)
    a0.fifth(sa.at[:, lanes[0]])
    a1.fifth(sa.at[:, lanes[1]])
    square += jnp.sum(sa[...] * sa[...]) + jnp.sum(sv[...] * sv[...])
    found = norm_sum(p, square, slots, nsend, nrecv)
    norm[...] = jnp.sqrt(found)
    for b in range(8):
        ba[b] = sa[:, b * BLOCK:(b + 1) * BLOCK]
    for s in (f0, f1, a0, a1, total):
        s.drain()


def attention_back(x, cot, ga, q, k, v, context, log_total, grad_resid, gvec, lens, keep, routes, hf):
    width = x.shape[1]
    outs = [jax.ShapeDtypeStruct(x.shape, BF), jax.ShapeDtypeStruct((16, BLOCK, BLOCK), F32),
            jax.ShapeDtypeStruct((8, BLOCK, BLOCK), F32), jax.ShapeDtypeStruct((8, 384), F32), jax.ShapeDtypeStruct((1, 1), F32)]
    dma = pltpu.SemaphoreType.DMA
    scratch = [pltpu.VMEM(x.shape, BF)] * 5
    scratch += [pltpu.VMEM(ga.shape, BF), pltpu.VMEM((5, ROWS, width), F32), pltpu.VMEM((6, ROWS, width), F32),
                pltpu.VMEM((2, 4, 4, BLOCK, width), BF), pltpu.VMEM((2, BLOCK, width), F32), pltpu.VMEM((BLOCK, width), F32),
                pltpu.VMEM((32, 8, 128), F32), dma((2,)), dma((32,)), dma((32,)), dma((6,)), dma((6,))]
    scratch += fold_scratch(width) * 2 + fold_scratch(width // 2) * 2
    vmem = pl.BlockSpec(memory_space=pltpu.VMEM)
    smem = pl.BlockSpec(memory_space=pltpu.SMEM)
    return pl.pallas_call(
        attention_back_kernel,
        out_shape=outs,
        in_specs=[vmem] * 10 + [smem] * 3 + [pl.BlockSpec(memory_space=pl.ANY)],
        out_specs=[vmem] * 5,
        scratch_shapes=scratch,
        compiler_params=pltpu.CompilerParams(collective_id=1, has_side_effects=True, vmem_limit_bytes=62 << 20),
        name="attention_back_scatter",
    )(x, cot, ga, q, k, v, context, log_total, grad_resid, gvec, lens, keep, routes, hf)


TOP = lax.Precision.HIGHEST


def shampoo_block(grad, w, st, ro, mo, st_new, mo_new, w_new, b, factor):
    clipped = grad * factor
    moment = momentum_decay * mo[b] + clipped
    left = lax.dot_general(clipped, clipped, (((1,), (1,)), ((), ())), precision=TOP, preferred_element_type=F32)
    right = lax.dot_general(clipped, clipped, (((0,), (0,)), ((), ())), precision=TOP, preferred_element_type=F32)
    st_new[b, 0] = stat_decay * st[b, 0] + (1.0 - stat_decay) * left
    st_new[b, 1] = stat_decay * st[b, 1] + (1.0 - stat_decay) * right
    mo_new[b] = moment
    turned = jnp.dot(ro[b, 0], moment, precision=TOP, preferred_element_type=F32)
    turned = jnp.dot(turned, ro[b, 1], precision=TOP, preferred_element_type=F32)
    w_new[b] = w[b] - matrix_rate * (turned + matrix_decay * w[b])


def optimizer_kernel(norm, ga, gf, sv, aw, ast, ar, am, fw, fst, fr, fm, vw, v1, v2,
                     ast_n, am_n, aw_n, fst_n, fm_n, fw_n, v1_n, v2_n, vw_n):
    factor = clip_bound / jnp.maximum(norm[...], clip_bound)
    shampoo_block(ga[0], aw, ast, ar, am, ast_n, am_n, aw_n, 0, factor)
    shampoo_block(gf[0], fw, fst, fr, fm, fst_n, fm_n, fw_n, 0, factor)
    shampoo_block(gf[1], fw, fst, fr, fm, fst_n, fm_n, fw_n, 1, factor)

    @pl.when(pl.program_id(0) == 0)
    def _():
        size = vw.shape[0]
        clipped = (sv[0:1, 0:size] * factor)[0]
        first_new = first_decay * v1[...] + (1.0 - first_decay) * clipped
        second_new = second_decay * v2[...] + (1.0 - second_decay) * clipped * clipped
        first_hat = first_new / (1.0 - first_decay**STEP)
        second_hat = second_new / (1.0 - second_decay**STEP)
        v1_n[...] = first_new
        v2_n[...] = second_new
        vw_n[...] = vw[...] - vector_rate * first_hat / (jnp.sqrt(second_hat) + adam_floor)


def optimizer(norm, ga, gf, sv, aw, ast, ar, am, fw, fst, fr, fm, vw, v1, v2):
    def steps(t, n):
        shape = (n,) + t.shape[1:]
        return pl.BlockSpec(shape, lambda g: (g,) + (0,) * (len(shape) - 1))

    def whole(t):
        return pl.BlockSpec(t.shape, lambda g: (0,) * t.ndim)

    like = lambda t: jax.ShapeDtypeStruct(t.shape, F32)
    args = (norm, ga, gf, sv, aw, ast, ar, am, fw, fst, fr, fm, vw, v1, v2)
    specs = [whole(norm), steps(ga, 1), steps(gf, 2), whole(sv)]
    specs += [steps(t, 1) for t in (aw, ast, ar, am)] + [steps(t, 2) for t in (fw, fst, fr, fm)]
    specs += [whole(t) for t in (vw, v1, v2)]
    outs = (ast, am, aw, fst, fm, fw, v1, v2, vw)
    return pl.pallas_call(
        optimizer_kernel,
        out_shape=[like(t) for t in outs],
        grid=(8,),
        in_specs=specs,
        out_specs=[steps(t, 1) for t in outs[:3]] + [steps(t, 2) for t in outs[3:6]] + [whole(t) for t in outs[6:]],
        name="optimizer",
    )(*args)


def per_device(
    inputs,
    output_gradient,
    keep,
    lengths,
    routes,
    attn_weights,
    attn_stats,
    attn_roots,
    attn_momentum,
    ffn_weights,
    ffn_stats,
    ffn_roots,
    ffn_momentum,
    vec_weights,
    vec_first,
    vec_second,
):
    slots, seq_len, width = inputs.shape
    tokens = slots * seq_len
    x = inputs.reshape(tokens, width)
    cot = output_gradient.reshape(tokens, width)
    gf, ga, vec, q, k, v, context, log_total, normed, factor = gather_attention(attn_weights, ffn_weights, vec_weights, x, lengths)
    out, hf, grad_resid, ffn_vec = feed(x, normed, factor, gf, vec, cot, keep, routes)
    in_grad, bf, ba, sv, norm = attention_back(
        x, cot, ga, q, k, v, context, log_total, grad_resid, ffn_vec, lengths, keep, routes, hf
    )
    rest = optimizer(
        norm, ba, bf, sv,
        attn_weights, attn_stats, attn_roots, attn_momentum,
        ffn_weights, ffn_stats, ffn_roots, ffn_momentum,
        vec_weights, vec_first, vec_second,
    )
    return (out.reshape(inputs.shape), in_grad.reshape(inputs.shape), norm.reshape(()), *rest)


def solution(mesh):
    small = mesh.shape["depth"] == 2 and mesh.shape["dp"] == 16
    return jax.shard_map(
        per_device if small else per_device_general,
        mesh=mesh,
        in_specs=(
            P(("depth", "dp"), None, None),
            P(("depth", "dp"), None, None),
            P(("depth", "dp")),
            P(("depth", "dp")),
            P(("depth", "dp")),
            P(("depth", "dp"), None, None),
            P(("depth", "dp"), None, None, None),
            P(("depth", "dp"), None, None, None),
            P(("depth", "dp"), None, None),
            P(("depth", "dp"), None, None),
            P(("depth", "dp"), None, None, None),
            P(("depth", "dp"), None, None, None),
            P(("depth", "dp"), None, None),
            P(("depth", "dp")),
            P(("depth", "dp")),
            P(("depth", "dp")),
        ),
        out_specs=(
            P(("depth", "dp"), None, None),
            P(("depth", "dp"), None, None),
            P(),
            P(("depth", "dp"), None, None, None),
            P(("depth", "dp"), None, None),
            P(("depth", "dp"), None, None),
            P(("depth", "dp"), None, None, None),
            P(("depth", "dp"), None, None),
            P(("depth", "dp"), None, None),
            P(("depth", "dp")),
            P(("depth", "dp")),
            P(("depth", "dp")),
        ),
        check_vma=False,
    )
```

```python
import functools
import math

import jax
import jax.numpy as jnp
from jax import lax
from jax.experimental import pallas as pl
from jax.experimental.pallas import tpu as pltpu
from jax.sharding import PartitionSpec as P

HEADS = 12
FF = 3072
BLOCK = 96
STEP = 10


norm_floor = 1e-05
masked_fill = -1000000000.0
momentum_decay = 0.9
stat_decay = 0.95
matrix_rate = 1.0
matrix_decay = 0.01
clip_bound = 1.0
first_decay = 0.9
second_decay = 0.999
vector_rate = 0.5
adam_floor = 1e-08


def serve_flags(keep_rows, route_rows):
    count = keep_rows.shape[-1]
    order = jnp.arange(count, dtype=jnp.int32)
    earlier = (order[None, :] < order[:, None]).astype(jnp.int32)
    same = (route_rows[:, :, None] == route_rows[:, None, :]).astype(jnp.int32)
    clash = jnp.sum(same * earlier[None, :, :] * keep_rows[:, None, :], axis=2)
    return keep_rows * (clash == 0).astype(jnp.int32)


def to_matrix(blocks, height, breadth):
    shaped = blocks.reshape(height // BLOCK, breadth // BLOCK, BLOCK, BLOCK)
    return shaped.transpose(0, 2, 1, 3).reshape(height, breadth)


def to_flat_blocks(matrix):
    height, breadth = matrix.shape
    shaped = matrix.reshape(height // BLOCK, BLOCK, breadth // BLOCK, BLOCK)
    return shaped.transpose(0, 2, 1, 3).reshape(-1, BLOCK * BLOCK)


def norm_parts(resid):
    center = resid - jnp.mean(resid, axis=-1, keepdims=True)
    factor = lax.rsqrt(jnp.mean(center * center, axis=-1, keepdims=True) + norm_floor)
    return (center * factor, factor)


def norm_back(grad_normed, normed, factor):
    middle = jnp.mean(grad_normed, axis=-1, keepdims=True)
    along = jnp.mean(grad_normed * normed, axis=-1, keepdims=True)
    return factor * (grad_normed - middle - normed * along)


def gelu_slope(value):
    cumulative = 0.5 * (1.0 + lax.erf(value * (1.0 / math.sqrt(2.0))))
    density = jnp.exp(-0.5 * value * value) * (1.0 / math.sqrt(2.0 * math.pi))
    return cumulative + value * density


def product(left, right):
    return jnp.dot(left, right, preferred_element_type=jnp.float32)


def contract_rows(left, right):
    return lax.dot_general(
        left, right, (((0,), (0,)), ((), ())), preferred_element_type=jnp.float32
    )


def times_transpose(left, right):
    return lax.dot_general(
        left, right, (((1,), (1,)), ((), ())), preferred_element_type=jnp.float32
    )


def masked_scores(query, keys, visible_len):
    scale = 1.0 / math.sqrt(query.shape[-1])
    scores = jnp.einsum("qhe,khe->hqk", query, keys, preferred_element_type=jnp.float32) * scale
    visible = jnp.arange(keys.shape[0], dtype=jnp.int32) < visible_len
    return jnp.where(visible[None, None, :], scores, masked_fill)


def attend_forward(pieces):
    query, keys, values, visible_len = pieces
    scores = masked_scores(query, keys, visible_len)
    peak = jnp.max(scores, axis=-1, keepdims=True)
    expo = jnp.exp(scores - peak)
    total = jnp.sum(expo, axis=-1, keepdims=True)
    probs_low = (expo / total).astype(jnp.bfloat16)
    context = jnp.einsum("hqk,khe->qhe", probs_low, values, preferred_element_type=jnp.float32)
    return (context, peak[..., 0] + jnp.log(total[..., 0]))


def attend_backward(pieces):
    query, keys, values, grad_ctx, log_total, visible_len = pieces
    scale = 1.0 / math.sqrt(query.shape[-1])
    scores = masked_scores(query, keys, visible_len)
    probs = jnp.exp(scores - log_total[..., None])
    probs_low = probs.astype(jnp.bfloat16)
    grad_probs = jnp.einsum("qhe,khe->hqk", grad_ctx, values, preferred_element_type=jnp.float32)
    grad_values = jnp.einsum(
        "hqk,qhe->khe", probs_low, grad_ctx, preferred_element_type=jnp.float32
    )
    along = jnp.sum(probs * grad_probs, axis=-1, keepdims=True)
    grad_scores = (probs * (grad_probs - along)).astype(jnp.bfloat16)
    grad_query = (
        jnp.einsum("hqk,khe->qhe", grad_scores, keys, preferred_element_type=jnp.float32) * scale
    )
    grad_keys = (
        jnp.einsum("hqk,qhe->khe", grad_scores, query, preferred_element_type=jnp.float32) * scale
    )
    return (grad_query, grad_keys, grad_values)


def shampoo(weights, stats, roots, momentum, grads, factor):
    highest = lax.Precision.HIGHEST
    clipped = grads * factor
    moment = momentum_decay * momentum + clipped
    left = jnp.einsum("nab,ncb->nac", clipped, clipped, precision=highest)
    right = jnp.einsum("nab,nac->nbc", clipped, clipped, precision=highest)
    fresh = stat_decay * stats + (1.0 - stat_decay) * jnp.stack([left, right], axis=1)
    turned = jnp.einsum("nab,nbc->nac", roots[:, 0], moment, precision=highest)
    turned = jnp.einsum("nab,nbc->nac", turned, roots[:, 1], precision=highest)
    updated = weights - matrix_rate * (turned + matrix_decay * weights)
    return (fresh, moment, updated)


def adam_step(weights, first, second, grads, factor):
    clipped = grads * factor
    first_new = first_decay * first + (1.0 - first_decay) * clipped
    second_new = second_decay * second + (1.0 - second_decay) * clipped * clipped
    first_hat = first_new / (1.0 - first_decay**STEP)
    second_hat = second_new / (1.0 - second_decay**STEP)
    updated = weights - vector_rate * first_hat / (jnp.sqrt(second_hat) + adam_floor)
    return (first_new, second_new, updated)


def per_device_general(
    inputs,
    output_gradient,
    keep,
    lengths,
    routes,
    attn_weights,
    attn_stats,
    attn_roots,
    attn_momentum,
    ffn_weights,
    ffn_stats,
    ffn_roots,
    ffn_momentum,
    vec_weights,
    vec_first,
    vec_second,
):
    slots, seq_len, width = inputs.shape
    tokens = slots * seq_len
    head_size = width // HEADS
    hidden_width = FF
    depth_count = lax.axis_size("depth")
    peer_slots = slots // depth_count
    grid = (width // BLOCK) ** 2
    half_ffn = width * hidden_width // (BLOCK * BLOCK)
    area = BLOCK * BLOCK
    low_type = jnp.bfloat16
    attn_flat = attn_weights.reshape(-1, area).astype(low_type)
    ffn_flat = ffn_weights.reshape(-1, area).astype(low_type)
    attn_all, ffn_all, vec_all = (
        lax.all_gather(attn_flat, ("depth", "dp"), axis=0, tiled=True),
        lax.all_gather(ffn_flat, ("depth", "dp"), axis=0, tiled=True),
        lax.all_gather(vec_weights.astype(low_type), ("depth", "dp"), axis=0, tiled=True),
    )
    table_keep, table_len, table_route = (
        lax.all_gather(keep, "depth", axis=0, tiled=True),
        lax.all_gather(lengths, "depth", axis=0, tiled=True),
        lax.all_gather(routes, "depth", axis=0, tiled=True),
    )
    mine = serve_flags(keep[None, :], routes[None, :])[0]
    slot_order = jnp.arange(slots, dtype=jnp.int32)
    selection = ((routes[None, :] == slot_order[:, None]).astype(jnp.int32) * mine[None, :]).astype(
        low_type
    )
    outgoing_rows = jnp.einsum(
        "gz,zrp->grp", selection, inputs, preferred_element_type=jnp.float32
    ).astype(low_type)
    send_grad = jnp.einsum(
        "gz,zrp->grp", selection, output_gradient, preferred_element_type=jnp.float32
    ).astype(low_type)
    come_rows, come_grad = (
        lax.all_to_all(outgoing_rows, "depth", split_axis=0, concat_axis=0, tiled=True),
        lax.all_to_all(send_grad, "depth", split_axis=0, concat_axis=0, tiled=True),
    )
    all_keep = table_keep.reshape(depth_count, slots)
    all_route = table_route.reshape(depth_count, slots)
    all_len = table_len.reshape(depth_count, slots)
    all_served = serve_flags(all_keep, all_route)
    here = lax.axis_index("depth")
    source = slot_order // peer_slots
    target = here * peer_slots + slot_order % peer_slots
    source_hot = (source[:, None] == jnp.arange(depth_count, dtype=jnp.int32)[None, :]).astype(
        jnp.int32
    )
    match = (all_route[None, :, :] == target[:, None, None]).astype(jnp.int32) * all_served[
        None, :, :
    ]
    slot_len = jnp.sum(source_hot[:, :, None] * match * all_len[None, :, :], axis=(1, 2))
    visible_len = jnp.maximum(slot_len, 1)
    query_w = to_matrix(attn_all[0:grid], width, width)
    key_w = to_matrix(attn_all[grid : 2 * grid], width, width)
    value_w = to_matrix(attn_all[2 * grid : 3 * grid], width, width)
    output_w = to_matrix(attn_all[3 * grid : 4 * grid], width, width)
    vectors = vec_all.astype(jnp.float32)
    q_bias = vectors[0:width]
    v_bias = vectors[width : 2 * width]
    out_bias = vectors[2 * width : 3 * width]
    hidden_bias = vectors[3 * width : 3 * width + hidden_width]
    ffn_bias = vectors[3 * width + hidden_width : 4 * width + hidden_width]
    gain_one = vectors[4 * width + hidden_width : 5 * width + hidden_width]
    shift_one = vectors[5 * width + hidden_width : 6 * width + hidden_width]
    gain_two = vectors[6 * width + hidden_width : 7 * width + hidden_width]
    shift_two = vectors[7 * width + hidden_width : 8 * width + hidden_width]
    flat = come_rows.reshape(tokens, width)
    four = (slots, seq_len, HEADS, head_size)
    query = (product(flat, query_w) + q_bias).astype(low_type).reshape(four)
    keys = product(flat, key_w).astype(low_type).reshape(four)
    values = (product(flat, value_w) + v_bias).astype(low_type).reshape(four)
    context, log_total = lax.map(attend_forward, (query, keys, values, visible_len))
    context_low = context.reshape(tokens, width).astype(low_type)
    attended = product(context_low, output_w) + out_bias
    normed_one, factor_one = norm_parts(flat.astype(jnp.float32) + attended)
    hidden_in = normed_one * gain_one + shift_one
    hidden_low = hidden_in.astype(low_type)
    hidden_w = to_matrix(ffn_all[0:half_ffn], width, hidden_width)
    return_weight = to_matrix(ffn_all[half_ffn:], hidden_width, width)
    before = product(hidden_low, hidden_w) + hidden_bias
    active_low = jax.nn.gelu(before, approximate=False).astype(low_type)
    branch = product(active_low, return_weight) + ffn_bias
    normed_two, factor_two = norm_parts(hidden_in + branch)
    result_low = (normed_two * gain_two + shift_two).astype(low_type)
    grad_rows = come_grad.reshape(tokens, width).astype(jnp.float32)
    grad_gain_two = jnp.sum(grad_rows * normed_two, axis=0)
    grad_shift_two = jnp.sum(grad_rows, axis=0)
    grad_resid_two = norm_back(grad_rows * gain_two, normed_two, factor_two)
    grad_branch = grad_resid_two.astype(low_type)
    grad_ffn_bias = jnp.sum(grad_branch.astype(jnp.float32), axis=0)
    gradient_return_weight = contract_rows(active_low, grad_branch)
    grad_active = times_transpose(grad_branch, return_weight)
    grad_before = (grad_active * gelu_slope(before)).astype(low_type)
    grad_hidden_bias = jnp.sum(grad_before.astype(jnp.float32), axis=0)
    grad_hidden_w = contract_rows(hidden_low, grad_before)
    grad_hidden = times_transpose(grad_before, hidden_w) + grad_resid_two
    grad_gain_one = jnp.sum(grad_hidden * normed_one, axis=0)
    grad_shift_one = jnp.sum(grad_hidden, axis=0)
    grad_resid_one = norm_back(grad_hidden * gain_one, normed_one, factor_one)
    ffn_grad = jnp.concatenate(
        [to_flat_blocks(grad_hidden_w), to_flat_blocks(gradient_return_weight)], axis=0
    )
    grad_attended = grad_resid_one.astype(low_type)
    grad_out_bias = jnp.sum(grad_attended.astype(jnp.float32), axis=0)
    grad_output_w = contract_rows(context_low, grad_attended)
    grad_context = times_transpose(grad_attended, output_w).astype(low_type).reshape(four)
    grad_query, grad_keys, grad_values = lax.map(
        attend_backward, (query, keys, values, grad_context, log_total, visible_len)
    )
    grad_query = grad_query.reshape(tokens, width).astype(low_type)
    grad_keys = grad_keys.reshape(tokens, width).astype(low_type)
    grad_values = grad_values.reshape(tokens, width).astype(low_type)
    grad_q_bias = jnp.sum(grad_query.astype(jnp.float32), axis=0)
    grad_v_bias = jnp.sum(grad_values.astype(jnp.float32), axis=0)
    grad_query_w = contract_rows(flat, grad_query)
    grad_key_w = contract_rows(flat, grad_keys)
    grad_value_w = contract_rows(flat, grad_values)
    in_rows = (
        grad_resid_one
        + times_transpose(grad_query, query_w)
        + times_transpose(grad_keys, key_w)
        + times_transpose(grad_values, value_w)
    )
    attn_grad = jnp.concatenate(
        [
            to_flat_blocks(grad_query_w),
            to_flat_blocks(grad_key_w),
            to_flat_blocks(grad_value_w),
            to_flat_blocks(grad_output_w),
        ],
        axis=0,
    )
    vec_grad = jnp.concatenate(
        [
            grad_q_bias,
            grad_v_bias,
            grad_out_bias,
            grad_hidden_bias,
            grad_ffn_bias,
            grad_gain_one,
            grad_shift_one,
            grad_gain_two,
            grad_shift_two,
        ]
    )
    attn_share, ffn_share, vec_share = (
        lax.psum_scatter(attn_grad, ("depth", "dp"), scatter_dimension=0, tiled=True),
        lax.psum_scatter(ffn_grad, ("depth", "dp"), scatter_dimension=0, tiled=True),
        lax.psum_scatter(vec_grad, ("depth", "dp"), scatter_dimension=0, tiled=True),
    )
    returned_rows, returned_gradient = (
        lax.all_to_all(
            result_low.reshape(slots, seq_len, width),
            "depth",
            split_axis=0,
            concat_axis=0,
            tiled=True,
        ),
        lax.all_to_all(
            in_rows.astype(low_type).reshape(slots, seq_len, width),
            "depth",
            split_axis=0,
            concat_axis=0,
            tiled=True,
        ),
    )
    stay = (1 - mine).astype(jnp.float32)[:, None, None]
    out = (
        jnp.einsum("rx,rmp->xmp", selection, returned_rows, preferred_element_type=jnp.float32)
        + stay * inputs.astype(jnp.float32)
    ).astype(low_type)
    in_grad = (
        jnp.einsum("rx,rmp->xmp", selection, returned_gradient, preferred_element_type=jnp.float32)
        + stay * output_gradient.astype(jnp.float32)
    ).astype(low_type)
    square = (
        jnp.sum(attn_share * attn_share)
        + jnp.sum(ffn_share * ffn_share)
        + jnp.sum(vec_share * vec_share)
    )
    total = lax.psum(square, ("depth", "dp"))
    grad_norm = jnp.sqrt(total)
    factor = clip_bound / jnp.maximum(grad_norm, clip_bound)
    attn_square = attn_share.reshape(-1, BLOCK, BLOCK)
    ffn_square = ffn_share.reshape(-1, BLOCK, BLOCK)
    attn_fresh, attn_moment, attn_updated = shampoo(
        attn_weights, attn_stats, attn_roots, attn_momentum, attn_square, factor
    )
    ffn_fresh, ffn_moment, ffn_updated = shampoo(
        ffn_weights, ffn_stats, ffn_roots, ffn_momentum, ffn_square, factor
    )
    first_new, second_new, vec_updated = adam_step(
        vec_weights, vec_first, vec_second, vec_share, factor
    )
    return (
        out,
        in_grad,
        grad_norm,
        attn_fresh,
        attn_moment,
        attn_updated,
        ffn_fresh,
        ffn_moment,
        ffn_updated,
        first_new,
        second_new,
        vec_updated,
    )


MESH = pl.DeviceIdType.MESH
BF = jnp.bfloat16
F32 = jnp.float32
LEN = 512
ROWS = 16


def place():
    d = lax.axis_index("depth")
    i = lax.axis_index("dp")
    x = i % 2
    y = (i // 2) % 2
    nx = i + 1 - 2 * x
    ny = i + 2 - 4 * y
    na = ny + d * (nx - ny)
    nb = nx + d * (ny - nx)
    return dict(d=d, i=i, z=i // 4, c=i % 4, na=na, nb=nb, ca=na % 4, cb=nb % 4, cd=3 - i % 4)


def near(p):
    peers = [(p["d"], p["na"]), (p["d"], p["nb"]), (1 - p["d"], p["i"])]
    return peers + [(p["d"], ((p["z"] + k) % 4) * 4 + p["c"]) for k in (1, 2, 3)]


def greet(peers):
    barrier = pltpu.get_barrier_semaphore()
    for peer in peers:
        pl.semaphore_signal(barrier, inc=1, device_id=peer, device_id_type=MESH)


def meet(peers):
    pl.semaphore_wait(pltpu.get_barrier_semaphore(), len(peers))


def remote(src, dst, send, recv, k, dev):
    return pltpu.make_async_remote_copy(src_ref=src, dst_ref=dst, send_sem=send.at[k], recv_sem=recv.at[k],
                                        device_id=dev, device_id_type=MESH)


class Mail:
    def __init__(self, p, send, recv):
        self.p, self.send, self.recv, self.sent = p, send, recv, []

    def go(self, src, dst, k, dev):
        copy = remote(src, dst, self.send, self.recv, k, dev)
        copy.start()
        self.sent.append(copy)

    def wait(self, dst, k):
        remote(dst, dst, self.send, self.recv, k, (self.p["d"], self.p["na"])).wait_recv()

    def drain(self):
        for copy in self.sent:
            copy.wait_send()


class Spread:
    def __init__(self, p, a, b, to_a, to_b, own, slot, column, send, recv, local):
        d, z, i, c = p["d"], p["z"], p["i"], p["c"]
        ca, cb = a % 4, b % 4
        self.keep = pltpu.make_async_copy(own, slot(d, z, c), local)
        lines = [(own, slot(d, z, c), (d, ((z + k) % 4) * 4 + c)) for k in (1, 2, 3)]
        takes = [slot(d, (z + 4 - k) % 4, c) for k in (1, 2, 3)]
        mine, from_a, from_b, far = (column(d, col) for col in (c, ca, cb, p["cd"]))
        core = (1 - d, i)
        sends = [(mine, 3, (d, a)), (mine, 4, (d, b)), (from_a, 5, (d, b)), (mine, 6, core), (from_a, to_a, core),
                 (from_b, to_b, core), (far, 9, core)]
        self.lines = [remote(src, dst, send, recv, k, dev) for k, (src, dst, dev) in enumerate(lines)]
        self.taken = [remote(dst, dst, send, recv, k, (d, a)) for k, dst in enumerate(takes)]
        self.sends = [remote(src, src, send, recv, k, dev) for src, k, dev in sends]
        waits = [(from_a, 3), (from_b, 4), (far, 5), (column(1 - d, c), 6), (column(1 - d, ca), to_a),
                 (column(1 - d, cb), to_b), (column(1 - d, p["cd"]), 9)]
        self.came = [remote(dst, dst, send, recv, k, (d, a)) for dst, k in waits]

    def push(self, *which):
        for n in which:
            self.sends[n].start()

    def start(self):
        self.keep.start()
        for k in (1, 0, 2):
            self.lines[k].start()

    def second(self):
        self.keep.wait()
        for copy in self.taken:
            copy.wait_recv()
        self.push(0, 1, 3)

    def third(self):
        self.came[0].wait_recv()
        self.push(2, 4)

    def fourth(self):
        self.came[1].wait_recv()
        self.push(5)

    def fifth(self):
        self.came[2].wait_recv()
        self.push(6)

    def sixth(self):
        for copy in self.came[3:]:
            copy.wait_recv()

    def drain(self):
        for copy in self.lines + self.sends:
            copy.wait_send()


def spread_sems():
    return [pltpu.SemaphoreType.DMA((10,)), pltpu.SemaphoreType.DMA((10,)), pltpu.SemaphoreType.DMA]


def on_core(p, core, *steps):
    @pl.when(p["d"] == core)
    def _():
        for s in steps:
            s()


def at_step(m, value, *steps):
    @pl.when(m == value)
    def _():
        for s in steps:
            s()


def square_links(p):
    dx = p["i"] + 1 - 2 * (p["i"] % 2)
    dy = p["i"] + 2 - 4 * ((p["i"] // 2) % 2)
    return dx, dy


def quarter(w, q):
    return w.at[q // 2, pl.ds(2 * (q % 2), 2)]


def one_hot(shape, row, col):
    r = lax.broadcasted_iota(jnp.int32, shape, 0)
    c = lax.broadcasted_iota(jnp.int32, shape, 1)
    return (row(r) == col(c)).astype(F32)


def unfold_vec(pieces, vec, share):
    per = share // BLOCK
    stack = pieces[...][:, :, :, 0, :].reshape(32, pieces.shape[-1])
    units = sum(
        jnp.dot(one_hot((32 * per, 32), lambda u: u, lambda k, a=a: per * k + a), stack[:, a * BLOCK:(a + 1) * BLOCK],
                preferred_element_type=F32)
        for a in range(per)
    )
    for b in range(8):
        vec[:, b * BLOCK:(b + 1) * BLOCK] = jnp.dot(
            one_hot((ROWS, 32 * per), lambda r, b=b: 8 * r + b, lambda u: u), units, preferred_element_type=F32)


def dot_nn(a, b):
    return lax.dot_general(a, b, (((1,), (0,)), ((), ())), preferred_element_type=F32)


def dot_nt(a, b):
    return lax.dot_general(a, b, (((1,), (1,)), ((), ())), preferred_element_type=F32)


def dot_tn(a, b):
    return lax.dot_general(a, b, (((0,), (0,)), ((), ())), preferred_element_type=F32)


def square_of(value):
    return value.reshape(value.shape[0] * value.shape[1] * value.shape[2], value.shape[3])


def seq_rows(s):
    return pl.ds(s * LEN, LEN) if isinstance(s, int) else pl.ds(pl.multiple_of(s * LEN, LEN), LEN)


def tile_rows(s, size):
    return pl.ds(pl.multiple_of(s * size, size), size)


def served_flag(keep, routes, s):
    other = keep[0] * (routes[0] == routes[1]).astype(jnp.int32)
    return jnp.where(s == 0, keep[0], keep[1] * (1 - other))


def projections(x, ga, vec, q, k, v):
    width = x.shape[1]

    def tile(s, carry):
        rows = seq_rows(s)
        xr = x[rows]
        q[rows] = (dot_nn(xr, square_of(ga[0, 0:2])) + vec[0:1]).astype(BF)
        k[rows] = dot_nn(xr, square_of(ga[0, 2:4])).astype(BF)
        v[rows] = (dot_nn(xr, square_of(ga[1, 0:2])) + vec[1:2]).astype(BF)
        return carry

    lax.fori_loop(0, x.shape[0] // LEN, tile, 0)


def head_pairs(n, lens):
    s, g = n // 6, n % 6
    first = lax.broadcasted_iota(jnp.int32, (1, 128), 1) < 64
    return s, seq_rows(s), pl.ds(pl.multiple_of(g * 128, 128), 128), (first, jnp.logical_not(first))


def attend(n, q, k, v, lens, context, log_total):
    s, rows, cols, halves = head_pairs(n, lens)
    qp, kp, vp = q[rows, cols], k[rows, cols], v[rows, cols]
    seen = lax.broadcasted_iota(jnp.int32, (1, LEN), 1) < lens[s]
    found = []
    for h in range(2):
        qm = jnp.where(halves[h], qp, jnp.zeros_like(qp))
        scores = jnp.where(seen, dot_nt(qm, kp) * 0.125, masked_fill)
        peak = jnp.max(scores, axis=1, keepdims=True)
        expo = jnp.exp(scores - peak)
        total = jnp.sum(expo, axis=1, keepdims=True)
        found.append(dot_nn((expo * (1.0 / total)).astype(BF), vp))
        log_total[n, h] = (peak + jnp.log(total))[:, 0]
    context[rows, cols] = jnp.where(halves[0], found[0], found[1]).astype(BF)


def attend_back(n, q, k, v, grad_context, log_total, lens, gq, gk, gv):
    s, rows, cols, halves = head_pairs(n, lens)
    kp, vp = k[rows, cols], v[rows, cols]
    seen = lax.broadcasted_iota(jnp.int32, (LEN, 1), 0) < lens[s]
    ak = av = jnp.zeros((LEN, 128), F32)
    size = LEN // 2
    for t in range(2):
        part = tile_rows(2 * s + t, size)
        qp, gp = q[part, cols], grad_context[part, cols]
        aq = jnp.zeros((size, 128), F32)
        for h in range(2):
            qm, km, gm = (jnp.where(halves[h], t, jnp.zeros_like(t)) for t in (qp, kp, gp))
            scores = jnp.where(seen, dot_nt(kp, qm) * 0.125, masked_fill)
            probs = jnp.exp(scores - log_total[n, h][None, t * size:(t + 1) * size])
            grad_probs = dot_nt(vp, gm)
            along = jnp.sum(probs * grad_probs, axis=0, keepdims=True)
            grad_scores = (probs * (grad_probs - along)).astype(BF)
            av += dot_nn(probs.astype(BF), gm)
            ak += dot_nn(grad_scores, qm)
            aq += dot_tn(grad_scores, km)
        gq[part, cols] = (aq * 0.125).astype(BF)
    gk[rows, cols] = (ak * 0.125).astype(BF)
    gv[rows, cols] = av.astype(BF)


def mean_of(t):
    return jnp.mean(t, axis=-1, keepdims=True)


def attention_end(x, context, ga, vec, normed, factor):
    width = x.shape[1]

    def tile(s, carry):
        rows = seq_rows(s)
        attended = dot_nn(context[rows], square_of(ga[1, 2:4])) + vec[2:3]
        resid = x[rows].astype(F32) + attended
        center = resid - mean_of(resid)
        scale = lax.rsqrt(mean_of(center * center) + norm_floor)
        normed[rows] = center * scale
        factor[rows] = scale
        return carry

    lax.fori_loop(0, x.shape[0] // LEN, tile, 0)


def vec_part(vec, n):
    return vec[n:n + 1]


def input_gradient(x, cot, ga, grad_resid, keep, routes, gq, gk, gv, in_grad):
    def tile(s, carry):
        rows = tile_rows(s, LEN // 2)
        total = grad_resid[rows] + dot_nt(gq[rows], square_of(ga[0, 0:2]))
        total += dot_nt(gk[rows], square_of(ga[0, 2:4]))
        total += dot_nt(gv[rows], square_of(ga[1, 0:2]))
        in_grad[rows] = jnp.where(served_flag(keep, routes, s // 2) > 0, total.astype(BF), cot[rows])
        return carry

    lax.fori_loop(0, 2 * x.shape[0] // LEN, tile, 0)


def gather_attention_kernel(aw, fw, vw, x, lens, gf, ga_out, vec, q_out, k_out, v_out, context_out, log_total, normed_out, factor,
                            active_out, slope_out,
                            ga, gv, strip, pair, own, q, k, v, context, normed, low, w1, active, slope, store, wload, *sems):
    p = place()
    peers = near(p)
    greet(peers)
    share = vw.shape[0]
    own[...] = jnp.zeros_like(own)
    own[0:1, 0:share] = vw[...].astype(BF).astype(F32).reshape(1, share)
    for b in range(8):
        strip[:, b * BLOCK:(b + 1) * BLOCK] = aw[b].astype(BF)
    for j in range(2):
        for b in range(8):
            pair[j, :, b * BLOCK:(b + 1) * BLOCK] = fw[8 * j + b].astype(BF)
    half = BLOCK // 2
    seqs = x.shape[0] // LEN
    dx, dy = square_links(p)
    both = (p["na"], p["nb"], 8 - p["d"], 7 + p["d"])

    def attn_part(h):
        rows = pl.ds(h * half, half)
        return both + (strip.at[rows], lambda d, z, c: ga.at[d, z, c, rows], lambda d, c: ga.at[d, :, c, rows])

    def feed_part(j):
        links = (dy, dx, 8, 7) if j == 0 else (dx, dy, 7, 8)
        return links + (pair.at[j], lambda d, z, c: gf.at[d, z, c, j], lambda d, c: gf.at[d, :, c, j])

    vec_piece = both + (own, lambda d, z, c: gv.at[d, z, c], lambda d, c: gv.at[d, :, c])
    parts = [attn_part(0), vec_piece, attn_part(1), feed_part(0), feed_part(1)]
    a0, w, a1, f0, f1 = every = [Spread(p, *part, *sems[3 * n:3 * n + 3]) for n, part in enumerate(parts)]
    meet(peers)
    for s in (a0, w, a1):
        s.start()
    on_core(p, 0, f0.start, f1.start)
    a0.second()
    w.second()
    a1.second()
    for s in (a0, w, a1):
        s.third()
        s.fourth()
    on_core(p, 0, f0.second, f1.second)
    on_core(p, 1, f0.start, f1.start)
    for s in (a0, w, a1):
        s.fifth()
    w.sixth()
    unfold_vec(gv, vec, share)
    a0.sixth()
    a1.sixth()
    stores = [pltpu.make_async_copy(src, dst, store.at[n])
              for n, (src, dst) in enumerate(((q, q_out), (k, k_out), (v, v_out), (context, context_out), (normed, normed_out),
                                              (ga, ga_out)))]
    stores[5].start()
    projections(x, ga, vec, q, k, v)
    for copy in stores[:3]:
        copy.start()

    def step(n, carry):
        attend(n, q, k, v, lens, context, log_total)
        at_step(n, 3, lambda: on_core(p, 0, f0.third, f1.third, f0.fourth, f1.fourth))
        at_step(n, 4, lambda: on_core(p, 1, f0.second, f1.second))
        at_step(n, 9, lambda: on_core(p, 0, f0.fifth, f1.fifth))
        return carry

    lax.fori_loop(0, 12, step, 0)
    stores[3].start()
    attention_end(x, context, ga, vec, normed, factor)
    stores[4].start()
    on_core(p, 1, f0.sixth, f1.sixth)

    def fetch(t, carry):
        n, s = t // 8, t % 8
        pltpu.make_async_copy(gf.at[0, s // 2, 2 * (s % 2) + n // 2, n % 2], w1.at[n // 2, 2 * (n % 2) + s // 4, s % 4],
                              wload.at[n]).start()
        return carry

    lax.fori_loop(0, 32, fetch, 0)

    def lower(s, carry):
        rows = seq_rows(s)
        low[rows] = (normed[rows] * vec_part(vec, 8) + vec_part(vec, 9)).astype(BF)
        return carry

    lax.fori_loop(0, seqs, lower, 0)

    def enter(n, carry):
        pltpu.make_async_copy(quarter(w1, n), quarter(w1, n), wload.at[n]).wait()

        def tile(s, inner):
            rows = seq_rows(s)
            before = dot_nn(low[rows], square_of(quarter(w1, n)[...])) + vec[pl.ds(3 + n, 1)]
            cumulative = 0.5 * (1.0 + lax.erf(before * (1.0 / math.sqrt(2.0))))
            active[n, rows] = (before * cumulative).astype(BF)
            density = jnp.exp(-0.5 * before * before) * (1.0 / math.sqrt(2.0 * math.pi))
            slope[n, rows] = (cumulative + before * density).astype(BF)
            return inner

        lax.fori_loop(0, seqs, tile, 0)
        pltpu.make_async_copy(active.at[n], active_out.at[n], store.at[6 + n]).start()
        pltpu.make_async_copy(slope.at[n], slope_out.at[n], store.at[10 + n]).start()
        at_step(n, 1, lambda: on_core(p, 1, f0.third, f1.third, f0.fourth, f1.fourth))
        return carry

    lax.fori_loop(0, 4, enter, 0)
    on_core(p, 1, f0.fifth, f1.fifth)
    on_core(p, 0, f0.sixth, f1.sixth)
    for s in every:
        s.drain()
    for copy in stores:
        copy.wait()
    for n in range(4):
        pltpu.make_async_copy(active.at[n], active_out.at[n], store.at[6 + n]).wait()
        pltpu.make_async_copy(slope.at[n], slope_out.at[n], store.at[10 + n]).wait()


def gather_attention(aw, fw, vw, x, lens):
    tokens, width = x.shape
    low = jax.ShapeDtypeStruct(x.shape, BF)
    four = jax.ShapeDtypeStruct((4, tokens, width), BF)
    outs = [jax.ShapeDtypeStruct((2, 4, 4, 2, BLOCK, width), BF), jax.ShapeDtypeStruct((2, 4, 4, BLOCK, width), BF),
            jax.ShapeDtypeStruct((ROWS, width), F32)] + [low] * 4
    outs += [jax.ShapeDtypeStruct((12, 2, LEN), F32), jax.ShapeDtypeStruct(x.shape, F32),
             jax.ShapeDtypeStruct((tokens, 1), F32), four, four]
    vmem = pl.BlockSpec(memory_space=pltpu.VMEM)
    hbm = pl.BlockSpec(memory_space=pl.ANY)
    strips = pltpu.VMEM((2, 4, 4, BLOCK, width), BF)
    rows = pltpu.VMEM(x.shape, BF)
    wide = pltpu.VMEM((4, tokens, width), BF)
    return pl.pallas_call(
        gather_attention_kernel,
        out_shape=outs,
        in_specs=[vmem] * 4 + [pl.BlockSpec(memory_space=pltpu.SMEM)],
        out_specs=[hbm, hbm, vmem] + [hbm] * 4 + [vmem, hbm, vmem, hbm, hbm],
        scratch_shapes=[strips, pltpu.VMEM((2, 4, 4, 8, 384), F32), pltpu.VMEM((BLOCK, width), BF),
                        pltpu.VMEM((2, BLOCK, width), BF), pltpu.VMEM((8, 384), F32)]
        + [rows] * 4 + [pltpu.VMEM(x.shape, F32), rows, strips, wide, wide,
                        pltpu.SemaphoreType.DMA((14,)), pltpu.SemaphoreType.DMA((4,))]
        + spread_sems() * 5,
        compiler_params=pltpu.CompilerParams(collective_id=0, has_side_effects=True, vmem_limit_bytes=62 << 20),
        name="gather_attention",
    )(aw, fw, vw, x, lens)


def fold_scratch(width):
    shape = (BLOCK, width)
    return [pltpu.VMEM((4, 4) + shape, BF), pltpu.VMEM((4,) + shape, BF), pltpu.VMEM((4,) + shape, BF),
            pltpu.VMEM((4,) + shape, BF), pltpu.VMEM((3,) + shape, BF),
            pltpu.SemaphoreType.DMA((7,)), pltpu.SemaphoreType.DMA((7,))]


class Total(Mail):
    def __init__(self, p, held, came, send, recv):
        Mail.__init__(self, p, send, recv)
        self.held, self.came = held, came
        self.peers = ((1 - p["d"], p["i"]), (p["d"], p["na"]), (p["d"], p["nb"]))

    def start(self):
        self.go(self.held.at[0], self.came.at[0], 0, self.peers[0])

    def hop(self, n):
        p = self.p
        self.wait(self.came.at[n], n)
        self.held[n + 1] = self.held[n] + self.came[n]
        if n < 2:
            self.go(self.held.at[n + 1], self.came.at[n + 1], n + 1, self.peers[n + 1])
        else:
            for k in (1, 2, 3):
                self.go(self.held.at[3], self.came.at[2 + k], 2 + k, (p["d"], ((p["z"] + k) % 4) * 4 + p["c"]))

    def end(self):
        total = self.held[3]
        for k in (1, 2, 3):
            self.wait(self.came.at[2 + k], 2 + k)
            total += self.came[2 + k]
        return total


def own_share(p, rows, out, share):
    per = share // BLOCK
    me = p["d"] * 16 + p["i"]
    units = sum(
        jnp.dot(one_hot((8, ROWS), lambda a: per * me + jnp.where(a < per, a, -8 * 32 * per), lambda r, b=b: 8 * r + b),
                rows[:, b * BLOCK:(b + 1) * BLOCK], precision=lax.Precision.HIGHEST, preferred_element_type=F32)
        for b in range(8)
    )
    for a in range(per):
        out[0:1, a * BLOCK:(a + 1) * BLOCK] = units[a:a + 1]


def everyone(p):
    me = p["d"] * 16 + p["i"]

    def other(k):
        t = (me + k) % 32
        return (t // 16, t % 16)

    return me, other


def greet_all(p):
    me, other = everyone(p)
    barrier = pltpu.get_barrier_semaphore()

    def one(k, carry):
        pl.semaphore_signal(barrier, inc=1, device_id=other(k), device_id_type=MESH)
        return carry

    lax.fori_loop(1, 32, one, 0)


def meet_all():
    pl.semaphore_wait(pltpu.get_barrier_semaphore(), 31)


def norm_sum(p, square, slots, send, recv):
    me, other = everyone(p)
    slots[me] = jnp.full((8, 128), square, F32)
    to = lambda k, slot: remote(slots.at[slot], slots.at[slot], send, recv, slot, other(k))

    def push(k, carry):
        remote(slots.at[me], slots.at[me], send.at[pl.ds(k, 1)], recv.at[pl.ds(me, 1)], 0, other(k)).start()
        return carry

    def take(k, carry):
        slot = (me + k) % 32
        remote(slots.at[slot], slots.at[slot], send.at[pl.ds(k, 1)], recv.at[pl.ds(slot, 1)], 0, other(k)).wait_recv()
        return carry

    def done(k, carry):
        remote(slots.at[me], slots.at[me], send.at[pl.ds(k, 1)], recv.at[pl.ds(me, 1)], 0, other(k)).wait_send()
        return carry

    lax.fori_loop(1, 32, push, 0)
    lax.fori_loop(1, 32, take, 0)
    total = jnp.sum(slots[...], axis=0)[0:1, 0:1]
    lax.fori_loop(1, 32, done, 0)
    return total


class Fold:
    def __init__(self, p, a, b, away, home, pair, diag, flat, late, line, send, recv):
        self.p, self.home, self.pair, self.diag, self.flat, self.late, self.line = p, home, pair, diag, flat, late, line
        self.ca, self.cb = a % 4, b % 4
        d, z, c = p["d"], p["z"], p["c"]
        pieces = [(away, pair, (1 - d, p["i"])), (pair.at[:, p["cd"]], diag, (d, b)), (pair.at[:, self.cb], flat, (d, b)),
                  (pair.at[:, self.ca], late, (d, a))]
        pieces += [(pair.at[(z + k) % 4, c], line.at[k - 1], (d, ((z + k) % 4) * 4 + c)) for k in (1, 2, 3)]
        self.copies = [remote(src, dst, send, recv, n, dev) for n, (src, dst, dev) in enumerate(pieces)]

    def add(self, dst, *others):
        total = dst[...].astype(F32)
        for o in others:
            total += o[...].astype(F32)
        dst[...] = total.astype(dst.dtype)

    def start(self):
        self.copies[0].start()

    def second(self):
        self.copies[0].wait_recv()
        for col, n in ((self.p["cd"], 1), (self.cb, 2)):
            self.add(self.pair.at[:, col], self.home.at[:, col])
            self.copies[n].start()
        for col in (self.ca, self.p["c"]):
            self.add(self.pair.at[:, col], self.home.at[:, col])

    def third(self):
        self.copies[1].wait_recv()
        self.add(self.pair.at[:, self.ca], self.diag)
        self.copies[3].start()

    def fourth(self):
        p = self.p
        self.copies[2].wait_recv()
        self.copies[3].wait_recv()
        for k in (2, 1, 3, 0):
            dst = (p["z"] + k) % 4
            self.add(self.pair.at[dst, p["c"]], self.flat.at[dst], self.late.at[dst])
            if k:
                self.copies[3 + k].start()

    def fifth(self, out):
        p = self.p
        total = self.pair[p["z"], p["c"]].astype(F32)
        for k in (1, 2, 3):
            self.copies[3 + k].wait_recv()
            total += self.line[k - 1].astype(F32)
        out[...] = total

    def drain(self):
        for copy in self.copies:
            copy.wait_send()


def layer_back_kernel(x_in, cot_in, normed_in, active_in, slope_in, factor, gf, ga, q_in, k_in, v_in, context_in, log_total, vec, lens, keep, routes,
                      out, in_grad, sf, sa, sv, norm,
                      x, cot, normed, middle, low, grad_low, image, w1, w2, active, slope, hf, gvec, held, came, slots,
                      load, wload, nsend, nrecv, tsend, trecv, *scratch):
    p = place()
    greet_all(p)
    tokens, width = x.shape
    seqs = tokens // LEN
    half = width // 2
    lanes = (pl.ds(0, half), pl.ds(half, half))

    def bring(src, dst, n):
        return pltpu.make_async_copy(src, dst, load.at[n])

    ahead = [bring(active_in, active, 0), bring(normed_in, normed, 1), bring(x_in, x, 2), bring(cot_in, cot, 9)]
    slopes = bring(slope_in, slope, 10)

    def fetch_down(t, carry):
        q, s = t // 8, t % 8
        pltpu.make_async_copy(gf.at[1, q, s // 2, s % 2], w2.at[q // 2, 2 * (q % 2) + s // 4, s % 4], wload.at[0]).start()
        return carry

    def fetch(t, carry):
        q, s = t // 8, t % 8
        pltpu.make_async_copy(gf.at[0, s // 2, 2 * (s % 2) + q // 2, q % 2], w1.at[q // 2, 2 * (q % 2) + s // 4, s % 4],
                              wload.at[1]).start()
        return carry

    ahead[0].start()
    lax.fori_loop(0, 32, fetch_down, 0)
    for copy in ahead[1:]:
        copy.start()
    slopes.start()
    lax.fori_loop(0, 32, fetch, 0)
    dx, dy = square_links(p)
    f0 = Fold(p, dy, dx, hf.at[1 - p["d"], :, :, 0], hf.at[p["d"], :, :, 0], *scratch[0:7])
    f1 = Fold(p, dx, dy, hf.at[1 - p["d"], :, :, 1], hf.at[p["d"], :, :, 1], *scratch[7:14])
    ha, ga_in = w1, w2
    a0, a1 = [Fold(p, p["na"], p["nb"], ha.at[1 - p["d"], :, :, :, lanes[n]], ha.at[p["d"], :, :, :, lanes[n]],
                   *scratch[14 + 7 * n:21 + 7 * n]) for n in range(2)]
    total = Total(p, held, came, tsend, trecv)

    def on(core, *steps):
        on_core(p, core, *steps)

    gvec[...] = jnp.zeros_like(gvec)

    def add_vec(n, value):
        gvec[n:n + 1] += value

    def lower(s, carry):
        rows = seq_rows(s)
        low[rows] = (normed[rows] * vec_part(vec, 8) + vec_part(vec, 9)).astype(BF)
        return carry

    for copy in ahead[1:2]:
        copy.wait()
    lax.fori_loop(0, seqs, lower, 0)
    pltpu.make_async_copy(w2, w2, wload.at[0]).wait()
    for copy in ahead[:1] + ahead[2:]:
        copy.wait()
    tile = LEN // 2

    def leave(t, carry):
        rows = tile_rows(t, tile)
        show = pltpu.make_async_copy(image, out.at[rows], load.at[3])
        branch = dot_nn(active[0, rows], square_of(quarter(w2, 0)[...]))
        for q in range(1, 4):
            branch += dot_nn(active[q, rows], square_of(quarter(w2, q)[...]))
        resid = normed[rows] * vec_part(vec, 8) + vec_part(vec, 9) + (branch + vec_part(vec, 7))
        center = resid - mean_of(resid)
        scale = lax.rsqrt(mean_of(center * center) + norm_floor)
        second = center * scale
        served = served_flag(keep, routes, t // 2) > 0
        result = second * vec_part(vec, 10) + vec_part(vec, 11)
        image[...] = jnp.where(served, result.astype(BF), x[rows])
        show.start()
        grad = jnp.where(served, cot[rows].astype(F32), 0.0)
        add_vec(10, jnp.sum(grad * second, axis=0, keepdims=True))
        add_vec(11, jnp.sum(grad, axis=0, keepdims=True))
        grad = grad * vec_part(vec, 10)
        grad = scale * (grad - mean_of(grad) - second * mean_of(grad * second))
        middle[rows] = grad
        grad_low[rows] = grad.astype(BF)
        add_vec(7, jnp.sum(grad.astype(BF).astype(F32), axis=0, keepdims=True))
        show.wait()
        return carry

    lax.fori_loop(0, 2 * seqs, leave, 0)
    def down_grad(t, carry):
        q, h = t // 2, t % 2
        found = dot_tn(active[q, :, pl.ds(pl.multiple_of(h * half, half), half)], grad_low[...])
        hf[1, q, pl.ds(2 * h, 2)] = found.astype(BF).reshape(2, 2, BLOCK, width)
        return carry

    lax.fori_loop(0, 8, down_grad, 0)
    meet_all()
    on(0, f0.start, f1.start)
    again = [bring(src, slope.at[n], 4 + n) for n, src in enumerate((context_in, q_in, k_in, v_in))]
    context, qs, ks, vs = (slope.at[n] for n in range(4))
    slopes.wait()

    def turn(q, carry):
        def part(s, inner):
            rows = seq_rows(s)
            back = dot_nt(grad_low[rows], square_of(quarter(w2, q)[...])) * slope[q, rows].astype(F32)
            active[q, rows] = back.astype(BF)
            gvec[pl.ds(3 + q, 1)] += jnp.sum(back.astype(BF).astype(F32), axis=0, keepdims=True)
            return inner

        def up_grad(h, inner):
            found = dot_tn(low[:, pl.ds(pl.multiple_of(h * half, half), half)], active[q]).astype(BF).reshape(2, 2, BLOCK, width)
            for y in range(2):
                hf[0, pl.ds(2 * h, 2), 2 * y + q // 2, q % 2] = found[:, y]
            return inner

        lax.fori_loop(0, seqs, part, 0)
        lax.fori_loop(0, 2, up_grad, 0)
        at_step(q, 1, lambda: on(1, f0.second))
        at_step(q, 2, lambda: on(1, f1.second))
        return carry

    lax.fori_loop(0, 4, turn, 0)
    for copy in again:
        copy.start()
    pltpu.make_async_copy(w1, w1, wload.at[1]).wait()
    square_in = bring(ga, ga_in, 8)
    square_in.start()
    on(1, f0.start, f1.start)

    def close(t, carry):
        rows = tile_rows(t, tile)
        grad = middle[rows]
        for q in range(4):
            grad += dot_nt(active[q, rows], square_of(quarter(w1, q)[...]))
        head = normed[rows]
        add_vec(8, jnp.sum(grad * head, axis=0, keepdims=True))
        add_vec(9, jnp.sum(grad, axis=0, keepdims=True))
        grad = grad * vec_part(vec, 8)
        grad = factor[rows] * (grad - mean_of(grad) - head * mean_of(grad * head))
        middle[rows] = grad
        grad_low[rows] = grad.astype(BF)
        return carry

    lax.fori_loop(0, seqs, close, 0)
    on(1, f0.third)
    lax.fori_loop(seqs, 2 * seqs, close, 0)
    on(1, f1.third)
    on(0, f0.second)
    gq, gk, gv, grad_context = (active.at[n] for n in range(4))
    square_in.wait()
    again[0].wait()

    def open_attention(s, carry):
        rows = seq_rows(s)
        grad_context[rows] = dot_nt(grad_low[rows], square_of(ga_in[1, 2:4])).astype(BF)
        return carry

    lax.fori_loop(0, seqs, open_attention, 0)
    held[0] = gvec[...]
    held[0, 2:3] = jnp.sum(grad_low[...].astype(F32), axis=0, keepdims=True)
    for h in range(2):
        ha[1, 2 + h] = dot_tn(context[:, h * half:(h + 1) * half], grad_low[...]).astype(BF).reshape(4, BLOCK, width)
    on(0, f1.second)
    for copy in again[1:]:
        copy.wait()

    def step(m, carry):
        n = ((m % 6) // 3) * 6 + (m // 6) * 3 + m % 3
        attend_back(n, qs, ks, vs, grad_context, log_total, lens, gq, gk, gv)
        at_step(m, 1, lambda: on(1, f0.fourth))
        at_step(m, 2, lambda: on(1, f1.fourth))
        at_step(m, 3, lambda: on(0, f0.third))
        at_step(m, 4, lambda: on(0, f1.third))
        at_step(m, 5, lambda: weight_grads(0), a0.start)
        at_step(m, 7, a0.second)
        at_step(m, 9, lambda: on(0, f0.fourth))
        at_step(m, 11, lambda: on(0, f1.fourth), lambda: weight_grads(1))
        return carry

    def weight_grads(n):
        cols = lanes[n]
        for dst, src in ((ha.at[0, 0:2], gq), (ha.at[0, 2:4], gk), (ha.at[1, 0:2], gv)):
            dst[:, :, :, cols] = dot_tn(x[...], src[:, cols]).astype(BF).reshape(2, 4, BLOCK, half)

    lax.fori_loop(0, 12, step, 0)
    a1.start()
    held[0, 0:1] = jnp.sum(gq[...].astype(F32), axis=0, keepdims=True)
    held[0, 1:2] = jnp.sum(gv[...].astype(F32), axis=0, keepdims=True)
    total.start()
    a0.third()
    a1.second()
    total.hop(0)
    input_gradient(x, cot, ga_in, middle, keep, routes, gq, gk, gv, cot)
    last = bring(cot, in_grad, 3)
    last.start()
    total.hop(1)
    a0.fourth()
    a1.third()
    total.hop(2)
    f0.fifth(sf.at[0])
    f1.fifth(sf.at[1])
    square = jnp.sum(sf[...] * sf[...])
    a1.fourth()
    held[4] = total.end()
    sv[...] = jnp.zeros_like(sv)
    own_share(p, held[4], sv, 12 * width // 32)
    a0.fifth(sa.at[:, lanes[0]])
    a1.fifth(sa.at[:, lanes[1]])
    square += jnp.sum(sa[...] * sa[...]) + jnp.sum(sv[...] * sv[...])
    found = norm_sum(p, square, slots, nsend, nrecv)
    norm[...] = jnp.sqrt(found)
    for s in (f0, f1, a0, a1, total):
        s.drain()
    last.wait()


def layer_back(x, cot, normed, active, slope, factor, gf, ga, q, k, v, context, log_total, vec, lens, keep, routes):
    tokens, width = x.shape
    outs = [jax.ShapeDtypeStruct(x.shape, BF), jax.ShapeDtypeStruct(x.shape, BF), jax.ShapeDtypeStruct((2, BLOCK, width), F32),
            jax.ShapeDtypeStruct((BLOCK, width), F32), jax.ShapeDtypeStruct((8, 384), F32), jax.ShapeDtypeStruct((1, 1), F32)]
    dma = pltpu.SemaphoreType.DMA
    rows = pltpu.VMEM(x.shape, BF)
    wide = pltpu.VMEM(x.shape, F32)
    strips = pltpu.VMEM(ga.shape, BF)
    scratch = [rows, rows, wide, wide, rows, rows, pltpu.VMEM((LEN // 2, width), BF), strips, strips,
               pltpu.VMEM((4, tokens, width), BF), pltpu.VMEM((4, tokens, width), BF), pltpu.VMEM(gf.shape, BF),
               pltpu.VMEM(vec.shape, F32), pltpu.VMEM((5, ROWS, width), F32), pltpu.VMEM((6, ROWS, width), F32),
               pltpu.VMEM((32, 8, 128), F32),
               dma((11,)), dma((2,)), dma((32,)), dma((32,)), dma((6,)), dma((6,))]
    scratch += fold_scratch(width) * 2 + fold_scratch(width // 2) * 2
    vmem = pl.BlockSpec(memory_space=pltpu.VMEM)
    smem = pl.BlockSpec(memory_space=pltpu.SMEM)
    hbm = pl.BlockSpec(memory_space=pl.ANY)
    return pl.pallas_call(
        layer_back_kernel,
        out_shape=outs,
        in_specs=[hbm] * 5 + [vmem] + [hbm] * 6 + [vmem] * 2 + [smem] * 3,
        out_specs=[hbm] * 2 + [vmem] * 4,
        scratch_shapes=scratch,
        compiler_params=pltpu.CompilerParams(collective_id=1, has_side_effects=True, vmem_limit_bytes=67043328),
        name="feed_and_back",
    )(x, cot, normed, active, slope, factor, gf, ga, q, k, v, context, log_total, vec, lens, keep, routes)


def halves_of(t):
    high = t.astype(BF)
    return high, (t - high.astype(F32)).astype(BF)


def exact_dot(a, b, dims):
    dot = lambda x, y: lax.dot_general(x, y, (dims, ((), ())), preferred_element_type=F32)
    return dot(a[0], b[0]) + (dot(a[0], b[1]) + dot(a[1], b[0]))


def shampoo_block(grad, w, st, ro, mo, st_new, mo_new, w_new, b, factor):
    clipped = grad * factor
    moment = momentum_decay * mo[b] + clipped
    both = halves_of(clipped)
    left = exact_dot(both, both, ((1,), (1,)))
    right = exact_dot(both, both, ((0,), (0,)))
    st_new[b, 0] = stat_decay * st[b, 0] + (1.0 - stat_decay) * left
    st_new[b, 1] = stat_decay * st[b, 1] + (1.0 - stat_decay) * right
    mo_new[b] = moment
    turned = exact_dot(halves_of(ro[b, 0]), halves_of(moment), ((1,), (0,)))
    turned = exact_dot(halves_of(turned), halves_of(ro[b, 1]), ((1,), (0,)))
    w_new[b] = w[b] - matrix_rate * (turned + matrix_decay * w[b])


def optimizer_kernel(norm, sa, sf, sv, aw, ast, ar, am, fw, fst, fr, fm, vw, v1, v2,
                     ast_n, am_n, aw_n, fst_n, fm_n, fw_n, v1_n, v2_n, vw_n, ga, gf):
    factor = clip_bound / jnp.maximum(norm[...], clip_bound)
    g = pl.program_id(0)
    many = aw.shape[0]

    @pl.when(g == 0)
    def _():
        for b in range(8):
            ga[b] = sa[:, b * BLOCK:(b + 1) * BLOCK]
            for j in range(2):
                gf[8 * j + b] = sf[j, :, b * BLOCK:(b + 1) * BLOCK]
        size = vw.shape[0]
        clipped = (sv[0:1, 0:size] * factor)[0]
        first_new = first_decay * v1[...] + (1.0 - first_decay) * clipped
        second_new = second_decay * v2[...] + (1.0 - second_decay) * clipped * clipped
        first_hat = first_new / (1.0 - first_decay**STEP)
        second_hat = second_new / (1.0 - second_decay**STEP)
        v1_n[...] = first_new
        v2_n[...] = second_new
        vw_n[...] = vw[...] - vector_rate * first_hat / (jnp.sqrt(second_hat) + adam_floor)

    for b in range(many):
        shampoo_block(ga[g * many + b], aw, ast, ar, am, ast_n, am_n, aw_n, b, factor)
    for b in range(2 * many):
        shampoo_block(gf[g * 2 * many + b], fw, fst, fr, fm, fst_n, fm_n, fw_n, b, factor)


def optimizer(norm, sa, sf, sv, aw, ast, ar, am, fw, fst, fr, fm, vw, v1, v2):
    many = 2

    def steps(t, n):
        shape = (n,) + t.shape[1:]
        return pl.BlockSpec(shape, lambda g: (g,) + (0,) * (len(shape) - 1))

    def whole(t):
        return pl.BlockSpec(t.shape, lambda g: (0,) * t.ndim)

    like = lambda t: jax.ShapeDtypeStruct(t.shape, F32)
    args = (norm, sa, sf, sv, aw, ast, ar, am, fw, fst, fr, fm, vw, v1, v2)
    specs = [whole(t) for t in args[:4]]
    specs += [steps(t, many) for t in (aw, ast, ar, am)] + [steps(t, 2 * many) for t in (fw, fst, fr, fm)]
    specs += [whole(t) for t in (vw, v1, v2)]
    outs = (ast, am, aw, fst, fm, fw, v1, v2, vw)
    return pl.pallas_call(
        optimizer_kernel,
        out_shape=[like(t) for t in outs],
        grid=(aw.shape[0] // many,),
        in_specs=specs,
        out_specs=[steps(t, many) for t in outs[:3]] + [steps(t, 2 * many) for t in outs[3:6]] + [whole(t) for t in outs[6:]],
        scratch_shapes=[pltpu.VMEM(aw.shape, F32), pltpu.VMEM(fw.shape, F32)],
        name="optimizer",
    )(*args)


def per_device(
    inputs,
    output_gradient,
    keep,
    lengths,
    routes,
    attn_weights,
    attn_stats,
    attn_roots,
    attn_momentum,
    ffn_weights,
    ffn_stats,
    ffn_roots,
    ffn_momentum,
    vec_weights,
    vec_first,
    vec_second,
):
    slots, seq_len, width = inputs.shape
    tokens = slots * seq_len
    x = inputs.reshape(tokens, width)
    cot = output_gradient.reshape(tokens, width)
    gf, ga, vec, q, k, v, context, log_total, normed, factor, active, slope = gather_attention(attn_weights, ffn_weights, vec_weights, x, lengths)
    out, in_grad, sf, sa, sv, norm = layer_back(
        x, cot, normed, active, slope, factor, gf, ga, q, k, v, context, log_total, vec, lengths, keep, routes
    )
    rest = optimizer(
        norm, sa, sf, sv,
        attn_weights, attn_stats, attn_roots, attn_momentum,
        ffn_weights, ffn_stats, ffn_roots, ffn_momentum,
        vec_weights, vec_first, vec_second,
    )
    return (out.reshape(inputs.shape), in_grad.reshape(inputs.shape), norm.reshape(()), *rest)


def solution(mesh):
    small = mesh.shape["depth"] == 2 and mesh.shape["dp"] == 16
    return jax.shard_map(
        per_device if small else per_device_general,
        mesh=mesh,
        in_specs=(
            P(("depth", "dp"), None, None),
            P(("depth", "dp"), None, None),
            P(("depth", "dp")),
            P(("depth", "dp")),
            P(("depth", "dp")),
            P(("depth", "dp"), None, None),
            P(("depth", "dp"), None, None, None),
            P(("depth", "dp"), None, None, None),
            P(("depth", "dp"), None, None),
            P(("depth", "dp"), None, None),
            P(("depth", "dp"), None, None, None),
            P(("depth", "dp"), None, None, None),
            P(("depth", "dp"), None, None),
            P(("depth", "dp")),
            P(("depth", "dp")),
            P(("depth", "dp")),
        ),
        out_specs=(
            P(("depth", "dp"), None, None),
            P(("depth", "dp"), None, None),
            P(),
            P(("depth", "dp"), None, None, None),
            P(("depth", "dp"), None, None),
            P(("depth", "dp"), None, None),
            P(("depth", "dp"), None, None, None),
            P(("depth", "dp"), None, None),
            P(("depth", "dp"), None, None),
            P(("depth", "dp")),
            P(("depth", "dp")),
            P(("depth", "dp")),
        ),
        check_vma=False,
    )
```

```python
import functools
import math

import jax
import jax.numpy as jnp
from jax import lax
from jax.experimental import pallas as pl
from jax.experimental.pallas import tpu as pltpu
from jax.sharding import PartitionSpec as P

HEADS = 12
FF = 3072
BLOCK = 96
STEP = 10


norm_floor = 1e-05
masked_fill = -1000000000.0
momentum_decay = 0.9
stat_decay = 0.95
matrix_rate = 1.0
matrix_decay = 0.01
clip_bound = 1.0
first_decay = 0.9
second_decay = 0.999
vector_rate = 0.5
adam_floor = 1e-08


def serve_flags(keep_rows, route_rows):
    count = keep_rows.shape[-1]
    order = jnp.arange(count, dtype=jnp.int32)
    earlier = (order[None, :] < order[:, None]).astype(jnp.int32)
    same = (route_rows[:, :, None] == route_rows[:, None, :]).astype(jnp.int32)
    clash = jnp.sum(same * earlier[None, :, :] * keep_rows[:, None, :], axis=2)
    return keep_rows * (clash == 0).astype(jnp.int32)


def to_matrix(blocks, height, breadth):
    shaped = blocks.reshape(height // BLOCK, breadth // BLOCK, BLOCK, BLOCK)
    return shaped.transpose(0, 2, 1, 3).reshape(height, breadth)


def to_flat_blocks(matrix):
    height, breadth = matrix.shape
    shaped = matrix.reshape(height // BLOCK, BLOCK, breadth // BLOCK, BLOCK)
    return shaped.transpose(0, 2, 1, 3).reshape(-1, BLOCK * BLOCK)


def norm_parts(resid):
    center = resid - jnp.mean(resid, axis=-1, keepdims=True)
    factor = lax.rsqrt(jnp.mean(center * center, axis=-1, keepdims=True) + norm_floor)
    return (center * factor, factor)


def norm_back(grad_normed, normed, factor):
    middle = jnp.mean(grad_normed, axis=-1, keepdims=True)
    along = jnp.mean(grad_normed * normed, axis=-1, keepdims=True)
    return factor * (grad_normed - middle - normed * along)


def gelu_slope(value):
    cumulative = 0.5 * (1.0 + lax.erf(value * (1.0 / math.sqrt(2.0))))
    density = jnp.exp(-0.5 * value * value) * (1.0 / math.sqrt(2.0 * math.pi))
    return cumulative + value * density


def product(left, right):
    return jnp.dot(left, right, preferred_element_type=jnp.float32)


def contract_rows(left, right):
    return lax.dot_general(
        left, right, (((0,), (0,)), ((), ())), preferred_element_type=jnp.float32
    )


def times_transpose(left, right):
    return lax.dot_general(
        left, right, (((1,), (1,)), ((), ())), preferred_element_type=jnp.float32
    )


def masked_scores(query, keys, visible_len):
    scale = 1.0 / math.sqrt(query.shape[-1])
    scores = jnp.einsum("qhe,khe->hqk", query, keys, preferred_element_type=jnp.float32) * scale
    visible = jnp.arange(keys.shape[0], dtype=jnp.int32) < visible_len
    return jnp.where(visible[None, None, :], scores, masked_fill)


def attend_forward(pieces):
    query, keys, values, visible_len = pieces
    scores = masked_scores(query, keys, visible_len)
    peak = jnp.max(scores, axis=-1, keepdims=True)
    expo = jnp.exp(scores - peak)
    total = jnp.sum(expo, axis=-1, keepdims=True)
    probs_low = (expo / total).astype(jnp.bfloat16)
    context = jnp.einsum("hqk,khe->qhe", probs_low, values, preferred_element_type=jnp.float32)
    return (context, peak[..., 0] + jnp.log(total[..., 0]))


def attend_backward(pieces):
    query, keys, values, grad_ctx, log_total, visible_len = pieces
    scale = 1.0 / math.sqrt(query.shape[-1])
    scores = masked_scores(query, keys, visible_len)
    probs = jnp.exp(scores - log_total[..., None])
    probs_low = probs.astype(jnp.bfloat16)
    grad_probs = jnp.einsum("qhe,khe->hqk", grad_ctx, values, preferred_element_type=jnp.float32)
    grad_values = jnp.einsum(
        "hqk,qhe->khe", probs_low, grad_ctx, preferred_element_type=jnp.float32
    )
    along = jnp.sum(probs * grad_probs, axis=-1, keepdims=True)
    grad_scores = (probs * (grad_probs - along)).astype(jnp.bfloat16)
    grad_query = (
        jnp.einsum("hqk,khe->qhe", grad_scores, keys, preferred_element_type=jnp.float32) * scale
    )
    grad_keys = (
        jnp.einsum("hqk,qhe->khe", grad_scores, query, preferred_element_type=jnp.float32) * scale
    )
    return (grad_query, grad_keys, grad_values)


def shampoo(weights, stats, roots, momentum, grads, factor):
    highest = lax.Precision.HIGHEST
    clipped = grads * factor
    moment = momentum_decay * momentum + clipped
    left = jnp.einsum("nab,ncb->nac", clipped, clipped, precision=highest)
    right = jnp.einsum("nab,nac->nbc", clipped, clipped, precision=highest)
    fresh = stat_decay * stats + (1.0 - stat_decay) * jnp.stack([left, right], axis=1)
    turned = jnp.einsum("nab,nbc->nac", roots[:, 0], moment, precision=highest)
    turned = jnp.einsum("nab,nbc->nac", turned, roots[:, 1], precision=highest)
    updated = weights - matrix_rate * (turned + matrix_decay * weights)
    return (fresh, moment, updated)


def adam_step(weights, first, second, grads, factor):
    clipped = grads * factor
    first_new = first_decay * first + (1.0 - first_decay) * clipped
    second_new = second_decay * second + (1.0 - second_decay) * clipped * clipped
    first_hat = first_new / (1.0 - first_decay**STEP)
    second_hat = second_new / (1.0 - second_decay**STEP)
    updated = weights - vector_rate * first_hat / (jnp.sqrt(second_hat) + adam_floor)
    return (first_new, second_new, updated)


def per_device_general(
    inputs,
    output_gradient,
    keep,
    lengths,
    routes,
    attn_weights,
    attn_stats,
    attn_roots,
    attn_momentum,
    ffn_weights,
    ffn_stats,
    ffn_roots,
    ffn_momentum,
    vec_weights,
    vec_first,
    vec_second,
):
    slots, seq_len, width = inputs.shape
    tokens = slots * seq_len
    head_size = width // HEADS
    hidden_width = FF
    depth_count = lax.axis_size("depth")
    peer_slots = slots // depth_count
    grid = (width // BLOCK) ** 2
    half_ffn = width * hidden_width // (BLOCK * BLOCK)
    area = BLOCK * BLOCK
    low_type = jnp.bfloat16
    attn_flat = attn_weights.reshape(-1, area).astype(low_type)
    ffn_flat = ffn_weights.reshape(-1, area).astype(low_type)
    attn_all, ffn_all, vec_all = (
        lax.all_gather(attn_flat, ("depth", "dp"), axis=0, tiled=True),
        lax.all_gather(ffn_flat, ("depth", "dp"), axis=0, tiled=True),
        lax.all_gather(vec_weights.astype(low_type), ("depth", "dp"), axis=0, tiled=True),
    )
    table_keep, table_len, table_route = (
        lax.all_gather(keep, "depth", axis=0, tiled=True),
        lax.all_gather(lengths, "depth", axis=0, tiled=True),
        lax.all_gather(routes, "depth", axis=0, tiled=True),
    )
    mine = serve_flags(keep[None, :], routes[None, :])[0]
    slot_order = jnp.arange(slots, dtype=jnp.int32)
    selection = ((routes[None, :] == slot_order[:, None]).astype(jnp.int32) * mine[None, :]).astype(
        low_type
    )
    outgoing_rows = jnp.einsum(
        "gz,zrp->grp", selection, inputs, preferred_element_type=jnp.float32
    ).astype(low_type)
    send_grad = jnp.einsum(
        "gz,zrp->grp", selection, output_gradient, preferred_element_type=jnp.float32
    ).astype(low_type)
    come_rows, come_grad = (
        lax.all_to_all(outgoing_rows, "depth", split_axis=0, concat_axis=0, tiled=True),
        lax.all_to_all(send_grad, "depth", split_axis=0, concat_axis=0, tiled=True),
    )
    all_keep = table_keep.reshape(depth_count, slots)
    all_route = table_route.reshape(depth_count, slots)
    all_len = table_len.reshape(depth_count, slots)
    all_served = serve_flags(all_keep, all_route)
    here = lax.axis_index("depth")
    source = slot_order // peer_slots
    target = here * peer_slots + slot_order % peer_slots
    source_hot = (source[:, None] == jnp.arange(depth_count, dtype=jnp.int32)[None, :]).astype(
        jnp.int32
    )
    match = (all_route[None, :, :] == target[:, None, None]).astype(jnp.int32) * all_served[
        None, :, :
    ]
    slot_len = jnp.sum(source_hot[:, :, None] * match * all_len[None, :, :], axis=(1, 2))
    visible_len = jnp.maximum(slot_len, 1)
    query_w = to_matrix(attn_all[0:grid], width, width)
    key_w = to_matrix(attn_all[grid : 2 * grid], width, width)
    value_w = to_matrix(attn_all[2 * grid : 3 * grid], width, width)
    output_w = to_matrix(attn_all[3 * grid : 4 * grid], width, width)
    vectors = vec_all.astype(jnp.float32)
    q_bias = vectors[0:width]
    v_bias = vectors[width : 2 * width]
    out_bias = vectors[2 * width : 3 * width]
    hidden_bias = vectors[3 * width : 3 * width + hidden_width]
    ffn_bias = vectors[3 * width + hidden_width : 4 * width + hidden_width]
    gain_one = vectors[4 * width + hidden_width : 5 * width + hidden_width]
    shift_one = vectors[5 * width + hidden_width : 6 * width + hidden_width]
    gain_two = vectors[6 * width + hidden_width : 7 * width + hidden_width]
    shift_two = vectors[7 * width + hidden_width : 8 * width + hidden_width]
    flat = come_rows.reshape(tokens, width)
    four = (slots, seq_len, HEADS, head_size)
    query = (product(flat, query_w) + q_bias).astype(low_type).reshape(four)
    keys = product(flat, key_w).astype(low_type).reshape(four)
    values = (product(flat, value_w) + v_bias).astype(low_type).reshape(four)
    context, log_total = lax.map(attend_forward, (query, keys, values, visible_len))
    context_low = context.reshape(tokens, width).astype(low_type)
    attended = product(context_low, output_w) + out_bias
    normed_one, factor_one = norm_parts(flat.astype(jnp.float32) + attended)
    hidden_in = normed_one * gain_one + shift_one
    hidden_low = hidden_in.astype(low_type)
    hidden_w = to_matrix(ffn_all[0:half_ffn], width, hidden_width)
    return_weight = to_matrix(ffn_all[half_ffn:], hidden_width, width)
    before = product(hidden_low, hidden_w) + hidden_bias
    active_low = jax.nn.gelu(before, approximate=False).astype(low_type)
    branch = product(active_low, return_weight) + ffn_bias
    normed_two, factor_two = norm_parts(hidden_in + branch)
    result_low = (normed_two * gain_two + shift_two).astype(low_type)
    grad_rows = come_grad.reshape(tokens, width).astype(jnp.float32)
    grad_gain_two = jnp.sum(grad_rows * normed_two, axis=0)
    grad_shift_two = jnp.sum(grad_rows, axis=0)
    grad_resid_two = norm_back(grad_rows * gain_two, normed_two, factor_two)
    grad_branch = grad_resid_two.astype(low_type)
    grad_ffn_bias = jnp.sum(grad_branch.astype(jnp.float32), axis=0)
    gradient_return_weight = contract_rows(active_low, grad_branch)
    grad_active = times_transpose(grad_branch, return_weight)
    grad_before = (grad_active * gelu_slope(before)).astype(low_type)
    grad_hidden_bias = jnp.sum(grad_before.astype(jnp.float32), axis=0)
    grad_hidden_w = contract_rows(hidden_low, grad_before)
    grad_hidden = times_transpose(grad_before, hidden_w) + grad_resid_two
    grad_gain_one = jnp.sum(grad_hidden * normed_one, axis=0)
    grad_shift_one = jnp.sum(grad_hidden, axis=0)
    grad_resid_one = norm_back(grad_hidden * gain_one, normed_one, factor_one)
    ffn_grad = jnp.concatenate(
        [to_flat_blocks(grad_hidden_w), to_flat_blocks(gradient_return_weight)], axis=0
    )
    grad_attended = grad_resid_one.astype(low_type)
    grad_out_bias = jnp.sum(grad_attended.astype(jnp.float32), axis=0)
    grad_output_w = contract_rows(context_low, grad_attended)
    grad_context = times_transpose(grad_attended, output_w).astype(low_type).reshape(four)
    grad_query, grad_keys, grad_values = lax.map(
        attend_backward, (query, keys, values, grad_context, log_total, visible_len)
    )
    grad_query = grad_query.reshape(tokens, width).astype(low_type)
    grad_keys = grad_keys.reshape(tokens, width).astype(low_type)
    grad_values = grad_values.reshape(tokens, width).astype(low_type)
    grad_q_bias = jnp.sum(grad_query.astype(jnp.float32), axis=0)
    grad_v_bias = jnp.sum(grad_values.astype(jnp.float32), axis=0)
    grad_query_w = contract_rows(flat, grad_query)
    grad_key_w = contract_rows(flat, grad_keys)
    grad_value_w = contract_rows(flat, grad_values)
    in_rows = (
        grad_resid_one
        + times_transpose(grad_query, query_w)
        + times_transpose(grad_keys, key_w)
        + times_transpose(grad_values, value_w)
    )
    attn_grad = jnp.concatenate(
        [
            to_flat_blocks(grad_query_w),
            to_flat_blocks(grad_key_w),
            to_flat_blocks(grad_value_w),
            to_flat_blocks(grad_output_w),
        ],
        axis=0,
    )
    vec_grad = jnp.concatenate(
        [
            grad_q_bias,
            grad_v_bias,
            grad_out_bias,
            grad_hidden_bias,
            grad_ffn_bias,
            grad_gain_one,
            grad_shift_one,
            grad_gain_two,
            grad_shift_two,
        ]
    )
    attn_share, ffn_share, vec_share = (
        lax.psum_scatter(attn_grad, ("depth", "dp"), scatter_dimension=0, tiled=True),
        lax.psum_scatter(ffn_grad, ("depth", "dp"), scatter_dimension=0, tiled=True),
        lax.psum_scatter(vec_grad, ("depth", "dp"), scatter_dimension=0, tiled=True),
    )
    returned_rows, returned_gradient = (
        lax.all_to_all(
            result_low.reshape(slots, seq_len, width),
            "depth",
            split_axis=0,
            concat_axis=0,
            tiled=True,
        ),
        lax.all_to_all(
            in_rows.astype(low_type).reshape(slots, seq_len, width),
            "depth",
            split_axis=0,
            concat_axis=0,
            tiled=True,
        ),
    )
    stay = (1 - mine).astype(jnp.float32)[:, None, None]
    out = (
        jnp.einsum("rx,rmp->xmp", selection, returned_rows, preferred_element_type=jnp.float32)
        + stay * inputs.astype(jnp.float32)
    ).astype(low_type)
    in_grad = (
        jnp.einsum("rx,rmp->xmp", selection, returned_gradient, preferred_element_type=jnp.float32)
        + stay * output_gradient.astype(jnp.float32)
    ).astype(low_type)
    square = (
        jnp.sum(attn_share * attn_share)
        + jnp.sum(ffn_share * ffn_share)
        + jnp.sum(vec_share * vec_share)
    )
    total = lax.psum(square, ("depth", "dp"))
    grad_norm = jnp.sqrt(total)
    factor = clip_bound / jnp.maximum(grad_norm, clip_bound)
    attn_square = attn_share.reshape(-1, BLOCK, BLOCK)
    ffn_square = ffn_share.reshape(-1, BLOCK, BLOCK)
    attn_fresh, attn_moment, attn_updated = shampoo(
        attn_weights, attn_stats, attn_roots, attn_momentum, attn_square, factor
    )
    ffn_fresh, ffn_moment, ffn_updated = shampoo(
        ffn_weights, ffn_stats, ffn_roots, ffn_momentum, ffn_square, factor
    )
    first_new, second_new, vec_updated = adam_step(
        vec_weights, vec_first, vec_second, vec_share, factor
    )
    return (
        out,
        in_grad,
        grad_norm,
        attn_fresh,
        attn_moment,
        attn_updated,
        ffn_fresh,
        ffn_moment,
        ffn_updated,
        first_new,
        second_new,
        vec_updated,
    )


MESH = pl.DeviceIdType.MESH
BF = jnp.bfloat16
F32 = jnp.float32
LEN = 512
ROWS = 16


def place():
    d = lax.axis_index("depth")
    i = lax.axis_index("dp")
    x = i % 2
    y = (i // 2) % 2
    nx = i + 1 - 2 * x
    ny = i + 2 - 4 * y
    na = ny + d * (nx - ny)
    nb = nx + d * (ny - nx)
    return dict(d=d, i=i, z=i // 4, c=i % 4, na=na, nb=nb, ca=na % 4, cb=nb % 4, cd=3 - i % 4)


def near(p):
    peers = [(p["d"], p["na"]), (p["d"], p["nb"]), (1 - p["d"], p["i"])]
    return peers + [(p["d"], ((p["z"] + k) % 4) * 4 + p["c"]) for k in (1, 2, 3)]


def greet(peers):
    barrier = pltpu.get_barrier_semaphore()
    for peer in peers:
        pl.semaphore_signal(barrier, inc=1, device_id=peer, device_id_type=MESH)


def meet(peers):
    pl.semaphore_wait(pltpu.get_barrier_semaphore(), len(peers))


def remote(src, dst, send, recv, k, dev):
    return pltpu.make_async_remote_copy(src_ref=src, dst_ref=dst, send_sem=send.at[k], recv_sem=recv.at[k],
                                        device_id=dev, device_id_type=MESH)


class Mail:
    def __init__(self, p, send, recv):
        self.p, self.send, self.recv, self.sent = p, send, recv, []

    def go(self, src, dst, k, dev):
        copy = remote(src, dst, self.send, self.recv, k, dev)
        copy.start()
        self.sent.append(copy)

    def wait(self, dst, k):
        remote(dst, dst, self.send, self.recv, k, (self.p["d"], self.p["na"])).wait_recv()

    def drain(self):
        for copy in self.sent:
            copy.wait_send()


class Spread:
    def __init__(self, p, a, b, to_a, to_b, own, slot, column, send, recv, local):
        d, z, i, c = p["d"], p["z"], p["i"], p["c"]
        ca, cb = a % 4, b % 4
        self.keep = pltpu.make_async_copy(own, slot(d, z, c), local)
        lines = [(own, slot(d, z, c), (d, ((z + k) % 4) * 4 + c)) for k in (1, 2, 3)]
        takes = [slot(d, (z + 4 - k) % 4, c) for k in (1, 2, 3)]
        mine, from_a, from_b, far = (column(d, col) for col in (c, ca, cb, p["cd"]))
        core = (1 - d, i)
        sends = [(mine, 3, (d, a)), (mine, 4, (d, b)), (from_a, 5, (d, b)), (mine, 6, core), (from_a, to_a, core),
                 (from_b, to_b, core), (far, 9, core)]
        self.lines = [remote(src, dst, send, recv, k, dev) for k, (src, dst, dev) in enumerate(lines)]
        self.taken = [remote(dst, dst, send, recv, k, (d, a)) for k, dst in enumerate(takes)]
        self.sends = [remote(src, src, send, recv, k, dev) for src, k, dev in sends]
        waits = [(from_a, 3), (from_b, 4), (far, 5), (column(1 - d, c), 6), (column(1 - d, ca), to_a),
                 (column(1 - d, cb), to_b), (column(1 - d, p["cd"]), 9)]
        self.came = [remote(dst, dst, send, recv, k, (d, a)) for dst, k in waits]

    def push(self, *which):
        for n in which:
            self.sends[n].start()

    def start(self):
        self.keep.start()
        for k in (1, 0, 2):
            self.lines[k].start()

    def second(self):
        self.keep.wait()
        for copy in self.taken:
            copy.wait_recv()
        self.push(0, 1, 3)

    def third(self):
        self.came[0].wait_recv()
        self.push(2, 4)

    def fourth(self):
        self.came[1].wait_recv()
        self.push(5)

    def fifth(self):
        self.came[2].wait_recv()
        self.push(6)

    def sixth(self):
        for copy in self.came[3:]:
            copy.wait_recv()

    def drain(self):
        for copy in self.lines + self.sends:
            copy.wait_send()


def spread_sems():
    return [pltpu.SemaphoreType.DMA((10,)), pltpu.SemaphoreType.DMA((10,)), pltpu.SemaphoreType.DMA]


def on_core(p, core, *steps):
    @pl.when(p["d"] == core)
    def _():
        for s in steps:
            s()


def at_step(m, value, *steps):
    @pl.when(m == value)
    def _():
        for s in steps:
            s()


def square_links(p):
    dx = p["i"] + 1 - 2 * (p["i"] % 2)
    dy = p["i"] + 2 - 4 * ((p["i"] // 2) % 2)
    return dx, dy


def quarter(w, q):
    return w.at[q // 2, pl.ds(2 * (q % 2), 2)]


def one_hot(shape, row, col):
    r = lax.broadcasted_iota(jnp.int32, shape, 0)
    c = lax.broadcasted_iota(jnp.int32, shape, 1)
    return (row(r) == col(c)).astype(F32)


def unfold_vec(pieces, vec, share):
    per = share // BLOCK
    stack = pieces[...][:, :, :, 0, :].reshape(32, pieces.shape[-1])
    units = sum(
        jnp.dot(one_hot((32 * per, 32), lambda u: u, lambda k, a=a: per * k + a), stack[:, a * BLOCK:(a + 1) * BLOCK],
                preferred_element_type=F32)
        for a in range(per)
    )
    for b in range(8):
        vec[:, b * BLOCK:(b + 1) * BLOCK] = jnp.dot(
            one_hot((ROWS, 32 * per), lambda r, b=b: 8 * r + b, lambda u: u), units, preferred_element_type=F32)


def dot_nn(a, b):
    return lax.dot_general(a, b, (((1,), (0,)), ((), ())), preferred_element_type=F32)


def dot_nt(a, b):
    return lax.dot_general(a, b, (((1,), (1,)), ((), ())), preferred_element_type=F32)


def dot_tn(a, b):
    return lax.dot_general(a, b, (((0,), (0,)), ((), ())), preferred_element_type=F32)


def square_of(value):
    return value.reshape(value.shape[0] * value.shape[1] * value.shape[2], value.shape[3])


def seq_rows(s):
    return pl.ds(s * LEN, LEN) if isinstance(s, int) else pl.ds(pl.multiple_of(s * LEN, LEN), LEN)


def tile_rows(s, size):
    return pl.ds(pl.multiple_of(s * size, size), size)


def served_flag(keep, routes, s):
    other = keep[0] * (routes[0] == routes[1]).astype(jnp.int32)
    return jnp.where(s == 0, keep[0], keep[1] * (1 - other))


def projections(x, ga, vec, q, k, v):
    width = x.shape[1]

    def tile(s, carry):
        rows = seq_rows(s)
        xr = x[rows]
        q[rows] = (dot_nn(xr, square_of(ga[0, 0:2])) + vec[0:1]).astype(BF)
        k[rows] = dot_nn(xr, square_of(ga[0, 2:4])).astype(BF)
        v[rows] = (dot_nn(xr, square_of(ga[1, 0:2])) + vec[1:2]).astype(BF)
        return carry

    lax.fori_loop(0, x.shape[0] // LEN, tile, 0)


def head_pairs(n, lens):
    s, g = n // 6, n % 6
    first = lax.broadcasted_iota(jnp.int32, (1, 128), 1) < 64
    return s, seq_rows(s), pl.ds(pl.multiple_of(g * 128, 128), 128), (first, jnp.logical_not(first))


def attend(n, q, k, v, lens, context, log_total):
    s, rows, cols, halves = head_pairs(n, lens)
    qp, kp, vp = q[rows, cols], k[rows, cols], v[rows, cols]
    seen = lax.broadcasted_iota(jnp.int32, (1, LEN), 1) < lens[s]
    found = []
    for h in range(2):
        qm = jnp.where(halves[h], qp, jnp.zeros_like(qp))
        scores = jnp.where(seen, dot_nt(qm, kp) * 0.125, masked_fill)
        peak = jnp.max(scores, axis=1, keepdims=True)
        expo = jnp.exp(scores - peak)
        total = jnp.sum(expo, axis=1, keepdims=True)
        found.append(dot_nn((expo * (1.0 / total)).astype(BF), vp))
        log_total[n, h] = (peak + jnp.log(total))[:, 0]
    context[rows, cols] = jnp.where(halves[0], found[0], found[1]).astype(BF)


def attend_back(n, q, k, v, grad_context, log_total, lens, gq, gk, gv):
    s, rows, cols, halves = head_pairs(n, lens)
    kp, vp = k[rows, cols], v[rows, cols]
    seen = lax.broadcasted_iota(jnp.int32, (LEN, 1), 0) < lens[s]
    ak = av = jnp.zeros((LEN, 128), F32)
    size = LEN // 2
    for t in range(2):
        part = tile_rows(2 * s + t, size)
        qp, gp = q[part, cols], grad_context[part, cols]
        aq = jnp.zeros((size, 128), F32)
        for h in range(2):
            qm, km, gm = (jnp.where(halves[h], t, jnp.zeros_like(t)) for t in (qp, kp, gp))
            scores = jnp.where(seen, dot_nt(kp, qm) * 0.125, masked_fill)
            probs = jnp.exp(scores - log_total[n, h][None, t * size:(t + 1) * size])
            grad_probs = dot_nt(vp, gm)
            along = jnp.sum(probs * grad_probs, axis=0, keepdims=True)
            grad_scores = (probs * (grad_probs - along)).astype(BF)
            av += dot_nn(probs.astype(BF), gm)
            ak += dot_nn(grad_scores, qm)
            aq += dot_tn(grad_scores, km)
        gq[part, cols] = (aq * 0.125).astype(BF)
    gk[rows, cols] = (ak * 0.125).astype(BF)
    gv[rows, cols] = av.astype(BF)


def mean_of(t):
    return jnp.mean(t, axis=-1, keepdims=True)


def attention_end(x, context, ga, vec, normed, factor):
    width = x.shape[1]

    def tile(s, carry):
        rows = seq_rows(s)
        attended = dot_nn(context[rows], square_of(ga[1, 2:4])) + vec[2:3]
        resid = x[rows].astype(F32) + attended
        center = resid - mean_of(resid)
        scale = lax.rsqrt(mean_of(center * center) + norm_floor)
        normed[rows] = center * scale
        factor[rows] = scale
        return carry

    lax.fori_loop(0, x.shape[0] // LEN, tile, 0)


def vec_part(vec, n):
    return vec[n:n + 1]


def input_gradient(x, cot, ga, grad_resid, keep, routes, gq, gk, gv, in_grad):
    def tile(s, carry):
        rows = tile_rows(s, LEN // 2)
        total = grad_resid[rows] + dot_nt(gq[rows], square_of(ga[0, 0:2]))
        total += dot_nt(gk[rows], square_of(ga[0, 2:4]))
        total += dot_nt(gv[rows], square_of(ga[1, 0:2]))
        in_grad[rows] = jnp.where(served_flag(keep, routes, s // 2) > 0, total.astype(BF), cot[rows])
        return carry

    lax.fori_loop(0, 2 * x.shape[0] // LEN, tile, 0)


def gather_attention_kernel(aw, fw, vw, x, lens, gf, ga_out, vec, q_out, k_out, v_out, context_out, log_total, normed_out, factor,
                            active_out, slope_out,
                            ga, gv, strip, pair, own, q, k, v, context, normed, low, w1, active, slope, store, wload, *sems):
    p = place()
    peers = near(p)
    greet(peers)
    share = vw.shape[0]
    own[...] = jnp.zeros_like(own)
    own[0:1, 0:share] = vw[...].astype(BF).astype(F32).reshape(1, share)
    for b in range(8):
        strip[:, b * BLOCK:(b + 1) * BLOCK] = aw[b].astype(BF)
    for j in range(2):
        for b in range(8):
            pair[j, :, b * BLOCK:(b + 1) * BLOCK] = fw[8 * j + b].astype(BF)
    half = BLOCK // 2
    seqs = x.shape[0] // LEN
    dx, dy = square_links(p)
    both = (p["na"], p["nb"], 8 - p["d"], 7 + p["d"])

    def attn_part(h):
        rows = pl.ds(h * half, half)
        return both + (strip.at[rows], lambda d, z, c: ga.at[d, z, c, rows], lambda d, c: ga.at[d, :, c, rows])

    def feed_part(j):
        links = (dy, dx, 8, 7) if j == 0 else (dx, dy, 7, 8)
        return links + (pair.at[j], lambda d, z, c: gf.at[d, z, c, j], lambda d, c: gf.at[d, :, c, j])

    vec_piece = both + (own, lambda d, z, c: gv.at[d, z, c], lambda d, c: gv.at[d, :, c])
    parts = [attn_part(0), vec_piece, attn_part(1), feed_part(0), feed_part(1)]
    a0, w, a1, f0, f1 = every = [Spread(p, *part, *sems[3 * n:3 * n + 3]) for n, part in enumerate(parts)]
    meet(peers)
    for s in (a0, w, a1):
        s.start()
    on_core(p, 0, f0.start, f1.start)
    a0.second()
    w.second()
    a1.second()
    for s in (a0, w, a1):
        s.third()
        s.fourth()
    on_core(p, 0, f0.second, f1.second)
    on_core(p, 1, f0.start, f1.start)
    for s in (a0, w, a1):
        s.fifth()
    w.sixth()
    unfold_vec(gv, vec, share)
    a0.sixth()
    a1.sixth()
    stores = [pltpu.make_async_copy(src, dst, store.at[n])
              for n, (src, dst) in enumerate(((q, q_out), (k, k_out), (v, v_out), (context, context_out), (normed, normed_out),
                                              (ga, ga_out)))]
    stores[5].start()
    projections(x, ga, vec, q, k, v)
    for copy in stores[:3]:
        copy.start()

    def step(n, carry):
        attend(n, q, k, v, lens, context, log_total)
        at_step(n, 3, lambda: on_core(p, 0, f0.third, f1.third, f0.fourth, f1.fourth))
        at_step(n, 4, lambda: on_core(p, 1, f0.second, f1.second))
        at_step(n, 9, lambda: on_core(p, 0, f0.fifth, f1.fifth))
        return carry

    lax.fori_loop(0, 12, step, 0)
    stores[3].start()
    attention_end(x, context, ga, vec, normed, factor)
    stores[4].start()
    on_core(p, 1, f0.sixth, f1.sixth)

    def fetch(t, carry):
        n, s = t // 8, t % 8
        pltpu.make_async_copy(gf.at[0, s // 2, 2 * (s % 2) + n // 2, n % 2], w1.at[n // 2, 2 * (n % 2) + s // 4, s % 4],
                              wload.at[n]).start()
        return carry

    lax.fori_loop(0, 32, fetch, 0)

    def lower(s, carry):
        rows = seq_rows(s)
        low[rows] = (normed[rows] * vec_part(vec, 8) + vec_part(vec, 9)).astype(BF)
        return carry

    lax.fori_loop(0, seqs, lower, 0)

    def enter(n, carry):
        pltpu.make_async_copy(quarter(w1, n), quarter(w1, n), wload.at[n]).wait()

        def tile(s, inner):
            rows = seq_rows(s)
            before = dot_nn(low[rows], square_of(quarter(w1, n)[...])) + vec[pl.ds(3 + n, 1)]
            cumulative = 0.5 * (1.0 + lax.erf(before * (1.0 / math.sqrt(2.0))))
            active[n, rows] = (before * cumulative).astype(BF)
            density = jnp.exp(-0.5 * before * before) * (1.0 / math.sqrt(2.0 * math.pi))
            slope[n, rows] = (cumulative + before * density).astype(BF)
            return inner

        lax.fori_loop(0, seqs, tile, 0)
        pltpu.make_async_copy(active.at[n], active_out.at[n], store.at[6 + n]).start()
        pltpu.make_async_copy(slope.at[n], slope_out.at[n], store.at[10 + n]).start()
        at_step(n, 1, lambda: on_core(p, 1, f0.third, f1.third, f0.fourth, f1.fourth))
        return carry

    lax.fori_loop(0, 4, enter, 0)
    on_core(p, 1, f0.fifth, f1.fifth)
    on_core(p, 0, f0.sixth, f1.sixth)
    for s in every:
        s.drain()
    for copy in stores:
        copy.wait()
    for n in range(4):
        pltpu.make_async_copy(active.at[n], active_out.at[n], store.at[6 + n]).wait()
        pltpu.make_async_copy(slope.at[n], slope_out.at[n], store.at[10 + n]).wait()


def gather_attention(aw, fw, vw, x, lens):
    tokens, width = x.shape
    low = jax.ShapeDtypeStruct(x.shape, BF)
    four = jax.ShapeDtypeStruct((4, tokens, width), BF)
    outs = [jax.ShapeDtypeStruct((2, 4, 4, 2, BLOCK, width), BF), jax.ShapeDtypeStruct((2, 4, 4, BLOCK, width), BF),
            jax.ShapeDtypeStruct((ROWS, width), F32)] + [low] * 4
    outs += [jax.ShapeDtypeStruct((12, 2, LEN), F32), jax.ShapeDtypeStruct(x.shape, F32),
             jax.ShapeDtypeStruct((tokens, 1), F32), four, four]
    vmem = pl.BlockSpec(memory_space=pltpu.VMEM)
    hbm = pl.BlockSpec(memory_space=pl.ANY)
    strips = pltpu.VMEM((2, 4, 4, BLOCK, width), BF)
    rows = pltpu.VMEM(x.shape, BF)
    wide = pltpu.VMEM((4, tokens, width), BF)
    return pl.pallas_call(
        gather_attention_kernel,
        out_shape=outs,
        in_specs=[vmem] * 4 + [pl.BlockSpec(memory_space=pltpu.SMEM)],
        out_specs=[hbm, hbm, vmem] + [hbm] * 4 + [vmem, hbm, vmem, hbm, hbm],
        scratch_shapes=[strips, pltpu.VMEM((2, 4, 4, 8, 384), F32), pltpu.VMEM((BLOCK, width), BF),
                        pltpu.VMEM((2, BLOCK, width), BF), pltpu.VMEM((8, 384), F32)]
        + [rows] * 4 + [pltpu.VMEM(x.shape, F32), rows, strips, wide, wide,
                        pltpu.SemaphoreType.DMA((14,)), pltpu.SemaphoreType.DMA((4,))]
        + spread_sems() * 5,
        compiler_params=pltpu.CompilerParams(collective_id=0, has_side_effects=True, vmem_limit_bytes=62 << 20),
        name="gather_attention",
    )(aw, fw, vw, x, lens)


def fold_scratch(width):
    shape = (BLOCK, width)
    return [pltpu.VMEM((4, 4) + shape, BF), pltpu.VMEM((4,) + shape, BF), pltpu.VMEM((4,) + shape, BF),
            pltpu.VMEM((4,) + shape, BF), pltpu.VMEM((3,) + shape, BF),
            pltpu.SemaphoreType.DMA((10,)), pltpu.SemaphoreType.DMA((10,))]


class Total(Mail):
    def __init__(self, p, held, came, send, recv):
        Mail.__init__(self, p, send, recv)
        self.held, self.came = held, came
        self.peers = ((1 - p["d"], p["i"]), (p["d"], p["na"]), (p["d"], p["nb"]))

    def start(self):
        self.go(self.held.at[0], self.came.at[0], 0, self.peers[0])

    def hop(self, n):
        p = self.p
        self.wait(self.came.at[n], n)
        self.held[n + 1] = self.held[n] + self.came[n]
        if n < 2:
            self.go(self.held.at[n + 1], self.came.at[n + 1], n + 1, self.peers[n + 1])
        else:
            for k in (1, 2, 3):
                self.go(self.held.at[3], self.came.at[2 + k], 2 + k, (p["d"], ((p["z"] + k) % 4) * 4 + p["c"]))

    def end(self):
        total = self.held[3]
        for k in (1, 2, 3):
            self.wait(self.came.at[2 + k], 2 + k)
            total += self.came[2 + k]
        return total


def own_share(p, rows, out, share):
    per = share // BLOCK
    me = p["d"] * 16 + p["i"]
    units = sum(
        jnp.dot(one_hot((8, ROWS), lambda a: per * me + jnp.where(a < per, a, -8 * 32 * per), lambda r, b=b: 8 * r + b),
                rows[:, b * BLOCK:(b + 1) * BLOCK], precision=lax.Precision.HIGHEST, preferred_element_type=F32)
        for b in range(8)
    )
    for a in range(per):
        out[0:1, a * BLOCK:(a + 1) * BLOCK] = units[a:a + 1]


def everyone(p):
    me = p["d"] * 16 + p["i"]

    def other(k):
        t = (me + k) % 32
        return (t // 16, t % 16)

    return me, other


def greet_all(p):
    me, other = everyone(p)
    barrier = pltpu.get_barrier_semaphore()

    def one(k, carry):
        pl.semaphore_signal(barrier, inc=1, device_id=other(k), device_id_type=MESH)
        return carry

    lax.fori_loop(1, 32, one, 0)


def meet_all():
    pl.semaphore_wait(pltpu.get_barrier_semaphore(), 31)


def norm_sum(p, square, slots, send, recv):
    me, other = everyone(p)
    slots[me] = jnp.full((8, 128), square, F32)
    to = lambda k, slot: remote(slots.at[slot], slots.at[slot], send, recv, slot, other(k))

    def push(k, carry):
        remote(slots.at[me], slots.at[me], send.at[pl.ds(k, 1)], recv.at[pl.ds(me, 1)], 0, other(k)).start()
        return carry

    def take(k, carry):
        slot = (me + k) % 32
        remote(slots.at[slot], slots.at[slot], send.at[pl.ds(k, 1)], recv.at[pl.ds(slot, 1)], 0, other(k)).wait_recv()
        return carry

    def done(k, carry):
        remote(slots.at[me], slots.at[me], send.at[pl.ds(k, 1)], recv.at[pl.ds(me, 1)], 0, other(k)).wait_send()
        return carry

    lax.fori_loop(1, 32, push, 0)
    lax.fori_loop(1, 32, take, 0)
    total = jnp.sum(slots[...], axis=0)[0:1, 0:1]
    lax.fori_loop(1, 32, done, 0)
    return total


class Fold:
    def __init__(self, p, a, b, away, home, pair, diag, flat, late, line, send, recv):
        self.p, self.home, self.pair, self.diag, self.flat, self.late, self.line = p, home, pair, diag, flat, late, line
        self.ca, self.cb = a % 4, b % 4
        d, z, c = p["d"], p["z"], p["c"]
        self.away, self.send, self.recv, self.core = away, send, recv, (1 - d, p["i"])
        pieces = [(pair.at[:, p["cd"]], diag, (d, b)), (pair.at[:, self.cb], flat, (d, b)),
                  (pair.at[:, self.ca], late, (d, a))]
        pieces += [(pair.at[(z + k) % 4, c], line.at[k - 1], (d, ((z + k) % 4) * 4 + c)) for k in (1, 2, 3)]
        self.copies = [None] + [remote(src, dst, send, recv, n, dev) for n, (src, dst, dev) in enumerate(pieces)]

    def part(self, z):
        return pltpu.make_async_remote_copy(
            src_ref=self.away.at[z], dst_ref=self.pair.at[z], send_sem=self.send.at[6 + z], recv_sem=self.recv.at[6 + z],
            device_id=self.core, device_id_type=MESH)

    def add(self, dst, *others):
        total = dst[...].astype(F32)
        for o in others:
            total += o[...].astype(F32)
        dst[...] = total.astype(dst.dtype)

    def column_part(self, c):
        return pltpu.make_async_remote_copy(
            src_ref=self.away.at[:, c], dst_ref=self.pair.at[:, c], send_sem=self.send.at[6 + c], recv_sem=self.recv.at[6 + c],
            device_id=self.core, device_id_type=MESH)

    def start(self):
        for z in range(4):
            self.part(z).start()

    def second(self):
        for z in range(4):
            self.part(z).wait_recv()
        for col, n in ((self.p["cd"], 1), (self.cb, 2)):
            self.add(self.pair.at[:, col], self.home.at[:, col])
            self.copies[n].start()
        for col in (self.ca, self.p["c"]):
            self.add(self.pair.at[:, col], self.home.at[:, col])

    def third(self):
        self.copies[1].wait_recv()
        self.add(self.pair.at[:, self.ca], self.diag)
        self.copies[3].start()

    def fourth(self):
        p = self.p
        self.copies[2].wait_recv()
        self.copies[3].wait_recv()
        for k in (2, 1, 3, 0):
            dst = (p["z"] + k) % 4
            self.add(self.pair.at[dst, p["c"]], self.flat.at[dst], self.late.at[dst])
            if k:
                self.copies[3 + k].start()

    def fifth(self, out):
        p = self.p
        total = self.pair[p["z"], p["c"]].astype(F32)
        for k in (1, 2, 3):
            self.copies[3 + k].wait_recv()
            total += self.line[k - 1].astype(F32)
        out[...] = total

    def drain(self):
        for copy in self.copies[1:] + [self.part(z) for z in range(4)]:
            copy.wait_send()


def layer_back_kernel(x_in, cot_in, normed_in, active_in, slope_in, factor, gf, ga, q_in, k_in, v_in, context_in, log_total, vec, lens, keep, routes,
                      out, in_grad, sf, sa, sv, norm,
                      x, cot, normed, middle, low, grad_low, image, w1, w2, active, slope, hf, gvec, held, came, slots,
                      load, wload, nsend, nrecv, tsend, trecv, *scratch):
    p = place()
    greet_all(p)
    tokens, width = x.shape
    seqs = tokens // LEN
    half = width // 2
    lanes = (pl.ds(0, half), pl.ds(half, half))

    def bring(src, dst, n):
        return pltpu.make_async_copy(src, dst, load.at[n])

    quarters = [bring(active_in.at[q], active.at[q], q) for q in range(4)]
    others = [bring(normed_in, normed, 4), bring(x_in, x, 5), bring(cot_in, cot, 6)]
    slopes = bring(slope_in, slope, 7)

    def fetch_down(t, carry):
        q, s = t // 8, t % 8
        pltpu.make_async_copy(gf.at[1, q, s // 2, s % 2], w2.at[q // 2, 2 * (q % 2) + s // 4, s % 4], wload.at[q]).start()
        return carry

    def fetch(t, carry):
        q, s = t // 8, t % 8
        pltpu.make_async_copy(gf.at[0, s // 2, 2 * (s % 2) + q // 2, q % 2], w1.at[q // 2, 2 * (q % 2) + s // 4, s % 4],
                              wload.at[4]).start()
        return carry

    for q in range(4):
        quarters[q].start()
        lax.fori_loop(8 * q, 8 * q + 8, fetch_down, 0)
    for copy in others:
        copy.start()
    slopes.start()
    lax.fori_loop(0, 32, fetch, 0)
    dx, dy = square_links(p)
    f0 = Fold(p, dy, dx, hf.at[1 - p["d"], :, :, 0], hf.at[p["d"], :, :, 0], *scratch[0:7])
    f1 = Fold(p, dx, dy, hf.at[1 - p["d"], :, :, 1], hf.at[p["d"], :, :, 1], *scratch[7:14])
    ha, ga_in = w1, w2
    a0, a1 = [Fold(p, p["na"], p["nb"], ha.at[1 - p["d"], :, :, :, lanes[n]], ha.at[p["d"], :, :, :, lanes[n]],
                   *scratch[14 + 7 * n:21 + 7 * n]) for n in range(2)]
    total = Total(p, held, came, tsend, trecv)

    def on(core, *steps):
        on_core(p, core, *steps)

    gvec[...] = jnp.zeros_like(gvec)

    def add_vec(n, value):
        gvec[n:n + 1] += value

    for q in range(4):
        quarters[q].wait()
        pltpu.make_async_copy(quarter(w2, q), quarter(w2, q), wload.at[q]).wait()

        def gain(s, carry):
            rows = seq_rows(s)
            found = dot_nn(active[q, rows], square_of(quarter(w2, q)[...]))
            middle[rows] = found if q == 0 else middle[rows] + found
            return carry

        lax.fori_loop(0, seqs, gain, 0)
    for copy in others:
        copy.wait()
    tile = LEN // 2

    def leave(t, carry):
        rows = tile_rows(t, tile)
        show = pltpu.make_async_copy(image, out.at[rows], load.at[14])
        hidden = normed[rows] * vec_part(vec, 8) + vec_part(vec, 9)
        low[rows] = hidden.astype(BF)
        resid = hidden + (middle[rows] + vec_part(vec, 7))
        center = resid - mean_of(resid)
        scale = lax.rsqrt(mean_of(center * center) + norm_floor)
        second = center * scale
        served = served_flag(keep, routes, t // 2) > 0
        result = second * vec_part(vec, 10) + vec_part(vec, 11)
        image[...] = jnp.where(served, result.astype(BF), x[rows])
        show.start()
        grad = jnp.where(served, cot[rows].astype(F32), 0.0)
        add_vec(10, jnp.sum(grad * second, axis=0, keepdims=True))
        add_vec(11, jnp.sum(grad, axis=0, keepdims=True))
        grad = grad * vec_part(vec, 10)
        grad = scale * (grad - mean_of(grad) - second * mean_of(grad * second))
        middle[rows] = grad
        grad_low[rows] = grad.astype(BF)
        add_vec(7, jnp.sum(grad.astype(BF).astype(F32), axis=0, keepdims=True))
        show.wait()
        return carry

    lax.fori_loop(0, 2 * seqs, leave, 0)
    meet_all()

    def down_grad(t, carry):
        q, h = t // 2, t % 2
        found = dot_tn(active[q, :, pl.ds(pl.multiple_of(h * half, half), half)], grad_low[...])
        hf[1, q, pl.ds(2 * h, 2)] = found.astype(BF).reshape(2, 2, BLOCK, width)
        at_step(h, 1, lambda: on(0, lambda: f0.part(q).start(), lambda: f1.part(q).start()))
        return carry

    lax.fori_loop(0, 8, down_grad, 0)
    again = [bring(src, slope.at[n], 8 + n) for n, src in enumerate((context_in, q_in, k_in, v_in))]
    context, qs, ks, vs = (slope.at[n] for n in range(4))
    slopes.wait()

    def turn(q, carry):
        def part(s, inner):
            rows = seq_rows(s)
            back = dot_nt(grad_low[rows], square_of(quarter(w2, q)[...])) * slope[q, rows].astype(F32)
            active[q, rows] = back.astype(BF)
            gvec[pl.ds(3 + q, 1)] += jnp.sum(back.astype(BF).astype(F32), axis=0, keepdims=True)
            return inner

        def up_grad(h, inner):
            found = dot_tn(low[:, pl.ds(pl.multiple_of(h * half, half), half)], active[q]).astype(BF).reshape(2, 2, BLOCK, width)
            for y in range(2):
                hf[0, pl.ds(2 * h, 2), 2 * y + q // 2, q % 2] = found[:, y]
            return inner

        lax.fori_loop(0, seqs, part, 0)
        lax.fori_loop(0, 2, up_grad, 0)
        at_step(q, 0, lambda: on(1, f0.second, f1.second))
        for j, f in enumerate((f0, f1)):
            at_step(q % 2, j, lambda f=f: on(1, lambda: f.column_part(q // 2).start(), lambda: f.column_part(2 + q // 2).start()))
        at_step(q, 2, lambda: on(1, f0.third))
        at_step(q, 3, lambda: on(1, f1.third))
        return carry

    lax.fori_loop(0, 4, turn, 0)
    for copy in again:
        copy.start()
    pltpu.make_async_copy(w1, w1, wload.at[4]).wait()
    square_in = bring(ga, ga_in, 12)
    square_in.start()

    def close(t, carry):
        rows = tile_rows(t, tile)
        grad = middle[rows]
        for q in range(4):
            grad += dot_nt(active[q, rows], square_of(quarter(w1, q)[...]))
        head = normed[rows]
        add_vec(8, jnp.sum(grad * head, axis=0, keepdims=True))
        add_vec(9, jnp.sum(grad, axis=0, keepdims=True))
        grad = grad * vec_part(vec, 8)
        grad = factor[rows] * (grad - mean_of(grad) - head * mean_of(grad * head))
        middle[rows] = grad
        grad_low[rows] = grad.astype(BF)
        return carry

    lax.fori_loop(0, seqs, close, 0)
    on(0, f0.second)
    lax.fori_loop(seqs, 2 * seqs, close, 0)
    on(1, f0.fourth)
    on(0, f1.second)
    gq, gk, gv, grad_context = (active.at[n] for n in range(4))
    square_in.wait()
    again[0].wait()

    def open_attention(s, carry):
        rows = seq_rows(s)
        grad_context[rows] = dot_nt(grad_low[rows], square_of(ga_in[1, 2:4])).astype(BF)
        return carry

    lax.fori_loop(0, seqs, open_attention, 0)
    held[0] = gvec[...]
    held[0, 2:3] = jnp.sum(grad_low[...].astype(F32), axis=0, keepdims=True)
    for h in range(2):
        ha[1, 2 + h] = dot_tn(context[:, h * half:(h + 1) * half], grad_low[...]).astype(BF).reshape(4, BLOCK, width)
    on(1, f1.fourth)
    for copy in again[1:]:
        copy.wait()

    def step(m, carry):
        n = ((m % 6) // 3) * 6 + (m // 6) * 3 + m % 3
        attend_back(n, qs, ks, vs, grad_context, log_total, lens, gq, gk, gv)
        at_step(m, 0, lambda: on(0, f0.third))
        at_step(m, 1, lambda: on(0, f1.third))
        at_step(m, 5, lambda: weight_grads(0), a0.start, lambda: on(0, f0.fourth))
        at_step(m, 6, lambda: on(0, f1.fourth))
        at_step(m, 7, a0.second)
        at_step(m, 10, a0.third)
        at_step(m, 11, lambda: weight_grads(1))
        return carry

    def weight_grads(n):
        cols = lanes[n]
        for dst, src in ((ha.at[0, 0:2], gq), (ha.at[0, 2:4], gk), (ha.at[1, 0:2], gv)):
            dst[:, :, :, cols] = dot_tn(x[...], src[:, cols]).astype(BF).reshape(2, 4, BLOCK, half)

    lax.fori_loop(0, 12, step, 0)
    a1.start()
    held[0, 0:1] = jnp.sum(gq[...].astype(F32), axis=0, keepdims=True)
    held[0, 1:2] = jnp.sum(gv[...].astype(F32), axis=0, keepdims=True)
    total.start()
    a1.second()
    a0.fourth()
    total.hop(0)
    input_gradient(x, cot, ga_in, middle, keep, routes, gq, gk, gv, cot)
    last = bring(cot, in_grad, 13)
    last.start()
    a1.third()
    total.hop(1)
    total.hop(2)
    f0.fifth(sf.at[0])
    f1.fifth(sf.at[1])
    square = jnp.sum(sf[...] * sf[...])
    a1.fourth()
    held[4] = total.end()
    sv[...] = jnp.zeros_like(sv)
    own_share(p, held[4], sv, 12 * width // 32)
    a0.fifth(sa.at[:, lanes[0]])
    a1.fifth(sa.at[:, lanes[1]])
    square += jnp.sum(sa[...] * sa[...]) + jnp.sum(sv[...] * sv[...])
    found = norm_sum(p, square, slots, nsend, nrecv)
    norm[...] = jnp.sqrt(found)
    for s in (f0, f1, a0, a1, total):
        s.drain()
    last.wait()


def layer_back(x, cot, normed, active, slope, factor, gf, ga, q, k, v, context, log_total, vec, lens, keep, routes):
    tokens, width = x.shape
    outs = [jax.ShapeDtypeStruct(x.shape, BF), jax.ShapeDtypeStruct(x.shape, BF), jax.ShapeDtypeStruct((2, BLOCK, width), F32),
            jax.ShapeDtypeStruct((BLOCK, width), F32), jax.ShapeDtypeStruct((8, 384), F32), jax.ShapeDtypeStruct((1, 1), F32)]
    dma = pltpu.SemaphoreType.DMA
    rows = pltpu.VMEM(x.shape, BF)
    wide = pltpu.VMEM(x.shape, F32)
    strips = pltpu.VMEM(ga.shape, BF)
    scratch = [rows, rows, wide, wide, rows, rows, pltpu.VMEM((LEN // 2, width), BF), strips, strips,
               pltpu.VMEM((4, tokens, width), BF), pltpu.VMEM((4, tokens, width), BF), pltpu.VMEM(gf.shape, BF),
               pltpu.VMEM(vec.shape, F32), pltpu.VMEM((5, ROWS, width), F32), pltpu.VMEM((6, ROWS, width), F32),
               pltpu.VMEM((32, 8, 128), F32),
               dma((15,)), dma((5,)), dma((32,)), dma((32,)), dma((6,)), dma((6,))]
    scratch += fold_scratch(width) * 2 + fold_scratch(width // 2) * 2
    vmem = pl.BlockSpec(memory_space=pltpu.VMEM)
    smem = pl.BlockSpec(memory_space=pltpu.SMEM)
    hbm = pl.BlockSpec(memory_space=pl.ANY)
    return pl.pallas_call(
        layer_back_kernel,
        out_shape=outs,
        in_specs=[hbm] * 5 + [vmem] + [hbm] * 6 + [vmem] * 2 + [smem] * 3,
        out_specs=[hbm] * 2 + [vmem] * 4,
        scratch_shapes=scratch,
        compiler_params=pltpu.CompilerParams(collective_id=1, has_side_effects=True, vmem_limit_bytes=67043328),
        name="feed_and_back",
    )(x, cot, normed, active, slope, factor, gf, ga, q, k, v, context, log_total, vec, lens, keep, routes)


def halves_of(t):
    high = t.astype(BF)
    return high, (t - high.astype(F32)).astype(BF)


def exact_dot(a, b, dims):
    dot = lambda x, y: lax.dot_general(x, y, (dims, ((), ())), preferred_element_type=F32)
    return dot(a[0], b[0]) + (dot(a[0], b[1]) + dot(a[1], b[0]))


def shampoo_block(grad, w, st, ro, mo, st_new, mo_new, w_new, b, factor):
    clipped = grad * factor
    moment = momentum_decay * mo[b] + clipped
    both = halves_of(clipped)
    left = exact_dot(both, both, ((1,), (1,)))
    right = exact_dot(both, both, ((0,), (0,)))
    st_new[b, 0] = stat_decay * st[b, 0] + (1.0 - stat_decay) * left
    st_new[b, 1] = stat_decay * st[b, 1] + (1.0 - stat_decay) * right
    mo_new[b] = moment
    turned = exact_dot(halves_of(ro[b, 0]), halves_of(moment), ((1,), (0,)))
    turned = exact_dot(halves_of(turned), halves_of(ro[b, 1]), ((1,), (0,)))
    w_new[b] = w[b] - matrix_rate * (turned + matrix_decay * w[b])


def optimizer_kernel(norm, sa, sf, sv, aw, ast, ar, am, fw, fst, fr, fm, vw, v1, v2, rows, grads,
                     rows_n, grads_n, ast_n, am_n, aw_n, fst_n, fm_n, fw_n, v1_n, v2_n, vw_n, ga, gf):
    factor = clip_bound / jnp.maximum(norm[...], clip_bound)
    g = pl.program_id(0)
    many = aw.shape[0]
    rows_n[...] = rows[...]
    grads_n[...] = grads[...]

    @pl.when(g == 0)
    def _():
        for b in range(8):
            ga[b] = sa[:, b * BLOCK:(b + 1) * BLOCK]
            for j in range(2):
                gf[8 * j + b] = sf[j, :, b * BLOCK:(b + 1) * BLOCK]
        size = vw.shape[0]
        clipped = (sv[0:1, 0:size] * factor)[0]
        first_new = first_decay * v1[...] + (1.0 - first_decay) * clipped
        second_new = second_decay * v2[...] + (1.0 - second_decay) * clipped * clipped
        first_hat = first_new / (1.0 - first_decay**STEP)
        second_hat = second_new / (1.0 - second_decay**STEP)
        v1_n[...] = first_new
        v2_n[...] = second_new
        vw_n[...] = vw[...] - vector_rate * first_hat / (jnp.sqrt(second_hat) + adam_floor)

    for b in range(many):
        shampoo_block(ga[g * many + b], aw, ast, ar, am, ast_n, am_n, aw_n, b, factor)
    for b in range(2 * many):
        shampoo_block(gf[g * 2 * many + b], fw, fst, fr, fm, fst_n, fm_n, fw_n, b, factor)


def optimizer(norm, sa, sf, sv, aw, ast, ar, am, fw, fst, fr, fm, vw, v1, v2, rows, grads):
    many = 2

    def steps(t, n):
        shape = (n,) + t.shape[1:]
        return pl.BlockSpec(shape, lambda g: (g,) + (0,) * (len(shape) - 1))

    def whole(t):
        return pl.BlockSpec(t.shape, lambda g: (0,) * t.ndim)

    like = lambda t: jax.ShapeDtypeStruct(t.shape, t.dtype)
    args = (norm, sa, sf, sv, aw, ast, ar, am, fw, fst, fr, fm, vw, v1, v2, rows, grads)
    part = rows.shape[0] * many // aw.shape[0]
    specs = [whole(t) for t in args[:4]]
    specs += [steps(t, many) for t in (aw, ast, ar, am)] + [steps(t, 2 * many) for t in (fw, fst, fr, fm)]
    specs += [whole(t) for t in (vw, v1, v2)] + [steps(t, part) for t in (rows, grads)]
    outs = (rows, grads, ast, am, aw, fst, fm, fw, v1, v2, vw)
    return pl.pallas_call(
        optimizer_kernel,
        out_shape=[like(t) for t in outs],
        grid=(aw.shape[0] // many,),
        in_specs=specs,
        out_specs=[steps(t, part) for t in outs[:2]] + [steps(t, many) for t in outs[2:5]] + [steps(t, 2 * many) for t in outs[5:8]]
        + [whole(t) for t in outs[8:]],
        scratch_shapes=[pltpu.VMEM(aw.shape, F32), pltpu.VMEM(fw.shape, F32)],
        name="optimizer",
    )(*args)


def per_device(
    inputs,
    output_gradient,
    keep,
    lengths,
    routes,
    attn_weights,
    attn_stats,
    attn_roots,
    attn_momentum,
    ffn_weights,
    ffn_stats,
    ffn_roots,
    ffn_momentum,
    vec_weights,
    vec_first,
    vec_second,
):
    slots, seq_len, width = inputs.shape
    tokens = slots * seq_len
    x = inputs.reshape(tokens, width)
    cot = output_gradient.reshape(tokens, width)
    gf, ga, vec, q, k, v, context, log_total, normed, factor, active, slope = gather_attention(attn_weights, ffn_weights, vec_weights, x, lengths)
    out, in_grad, sf, sa, sv, norm = layer_back(
        x, cot, normed, active, slope, factor, gf, ga, q, k, v, context, log_total, vec, lengths, keep, routes
    )
    out, in_grad, *rest = optimizer(
        norm, sa, sf, sv,
        attn_weights, attn_stats, attn_roots, attn_momentum,
        ffn_weights, ffn_stats, ffn_roots, ffn_momentum,
        vec_weights, vec_first, vec_second, out, in_grad,
    )
    return (out.reshape(inputs.shape), in_grad.reshape(inputs.shape), norm.reshape(()), *rest)


def solution(mesh):
    small = mesh.shape["depth"] == 2 and mesh.shape["dp"] == 16
    return jax.shard_map(
        per_device if small else per_device_general,
        mesh=mesh,
        in_specs=(
            P(("depth", "dp"), None, None),
            P(("depth", "dp"), None, None),
            P(("depth", "dp")),
            P(("depth", "dp")),
            P(("depth", "dp")),
            P(("depth", "dp"), None, None),
            P(("depth", "dp"), None, None, None),
            P(("depth", "dp"), None, None, None),
            P(("depth", "dp"), None, None),
            P(("depth", "dp"), None, None),
            P(("depth", "dp"), None, None, None),
            P(("depth", "dp"), None, None, None),
            P(("depth", "dp"), None, None),
            P(("depth", "dp")),
            P(("depth", "dp")),
            P(("depth", "dp")),
        ),
        out_specs=(
            P(("depth", "dp"), None, None),
            P(("depth", "dp"), None, None),
            P(),
            P(("depth", "dp"), None, None, None),
            P(("depth", "dp"), None, None),
            P(("depth", "dp"), None, None),
            P(("depth", "dp"), None, None, None),
            P(("depth", "dp"), None, None),
            P(("depth", "dp"), None, None),
            P(("depth", "dp")),
            P(("depth", "dp")),
            P(("depth", "dp")),
        ),
        check_vma=False,
    )
```

```python
import functools
import math

import jax
import jax.numpy as jnp
from jax import lax
from jax.experimental import pallas as pl
from jax.experimental.pallas import tpu as pltpu
from jax.sharding import PartitionSpec as P

HEADS = 12
FF = 3072
BLOCK = 96
STEP = 10


norm_floor = 1e-05
masked_fill = -1000000000.0
momentum_decay = 0.9
stat_decay = 0.95
matrix_rate = 1.0
matrix_decay = 0.01
clip_bound = 1.0
first_decay = 0.9
second_decay = 0.999
vector_rate = 0.5
adam_floor = 1e-08


def serve_flags(keep_rows, route_rows):
    count = keep_rows.shape[-1]
    order = jnp.arange(count, dtype=jnp.int32)
    earlier = (order[None, :] < order[:, None]).astype(jnp.int32)
    same = (route_rows[:, :, None] == route_rows[:, None, :]).astype(jnp.int32)
    clash = jnp.sum(same * earlier[None, :, :] * keep_rows[:, None, :], axis=2)
    return keep_rows * (clash == 0).astype(jnp.int32)


def to_matrix(blocks, height, breadth):
    shaped = blocks.reshape(height // BLOCK, breadth // BLOCK, BLOCK, BLOCK)
    return shaped.transpose(0, 2, 1, 3).reshape(height, breadth)


def to_flat_blocks(matrix):
    height, breadth = matrix.shape
    shaped = matrix.reshape(height // BLOCK, BLOCK, breadth // BLOCK, BLOCK)
    return shaped.transpose(0, 2, 1, 3).reshape(-1, BLOCK * BLOCK)


def norm_parts(resid):
    center = resid - jnp.mean(resid, axis=-1, keepdims=True)
    factor = lax.rsqrt(jnp.mean(center * center, axis=-1, keepdims=True) + norm_floor)
    return (center * factor, factor)


def norm_back(grad_normed, normed, factor):
    middle = jnp.mean(grad_normed, axis=-1, keepdims=True)
    along = jnp.mean(grad_normed * normed, axis=-1, keepdims=True)
    return factor * (grad_normed - middle - normed * along)


def gelu_slope(value):
    cumulative = 0.5 * (1.0 + lax.erf(value * (1.0 / math.sqrt(2.0))))
    density = jnp.exp(-0.5 * value * value) * (1.0 / math.sqrt(2.0 * math.pi))
    return cumulative + value * density


def product(left, right):
    return jnp.dot(left, right, preferred_element_type=jnp.float32)


def contract_rows(left, right):
    return lax.dot_general(
        left, right, (((0,), (0,)), ((), ())), preferred_element_type=jnp.float32
    )


def times_transpose(left, right):
    return lax.dot_general(
        left, right, (((1,), (1,)), ((), ())), preferred_element_type=jnp.float32
    )


def masked_scores(query, keys, visible_len):
    scale = 1.0 / math.sqrt(query.shape[-1])
    scores = jnp.einsum("qhe,khe->hqk", query, keys, preferred_element_type=jnp.float32) * scale
    visible = jnp.arange(keys.shape[0], dtype=jnp.int32) < visible_len
    return jnp.where(visible[None, None, :], scores, masked_fill)


def attend_forward(pieces):
    query, keys, values, visible_len = pieces
    scores = masked_scores(query, keys, visible_len)
    peak = jnp.max(scores, axis=-1, keepdims=True)
    expo = jnp.exp(scores - peak)
    total = jnp.sum(expo, axis=-1, keepdims=True)
    probs_low = (expo / total).astype(jnp.bfloat16)
    context = jnp.einsum("hqk,khe->qhe", probs_low, values, preferred_element_type=jnp.float32)
    return (context, peak[..., 0] + jnp.log(total[..., 0]))


def attend_backward(pieces):
    query, keys, values, grad_ctx, log_total, visible_len = pieces
    scale = 1.0 / math.sqrt(query.shape[-1])
    scores = masked_scores(query, keys, visible_len)
    probs = jnp.exp(scores - log_total[..., None])
    probs_low = probs.astype(jnp.bfloat16)
    grad_probs = jnp.einsum("qhe,khe->hqk", grad_ctx, values, preferred_element_type=jnp.float32)
    grad_values = jnp.einsum(
        "hqk,qhe->khe", probs_low, grad_ctx, preferred_element_type=jnp.float32
    )
    along = jnp.sum(probs * grad_probs, axis=-1, keepdims=True)
    grad_scores = (probs * (grad_probs - along)).astype(jnp.bfloat16)
    grad_query = (
        jnp.einsum("hqk,khe->qhe", grad_scores, keys, preferred_element_type=jnp.float32) * scale
    )
    grad_keys = (
        jnp.einsum("hqk,qhe->khe", grad_scores, query, preferred_element_type=jnp.float32) * scale
    )
    return (grad_query, grad_keys, grad_values)


def shampoo(weights, stats, roots, momentum, grads, factor):
    highest = lax.Precision.HIGHEST
    clipped = grads * factor
    moment = momentum_decay * momentum + clipped
    left = jnp.einsum("nab,ncb->nac", clipped, clipped, precision=highest)
    right = jnp.einsum("nab,nac->nbc", clipped, clipped, precision=highest)
    fresh = stat_decay * stats + (1.0 - stat_decay) * jnp.stack([left, right], axis=1)
    turned = jnp.einsum("nab,nbc->nac", roots[:, 0], moment, precision=highest)
    turned = jnp.einsum("nab,nbc->nac", turned, roots[:, 1], precision=highest)
    updated = weights - matrix_rate * (turned + matrix_decay * weights)
    return (fresh, moment, updated)


def adam_step(weights, first, second, grads, factor):
    clipped = grads * factor
    first_new = first_decay * first + (1.0 - first_decay) * clipped
    second_new = second_decay * second + (1.0 - second_decay) * clipped * clipped
    first_hat = first_new / (1.0 - first_decay**STEP)
    second_hat = second_new / (1.0 - second_decay**STEP)
    updated = weights - vector_rate * first_hat / (jnp.sqrt(second_hat) + adam_floor)
    return (first_new, second_new, updated)


def per_device_general(
    inputs,
    output_gradient,
    keep,
    lengths,
    routes,
    attn_weights,
    attn_stats,
    attn_roots,
    attn_momentum,
    ffn_weights,
    ffn_stats,
    ffn_roots,
    ffn_momentum,
    vec_weights,
    vec_first,
    vec_second,
):
    slots, seq_len, width = inputs.shape
    tokens = slots * seq_len
    head_size = width // HEADS
    hidden_width = FF
    depth_count = lax.axis_size("depth")
    peer_slots = slots // depth_count
    grid = (width // BLOCK) ** 2
    half_ffn = width * hidden_width // (BLOCK * BLOCK)
    area = BLOCK * BLOCK
    low_type = jnp.bfloat16
    attn_flat = attn_weights.reshape(-1, area).astype(low_type)
    ffn_flat = ffn_weights.reshape(-1, area).astype(low_type)
    attn_all, ffn_all, vec_all = (
        lax.all_gather(attn_flat, ("depth", "dp"), axis=0, tiled=True),
        lax.all_gather(ffn_flat, ("depth", "dp"), axis=0, tiled=True),
        lax.all_gather(vec_weights.astype(low_type), ("depth", "dp"), axis=0, tiled=True),
    )
    table_keep, table_len, table_route = (
        lax.all_gather(keep, "depth", axis=0, tiled=True),
        lax.all_gather(lengths, "depth", axis=0, tiled=True),
        lax.all_gather(routes, "depth", axis=0, tiled=True),
    )
    mine = serve_flags(keep[None, :], routes[None, :])[0]
    slot_order = jnp.arange(slots, dtype=jnp.int32)
    selection = ((routes[None, :] == slot_order[:, None]).astype(jnp.int32) * mine[None, :]).astype(
        low_type
    )
    outgoing_rows = jnp.einsum(
        "gz,zrp->grp", selection, inputs, preferred_element_type=jnp.float32
    ).astype(low_type)
    send_grad = jnp.einsum(
        "gz,zrp->grp", selection, output_gradient, preferred_element_type=jnp.float32
    ).astype(low_type)
    come_rows, come_grad = (
        lax.all_to_all(outgoing_rows, "depth", split_axis=0, concat_axis=0, tiled=True),
        lax.all_to_all(send_grad, "depth", split_axis=0, concat_axis=0, tiled=True),
    )
    all_keep = table_keep.reshape(depth_count, slots)
    all_route = table_route.reshape(depth_count, slots)
    all_len = table_len.reshape(depth_count, slots)
    all_served = serve_flags(all_keep, all_route)
    here = lax.axis_index("depth")
    source = slot_order // peer_slots
    target = here * peer_slots + slot_order % peer_slots
    source_hot = (source[:, None] == jnp.arange(depth_count, dtype=jnp.int32)[None, :]).astype(
        jnp.int32
    )
    match = (all_route[None, :, :] == target[:, None, None]).astype(jnp.int32) * all_served[
        None, :, :
    ]
    slot_len = jnp.sum(source_hot[:, :, None] * match * all_len[None, :, :], axis=(1, 2))
    visible_len = jnp.maximum(slot_len, 1)
    query_w = to_matrix(attn_all[0:grid], width, width)
    key_w = to_matrix(attn_all[grid : 2 * grid], width, width)
    value_w = to_matrix(attn_all[2 * grid : 3 * grid], width, width)
    output_w = to_matrix(attn_all[3 * grid : 4 * grid], width, width)
    vectors = vec_all.astype(jnp.float32)
    q_bias = vectors[0:width]
    v_bias = vectors[width : 2 * width]
    out_bias = vectors[2 * width : 3 * width]
    hidden_bias = vectors[3 * width : 3 * width + hidden_width]
    ffn_bias = vectors[3 * width + hidden_width : 4 * width + hidden_width]
    gain_one = vectors[4 * width + hidden_width : 5 * width + hidden_width]
    shift_one = vectors[5 * width + hidden_width : 6 * width + hidden_width]
    gain_two = vectors[6 * width + hidden_width : 7 * width + hidden_width]
    shift_two = vectors[7 * width + hidden_width : 8 * width + hidden_width]
    flat = come_rows.reshape(tokens, width)
    four = (slots, seq_len, HEADS, head_size)
    query = (product(flat, query_w) + q_bias).astype(low_type).reshape(four)
    keys = product(flat, key_w).astype(low_type).reshape(four)
    values = (product(flat, value_w) + v_bias).astype(low_type).reshape(four)
    context, log_total = lax.map(attend_forward, (query, keys, values, visible_len))
    context_low = context.reshape(tokens, width).astype(low_type)
    attended = product(context_low, output_w) + out_bias
    normed_one, factor_one = norm_parts(flat.astype(jnp.float32) + attended)
    hidden_in = normed_one * gain_one + shift_one
    hidden_low = hidden_in.astype(low_type)
    hidden_w = to_matrix(ffn_all[0:half_ffn], width, hidden_width)
    return_weight = to_matrix(ffn_all[half_ffn:], hidden_width, width)
    before = product(hidden_low, hidden_w) + hidden_bias
    active_low = jax.nn.gelu(before, approximate=False).astype(low_type)
    branch = product(active_low, return_weight) + ffn_bias
    normed_two, factor_two = norm_parts(hidden_in + branch)
    result_low = (normed_two * gain_two + shift_two).astype(low_type)
    grad_rows = come_grad.reshape(tokens, width).astype(jnp.float32)
    grad_gain_two = jnp.sum(grad_rows * normed_two, axis=0)
    grad_shift_two = jnp.sum(grad_rows, axis=0)
    grad_resid_two = norm_back(grad_rows * gain_two, normed_two, factor_two)
    grad_branch = grad_resid_two.astype(low_type)
    grad_ffn_bias = jnp.sum(grad_branch.astype(jnp.float32), axis=0)
    gradient_return_weight = contract_rows(active_low, grad_branch)
    grad_active = times_transpose(grad_branch, return_weight)
    grad_before = (grad_active * gelu_slope(before)).astype(low_type)
    grad_hidden_bias = jnp.sum(grad_before.astype(jnp.float32), axis=0)
    grad_hidden_w = contract_rows(hidden_low, grad_before)
    grad_hidden = times_transpose(grad_before, hidden_w) + grad_resid_two
    grad_gain_one = jnp.sum(grad_hidden * normed_one, axis=0)
    grad_shift_one = jnp.sum(grad_hidden, axis=0)
    grad_resid_one = norm_back(grad_hidden * gain_one, normed_one, factor_one)
    ffn_grad = jnp.concatenate(
        [to_flat_blocks(grad_hidden_w), to_flat_blocks(gradient_return_weight)], axis=0
    )
    grad_attended = grad_resid_one.astype(low_type)
    grad_out_bias = jnp.sum(grad_attended.astype(jnp.float32), axis=0)
    grad_output_w = contract_rows(context_low, grad_attended)
    grad_context = times_transpose(grad_attended, output_w).astype(low_type).reshape(four)
    grad_query, grad_keys, grad_values = lax.map(
        attend_backward, (query, keys, values, grad_context, log_total, visible_len)
    )
    grad_query = grad_query.reshape(tokens, width).astype(low_type)
    grad_keys = grad_keys.reshape(tokens, width).astype(low_type)
    grad_values = grad_values.reshape(tokens, width).astype(low_type)
    grad_q_bias = jnp.sum(grad_query.astype(jnp.float32), axis=0)
    grad_v_bias = jnp.sum(grad_values.astype(jnp.float32), axis=0)
    grad_query_w = contract_rows(flat, grad_query)
    grad_key_w = contract_rows(flat, grad_keys)
    grad_value_w = contract_rows(flat, grad_values)
    in_rows = (
        grad_resid_one
        + times_transpose(grad_query, query_w)
        + times_transpose(grad_keys, key_w)
        + times_transpose(grad_values, value_w)
    )
    attn_grad = jnp.concatenate(
        [
            to_flat_blocks(grad_query_w),
            to_flat_blocks(grad_key_w),
            to_flat_blocks(grad_value_w),
            to_flat_blocks(grad_output_w),
        ],
        axis=0,
    )
    vec_grad = jnp.concatenate(
        [
            grad_q_bias,
            grad_v_bias,
            grad_out_bias,
            grad_hidden_bias,
            grad_ffn_bias,
            grad_gain_one,
            grad_shift_one,
            grad_gain_two,
            grad_shift_two,
        ]
    )
    attn_share, ffn_share, vec_share = (
        lax.psum_scatter(attn_grad, ("depth", "dp"), scatter_dimension=0, tiled=True),
        lax.psum_scatter(ffn_grad, ("depth", "dp"), scatter_dimension=0, tiled=True),
        lax.psum_scatter(vec_grad, ("depth", "dp"), scatter_dimension=0, tiled=True),
    )
    returned_rows, returned_gradient = (
        lax.all_to_all(
            result_low.reshape(slots, seq_len, width),
            "depth",
            split_axis=0,
            concat_axis=0,
            tiled=True,
        ),
        lax.all_to_all(
            in_rows.astype(low_type).reshape(slots, seq_len, width),
            "depth",
            split_axis=0,
            concat_axis=0,
            tiled=True,
        ),
    )
    stay = (1 - mine).astype(jnp.float32)[:, None, None]
    out = (
        jnp.einsum("rx,rmp->xmp", selection, returned_rows, preferred_element_type=jnp.float32)
        + stay * inputs.astype(jnp.float32)
    ).astype(low_type)
    in_grad = (
        jnp.einsum("rx,rmp->xmp", selection, returned_gradient, preferred_element_type=jnp.float32)
        + stay * output_gradient.astype(jnp.float32)
    ).astype(low_type)
    square = (
        jnp.sum(attn_share * attn_share)
        + jnp.sum(ffn_share * ffn_share)
        + jnp.sum(vec_share * vec_share)
    )
    total = lax.psum(square, ("depth", "dp"))
    grad_norm = jnp.sqrt(total)
    factor = clip_bound / jnp.maximum(grad_norm, clip_bound)
    attn_square = attn_share.reshape(-1, BLOCK, BLOCK)
    ffn_square = ffn_share.reshape(-1, BLOCK, BLOCK)
    attn_fresh, attn_moment, attn_updated = shampoo(
        attn_weights, attn_stats, attn_roots, attn_momentum, attn_square, factor
    )
    ffn_fresh, ffn_moment, ffn_updated = shampoo(
        ffn_weights, ffn_stats, ffn_roots, ffn_momentum, ffn_square, factor
    )
    first_new, second_new, vec_updated = adam_step(
        vec_weights, vec_first, vec_second, vec_share, factor
    )
    return (
        out,
        in_grad,
        grad_norm,
        attn_fresh,
        attn_moment,
        attn_updated,
        ffn_fresh,
        ffn_moment,
        ffn_updated,
        first_new,
        second_new,
        vec_updated,
    )


MESH = pl.DeviceIdType.MESH
BF = jnp.bfloat16
F32 = jnp.float32
LEN = 512
ROWS = 16


def place():
    d = lax.axis_index("depth")
    i = lax.axis_index("dp")
    x = i % 2
    y = (i // 2) % 2
    nx = i + 1 - 2 * x
    ny = i + 2 - 4 * y
    na = ny + d * (nx - ny)
    nb = nx + d * (ny - nx)
    return dict(d=d, i=i, z=i // 4, c=i % 4, na=na, nb=nb, ca=na % 4, cb=nb % 4, cd=3 - i % 4)


def near(p):
    peers = [(p["d"], p["na"]), (p["d"], p["nb"]), (1 - p["d"], p["i"])]
    return peers + [(p["d"], ((p["z"] + k) % 4) * 4 + p["c"]) for k in (1, 2, 3)]


def greet(peers):
    barrier = pltpu.get_barrier_semaphore()
    for peer in peers:
        pl.semaphore_signal(barrier, inc=1, device_id=peer, device_id_type=MESH)


def meet(peers):
    pl.semaphore_wait(pltpu.get_barrier_semaphore(), len(peers))


def remote(src, dst, send, recv, k, dev):
    return pltpu.make_async_remote_copy(src_ref=src, dst_ref=dst, send_sem=send.at[k], recv_sem=recv.at[k],
                                        device_id=dev, device_id_type=MESH)


class Mail:
    def __init__(self, p, send, recv):
        self.p, self.send, self.recv, self.sent = p, send, recv, []

    def go(self, src, dst, k, dev):
        copy = remote(src, dst, self.send, self.recv, k, dev)
        copy.start()
        self.sent.append(copy)

    def wait(self, dst, k):
        remote(dst, dst, self.send, self.recv, k, (self.p["d"], self.p["na"])).wait_recv()

    def drain(self):
        for copy in self.sent:
            copy.wait_send()


class Spread:
    def __init__(self, p, a, b, to_a, to_b, own, slot, column, send, recv, local):
        d, z, i, c = p["d"], p["z"], p["i"], p["c"]
        ca, cb = a % 4, b % 4
        self.keep = pltpu.make_async_copy(own, slot(d, z, c), local)
        lines = [(own, slot(d, z, c), (d, ((z + k) % 4) * 4 + c)) for k in (1, 2, 3)]
        takes = [slot(d, (z + 4 - k) % 4, c) for k in (1, 2, 3)]
        mine, from_a, from_b, far = (column(d, col) for col in (c, ca, cb, p["cd"]))
        core = (1 - d, i)
        sends = [(mine, 3, (d, a)), (mine, 4, (d, b)), (from_a, 5, (d, b)), (mine, 6, core), (from_a, to_a, core),
                 (from_b, to_b, core), (far, 9, core)]
        self.lines = [remote(src, dst, send, recv, k, dev) for k, (src, dst, dev) in enumerate(lines)]
        self.taken = [remote(dst, dst, send, recv, k, (d, a)) for k, dst in enumerate(takes)]
        self.sends = [remote(src, src, send, recv, k, dev) for src, k, dev in sends]
        waits = [(from_a, 3), (from_b, 4), (far, 5), (column(1 - d, c), 6), (column(1 - d, ca), to_a),
                 (column(1 - d, cb), to_b), (column(1 - d, p["cd"]), 9)]
        self.came = [remote(dst, dst, send, recv, k, (d, a)) for dst, k in waits]

    def push(self, *which):
        for n in which:
            self.sends[n].start()

    def start(self):
        self.keep.start()
        for k in (1, 0, 2):
            self.lines[k].start()

    def second(self):
        self.keep.wait()
        for copy in self.taken:
            copy.wait_recv()
        self.push(0, 1, 3)

    def third(self):
        self.came[0].wait_recv()
        self.push(2, 4)

    def fourth(self):
        self.came[1].wait_recv()
        self.push(5)

    def fifth(self):
        self.came[2].wait_recv()
        self.push(6)

    def sixth(self):
        for copy in self.came[3:]:
            copy.wait_recv()

    def drain(self):
        for copy in self.lines + self.sends:
            copy.wait_send()


def spread_sems():
    return [pltpu.SemaphoreType.DMA((10,)), pltpu.SemaphoreType.DMA((10,)), pltpu.SemaphoreType.DMA]


def on_core(p, core, *steps):
    @pl.when(p["d"] == core)
    def _():
        for s in steps:
            s()


def at_step(m, value, *steps):
    @pl.when(m == value)
    def _():
        for s in steps:
            s()


def square_links(p):
    dx = p["i"] + 1 - 2 * (p["i"] % 2)
    dy = p["i"] + 2 - 4 * ((p["i"] // 2) % 2)
    return dx, dy


def quarter(w, q):
    return w.at[q // 2, pl.ds(2 * (q % 2), 2)]


def one_hot(shape, row, col):
    r = lax.broadcasted_iota(jnp.int32, shape, 0)
    c = lax.broadcasted_iota(jnp.int32, shape, 1)
    return (row(r) == col(c)).astype(F32)


def unfold_vec(pieces, vec, share):
    per = share // BLOCK
    stack = pieces[...][:, :, :, 0, :].reshape(32, pieces.shape[-1])
    units = sum(
        jnp.dot(one_hot((32 * per, 32), lambda u: u, lambda k, a=a: per * k + a), stack[:, a * BLOCK:(a + 1) * BLOCK],
                preferred_element_type=F32)
        for a in range(per)
    )
    for b in range(8):
        vec[:, b * BLOCK:(b + 1) * BLOCK] = jnp.dot(
            one_hot((ROWS, 32 * per), lambda r, b=b: 8 * r + b, lambda u: u), units, preferred_element_type=F32)


def dot_nn(a, b):
    return lax.dot_general(a, b, (((1,), (0,)), ((), ())), preferred_element_type=F32)


def dot_nt(a, b):
    return lax.dot_general(a, b, (((1,), (1,)), ((), ())), preferred_element_type=F32)


def dot_tn(a, b):
    return lax.dot_general(a, b, (((0,), (0,)), ((), ())), preferred_element_type=F32)


def square_of(value):
    return value.reshape(value.shape[0] * value.shape[1] * value.shape[2], value.shape[3])


def seq_rows(s):
    return pl.ds(s * LEN, LEN) if isinstance(s, int) else pl.ds(pl.multiple_of(s * LEN, LEN), LEN)


def tile_rows(s, size):
    return pl.ds(pl.multiple_of(s * size, size), size)


def served_flag(keep, routes, s):
    other = keep[0] * (routes[0] == routes[1]).astype(jnp.int32)
    return jnp.where(s == 0, keep[0], keep[1] * (1 - other))


def projections(x, ga, vec, q, k, v):
    width = x.shape[1]

    def tile(s, carry):
        rows = seq_rows(s)
        xr = x[rows]
        q[rows] = (dot_nn(xr, square_of(ga[0, 0:2])) + vec[0:1]).astype(BF)
        k[rows] = dot_nn(xr, square_of(ga[0, 2:4])).astype(BF)
        v[rows] = (dot_nn(xr, square_of(ga[1, 0:2])) + vec[1:2]).astype(BF)
        return carry

    lax.fori_loop(0, x.shape[0] // LEN, tile, 0)


def head_pairs(n, lens):
    s, g = n // 6, n % 6
    first = lax.broadcasted_iota(jnp.int32, (1, 128), 1) < 64
    return s, seq_rows(s), pl.ds(pl.multiple_of(g * 128, 128), 128), (first, jnp.logical_not(first))


def attend(n, q, k, v, lens, context, log_total):
    s, rows, cols, halves = head_pairs(n, lens)
    qp, kp, vp = q[rows, cols], k[rows, cols], v[rows, cols]
    seen = lax.broadcasted_iota(jnp.int32, (1, LEN), 1) < lens[s]
    found = []
    for h in range(2):
        qm = jnp.where(halves[h], qp, jnp.zeros_like(qp))
        scores = jnp.where(seen, dot_nt(qm, kp) * 0.125, masked_fill)
        peak = jnp.max(scores, axis=1, keepdims=True)
        expo = jnp.exp(scores - peak)
        total = jnp.sum(expo, axis=1, keepdims=True)
        found.append(dot_nn((expo * (1.0 / total)).astype(BF), vp))
        log_total[n, h] = (peak + jnp.log(total))[:, 0]
    context[rows, cols] = jnp.where(halves[0], found[0], found[1]).astype(BF)


def attend_back(n, q, k, v, grad_context, log_total, lens, gq, gk, gv):
    s, rows, cols, halves = head_pairs(n, lens)
    kp, vp = k[rows, cols], v[rows, cols]
    seen = lax.broadcasted_iota(jnp.int32, (LEN, 1), 0) < lens[s]
    ak = av = jnp.zeros((LEN, 128), F32)
    size = LEN // 2
    for t in range(2):
        part = tile_rows(2 * s + t, size)
        qp, gp = q[part, cols], grad_context[part, cols]
        aq = jnp.zeros((size, 128), F32)
        for h in range(2):
            qm, km, gm = (jnp.where(halves[h], t, jnp.zeros_like(t)) for t in (qp, kp, gp))
            scores = jnp.where(seen, dot_nt(kp, qm) * 0.125, masked_fill)
            probs = jnp.exp(scores - log_total[n, h][None, t * size:(t + 1) * size])
            grad_probs = dot_nt(vp, gm)
            along = jnp.sum(probs * grad_probs, axis=0, keepdims=True)
            grad_scores = (probs * (grad_probs - along)).astype(BF)
            av += dot_nn(probs.astype(BF), gm)
            ak += dot_nn(grad_scores, qm)
            aq += dot_tn(grad_scores, km)
        gq[part, cols] = (aq * 0.125).astype(BF)
    gk[rows, cols] = (ak * 0.125).astype(BF)
    gv[rows, cols] = av.astype(BF)


def mean_of(t):
    return jnp.mean(t, axis=-1, keepdims=True)


def attention_end(x, context, ga, vec, normed, factor):
    width = x.shape[1]

    def tile(s, carry):
        rows = seq_rows(s)
        attended = dot_nn(context[rows], square_of(ga[1, 2:4])) + vec[2:3]
        resid = x[rows].astype(F32) + attended
        center = resid - mean_of(resid)
        scale = lax.rsqrt(mean_of(center * center) + norm_floor)
        normed[rows] = center * scale
        factor[rows] = scale
        return carry

    lax.fori_loop(0, x.shape[0] // LEN, tile, 0)


def vec_part(vec, n):
    return vec[n:n + 1]


def input_gradient(x, cot, ga, grad_resid, keep, routes, gq, gk, gv, in_grad, first, last):
    def tile(s, carry):
        rows = tile_rows(s, LEN // 2)
        total = grad_resid[rows] + dot_nt(gq[rows], square_of(ga[0, 0:2]))
        total += dot_nt(gk[rows], square_of(ga[0, 2:4]))
        total += dot_nt(gv[rows], square_of(ga[1, 0:2]))
        in_grad[rows] = jnp.where(served_flag(keep, routes, s // 2) > 0, total.astype(BF), cot[rows])
        return carry

    lax.fori_loop(first, last, tile, 0)


def gather_attention_kernel(aw, fw, vw, x, lens, gf, ga_out, vec, q_out, k_out, v_out, context_out, log_total, normed_out, factor,
                            active_out, slope_out,
                            ga, gv, strip, pair, own, q, k, v, context, normed, low, w1, active, slope, store, wload, *sems):
    p = place()
    peers = near(p)
    greet(peers)
    share = vw.shape[0]
    own[...] = jnp.zeros_like(own)
    own[0:1, 0:share] = vw[...].astype(BF).astype(F32).reshape(1, share)
    for b in range(8):
        strip[:, b * BLOCK:(b + 1) * BLOCK] = aw[b].astype(BF)
    for j in range(2):
        for b in range(8):
            pair[j, :, b * BLOCK:(b + 1) * BLOCK] = fw[8 * j + b].astype(BF)
    half = BLOCK // 2
    seqs = x.shape[0] // LEN
    dx, dy = square_links(p)
    both = (p["na"], p["nb"], 8 - p["d"], 7 + p["d"])

    def attn_part(h):
        rows = pl.ds(h * half, half)
        return both + (strip.at[rows], lambda d, z, c: ga.at[d, z, c, rows], lambda d, c: ga.at[d, :, c, rows])

    def feed_part(j):
        links = (dy, dx, 8, 7) if j == 0 else (dx, dy, 7, 8)
        return links + (pair.at[j], lambda d, z, c: gf.at[d, z, c, j], lambda d, c: gf.at[d, :, c, j])

    vec_piece = both + (own, lambda d, z, c: gv.at[d, z, c], lambda d, c: gv.at[d, :, c])
    parts = [attn_part(0), vec_piece, attn_part(1), feed_part(0), feed_part(1)]
    a0, w, a1, f0, f1 = every = [Spread(p, *part, *sems[3 * n:3 * n + 3]) for n, part in enumerate(parts)]
    meet(peers)
    for s in (a0, w, a1):
        s.start()
    on_core(p, 0, f0.start, f1.start)
    a0.second()
    w.second()
    a1.second()
    for s in (a0, w, a1):
        s.third()
        s.fourth()
    on_core(p, 0, f0.second, f1.second)
    on_core(p, 1, f0.start, f1.start)
    for s in (a0, w, a1):
        s.fifth()
    w.sixth()
    unfold_vec(gv, vec, share)
    a0.sixth()
    a1.sixth()
    stores = [pltpu.make_async_copy(src, dst, store.at[n])
              for n, (src, dst) in enumerate(((q, q_out), (k, k_out), (v, v_out), (context, context_out), (normed, normed_out),
                                              (ga, ga_out)))]
    stores[5].start()
    projections(x, ga, vec, q, k, v)
    for copy in stores[:3]:
        copy.start()

    def step(n, carry):
        attend(n, q, k, v, lens, context, log_total)
        at_step(n, 3, lambda: on_core(p, 0, f0.third, f1.third, f0.fourth, f1.fourth))
        at_step(n, 4, lambda: on_core(p, 1, f0.second, f1.second))
        at_step(n, 9, lambda: on_core(p, 0, f0.fifth, f1.fifth))
        return carry

    lax.fori_loop(0, 12, step, 0)
    stores[3].start()
    attention_end(x, context, ga, vec, normed, factor)
    stores[4].start()
    on_core(p, 1, f0.sixth, f1.sixth)

    def fetch(t, carry):
        n, s = t // 8, t % 8
        pltpu.make_async_copy(gf.at[0, s // 2, 2 * (s % 2) + n // 2, n % 2], w1.at[n // 2, 2 * (n % 2) + s // 4, s % 4],
                              wload.at[n]).start()
        return carry

    lax.fori_loop(0, 32, fetch, 0)

    def lower(s, carry):
        rows = seq_rows(s)
        low[rows] = (normed[rows] * vec_part(vec, 8) + vec_part(vec, 9)).astype(BF)
        return carry

    lax.fori_loop(0, seqs, lower, 0)

    def enter(n, carry):
        pltpu.make_async_copy(quarter(w1, n), quarter(w1, n), wload.at[n]).wait()

        def tile(s, inner):
            rows = seq_rows(s)
            before = dot_nn(low[rows], square_of(quarter(w1, n)[...])) + vec[pl.ds(3 + n, 1)]
            cumulative = 0.5 * (1.0 + lax.erf(before * (1.0 / math.sqrt(2.0))))
            active[n, rows] = (before * cumulative).astype(BF)
            density = jnp.exp(-0.5 * before * before) * (1.0 / math.sqrt(2.0 * math.pi))
            slope[n, rows] = (cumulative + before * density).astype(BF)
            return inner

        lax.fori_loop(0, seqs, tile, 0)
        pltpu.make_async_copy(active.at[n], active_out.at[n], store.at[6 + n]).start()
        pltpu.make_async_copy(slope.at[n], slope_out.at[n], store.at[10 + n]).start()
        at_step(n, 1, lambda: on_core(p, 1, f0.third, f1.third, f0.fourth, f1.fourth))
        return carry

    lax.fori_loop(0, 4, enter, 0)
    on_core(p, 1, f0.fifth, f1.fifth)
    on_core(p, 0, f0.sixth, f1.sixth)
    for s in every:
        s.drain()
    for copy in stores:
        copy.wait()
    for n in range(4):
        pltpu.make_async_copy(active.at[n], active_out.at[n], store.at[6 + n]).wait()
        pltpu.make_async_copy(slope.at[n], slope_out.at[n], store.at[10 + n]).wait()


def gather_attention(aw, fw, vw, x, lens):
    tokens, width = x.shape
    low = jax.ShapeDtypeStruct(x.shape, BF)
    four = jax.ShapeDtypeStruct((4, tokens, width), BF)
    outs = [jax.ShapeDtypeStruct((2, 4, 4, 2, BLOCK, width), BF), jax.ShapeDtypeStruct((2, 4, 4, BLOCK, width), BF),
            jax.ShapeDtypeStruct((ROWS, width), F32)] + [low] * 4
    outs += [jax.ShapeDtypeStruct((12, 2, LEN), F32), jax.ShapeDtypeStruct(x.shape, F32),
             jax.ShapeDtypeStruct((tokens, 1), F32), four, four]
    vmem = pl.BlockSpec(memory_space=pltpu.VMEM)
    hbm = pl.BlockSpec(memory_space=pl.ANY)
    strips = pltpu.VMEM((2, 4, 4, BLOCK, width), BF)
    rows = pltpu.VMEM(x.shape, BF)
    wide = pltpu.VMEM((4, tokens, width), BF)
    return pl.pallas_call(
        gather_attention_kernel,
        out_shape=outs,
        in_specs=[vmem] * 4 + [pl.BlockSpec(memory_space=pltpu.SMEM)],
        out_specs=[hbm, hbm, vmem] + [hbm] * 4 + [vmem, hbm, vmem, hbm, hbm],
        scratch_shapes=[strips, pltpu.VMEM((2, 4, 4, 8, 384), F32), pltpu.VMEM((BLOCK, width), BF),
                        pltpu.VMEM((2, BLOCK, width), BF), pltpu.VMEM((8, 384), F32)]
        + [rows] * 4 + [pltpu.VMEM(x.shape, F32), rows, strips, wide, wide,
                        pltpu.SemaphoreType.DMA((14,)), pltpu.SemaphoreType.DMA((4,))]
        + spread_sems() * 5,
        compiler_params=pltpu.CompilerParams(collective_id=0, has_side_effects=True, vmem_limit_bytes=62 << 20),
        name="gather_attention",
    )(aw, fw, vw, x, lens)


def fold_scratch(width):
    shape = (BLOCK, width)
    return [pltpu.VMEM((4, 4) + shape, BF), pltpu.VMEM((4,) + shape, BF), pltpu.VMEM((4,) + shape, BF),
            pltpu.VMEM((4,) + shape, BF), pltpu.VMEM((3,) + shape, BF),
            pltpu.SemaphoreType.DMA((10,)), pltpu.SemaphoreType.DMA((10,))]


class Total(Mail):
    def __init__(self, p, held, came, send, recv):
        Mail.__init__(self, p, send, recv)
        self.held, self.came = held, came
        self.peers = ((1 - p["d"], p["i"]), (p["d"], p["na"]), (p["d"], p["nb"]))

    def start(self):
        self.go(self.held.at[0], self.came.at[0], 0, self.peers[0])

    def hop(self, n):
        p = self.p
        self.wait(self.came.at[n], n)
        self.held[n + 1] = self.held[n] + self.came[n]
        if n < 2:
            self.go(self.held.at[n + 1], self.came.at[n + 1], n + 1, self.peers[n + 1])
        else:
            for k in (1, 2, 3):
                self.go(self.held.at[3], self.came.at[2 + k], 2 + k, (p["d"], ((p["z"] + k) % 4) * 4 + p["c"]))

    def end(self):
        total = self.held[3]
        for k in (1, 2, 3):
            self.wait(self.came.at[2 + k], 2 + k)
            total += self.came[2 + k]
        return total


def own_share(p, rows, out, share):
    per = share // BLOCK
    me = p["d"] * 16 + p["i"]
    units = sum(
        jnp.dot(one_hot((8, ROWS), lambda a: per * me + jnp.where(a < per, a, -8 * 32 * per), lambda r, b=b: 8 * r + b),
                rows[:, b * BLOCK:(b + 1) * BLOCK], precision=lax.Precision.HIGHEST, preferred_element_type=F32)
        for b in range(8)
    )
    for a in range(per):
        out[0:1, a * BLOCK:(a + 1) * BLOCK] = units[a:a + 1]


def everyone(p):
    me = p["d"] * 16 + p["i"]

    def other(k):
        t = (me + k) % 32
        return (t // 16, t % 16)

    return me, other


def greet_all(p):
    me, other = everyone(p)
    barrier = pltpu.get_barrier_semaphore()

    def one(k, carry):
        pl.semaphore_signal(barrier, inc=1, device_id=other(k), device_id_type=MESH)
        return carry

    lax.fori_loop(1, 32, one, 0)


def meet_all():
    pl.semaphore_wait(pltpu.get_barrier_semaphore(), 31)


def norm_sum(p, square, slots, send, recv):
    me, other = everyone(p)
    slots[me] = jnp.full((8, 128), square, F32)
    to = lambda k, slot: remote(slots.at[slot], slots.at[slot], send, recv, slot, other(k))

    def push(k, carry):
        remote(slots.at[me], slots.at[me], send.at[pl.ds(k, 1)], recv.at[pl.ds(me, 1)], 0, other(k)).start()
        return carry

    def take(k, carry):
        slot = (me + k) % 32
        remote(slots.at[slot], slots.at[slot], send.at[pl.ds(k, 1)], recv.at[pl.ds(slot, 1)], 0, other(k)).wait_recv()
        return carry

    def done(k, carry):
        remote(slots.at[me], slots.at[me], send.at[pl.ds(k, 1)], recv.at[pl.ds(me, 1)], 0, other(k)).wait_send()
        return carry

    lax.fori_loop(1, 32, push, 0)
    lax.fori_loop(1, 32, take, 0)
    total = jnp.sum(slots[...], axis=0)[0:1, 0:1]
    lax.fori_loop(1, 32, done, 0)
    return total


class Fold:
    def __init__(self, p, a, b, away, home, pair, diag, flat, late, line, send, recv):
        self.p, self.home, self.pair, self.diag, self.flat, self.late, self.line = p, home, pair, diag, flat, late, line
        self.ca, self.cb = a % 4, b % 4
        d, z, c = p["d"], p["z"], p["c"]
        self.away, self.send, self.recv, self.core = away, send, recv, (1 - d, p["i"])
        pieces = [(pair.at[:, p["cd"]], diag, (d, b)), (pair.at[:, self.cb], flat, (d, b)),
                  (pair.at[:, self.ca], late, (d, a))]
        pieces += [(pair.at[(z + k) % 4, c], line.at[k - 1], (d, ((z + k) % 4) * 4 + c)) for k in (1, 2, 3)]
        self.copies = [None] + [remote(src, dst, send, recv, n, dev) for n, (src, dst, dev) in enumerate(pieces)]

    def part(self, z):
        return pltpu.make_async_remote_copy(
            src_ref=self.away.at[z], dst_ref=self.pair.at[z], send_sem=self.send.at[6 + z], recv_sem=self.recv.at[6 + z],
            device_id=self.core, device_id_type=MESH)

    def add(self, dst, *others):
        total = dst[...].astype(F32)
        for o in others:
            total += o[...].astype(F32)
        dst[...] = total.astype(dst.dtype)

    def column_part(self, c):
        return pltpu.make_async_remote_copy(
            src_ref=self.away.at[:, c], dst_ref=self.pair.at[:, c], send_sem=self.send.at[6 + c], recv_sem=self.recv.at[6 + c],
            device_id=self.core, device_id_type=MESH)

    def start(self):
        for z in range(4):
            self.part(z).start()

    def second(self):
        for z in range(4):
            self.part(z).wait_recv()
        for col, n in ((self.p["cd"], 1), (self.cb, 2)):
            self.add(self.pair.at[:, col], self.home.at[:, col])
            self.copies[n].start()
        for col in (self.ca, self.p["c"]):
            self.add(self.pair.at[:, col], self.home.at[:, col])

    def third(self):
        self.copies[1].wait_recv()
        self.add(self.pair.at[:, self.ca], self.diag)
        self.copies[3].start()

    def fourth(self):
        p = self.p
        self.copies[2].wait_recv()
        self.copies[3].wait_recv()
        for k in (2, 1, 3, 0):
            dst = (p["z"] + k) % 4
            self.add(self.pair.at[dst, p["c"]], self.flat.at[dst], self.late.at[dst])
            if k:
                self.copies[3 + k].start()

    def fifth(self, out):
        p = self.p
        total = self.pair[p["z"], p["c"]].astype(F32)
        for k in (1, 2, 3):
            self.copies[3 + k].wait_recv()
            total += self.line[k - 1].astype(F32)
        out[...] = total

    def drain(self):
        for copy in self.copies[1:] + [self.part(z) for z in range(4)]:
            copy.wait_send()


def layer_back_kernel(x_in, cot_in, normed_in, active_in, slope_in, factor, gf, ga, q_in, k_in, v_in, context_in, log_total, vec, lens, keep, routes,
                      out, in_grad, sf, sa, sv, norm,
                      x, cot, normed, middle, low, grad_low, image, w1, w2, active, slope, hf, gvec, held, came, slots,
                      load, wload, nsend, nrecv, tsend, trecv, *scratch):
    p = place()
    greet_all(p)
    tokens, width = x.shape
    seqs = tokens // LEN
    half = width // 2
    lanes = (pl.ds(0, half), pl.ds(half, half))

    def bring(src, dst, n):
        return pltpu.make_async_copy(src, dst, load.at[n])

    quarters = [bring(active_in.at[q], active.at[q], q) for q in range(4)]
    others = [bring(normed_in, normed, 4), bring(x_in, x, 5), bring(cot_in, cot, 6)]
    slopes = bring(slope_in, slope, 7)

    def fetch_down(t, carry):
        q, s = t // 8, t % 8
        pltpu.make_async_copy(gf.at[1, q, s // 2, s % 2], w2.at[q // 2, 2 * (q % 2) + s // 4, s % 4], wload.at[q]).start()
        return carry

    def fetch(t, carry):
        q, s = t // 8, t % 8
        pltpu.make_async_copy(gf.at[0, s // 2, 2 * (s % 2) + q // 2, q % 2], w1.at[q // 2, 2 * (q % 2) + s // 4, s % 4],
                              wload.at[4]).start()
        return carry

    for q in range(4):
        quarters[q].start()
        lax.fori_loop(8 * q, 8 * q + 8, fetch_down, 0)
    for copy in others:
        copy.start()
    slopes.start()
    lax.fori_loop(0, 32, fetch, 0)
    dx, dy = square_links(p)
    f0 = Fold(p, dy, dx, hf.at[1 - p["d"], :, :, 0], hf.at[p["d"], :, :, 0], *scratch[0:7])
    f1 = Fold(p, dx, dy, hf.at[1 - p["d"], :, :, 1], hf.at[p["d"], :, :, 1], *scratch[7:14])
    ha, ga_in = w1, w2
    a0, a1 = [Fold(p, p["na"], p["nb"], ha.at[1 - p["d"], :, :, :, lanes[n]], ha.at[p["d"], :, :, :, lanes[n]],
                   *scratch[14 + 7 * n:21 + 7 * n]) for n in range(2)]
    total = Total(p, held, came, tsend, trecv)

    def on(core, *steps):
        on_core(p, core, *steps)

    gvec[...] = jnp.zeros_like(gvec)

    def add_vec(n, value):
        gvec[n:n + 1] += value

    for q in range(4):
        quarters[q].wait()
        pltpu.make_async_copy(quarter(w2, q), quarter(w2, q), wload.at[q]).wait()

        def gain(s, carry):
            rows = seq_rows(s)
            found = dot_nn(active[q, rows], square_of(quarter(w2, q)[...]))
            middle[rows] = found if q == 0 else middle[rows] + found
            return carry

        lax.fori_loop(0, seqs, gain, 0)
    for copy in others:
        copy.wait()
    tile = LEN // 2

    def leave(t, carry):
        rows = tile_rows(t, tile)
        show = pltpu.make_async_copy(image, out.at[rows], load.at[14])
        hidden = normed[rows] * vec_part(vec, 8) + vec_part(vec, 9)
        low[rows] = hidden.astype(BF)
        resid = hidden + (middle[rows] + vec_part(vec, 7))
        center = resid - mean_of(resid)
        scale = lax.rsqrt(mean_of(center * center) + norm_floor)
        second = center * scale
        served = served_flag(keep, routes, t // 2) > 0
        result = second * vec_part(vec, 10) + vec_part(vec, 11)
        image[...] = jnp.where(served, result.astype(BF), x[rows])
        show.start()
        grad = jnp.where(served, cot[rows].astype(F32), 0.0)
        add_vec(10, jnp.sum(grad * second, axis=0, keepdims=True))
        add_vec(11, jnp.sum(grad, axis=0, keepdims=True))
        grad = grad * vec_part(vec, 10)
        grad = scale * (grad - mean_of(grad) - second * mean_of(grad * second))
        middle[rows] = grad
        grad_low[rows] = grad.astype(BF)
        add_vec(7, jnp.sum(grad.astype(BF).astype(F32), axis=0, keepdims=True))
        show.wait()
        return carry

    lax.fori_loop(0, 2 * seqs, leave, 0)
    meet_all()

    def down_grad(t, carry):
        q, h = t // 2, t % 2
        found = dot_tn(active[q, :, pl.ds(pl.multiple_of(h * half, half), half)], grad_low[...])
        hf[1, q, pl.ds(2 * h, 2)] = found.astype(BF).reshape(2, 2, BLOCK, width)
        at_step(h, 1, lambda: on(0, lambda: f0.part(q).start(), lambda: f1.part(q).start()))
        return carry

    lax.fori_loop(0, 8, down_grad, 0)
    again = [bring(src, slope.at[n], 8 + n) for n, src in enumerate((context_in, q_in, k_in, v_in))]
    context, qs, ks, vs = (slope.at[n] for n in range(4))
    slopes.wait()

    def turn(q, carry):
        def part(s, inner):
            rows = seq_rows(s)
            back = dot_nt(grad_low[rows], square_of(quarter(w2, q)[...])) * slope[q, rows].astype(F32)
            active[q, rows] = back.astype(BF)
            gvec[pl.ds(3 + q, 1)] += jnp.sum(back.astype(BF).astype(F32), axis=0, keepdims=True)
            return inner

        def up_grad(h, inner):
            found = dot_tn(low[:, pl.ds(pl.multiple_of(h * half, half), half)], active[q]).astype(BF).reshape(2, 2, BLOCK, width)
            for y in range(2):
                hf[0, pl.ds(2 * h, 2), 2 * y + q // 2, q % 2] = found[:, y]
            return inner

        lax.fori_loop(0, seqs, part, 0)
        lax.fori_loop(0, 2, up_grad, 0)
        at_step(q, 0, lambda: on(1, f0.second, f1.second))
        for j, f in enumerate((f0, f1)):
            at_step(q % 2, j, lambda f=f: on(1, lambda: f.column_part(q // 2).start(), lambda: f.column_part(2 + q // 2).start()))
        at_step(q, 2, lambda: on(1, f0.third))
        at_step(q, 3, lambda: on(1, f1.third))
        return carry

    lax.fori_loop(0, 4, turn, 0)
    for copy in again:
        copy.start()
    pltpu.make_async_copy(w1, w1, wload.at[4]).wait()
    square_in = bring(ga, ga_in, 12)
    square_in.start()

    def close(t, carry):
        rows = tile_rows(t, tile)
        grad = middle[rows]
        for q in range(4):
            grad += dot_nt(active[q, rows], square_of(quarter(w1, q)[...]))
        head = normed[rows]
        add_vec(8, jnp.sum(grad * head, axis=0, keepdims=True))
        add_vec(9, jnp.sum(grad, axis=0, keepdims=True))
        grad = grad * vec_part(vec, 8)
        grad = factor[rows] * (grad - mean_of(grad) - head * mean_of(grad * head))
        middle[rows] = grad
        grad_low[rows] = grad.astype(BF)
        return carry

    lax.fori_loop(0, seqs, close, 0)
    on(0, f0.second)
    lax.fori_loop(seqs, 2 * seqs, close, 0)
    on(1, f0.fourth)
    on(0, f1.second)
    gq, gk, gv, grad_context = (active.at[n] for n in range(4))
    square_in.wait()
    again[0].wait()

    def open_attention(s, carry):
        rows = seq_rows(s)
        grad_context[rows] = dot_nt(grad_low[rows], square_of(ga_in[1, 2:4])).astype(BF)
        return carry

    lax.fori_loop(0, seqs, open_attention, 0)
    held[0] = gvec[...]
    held[0, 2:3] = jnp.sum(grad_low[...].astype(F32), axis=0, keepdims=True)
    for h in range(2):
        ha[1, 2 + h] = dot_tn(context[:, h * half:(h + 1) * half], grad_low[...]).astype(BF).reshape(4, BLOCK, width)
    on(1, f1.fourth)
    for copy in again[1:]:
        copy.wait()

    def step(m, carry):
        n = ((m % 6) // 3) * 6 + (m // 6) * 3 + m % 3
        attend_back(n, qs, ks, vs, grad_context, log_total, lens, gq, gk, gv)
        at_step(m, 0, lambda: on(0, f0.third))
        at_step(m, 1, lambda: on(0, f1.third))
        at_step(m, 5, lambda: weight_grads(0), a0.start, lambda: on(0, f0.fourth))
        at_step(m, 6, lambda: on(0, f1.fourth))
        at_step(m, 7, a0.second)
        at_step(m, 10, a0.third)
        at_step(m, 11, lambda: weight_grads(1))
        return carry

    def weight_grads(n):
        cols = lanes[n]
        for dst, src in ((ha.at[0, 0:2], gq), (ha.at[0, 2:4], gk), (ha.at[1, 0:2], gv)):
            dst[:, :, :, cols] = dot_tn(x[...], src[:, cols]).astype(BF).reshape(2, 4, BLOCK, half)

    lax.fori_loop(0, 12, step, 0)
    a1.start()
    held[0, 0:1] = jnp.sum(gq[...].astype(F32), axis=0, keepdims=True)
    held[0, 1:2] = jnp.sum(gv[...].astype(F32), axis=0, keepdims=True)
    total.start()
    input_gradient(x, cot, ga_in, middle, keep, routes, gq, gk, gv, cot, 0, seqs)
    a1.second()
    total.hop(0)
    a0.fourth()
    input_gradient(x, cot, ga_in, middle, keep, routes, gq, gk, gv, cot, seqs, 2 * seqs)
    total.hop(1)
    last = bring(cot, in_grad, 13)
    last.start()
    a1.third()
    total.hop(2)
    f0.fifth(sf.at[0])
    f1.fifth(sf.at[1])
    square = jnp.sum(sf[...] * sf[...])
    a1.fourth()
    held[4] = total.end()
    sv[...] = jnp.zeros_like(sv)
    own_share(p, held[4], sv, 12 * width // 32)
    a0.fifth(sa.at[:, lanes[0]])
    a1.fifth(sa.at[:, lanes[1]])
    square += jnp.sum(sa[...] * sa[...]) + jnp.sum(sv[...] * sv[...])
    found = norm_sum(p, square, slots, nsend, nrecv)
    norm[...] = jnp.sqrt(found)
    for s in (f0, f1, a0, a1, total):
        s.drain()
    last.wait()


def layer_back(x, cot, normed, active, slope, factor, gf, ga, q, k, v, context, log_total, vec, lens, keep, routes):
    tokens, width = x.shape
    outs = [jax.ShapeDtypeStruct(x.shape, BF), jax.ShapeDtypeStruct(x.shape, BF), jax.ShapeDtypeStruct((2, BLOCK, width), F32),
            jax.ShapeDtypeStruct((BLOCK, width), F32), jax.ShapeDtypeStruct((8, 384), F32), jax.ShapeDtypeStruct((1, 1), F32)]
    dma = pltpu.SemaphoreType.DMA
    rows = pltpu.VMEM(x.shape, BF)
    wide = pltpu.VMEM(x.shape, F32)
    strips = pltpu.VMEM(ga.shape, BF)
    scratch = [rows, rows, wide, wide, rows, rows, pltpu.VMEM((LEN // 2, width), BF), strips, strips,
               pltpu.VMEM((4, tokens, width), BF), pltpu.VMEM((4, tokens, width), BF), pltpu.VMEM(gf.shape, BF),
               pltpu.VMEM(vec.shape, F32), pltpu.VMEM((5, ROWS, width), F32), pltpu.VMEM((6, ROWS, width), F32),
               pltpu.VMEM((32, 8, 128), F32),
               dma((15,)), dma((5,)), dma((32,)), dma((32,)), dma((6,)), dma((6,))]
    scratch += fold_scratch(width) * 2 + fold_scratch(width // 2) * 2
    vmem = pl.BlockSpec(memory_space=pltpu.VMEM)
    smem = pl.BlockSpec(memory_space=pltpu.SMEM)
    hbm = pl.BlockSpec(memory_space=pl.ANY)
    return pl.pallas_call(
        layer_back_kernel,
        out_shape=outs,
        in_specs=[hbm] * 5 + [vmem] + [hbm] * 6 + [vmem] * 2 + [smem] * 3,
        out_specs=[hbm] * 2 + [vmem] * 4,
        scratch_shapes=scratch,
        compiler_params=pltpu.CompilerParams(collective_id=1, has_side_effects=True, vmem_limit_bytes=67043328),
        name="feed_and_back",
    )(x, cot, normed, active, slope, factor, gf, ga, q, k, v, context, log_total, vec, lens, keep, routes)


def halves_of(t):
    high = t.astype(BF)
    return high, (t - high.astype(F32)).astype(BF)


def exact_dot(a, b, dims):
    dot = lambda x, y: lax.dot_general(x, y, (dims, ((), ())), preferred_element_type=F32)
    return dot(a[0], b[0]) + (dot(a[0], b[1]) + dot(a[1], b[0]))


def shampoo_block(grad, w, st, ro, mo, st_new, mo_new, w_new, b, factor):
    clipped = grad * factor
    moment = momentum_decay * mo[b] + clipped
    both = halves_of(clipped)
    left = exact_dot(both, both, ((1,), (1,)))
    right = exact_dot(both, both, ((0,), (0,)))
    st_new[b, 0] = stat_decay * st[b, 0] + (1.0 - stat_decay) * left
    st_new[b, 1] = stat_decay * st[b, 1] + (1.0 - stat_decay) * right
    mo_new[b] = moment
    turned = exact_dot(halves_of(ro[b, 0]), halves_of(moment), ((1,), (0,)))
    turned = exact_dot(halves_of(turned), halves_of(ro[b, 1]), ((1,), (0,)))
    w_new[b] = w[b] - matrix_rate * (turned + matrix_decay * w[b])


def optimizer_kernel(norm, sa, sf, sv, aw, ast, ar, am, fw, fst, fr, fm, vw, v1, v2, rows, grads,
                     rows_n, grads_n, ast_n, am_n, aw_n, fst_n, fm_n, fw_n, v1_n, v2_n, vw_n, ga, gf):
    factor = clip_bound / jnp.maximum(norm[...], clip_bound)
    g = pl.program_id(0)
    many = aw.shape[0]
    rows_n[...] = rows[...]
    grads_n[...] = grads[...]

    @pl.when(g == 0)
    def _():
        for b in range(8):
            ga[b] = sa[:, b * BLOCK:(b + 1) * BLOCK]
            for j in range(2):
                gf[8 * j + b] = sf[j, :, b * BLOCK:(b + 1) * BLOCK]
        size = vw.shape[0]
        clipped = (sv[0:1, 0:size] * factor)[0]
        first_new = first_decay * v1[...] + (1.0 - first_decay) * clipped
        second_new = second_decay * v2[...] + (1.0 - second_decay) * clipped * clipped
        first_hat = first_new / (1.0 - first_decay**STEP)
        second_hat = second_new / (1.0 - second_decay**STEP)
        v1_n[...] = first_new
        v2_n[...] = second_new
        vw_n[...] = vw[...] - vector_rate * first_hat / (jnp.sqrt(second_hat) + adam_floor)

    for b in range(many):
        shampoo_block(ga[g * many + b], aw, ast, ar, am, ast_n, am_n, aw_n, b, factor)
    for b in range(2 * many):
        shampoo_block(gf[g * 2 * many + b], fw, fst, fr, fm, fst_n, fm_n, fw_n, b, factor)


def optimizer(norm, sa, sf, sv, aw, ast, ar, am, fw, fst, fr, fm, vw, v1, v2, rows, grads):
    many = 2

    def steps(t, n):
        shape = (n,) + t.shape[1:]
        return pl.BlockSpec(shape, lambda g: (g,) + (0,) * (len(shape) - 1))

    def whole(t):
        return pl.BlockSpec(t.shape, lambda g: (0,) * t.ndim)

    like = lambda t: jax.ShapeDtypeStruct(t.shape, t.dtype)
    args = (norm, sa, sf, sv, aw, ast, ar, am, fw, fst, fr, fm, vw, v1, v2, rows, grads)
    part = rows.shape[0] * many // aw.shape[0]
    specs = [whole(t) for t in args[:4]]
    specs += [steps(t, many) for t in (aw, ast, ar, am)] + [steps(t, 2 * many) for t in (fw, fst, fr, fm)]
    specs += [whole(t) for t in (vw, v1, v2)] + [steps(t, part) for t in (rows, grads)]
    outs = (rows, grads, ast, am, aw, fst, fm, fw, v1, v2, vw)
    return pl.pallas_call(
        optimizer_kernel,
        out_shape=[like(t) for t in outs],
        grid=(aw.shape[0] // many,),
        in_specs=specs,
        out_specs=[steps(t, part) for t in outs[:2]] + [steps(t, many) for t in outs[2:5]] + [steps(t, 2 * many) for t in outs[5:8]]
        + [whole(t) for t in outs[8:]],
        scratch_shapes=[pltpu.VMEM(aw.shape, F32), pltpu.VMEM(fw.shape, F32)],
        name="optimizer",
    )(*args)


def per_device(
    inputs,
    output_gradient,
    keep,
    lengths,
    routes,
    attn_weights,
    attn_stats,
    attn_roots,
    attn_momentum,
    ffn_weights,
    ffn_stats,
    ffn_roots,
    ffn_momentum,
    vec_weights,
    vec_first,
    vec_second,
):
    slots, seq_len, width = inputs.shape
    tokens = slots * seq_len
    x = inputs.reshape(tokens, width)
    cot = output_gradient.reshape(tokens, width)
    gf, ga, vec, q, k, v, context, log_total, normed, factor, active, slope = gather_attention(attn_weights, ffn_weights, vec_weights, x, lengths)
    out, in_grad, sf, sa, sv, norm = layer_back(
        x, cot, normed, active, slope, factor, gf, ga, q, k, v, context, log_total, vec, lengths, keep, routes
    )
    out, in_grad, *rest = optimizer(
        norm, sa, sf, sv,
        attn_weights, attn_stats, attn_roots, attn_momentum,
        ffn_weights, ffn_stats, ffn_roots, ffn_momentum,
        vec_weights, vec_first, vec_second, out, in_grad,
    )
    return (out.reshape(inputs.shape), in_grad.reshape(inputs.shape), norm.reshape(()), *rest)


def solution(mesh):
    small = mesh.shape["depth"] == 2 and mesh.shape["dp"] == 16
    return jax.shard_map(
        per_device if small else per_device_general,
        mesh=mesh,
        in_specs=(
            P(("depth", "dp"), None, None),
            P(("depth", "dp"), None, None),
            P(("depth", "dp")),
            P(("depth", "dp")),
            P(("depth", "dp")),
            P(("depth", "dp"), None, None),
            P(("depth", "dp"), None, None, None),
            P(("depth", "dp"), None, None, None),
            P(("depth", "dp"), None, None),
            P(("depth", "dp"), None, None),
            P(("depth", "dp"), None, None, None),
            P(("depth", "dp"), None, None, None),
            P(("depth", "dp"), None, None),
            P(("depth", "dp")),
            P(("depth", "dp")),
            P(("depth", "dp")),
        ),
        out_specs=(
            P(("depth", "dp"), None, None),
            P(("depth", "dp"), None, None),
            P(),
            P(("depth", "dp"), None, None, None),
            P(("depth", "dp"), None, None),
            P(("depth", "dp"), None, None),
            P(("depth", "dp"), None, None, None),
            P(("depth", "dp"), None, None),
            P(("depth", "dp"), None, None),
            P(("depth", "dp")),
            P(("depth", "dp")),
            P(("depth", "dp")),
        ),
        check_vma=False,
    )
```

```python
import functools
import math

import jax
import jax.numpy as jnp
from jax import lax
from jax.experimental import pallas as pl
from jax.experimental.pallas import tpu as pltpu
from jax.sharding import PartitionSpec as P

HEADS = 12
FF = 3072
BLOCK = 96
STEP = 10


norm_floor = 1e-05
masked_fill = -1000000000.0
momentum_decay = 0.9
stat_decay = 0.95
matrix_rate = 1.0
matrix_decay = 0.01
clip_bound = 1.0
first_decay = 0.9
second_decay = 0.999
vector_rate = 0.5
adam_floor = 1e-08


def serve_flags(keep_rows, route_rows):
    count = keep_rows.shape[-1]
    order = jnp.arange(count, dtype=jnp.int32)
    earlier = (order[None, :] < order[:, None]).astype(jnp.int32)
    same = (route_rows[:, :, None] == route_rows[:, None, :]).astype(jnp.int32)
    clash = jnp.sum(same * earlier[None, :, :] * keep_rows[:, None, :], axis=2)
    return keep_rows * (clash == 0).astype(jnp.int32)


def to_matrix(blocks, height, breadth):
    shaped = blocks.reshape(height // BLOCK, breadth // BLOCK, BLOCK, BLOCK)
    return shaped.transpose(0, 2, 1, 3).reshape(height, breadth)


def to_flat_blocks(matrix):
    height, breadth = matrix.shape
    shaped = matrix.reshape(height // BLOCK, BLOCK, breadth // BLOCK, BLOCK)
    return shaped.transpose(0, 2, 1, 3).reshape(-1, BLOCK * BLOCK)


def norm_parts(resid):
    center = resid - jnp.mean(resid, axis=-1, keepdims=True)
    factor = lax.rsqrt(jnp.mean(center * center, axis=-1, keepdims=True) + norm_floor)
    return (center * factor, factor)


def norm_back(grad_normed, normed, factor):
    middle = jnp.mean(grad_normed, axis=-1, keepdims=True)
    along = jnp.mean(grad_normed * normed, axis=-1, keepdims=True)
    return factor * (grad_normed - middle - normed * along)


def gelu_slope(value):
    cumulative = 0.5 * (1.0 + lax.erf(value * (1.0 / math.sqrt(2.0))))
    density = jnp.exp(-0.5 * value * value) * (1.0 / math.sqrt(2.0 * math.pi))
    return cumulative + value * density


def product(left, right):
    return jnp.dot(left, right, preferred_element_type=jnp.float32)


def contract_rows(left, right):
    return lax.dot_general(
        left, right, (((0,), (0,)), ((), ())), preferred_element_type=jnp.float32
    )


def times_transpose(left, right):
    return lax.dot_general(
        left, right, (((1,), (1,)), ((), ())), preferred_element_type=jnp.float32
    )


def masked_scores(query, keys, visible_len):
    scale = 1.0 / math.sqrt(query.shape[-1])
    scores = jnp.einsum("qhe,khe->hqk", query, keys, preferred_element_type=jnp.float32) * scale
    visible = jnp.arange(keys.shape[0], dtype=jnp.int32) < visible_len
    return jnp.where(visible[None, None, :], scores, masked_fill)


def attend_forward(pieces):
    query, keys, values, visible_len = pieces
    scores = masked_scores(query, keys, visible_len)
    peak = jnp.max(scores, axis=-1, keepdims=True)
    expo = jnp.exp(scores - peak)
    total = jnp.sum(expo, axis=-1, keepdims=True)
    probs_low = (expo / total).astype(jnp.bfloat16)
    context = jnp.einsum("hqk,khe->qhe", probs_low, values, preferred_element_type=jnp.float32)
    return (context, peak[..., 0] + jnp.log(total[..., 0]))


def attend_backward(pieces):
    query, keys, values, grad_ctx, log_total, visible_len = pieces
    scale = 1.0 / math.sqrt(query.shape[-1])
    scores = masked_scores(query, keys, visible_len)
    probs = jnp.exp(scores - log_total[..., None])
    probs_low = probs.astype(jnp.bfloat16)
    grad_probs = jnp.einsum("qhe,khe->hqk", grad_ctx, values, preferred_element_type=jnp.float32)
    grad_values = jnp.einsum(
        "hqk,qhe->khe", probs_low, grad_ctx, preferred_element_type=jnp.float32
    )
    along = jnp.sum(probs * grad_probs, axis=-1, keepdims=True)
    grad_scores = (probs * (grad_probs - along)).astype(jnp.bfloat16)
    grad_query = (
        jnp.einsum("hqk,khe->qhe", grad_scores, keys, preferred_element_type=jnp.float32) * scale
    )
    grad_keys = (
        jnp.einsum("hqk,qhe->khe", grad_scores, query, preferred_element_type=jnp.float32) * scale
    )
    return (grad_query, grad_keys, grad_values)


def shampoo(weights, stats, roots, momentum, grads, factor):
    highest = lax.Precision.HIGHEST
    clipped = grads * factor
    moment = momentum_decay * momentum + clipped
    left = jnp.einsum("nab,ncb->nac", clipped, clipped, precision=highest)
    right = jnp.einsum("nab,nac->nbc", clipped, clipped, precision=highest)
    fresh = stat_decay * stats + (1.0 - stat_decay) * jnp.stack([left, right], axis=1)
    turned = jnp.einsum("nab,nbc->nac", roots[:, 0], moment, precision=highest)
    turned = jnp.einsum("nab,nbc->nac", turned, roots[:, 1], precision=highest)
    updated = weights - matrix_rate * (turned + matrix_decay * weights)
    return (fresh, moment, updated)


def adam_step(weights, first, second, grads, factor):
    clipped = grads * factor
    first_new = first_decay * first + (1.0 - first_decay) * clipped
    second_new = second_decay * second + (1.0 - second_decay) * clipped * clipped
    first_hat = first_new / (1.0 - first_decay**STEP)
    second_hat = second_new / (1.0 - second_decay**STEP)
    updated = weights - vector_rate * first_hat / (jnp.sqrt(second_hat) + adam_floor)
    return (first_new, second_new, updated)


def per_device_general(
    inputs,
    output_gradient,
    keep,
    lengths,
    routes,
    attn_weights,
    attn_stats,
    attn_roots,
    attn_momentum,
    ffn_weights,
    ffn_stats,
    ffn_roots,
    ffn_momentum,
    vec_weights,
    vec_first,
    vec_second,
):
    slots, seq_len, width = inputs.shape
    tokens = slots * seq_len
    head_size = width // HEADS
    hidden_width = FF
    depth_count = lax.axis_size("depth")
    peer_slots = slots // depth_count
    grid = (width // BLOCK) ** 2
    half_ffn = width * hidden_width // (BLOCK * BLOCK)
    area = BLOCK * BLOCK
    low_type = jnp.bfloat16
    attn_flat = attn_weights.reshape(-1, area).astype(low_type)
    ffn_flat = ffn_weights.reshape(-1, area).astype(low_type)
    attn_all, ffn_all, vec_all = (
        lax.all_gather(attn_flat, ("depth", "dp"), axis=0, tiled=True),
        lax.all_gather(ffn_flat, ("depth", "dp"), axis=0, tiled=True),
        lax.all_gather(vec_weights.astype(low_type), ("depth", "dp"), axis=0, tiled=True),
    )
    table_keep, table_len, table_route = (
        lax.all_gather(keep, "depth", axis=0, tiled=True),
        lax.all_gather(lengths, "depth", axis=0, tiled=True),
        lax.all_gather(routes, "depth", axis=0, tiled=True),
    )
    mine = serve_flags(keep[None, :], routes[None, :])[0]
    slot_order = jnp.arange(slots, dtype=jnp.int32)
    selection = ((routes[None, :] == slot_order[:, None]).astype(jnp.int32) * mine[None, :]).astype(
        low_type
    )
    outgoing_rows = jnp.einsum(
        "gz,zrp->grp", selection, inputs, preferred_element_type=jnp.float32
    ).astype(low_type)
    send_grad = jnp.einsum(
        "gz,zrp->grp", selection, output_gradient, preferred_element_type=jnp.float32
    ).astype(low_type)
    come_rows, come_grad = (
        lax.all_to_all(outgoing_rows, "depth", split_axis=0, concat_axis=0, tiled=True),
        lax.all_to_all(send_grad, "depth", split_axis=0, concat_axis=0, tiled=True),
    )
    all_keep = table_keep.reshape(depth_count, slots)
    all_route = table_route.reshape(depth_count, slots)
    all_len = table_len.reshape(depth_count, slots)
    all_served = serve_flags(all_keep, all_route)
    here = lax.axis_index("depth")
    source = slot_order // peer_slots
    target = here * peer_slots + slot_order % peer_slots
    source_hot = (source[:, None] == jnp.arange(depth_count, dtype=jnp.int32)[None, :]).astype(
        jnp.int32
    )
    match = (all_route[None, :, :] == target[:, None, None]).astype(jnp.int32) * all_served[
        None, :, :
    ]
    slot_len = jnp.sum(source_hot[:, :, None] * match * all_len[None, :, :], axis=(1, 2))
    visible_len = jnp.maximum(slot_len, 1)
    query_w = to_matrix(attn_all[0:grid], width, width)
    key_w = to_matrix(attn_all[grid : 2 * grid], width, width)
    value_w = to_matrix(attn_all[2 * grid : 3 * grid], width, width)
    output_w = to_matrix(attn_all[3 * grid : 4 * grid], width, width)
    vectors = vec_all.astype(jnp.float32)
    q_bias = vectors[0:width]
    v_bias = vectors[width : 2 * width]
    out_bias = vectors[2 * width : 3 * width]
    hidden_bias = vectors[3 * width : 3 * width + hidden_width]
    ffn_bias = vectors[3 * width + hidden_width : 4 * width + hidden_width]
    gain_one = vectors[4 * width + hidden_width : 5 * width + hidden_width]
    shift_one = vectors[5 * width + hidden_width : 6 * width + hidden_width]
    gain_two = vectors[6 * width + hidden_width : 7 * width + hidden_width]
    shift_two = vectors[7 * width + hidden_width : 8 * width + hidden_width]
    flat = come_rows.reshape(tokens, width)
    four = (slots, seq_len, HEADS, head_size)
    query = (product(flat, query_w) + q_bias).astype(low_type).reshape(four)
    keys = product(flat, key_w).astype(low_type).reshape(four)
    values = (product(flat, value_w) + v_bias).astype(low_type).reshape(four)
    context, log_total = lax.map(attend_forward, (query, keys, values, visible_len))
    context_low = context.reshape(tokens, width).astype(low_type)
    attended = product(context_low, output_w) + out_bias
    normed_one, factor_one = norm_parts(flat.astype(jnp.float32) + attended)
    hidden_in = normed_one * gain_one + shift_one
    hidden_low = hidden_in.astype(low_type)
    hidden_w = to_matrix(ffn_all[0:half_ffn], width, hidden_width)
    return_weight = to_matrix(ffn_all[half_ffn:], hidden_width, width)
    before = product(hidden_low, hidden_w) + hidden_bias
    active_low = jax.nn.gelu(before, approximate=False).astype(low_type)
    branch = product(active_low, return_weight) + ffn_bias
    normed_two, factor_two = norm_parts(hidden_in + branch)
    result_low = (normed_two * gain_two + shift_two).astype(low_type)
    grad_rows = come_grad.reshape(tokens, width).astype(jnp.float32)
    grad_gain_two = jnp.sum(grad_rows * normed_two, axis=0)
    grad_shift_two = jnp.sum(grad_rows, axis=0)
    grad_resid_two = norm_back(grad_rows * gain_two, normed_two, factor_two)
    grad_branch = grad_resid_two.astype(low_type)
    grad_ffn_bias = jnp.sum(grad_branch.astype(jnp.float32), axis=0)
    gradient_return_weight = contract_rows(active_low, grad_branch)
    grad_active = times_transpose(grad_branch, return_weight)
    grad_before = (grad_active * gelu_slope(before)).astype(low_type)
    grad_hidden_bias = jnp.sum(grad_before.astype(jnp.float32), axis=0)
    grad_hidden_w = contract_rows(hidden_low, grad_before)
    grad_hidden = times_transpose(grad_before, hidden_w) + grad_resid_two
    grad_gain_one = jnp.sum(grad_hidden * normed_one, axis=0)
    grad_shift_one = jnp.sum(grad_hidden, axis=0)
    grad_resid_one = norm_back(grad_hidden * gain_one, normed_one, factor_one)
    ffn_grad = jnp.concatenate(
        [to_flat_blocks(grad_hidden_w), to_flat_blocks(gradient_return_weight)], axis=0
    )
    grad_attended = grad_resid_one.astype(low_type)
    grad_out_bias = jnp.sum(grad_attended.astype(jnp.float32), axis=0)
    grad_output_w = contract_rows(context_low, grad_attended)
    grad_context = times_transpose(grad_attended, output_w).astype(low_type).reshape(four)
    grad_query, grad_keys, grad_values = lax.map(
        attend_backward, (query, keys, values, grad_context, log_total, visible_len)
    )
    grad_query = grad_query.reshape(tokens, width).astype(low_type)
    grad_keys = grad_keys.reshape(tokens, width).astype(low_type)
    grad_values = grad_values.reshape(tokens, width).astype(low_type)
    grad_q_bias = jnp.sum(grad_query.astype(jnp.float32), axis=0)
    grad_v_bias = jnp.sum(grad_values.astype(jnp.float32), axis=0)
    grad_query_w = contract_rows(flat, grad_query)
    grad_key_w = contract_rows(flat, grad_keys)
    grad_value_w = contract_rows(flat, grad_values)
    in_rows = (
        grad_resid_one
        + times_transpose(grad_query, query_w)
        + times_transpose(grad_keys, key_w)
        + times_transpose(grad_values, value_w)
    )
    attn_grad = jnp.concatenate(
        [
            to_flat_blocks(grad_query_w),
            to_flat_blocks(grad_key_w),
            to_flat_blocks(grad_value_w),
            to_flat_blocks(grad_output_w),
        ],
        axis=0,
    )
    vec_grad = jnp.concatenate(
        [
            grad_q_bias,
            grad_v_bias,
            grad_out_bias,
            grad_hidden_bias,
            grad_ffn_bias,
            grad_gain_one,
            grad_shift_one,
            grad_gain_two,
            grad_shift_two,
        ]
    )
    attn_share, ffn_share, vec_share = (
        lax.psum_scatter(attn_grad, ("depth", "dp"), scatter_dimension=0, tiled=True),
        lax.psum_scatter(ffn_grad, ("depth", "dp"), scatter_dimension=0, tiled=True),
        lax.psum_scatter(vec_grad, ("depth", "dp"), scatter_dimension=0, tiled=True),
    )
    returned_rows, returned_gradient = (
        lax.all_to_all(
            result_low.reshape(slots, seq_len, width),
            "depth",
            split_axis=0,
            concat_axis=0,
            tiled=True,
        ),
        lax.all_to_all(
            in_rows.astype(low_type).reshape(slots, seq_len, width),
            "depth",
            split_axis=0,
            concat_axis=0,
            tiled=True,
        ),
    )
    stay = (1 - mine).astype(jnp.float32)[:, None, None]
    out = (
        jnp.einsum("rx,rmp->xmp", selection, returned_rows, preferred_element_type=jnp.float32)
        + stay * inputs.astype(jnp.float32)
    ).astype(low_type)
    in_grad = (
        jnp.einsum("rx,rmp->xmp", selection, returned_gradient, preferred_element_type=jnp.float32)
        + stay * output_gradient.astype(jnp.float32)
    ).astype(low_type)
    square = (
        jnp.sum(attn_share * attn_share)
        + jnp.sum(ffn_share * ffn_share)
        + jnp.sum(vec_share * vec_share)
    )
    total = lax.psum(square, ("depth", "dp"))
    grad_norm = jnp.sqrt(total)
    factor = clip_bound / jnp.maximum(grad_norm, clip_bound)
    attn_square = attn_share.reshape(-1, BLOCK, BLOCK)
    ffn_square = ffn_share.reshape(-1, BLOCK, BLOCK)
    attn_fresh, attn_moment, attn_updated = shampoo(
        attn_weights, attn_stats, attn_roots, attn_momentum, attn_square, factor
    )
    ffn_fresh, ffn_moment, ffn_updated = shampoo(
        ffn_weights, ffn_stats, ffn_roots, ffn_momentum, ffn_square, factor
    )
    first_new, second_new, vec_updated = adam_step(
        vec_weights, vec_first, vec_second, vec_share, factor
    )
    return (
        out,
        in_grad,
        grad_norm,
        attn_fresh,
        attn_moment,
        attn_updated,
        ffn_fresh,
        ffn_moment,
        ffn_updated,
        first_new,
        second_new,
        vec_updated,
    )


MESH = pl.DeviceIdType.MESH
BF = jnp.bfloat16
F32 = jnp.float32
LEN = 512
ROWS = 16


def place():
    d = lax.axis_index("depth")
    i = lax.axis_index("dp")
    x = i % 2
    y = (i // 2) % 2
    nx = i + 1 - 2 * x
    ny = i + 2 - 4 * y
    na = ny + d * (nx - ny)
    nb = nx + d * (ny - nx)
    return dict(d=d, i=i, z=i // 4, c=i % 4, na=na, nb=nb, ca=na % 4, cb=nb % 4, cd=3 - i % 4)


def near(p):
    peers = [(p["d"], p["na"]), (p["d"], p["nb"]), (1 - p["d"], p["i"])]
    return peers + [(p["d"], ((p["z"] + k) % 4) * 4 + p["c"]) for k in (1, 2, 3)]


def greet(peers):
    barrier = pltpu.get_barrier_semaphore()
    for peer in peers:
        pl.semaphore_signal(barrier, inc=1, device_id=peer, device_id_type=MESH)


def meet(peers):
    pl.semaphore_wait(pltpu.get_barrier_semaphore(), len(peers))


def remote(src, dst, send, recv, k, dev):
    return pltpu.make_async_remote_copy(src_ref=src, dst_ref=dst, send_sem=send.at[k], recv_sem=recv.at[k],
                                        device_id=dev, device_id_type=MESH)


class Mail:
    def __init__(self, p, send, recv):
        self.p, self.send, self.recv, self.sent = p, send, recv, []

    def go(self, src, dst, k, dev):
        copy = remote(src, dst, self.send, self.recv, k, dev)
        copy.start()
        self.sent.append(copy)

    def wait(self, dst, k):
        remote(dst, dst, self.send, self.recv, k, (self.p["d"], self.p["na"])).wait_recv()

    def drain(self):
        for copy in self.sent:
            copy.wait_send()


class Spread:
    def __init__(self, p, a, b, to_a, to_b, own, slot, column, send, recv, local):
        d, z, i, c = p["d"], p["z"], p["i"], p["c"]
        ca, cb = a % 4, b % 4
        self.keep = pltpu.make_async_copy(own, slot(d, z, c), local)
        lines = [(own, slot(d, z, c), (d, ((z + k) % 4) * 4 + c)) for k in (1, 2, 3)]
        takes = [slot(d, (z + 4 - k) % 4, c) for k in (1, 2, 3)]
        mine, from_a, from_b, far = (column(d, col) for col in (c, ca, cb, p["cd"]))
        core = (1 - d, i)
        sends = [(mine, 3, (d, a)), (mine, 4, (d, b)), (from_a, 5, (d, b)), (mine, 6, core), (from_a, to_a, core),
                 (from_b, to_b, core), (far, 9, core)]
        self.lines = [remote(src, dst, send, recv, k, dev) for k, (src, dst, dev) in enumerate(lines)]
        self.taken = [remote(dst, dst, send, recv, k, (d, a)) for k, dst in enumerate(takes)]
        self.sends = [remote(src, src, send, recv, k, dev) for src, k, dev in sends]
        waits = [(from_a, 3), (from_b, 4), (far, 5), (column(1 - d, c), 6), (column(1 - d, ca), to_a),
                 (column(1 - d, cb), to_b), (column(1 - d, p["cd"]), 9)]
        self.came = [remote(dst, dst, send, recv, k, (d, a)) for dst, k in waits]

    def push(self, *which):
        for n in which:
            self.sends[n].start()

    def start(self):
        self.keep.start()
        for k in (1, 0, 2):
            self.lines[k].start()

    def second(self):
        self.keep.wait()
        for copy in self.taken:
            copy.wait_recv()
        self.push(0, 1, 3)

    def third(self):
        self.came[0].wait_recv()
        self.push(2, 4)

    def fourth(self):
        self.came[1].wait_recv()
        self.push(5)

    def fifth(self):
        self.came[2].wait_recv()
        self.push(6)

    def sixth(self):
        for copy in self.came[3:]:
            copy.wait_recv()

    def drain(self):
        for copy in self.lines + self.sends:
            copy.wait_send()


def spread_sems():
    return [pltpu.SemaphoreType.DMA((10,)), pltpu.SemaphoreType.DMA((10,)), pltpu.SemaphoreType.DMA]


def on_core(p, core, *steps):
    @pl.when(p["d"] == core)
    def _():
        for s in steps:
            s()


def at_step(m, value, *steps):
    @pl.when(m == value)
    def _():
        for s in steps:
            s()


def square_links(p):
    dx = p["i"] + 1 - 2 * (p["i"] % 2)
    dy = p["i"] + 2 - 4 * ((p["i"] // 2) % 2)
    return dx, dy


def quarter(w, q):
    return w.at[q // 2, pl.ds(2 * (q % 2), 2)]


def one_hot(shape, row, col):
    r = lax.broadcasted_iota(jnp.int32, shape, 0)
    c = lax.broadcasted_iota(jnp.int32, shape, 1)
    return (row(r) == col(c)).astype(F32)


def unfold_vec(pieces, vec, share):
    per = share // BLOCK
    stack = pieces[...][:, :, :, 0, :].reshape(32, pieces.shape[-1])
    units = sum(
        jnp.dot(one_hot((32 * per, 32), lambda u: u, lambda k, a=a: per * k + a), stack[:, a * BLOCK:(a + 1) * BLOCK],
                preferred_element_type=F32)
        for a in range(per)
    )
    for b in range(8):
        vec[:, b * BLOCK:(b + 1) * BLOCK] = jnp.dot(
            one_hot((ROWS, 32 * per), lambda r, b=b: 8 * r + b, lambda u: u), units, preferred_element_type=F32)


def dot_nn(a, b):
    return lax.dot_general(a, b, (((1,), (0,)), ((), ())), preferred_element_type=F32)


def dot_nt(a, b):
    return lax.dot_general(a, b, (((1,), (1,)), ((), ())), preferred_element_type=F32)


def dot_tn(a, b):
    return lax.dot_general(a, b, (((0,), (0,)), ((), ())), preferred_element_type=F32)


def square_of(value):
    return value.reshape(value.shape[0] * value.shape[1] * value.shape[2], value.shape[3])


def seq_rows(s):
    return pl.ds(s * LEN, LEN) if isinstance(s, int) else pl.ds(pl.multiple_of(s * LEN, LEN), LEN)


def tile_rows(s, size):
    return pl.ds(pl.multiple_of(s * size, size), size)


def served_flag(keep, routes, s):
    other = keep[0] * (routes[0] == routes[1]).astype(jnp.int32)
    return jnp.where(s == 0, keep[0], keep[1] * (1 - other))


def projections(x, ga, vec, q, k, v):
    width = x.shape[1]

    def tile(s, carry):
        rows = seq_rows(s)
        xr = x[rows]
        q[rows] = (dot_nn(xr, square_of(ga[0, 0:2])) + vec[0:1]).astype(BF)
        k[rows] = dot_nn(xr, square_of(ga[0, 2:4])).astype(BF)
        v[rows] = (dot_nn(xr, square_of(ga[1, 0:2])) + vec[1:2]).astype(BF)
        return carry

    lax.fori_loop(0, x.shape[0] // LEN, tile, 0)


def head_pairs(n, lens):
    s, g = n // 6, n % 6
    first = lax.broadcasted_iota(jnp.int32, (1, 128), 1) < 64
    return s, seq_rows(s), pl.ds(pl.multiple_of(g * 128, 128), 128), (first, jnp.logical_not(first))


def attend(n, q, k, v, lens, context, log_total):
    s, rows, cols, halves = head_pairs(n, lens)
    qp, kp, vp = q[rows, cols], k[rows, cols], v[rows, cols]
    seen = lax.broadcasted_iota(jnp.int32, (1, LEN), 1) < lens[s]
    found = []
    for h in range(2):
        qm = jnp.where(halves[h], qp, jnp.zeros_like(qp))
        scores = jnp.where(seen, dot_nt(qm, kp) * 0.125, masked_fill)
        peak = jnp.max(scores, axis=1, keepdims=True)
        expo = jnp.exp(scores - peak)
        total = jnp.sum(expo, axis=1, keepdims=True)
        found.append(dot_nn((expo * (1.0 / total)).astype(BF), vp))
        log_total[n, h] = (peak + jnp.log(total))[:, 0]
    context[rows, cols] = jnp.where(halves[0], found[0], found[1]).astype(BF)


def attend_back(n, q, k, v, grad_context, log_total, lens, gq, gk, gv):
    s, rows, cols, halves = head_pairs(n, lens)
    kp, vp = k[rows, cols], v[rows, cols]
    seen = lax.broadcasted_iota(jnp.int32, (LEN, 1), 0) < lens[s]
    ak = av = jnp.zeros((LEN, 128), F32)
    size = LEN // 2
    for t in range(2):
        part = tile_rows(2 * s + t, size)
        qp, gp = q[part, cols], grad_context[part, cols]
        aq = jnp.zeros((size, 128), F32)
        for h in range(2):
            qm, km, gm = (jnp.where(halves[h], t, jnp.zeros_like(t)) for t in (qp, kp, gp))
            scores = jnp.where(seen, dot_nt(kp, qm) * 0.125, masked_fill)
            probs = jnp.exp(scores - log_total[n, h][None, t * size:(t + 1) * size])
            grad_probs = dot_nt(vp, gm)
            along = jnp.sum(probs * grad_probs, axis=0, keepdims=True)
            grad_scores = (probs * (grad_probs - along)).astype(BF)
            av += dot_nn(probs.astype(BF), gm)
            ak += dot_nn(grad_scores, qm)
            aq += dot_tn(grad_scores, km)
        gq[part, cols] = (aq * 0.125).astype(BF)
    gk[rows, cols] = (ak * 0.125).astype(BF)
    gv[rows, cols] = av.astype(BF)


def mean_of(t):
    return jnp.mean(t, axis=-1, keepdims=True)


def attention_end(x, context, ga, vec, normed, factor):
    width = x.shape[1]

    def tile(s, carry):
        rows = seq_rows(s)
        attended = dot_nn(context[rows], square_of(ga[1, 2:4])) + vec[2:3]
        resid = x[rows].astype(F32) + attended
        center = resid - mean_of(resid)
        scale = lax.rsqrt(mean_of(center * center) + norm_floor)
        normed[rows] = center * scale
        factor[rows] = scale
        return carry

    lax.fori_loop(0, x.shape[0] // LEN, tile, 0)


def vec_part(vec, n):
    return vec[n:n + 1]


def input_gradient(x, cot, ga, grad_resid, keep, routes, gq, gk, gv, in_grad):
    def tile(s, carry):
        rows = tile_rows(s, LEN // 2)
        total = grad_resid[rows] + dot_nt(gq[rows], square_of(ga[0, 0:2]))
        total += dot_nt(gk[rows], square_of(ga[0, 2:4]))
        total += dot_nt(gv[rows], square_of(ga[1, 0:2]))
        in_grad[rows] = jnp.where(served_flag(keep, routes, s // 2) > 0, total.astype(BF), cot[rows])
        return carry

    lax.fori_loop(0, 2 * x.shape[0] // LEN, tile, 0)


def gather_attention_kernel(aw, fw, vw, x, lens, gf, ga_out, vec, q_out, k_out, v_out, context_out, log_total, normed_out, factor,
                            active_out, slope_out,
                            ga, gv, strip, pair, own, q, k, v, context, normed, low, w1, active, slope, store, wload, *sems):
    p = place()
    peers = near(p)
    greet(peers)
    share = vw.shape[0]
    own[...] = jnp.zeros_like(own)
    own[0:1, 0:share] = vw[...].astype(BF).astype(F32).reshape(1, share)
    for b in range(8):
        strip[:, b * BLOCK:(b + 1) * BLOCK] = aw[b].astype(BF)
    for j in range(2):
        for b in range(8):
            pair[j, :, b * BLOCK:(b + 1) * BLOCK] = fw[8 * j + b].astype(BF)
    half = BLOCK // 2
    seqs = x.shape[0] // LEN
    dx, dy = square_links(p)
    both = (p["na"], p["nb"], 8 - p["d"], 7 + p["d"])

    def attn_part(h):
        rows = pl.ds(h * half, half)
        return both + (strip.at[rows], lambda d, z, c: ga.at[d, z, c, rows], lambda d, c: ga.at[d, :, c, rows])

    def feed_part(j):
        links = (dy, dx, 8, 7) if j == 0 else (dx, dy, 7, 8)
        return links + (pair.at[j], lambda d, z, c: gf.at[d, z, c, j], lambda d, c: gf.at[d, :, c, j])

    vec_piece = both + (own, lambda d, z, c: gv.at[d, z, c], lambda d, c: gv.at[d, :, c])
    parts = [attn_part(0), vec_piece, attn_part(1), feed_part(0), feed_part(1)]
    a0, w, a1, f0, f1 = every = [Spread(p, *part, *sems[3 * n:3 * n + 3]) for n, part in enumerate(parts)]
    meet(peers)
    for s in (a0, w, a1):
        s.start()
    on_core(p, 0, f0.start, f1.start)
    a0.second()
    w.second()
    a1.second()
    for s in (a0, w, a1):
        s.third()
        s.fourth()
    on_core(p, 0, f0.second, f1.second)
    on_core(p, 1, f0.start, f1.start)
    for s in (a0, w, a1):
        s.fifth()
    w.sixth()
    unfold_vec(gv, vec, share)
    a0.sixth()
    a1.sixth()
    stores = [pltpu.make_async_copy(src, dst, store.at[n])
              for n, (src, dst) in enumerate(((q, q_out), (k, k_out), (v, v_out), (context, context_out), (normed, normed_out),
                                              (ga, ga_out)))]
    stores[5].start()
    projections(x, ga, vec, q, k, v)
    for copy in stores[:3]:
        copy.start()

    def step(n, carry):
        attend(n, q, k, v, lens, context, log_total)
        at_step(n, 3, lambda: on_core(p, 0, f0.third, f1.third, f0.fourth, f1.fourth))
        at_step(n, 4, lambda: on_core(p, 1, f0.second, f1.second))
        at_step(n, 9, lambda: on_core(p, 0, f0.fifth, f1.fifth))
        return carry

    lax.fori_loop(0, 12, step, 0)
    stores[3].start()
    attention_end(x, context, ga, vec, normed, factor)
    stores[4].start()
    on_core(p, 1, f0.sixth, f1.sixth)

    def fetch(t, carry):
        n, s = t // 8, t % 8
        pltpu.make_async_copy(gf.at[0, s // 2, 2 * (s % 2) + n // 2, n % 2], w1.at[n // 2, 2 * (n % 2) + s // 4, s % 4],
                              wload.at[n]).start()
        return carry

    lax.fori_loop(0, 32, fetch, 0)

    def lower(s, carry):
        rows = seq_rows(s)
        low[rows] = (normed[rows] * vec_part(vec, 8) + vec_part(vec, 9)).astype(BF)
        return carry

    lax.fori_loop(0, seqs, lower, 0)

    def enter(n, carry):
        pltpu.make_async_copy(quarter(w1, n), quarter(w1, n), wload.at[n]).wait()

        def tile(s, inner):
            rows = seq_rows(s)
            before = dot_nn(low[rows], square_of(quarter(w1, n)[...])) + vec[pl.ds(3 + n, 1)]
            cumulative = 0.5 * (1.0 + lax.erf(before * (1.0 / math.sqrt(2.0))))
            active[n, rows] = (before * cumulative).astype(BF)
            density = jnp.exp(-0.5 * before * before) * (1.0 / math.sqrt(2.0 * math.pi))
            slope[n, rows] = (cumulative + before * density).astype(BF)
            return inner

        lax.fori_loop(0, seqs, tile, 0)
        pltpu.make_async_copy(active.at[n], active_out.at[n], store.at[6 + n]).start()
        pltpu.make_async_copy(slope.at[n], slope_out.at[n], store.at[10 + n]).start()
        at_step(n, 1, lambda: on_core(p, 1, f0.third, f1.third, f0.fourth, f1.fourth))
        return carry

    lax.fori_loop(0, 4, enter, 0)
    on_core(p, 1, f0.fifth, f1.fifth)
    on_core(p, 0, f0.sixth, f1.sixth)
    for s in every:
        s.drain()
    for copy in stores:
        copy.wait()
    for n in range(4):
        pltpu.make_async_copy(active.at[n], active_out.at[n], store.at[6 + n]).wait()
        pltpu.make_async_copy(slope.at[n], slope_out.at[n], store.at[10 + n]).wait()


def gather_attention(aw, fw, vw, x, lens):
    tokens, width = x.shape
    low = jax.ShapeDtypeStruct(x.shape, BF)
    four = jax.ShapeDtypeStruct((4, tokens, width), BF)
    outs = [jax.ShapeDtypeStruct((2, 4, 4, 2, BLOCK, width), BF), jax.ShapeDtypeStruct((2, 4, 4, BLOCK, width), BF),
            jax.ShapeDtypeStruct((ROWS, width), F32)] + [low] * 4
    outs += [jax.ShapeDtypeStruct((12, 2, LEN), F32), jax.ShapeDtypeStruct(x.shape, F32),
             jax.ShapeDtypeStruct((tokens, 1), F32), four, four]
    vmem = pl.BlockSpec(memory_space=pltpu.VMEM)
    hbm = pl.BlockSpec(memory_space=pl.ANY)
    strips = pltpu.VMEM((2, 4, 4, BLOCK, width), BF)
    rows = pltpu.VMEM(x.shape, BF)
    wide = pltpu.VMEM((4, tokens, width), BF)
    return pl.pallas_call(
        gather_attention_kernel,
        out_shape=outs,
        in_specs=[vmem] * 4 + [pl.BlockSpec(memory_space=pltpu.SMEM)],
        out_specs=[hbm, hbm, vmem] + [hbm] * 4 + [vmem, hbm, vmem, hbm, hbm],
        scratch_shapes=[strips, pltpu.VMEM((2, 4, 4, 8, 384), F32), pltpu.VMEM((BLOCK, width), BF),
                        pltpu.VMEM((2, BLOCK, width), BF), pltpu.VMEM((8, 384), F32)]
        + [rows] * 4 + [pltpu.VMEM(x.shape, F32), rows, strips, wide, wide,
                        pltpu.SemaphoreType.DMA((14,)), pltpu.SemaphoreType.DMA((4,))]
        + spread_sems() * 5,
        compiler_params=pltpu.CompilerParams(collective_id=0, has_side_effects=True, vmem_limit_bytes=62 << 20),
        name="gather_attention",
    )(aw, fw, vw, x, lens)


def fold_scratch(width):
    shape = (BLOCK, width)
    return [pltpu.VMEM((4, 4) + shape, BF), pltpu.VMEM((4,) + shape, BF), pltpu.VMEM((4,) + shape, BF),
            pltpu.VMEM((4,) + shape, BF), pltpu.VMEM((3,) + shape, BF),
            pltpu.SemaphoreType.DMA((10,)), pltpu.SemaphoreType.DMA((10,))]


class Total(Mail):
    def __init__(self, p, held, came, send, recv):
        Mail.__init__(self, p, send, recv)
        self.held, self.came = held, came
        self.peers = ((1 - p["d"], p["i"]), (p["d"], p["na"]), (p["d"], p["nb"]))

    def start(self):
        self.go(self.held.at[0], self.came.at[0], 0, self.peers[0])

    def hop(self, n):
        p = self.p
        self.wait(self.came.at[n], n)
        self.held[n + 1] = self.held[n] + self.came[n]
        if n < 2:
            self.go(self.held.at[n + 1], self.came.at[n + 1], n + 1, self.peers[n + 1])
        else:
            for k in (1, 2, 3):
                self.go(self.held.at[3], self.came.at[2 + k], 2 + k, (p["d"], ((p["z"] + k) % 4) * 4 + p["c"]))

    def end(self):
        total = self.held[3]
        for k in (1, 2, 3):
            self.wait(self.came.at[2 + k], 2 + k)
            total += self.came[2 + k]
        return total


def own_share(p, rows, out, share):
    per = share // BLOCK
    me = p["d"] * 16 + p["i"]
    units = sum(
        jnp.dot(one_hot((8, ROWS), lambda a: per * me + jnp.where(a < per, a, -8 * 32 * per), lambda r, b=b: 8 * r + b),
                rows[:, b * BLOCK:(b + 1) * BLOCK], precision=lax.Precision.HIGHEST, preferred_element_type=F32)
        for b in range(8)
    )
    for a in range(per):
        out[0:1, a * BLOCK:(a + 1) * BLOCK] = units[a:a + 1]


def everyone(p):
    me = p["d"] * 16 + p["i"]

    def other(k):
        t = (me + k) % 32
        return (t // 16, t % 16)

    return me, other


def greet_all(p):
    me, other = everyone(p)
    barrier = pltpu.get_barrier_semaphore()

    def one(k, carry):
        pl.semaphore_signal(barrier, inc=1, device_id=other(k), device_id_type=MESH)
        return carry

    lax.fori_loop(1, 32, one, 0)


def meet_all():
    pl.semaphore_wait(pltpu.get_barrier_semaphore(), 31)


def norm_sum(p, square, slots, send, recv):
    me, other = everyone(p)
    slots[me] = jnp.full((8, 128), square, F32)
    to = lambda k, slot: remote(slots.at[slot], slots.at[slot], send, recv, slot, other(k))

    def push(k, carry):
        remote(slots.at[me], slots.at[me], send.at[pl.ds(k, 1)], recv.at[pl.ds(me, 1)], 0, other(k)).start()
        return carry

    def take(k, carry):
        slot = (me + k) % 32
        remote(slots.at[slot], slots.at[slot], send.at[pl.ds(k, 1)], recv.at[pl.ds(slot, 1)], 0, other(k)).wait_recv()
        return carry

    def done(k, carry):
        remote(slots.at[me], slots.at[me], send.at[pl.ds(k, 1)], recv.at[pl.ds(me, 1)], 0, other(k)).wait_send()
        return carry

    lax.fori_loop(1, 32, push, 0)
    lax.fori_loop(1, 32, take, 0)
    total = jnp.sum(slots[...], axis=0)[0:1, 0:1]
    lax.fori_loop(1, 32, done, 0)
    return total


class Fold:
    def __init__(self, p, a, b, away, home, pair, diag, flat, late, line, send, recv):
        self.p, self.home, self.pair, self.diag, self.flat, self.late, self.line = p, home, pair, diag, flat, late, line
        self.ca, self.cb = a % 4, b % 4
        d, z, c = p["d"], p["z"], p["c"]
        self.away, self.send, self.recv, self.core = away, send, recv, (1 - d, p["i"])
        pieces = [(pair.at[:, p["cd"]], diag, (d, b)), (pair.at[:, self.cb], flat, (d, b)),
                  (pair.at[:, self.ca], late, (d, a))]
        pieces += [(pair.at[(z + k) % 4, c], line.at[k - 1], (d, ((z + k) % 4) * 4 + c)) for k in (1, 2, 3)]
        self.copies = [None] + [remote(src, dst, send, recv, n, dev) for n, (src, dst, dev) in enumerate(pieces)]

    def part(self, z):
        return pltpu.make_async_remote_copy(
            src_ref=self.away.at[z], dst_ref=self.pair.at[z], send_sem=self.send.at[6 + z], recv_sem=self.recv.at[6 + z],
            device_id=self.core, device_id_type=MESH)

    def add(self, dst, *others):
        total = dst[...].astype(F32)
        for o in others:
            total += o[...].astype(F32)
        dst[...] = total.astype(dst.dtype)

    def column_part(self, c):
        return pltpu.make_async_remote_copy(
            src_ref=self.away.at[:, c], dst_ref=self.pair.at[:, c], send_sem=self.send.at[6 + c], recv_sem=self.recv.at[6 + c],
            device_id=self.core, device_id_type=MESH)

    def start(self):
        for z in range(4):
            self.part(z).start()

    def second(self):
        for z in range(4):
            self.part(z).wait_recv()
        for col, n in ((self.p["cd"], 1), (self.cb, 2)):
            self.add(self.pair.at[:, col], self.home.at[:, col])
            self.copies[n].start()
        for col in (self.ca, self.p["c"]):
            self.add(self.pair.at[:, col], self.home.at[:, col])

    def third(self):
        self.copies[1].wait_recv()
        self.add(self.pair.at[:, self.ca], self.diag)
        self.copies[3].start()

    def fourth(self):
        p = self.p
        self.copies[2].wait_recv()
        self.copies[3].wait_recv()
        for k in (2, 1, 3, 0):
            dst = (p["z"] + k) % 4
            self.add(self.pair.at[dst, p["c"]], self.flat.at[dst], self.late.at[dst])
            if k:
                self.copies[3 + k].start()

    def fifth(self, out):
        p = self.p
        total = self.pair[p["z"], p["c"]].astype(F32)
        for k in (1, 2, 3):
            self.copies[3 + k].wait_recv()
            total += self.line[k - 1].astype(F32)
        out[...] = total

    def drain(self):
        for copy in self.copies[1:] + [self.part(z) for z in range(4)]:
            copy.wait_send()


def layer_back_kernel(x_in, cot_in, normed_in, active_in, slope_in, factor, gf, ga, q_in, k_in, v_in, context_in, log_total, vec, lens, keep, routes,
                      out, in_grad, sf, sa, sv, norm,
                      x, cot, normed, middle, low, grad_low, image, w1, w2, active, slope, hf, gvec, held, came, slots,
                      load, wload, nsend, nrecv, tsend, trecv, *scratch):
    p = place()
    greet_all(p)
    tokens, width = x.shape
    seqs = tokens // LEN
    half = width // 2
    lanes = (pl.ds(0, half), pl.ds(half, half))

    def bring(src, dst, n):
        return pltpu.make_async_copy(src, dst, load.at[n])

    quarters = [bring(active_in.at[q], active.at[q], q) for q in range(4)]
    others = [bring(normed_in, normed, 4), bring(x_in, x, 5), bring(cot_in, cot, 6)]
    slopes = bring(slope_in, slope, 7)

    def fetch_down(t, carry):
        q, s = t // 8, t % 8
        pltpu.make_async_copy(gf.at[1, q, s // 2, s % 2], w2.at[q // 2, 2 * (q % 2) + s // 4, s % 4], wload.at[q]).start()
        return carry

    def fetch(t, carry):
        q, s = t // 8, t % 8
        pltpu.make_async_copy(gf.at[0, s // 2, 2 * (s % 2) + q // 2, q % 2], w1.at[q // 2, 2 * (q % 2) + s // 4, s % 4],
                              wload.at[4]).start()
        return carry

    for q in range(4):
        quarters[q].start()
        lax.fori_loop(8 * q, 8 * q + 8, fetch_down, 0)
    for copy in others:
        copy.start()
    slopes.start()
    lax.fori_loop(0, 32, fetch, 0)
    dx, dy = square_links(p)
    f0 = Fold(p, dy, dx, hf.at[1 - p["d"], :, :, 0], hf.at[p["d"], :, :, 0], *scratch[0:7])
    f1 = Fold(p, dx, dy, hf.at[1 - p["d"], :, :, 1], hf.at[p["d"], :, :, 1], *scratch[7:14])
    ha, ga_in = w1, w2
    a0, a1 = [Fold(p, p["na"], p["nb"], ha.at[1 - p["d"], :, :, :, lanes[n]], ha.at[p["d"], :, :, :, lanes[n]],
                   *scratch[14 + 7 * n:21 + 7 * n]) for n in range(2)]
    total = Total(p, held, came, tsend, trecv)

    def on(core, *steps):
        on_core(p, core, *steps)

    gvec[...] = jnp.zeros_like(gvec)

    def add_vec(n, value):
        gvec[n:n + 1] += value

    for q in range(4):
        quarters[q].wait()
        pltpu.make_async_copy(quarter(w2, q), quarter(w2, q), wload.at[q]).wait()

        def gain(s, carry):
            rows = seq_rows(s)
            found = dot_nn(active[q, rows], square_of(quarter(w2, q)[...]))
            middle[rows] = found if q == 0 else middle[rows] + found
            return carry

        lax.fori_loop(0, seqs, gain, 0)
    for copy in others:
        copy.wait()
    tile = LEN // 2

    def leave(t, carry):
        rows = tile_rows(t, tile)
        show = pltpu.make_async_copy(image, out.at[rows], load.at[14])
        hidden = normed[rows] * vec_part(vec, 8) + vec_part(vec, 9)
        low[rows] = hidden.astype(BF)
        resid = hidden + (middle[rows] + vec_part(vec, 7))
        center = resid - mean_of(resid)
        scale = lax.rsqrt(mean_of(center * center) + norm_floor)
        second = center * scale
        served = served_flag(keep, routes, t // 2) > 0
        result = second * vec_part(vec, 10) + vec_part(vec, 11)
        image[...] = jnp.where(served, result.astype(BF), x[rows])
        show.start()
        grad = jnp.where(served, cot[rows].astype(F32), 0.0)
        add_vec(10, jnp.sum(grad * second, axis=0, keepdims=True))
        add_vec(11, jnp.sum(grad, axis=0, keepdims=True))
        grad = grad * vec_part(vec, 10)
        grad = scale * (grad - mean_of(grad) - second * mean_of(grad * second))
        middle[rows] = grad
        grad_low[rows] = grad.astype(BF)
        add_vec(7, jnp.sum(grad.astype(BF).astype(F32), axis=0, keepdims=True))
        show.wait()
        return carry

    lax.fori_loop(0, 2 * seqs, leave, 0)
    meet_all()

    def down_grad(t, carry):
        q, h = t // 2, t % 2
        found = dot_tn(active[q, :, pl.ds(pl.multiple_of(h * half, half), half)], grad_low[...])
        hf[1, q, pl.ds(2 * h, 2)] = found.astype(BF).reshape(2, 2, BLOCK, width)
        at_step(h, 1, lambda: on(0, lambda: f0.part(q).start(), lambda: f1.part(q).start()))
        return carry

    lax.fori_loop(0, 8, down_grad, 0)
    again = [bring(src, slope.at[n], 8 + n) for n, src in enumerate((context_in, q_in, k_in, v_in))]
    context, qs, ks, vs = (slope.at[n] for n in range(4))
    slopes.wait()

    def turn(q, carry):
        def part(s, inner):
            rows = seq_rows(s)
            back = dot_nt(grad_low[rows], square_of(quarter(w2, q)[...])) * slope[q, rows].astype(F32)
            active[q, rows] = back.astype(BF)
            gvec[pl.ds(3 + q, 1)] += jnp.sum(back.astype(BF).astype(F32), axis=0, keepdims=True)
            return inner

        def up_grad(h, inner):
            found = dot_tn(low[:, pl.ds(pl.multiple_of(h * half, half), half)], active[q]).astype(BF).reshape(2, 2, BLOCK, width)
            for y in range(2):
                hf[0, pl.ds(2 * h, 2), 2 * y + q // 2, q % 2] = found[:, y]
            return inner

        lax.fori_loop(0, seqs, part, 0)
        lax.fori_loop(0, 2, up_grad, 0)
        at_step(q, 0, lambda: on(1, f0.second, f1.second))
        for j, f in enumerate((f0, f1)):
            at_step(q % 2, j, lambda f=f: on(1, lambda: f.column_part(q // 2).start(), lambda: f.column_part(2 + q // 2).start()))
        at_step(q, 2, lambda: on(1, f0.third))
        at_step(q, 3, lambda: on(1, f1.third))
        return carry

    lax.fori_loop(0, 4, turn, 0)
    for copy in again:
        copy.start()
    pltpu.make_async_copy(w1, w1, wload.at[4]).wait()
    square_in = bring(ga, ga_in, 12)
    square_in.start()

    def close(t, carry):
        rows = tile_rows(t, tile)
        grad = middle[rows]
        for q in range(4):
            grad += dot_nt(active[q, rows], square_of(quarter(w1, q)[...]))
        head = normed[rows]
        add_vec(8, jnp.sum(grad * head, axis=0, keepdims=True))
        add_vec(9, jnp.sum(grad, axis=0, keepdims=True))
        grad = grad * vec_part(vec, 8)
        grad = factor[rows] * (grad - mean_of(grad) - head * mean_of(grad * head))
        middle[rows] = grad
        grad_low[rows] = grad.astype(BF)
        return carry

    lax.fori_loop(0, seqs, close, 0)
    on(0, f0.second)
    lax.fori_loop(seqs, 2 * seqs, close, 0)
    on(1, f0.fourth)
    on(0, f1.second)
    gq, gk, gv, grad_context = (active.at[n] for n in range(4))
    square_in.wait()
    again[0].wait()

    def open_attention(s, carry):
        rows = seq_rows(s)
        grad_context[rows] = dot_nt(grad_low[rows], square_of(ga_in[1, 2:4])).astype(BF)
        return carry

    lax.fori_loop(0, seqs, open_attention, 0)
    held[0] = gvec[...]
    held[0, 2:3] = jnp.sum(grad_low[...].astype(F32), axis=0, keepdims=True)
    for h in range(2):
        ha[1, 2 + h] = dot_tn(context[:, h * half:(h + 1) * half], grad_low[...]).astype(BF).reshape(4, BLOCK, width)
    on(1, f1.fourth)
    for copy in again[1:]:
        copy.wait()

    def step(m, carry):
        n = ((m % 6) // 3) * 6 + (m // 6) * 3 + m % 3
        attend_back(n, qs, ks, vs, grad_context, log_total, lens, gq, gk, gv)
        at_step(m, 0, lambda: on(0, f0.third))
        at_step(m, 1, lambda: on(0, f1.third))
        at_step(m, 5, lambda: weight_grads(0), a0.start, lambda: on(0, f0.fourth))
        at_step(m, 6, lambda: on(0, f1.fourth))
        at_step(m, 7, a0.second)
        at_step(m, 10, a0.third)
        at_step(m, 11, lambda: weight_grads(1))
        return carry

    def weight_grads(n):
        cols = lanes[n]
        for dst, src in ((ha.at[0, 0:2], gq), (ha.at[0, 2:4], gk), (ha.at[1, 0:2], gv)):
            dst[:, :, :, cols] = dot_tn(x[...], src[:, cols]).astype(BF).reshape(2, 4, BLOCK, half)

    lax.fori_loop(0, 12, step, 0)
    a1.start()
    held[0, 0:1] = jnp.sum(gq[...].astype(F32), axis=0, keepdims=True)
    held[0, 1:2] = jnp.sum(gv[...].astype(F32), axis=0, keepdims=True)
    total.start()
    a1.second()
    a0.fourth()
    total.hop(0)
    input_gradient(x, cot, ga_in, middle, keep, routes, gq, gk, gv, cot)
    last = bring(cot, in_grad, 13)
    last.start()
    a1.third()
    total.hop(1)
    total.hop(2)
    f0.fifth(sf.at[0])
    f1.fifth(sf.at[1])
    square = jnp.sum(sf[...] * sf[...])
    a1.fourth()
    held[4] = total.end()
    sv[...] = jnp.zeros_like(sv)
    own_share(p, held[4], sv, 12 * width // 32)
    a0.fifth(sa.at[:, lanes[0]])
    a1.fifth(sa.at[:, lanes[1]])
    square += jnp.sum(sa[...] * sa[...]) + jnp.sum(sv[...] * sv[...])
    found = norm_sum(p, square, slots, nsend, nrecv)
    norm[...] = jnp.sqrt(found)
    for s in (f0, f1, a0, a1, total):
        s.drain()
    last.wait()


def layer_back(x, cot, normed, active, slope, factor, gf, ga, q, k, v, context, log_total, vec, lens, keep, routes):
    tokens, width = x.shape
    outs = [jax.ShapeDtypeStruct(x.shape, BF), jax.ShapeDtypeStruct(x.shape, BF), jax.ShapeDtypeStruct((2, BLOCK, width), F32),
            jax.ShapeDtypeStruct((BLOCK, width), F32), jax.ShapeDtypeStruct((8, 384), F32), jax.ShapeDtypeStruct((1, 1), F32)]
    dma = pltpu.SemaphoreType.DMA
    rows = pltpu.VMEM(x.shape, BF)
    wide = pltpu.VMEM(x.shape, F32)
    strips = pltpu.VMEM(ga.shape, BF)
    scratch = [rows, rows, wide, wide, rows, rows, pltpu.VMEM((LEN // 2, width), BF), strips, strips,
               pltpu.VMEM((4, tokens, width), BF), pltpu.VMEM((4, tokens, width), BF), pltpu.VMEM(gf.shape, BF),
               pltpu.VMEM(vec.shape, F32), pltpu.VMEM((5, ROWS, width), F32), pltpu.VMEM((6, ROWS, width), F32),
               pltpu.VMEM((32, 8, 128), F32),
               dma((15,)), dma((5,)), dma((32,)), dma((32,)), dma((6,)), dma((6,))]
    scratch += fold_scratch(width) * 2 + fold_scratch(width // 2) * 2
    vmem = pl.BlockSpec(memory_space=pltpu.VMEM)
    smem = pl.BlockSpec(memory_space=pltpu.SMEM)
    hbm = pl.BlockSpec(memory_space=pl.ANY)
    return pl.pallas_call(
        layer_back_kernel,
        out_shape=outs,
        in_specs=[hbm] * 5 + [vmem] + [hbm] * 6 + [vmem] * 2 + [smem] * 3,
        out_specs=[hbm] * 2 + [vmem] * 4,
        scratch_shapes=scratch,
        compiler_params=pltpu.CompilerParams(collective_id=1, has_side_effects=True, vmem_limit_bytes=67043328),
        name="feed_and_back",
    )(x, cot, normed, active, slope, factor, gf, ga, q, k, v, context, log_total, vec, lens, keep, routes)


def halves_of(t):
    high = t.astype(BF)
    return high, (t - high.astype(F32)).astype(BF)


def exact_dot(a, b, dims):
    dot = lambda x, y: lax.dot_general(x, y, (dims, ((), ())), preferred_element_type=F32)
    return dot(a[0], b[0]) + (dot(a[0], b[1]) + dot(a[1], b[0]))


def shampoo_block(grad, w, st, ro, mo, st_new, mo_new, w_new, b, factor):
    clipped = grad * factor
    moment = momentum_decay * mo[b] + clipped
    both = halves_of(clipped)
    left = exact_dot(both, both, ((1,), (1,)))
    right = exact_dot(both, both, ((0,), (0,)))
    st_new[b, 0] = stat_decay * st[b, 0] + (1.0 - stat_decay) * left
    st_new[b, 1] = stat_decay * st[b, 1] + (1.0 - stat_decay) * right
    mo_new[b] = moment
    turned = exact_dot(halves_of(ro[b, 0]), halves_of(moment), ((1,), (0,)))
    turned = exact_dot(halves_of(turned), halves_of(ro[b, 1]), ((1,), (0,)))
    w_new[b] = w[b] - matrix_rate * (turned + matrix_decay * w[b])


def optimizer_kernel(norm, sa, sf, sv, aw, ast, ar, am, fw, fst, fr, fm, vw, v1, v2, rows, grads,
                     rows_n, grads_n, ast_n, am_n, aw_n, fst_n, fm_n, fw_n, v1_n, v2_n, vw_n, ga, gf):
    factor = clip_bound / jnp.maximum(norm[...], clip_bound)
    g = pl.program_id(0)
    many = aw.shape[0]
    rows_n[...] = rows[...]
    grads_n[...] = grads[...]

    @pl.when(g == 0)
    def _():
        for b in range(8):
            ga[b] = sa[:, b * BLOCK:(b + 1) * BLOCK]
            for j in range(2):
                gf[8 * j + b] = sf[j, :, b * BLOCK:(b + 1) * BLOCK]
        size = vw.shape[0]
        clipped = (sv[0:1, 0:size] * factor)[0]
        first_new = first_decay * v1[...] + (1.0 - first_decay) * clipped
        second_new = second_decay * v2[...] + (1.0 - second_decay) * clipped * clipped
        first_hat = first_new / (1.0 - first_decay**STEP)
        second_hat = second_new / (1.0 - second_decay**STEP)
        v1_n[...] = first_new
        v2_n[...] = second_new
        vw_n[...] = vw[...] - vector_rate * first_hat / (jnp.sqrt(second_hat) + adam_floor)

    for b in range(many):
        shampoo_block(ga[g * many + b], aw, ast, ar, am, ast_n, am_n, aw_n, b, factor)
    for b in range(2 * many):
        shampoo_block(gf[g * 2 * many + b], fw, fst, fr, fm, fst_n, fm_n, fw_n, b, factor)


def optimizer(norm, sa, sf, sv, aw, ast, ar, am, fw, fst, fr, fm, vw, v1, v2, rows, grads):
    many = 1

    def steps(t, n):
        shape = (n,) + t.shape[1:]
        return pl.BlockSpec(shape, lambda g: (g,) + (0,) * (len(shape) - 1))

    def whole(t):
        return pl.BlockSpec(t.shape, lambda g: (0,) * t.ndim)

    like = lambda t: jax.ShapeDtypeStruct(t.shape, t.dtype)
    args = (norm, sa, sf, sv, aw, ast, ar, am, fw, fst, fr, fm, vw, v1, v2, rows, grads)
    part = rows.shape[0] * many // aw.shape[0]
    specs = [whole(t) for t in args[:4]]
    specs += [steps(t, many) for t in (aw, ast, ar, am)] + [steps(t, 2 * many) for t in (fw, fst, fr, fm)]
    specs += [whole(t) for t in (vw, v1, v2)] + [steps(t, part) for t in (rows, grads)]
    outs = (rows, grads, ast, am, aw, fst, fm, fw, v1, v2, vw)
    return pl.pallas_call(
        optimizer_kernel,
        out_shape=[like(t) for t in outs],
        grid=(aw.shape[0] // many,),
        in_specs=specs,
        out_specs=[steps(t, part) for t in outs[:2]] + [steps(t, many) for t in outs[2:5]] + [steps(t, 2 * many) for t in outs[5:8]]
        + [whole(t) for t in outs[8:]],
        scratch_shapes=[pltpu.VMEM(aw.shape, F32), pltpu.VMEM(fw.shape, F32)],
        name="optimizer",
    )(*args)


def per_device(
    inputs,
    output_gradient,
    keep,
    lengths,
    routes,
    attn_weights,
    attn_stats,
    attn_roots,
    attn_momentum,
    ffn_weights,
    ffn_stats,
    ffn_roots,
    ffn_momentum,
    vec_weights,
    vec_first,
    vec_second,
):
    slots, seq_len, width = inputs.shape
    tokens = slots * seq_len
    x = inputs.reshape(tokens, width)
    cot = output_gradient.reshape(tokens, width)
    gf, ga, vec, q, k, v, context, log_total, normed, factor, active, slope = gather_attention(attn_weights, ffn_weights, vec_weights, x, lengths)
    out, in_grad, sf, sa, sv, norm = layer_back(
        x, cot, normed, active, slope, factor, gf, ga, q, k, v, context, log_total, vec, lengths, keep, routes
    )
    out, in_grad, *rest = optimizer(
        norm, sa, sf, sv,
        attn_weights, attn_stats, attn_roots, attn_momentum,
        ffn_weights, ffn_stats, ffn_roots, ffn_momentum,
        vec_weights, vec_first, vec_second, out, in_grad,
    )
    return (out.reshape(inputs.shape), in_grad.reshape(inputs.shape), norm.reshape(()), *rest)


def solution(mesh):
    small = mesh.shape["depth"] == 2 and mesh.shape["dp"] == 16
    return jax.shard_map(
        per_device if small else per_device_general,
        mesh=mesh,
        in_specs=(
            P(("depth", "dp"), None, None),
            P(("depth", "dp"), None, None),
            P(("depth", "dp")),
            P(("depth", "dp")),
            P(("depth", "dp")),
            P(("depth", "dp"), None, None),
            P(("depth", "dp"), None, None, None),
            P(("depth", "dp"), None, None, None),
            P(("depth", "dp"), None, None),
            P(("depth", "dp"), None, None),
            P(("depth", "dp"), None, None, None),
            P(("depth", "dp"), None, None, None),
            P(("depth", "dp"), None, None),
            P(("depth", "dp")),
            P(("depth", "dp")),
            P(("depth", "dp")),
        ),
        out_specs=(
            P(("depth", "dp"), None, None),
            P(("depth", "dp"), None, None),
            P(),
            P(("depth", "dp"), None, None, None),
            P(("depth", "dp"), None, None),
            P(("depth", "dp"), None, None),
            P(("depth", "dp"), None, None, None),
            P(("depth", "dp"), None, None),
            P(("depth", "dp"), None, None),
            P(("depth", "dp")),
            P(("depth", "dp")),
            P(("depth", "dp")),
        ),
        check_vma=False,
    )
```
